32 devices in a mesh: seq: 4 (over y, x), fsdp: 8 (over z, core).
Axes of the slice: x: 2, y: 2, z: 4, core: 2. Of those that a mesh axis runs over, the one named last changes fastest.
Arguments:
- tokens: bfloat16 [8, 512, 1024], P('fsdp', 'seq'), may hold values from -6 to 6
- lengths: int32 [8, 3], P('fsdp'), may hold values from 1 to 384, 512 in all within a row
- w_qkv: bfloat16 [1024, 3072], P('fsdp', 'seq'), may hold values from -0.1875 to 0.1875
- w_out: bfloat16 [1024, 1024], P('fsdp', 'seq'), may hold values from -0.1875 to 0.1875
- w_uv: bfloat16 [1024, 8192], P('fsdp', 'seq'), may hold values from -0.1875 to 0.1875
- w_down: bfloat16 [4096, 1024], P('fsdp', 'seq'), may hold values from -0.09375 to 0.09375
- s_qk: bfloat16 [1024], P('fsdp'), may hold values from 0.8984375 to 1.796875
- alpha_a: bfloat16 [1024], P('fsdp'), may hold values from 0.099609375 to 0.59765625
- s_u: bfloat16 [4096], P('fsdp'), may hold values from 0.5 to 2
- s_v: bfloat16 [4096], P('fsdp'), may hold values from 0.5 to 2
- alpha_m: bfloat16 [1024], P('fsdp'), may hold values from 0.099609375 to 0.59765625
- cotangent: bfloat16 [8, 512, 1024], P('fsdp', 'seq'), may hold values from -6 to 6
Outputs:
- output: bfloat16 [8, 512, 1024], P('fsdp', 'seq')
- input_grad: float32 [8, 512, 1024], P('fsdp', 'seq')
- grad_w_qkv: float32 [1024, 3072], P('fsdp', 'seq')
- grad_w_out: float32 [1024, 1024], P('fsdp', 'seq')
- grad_w_uv: float32 [1024, 8192], P('fsdp', 'seq')
- grad_w_down: float32 [4096, 1024], P('fsdp', 'seq')
- grad_s_qk: float32 [1024], P('fsdp')
- grad_alpha_a: float32 [1024], P('fsdp')
- grad_s_u: float32 [4096], P('fsdp')
- grad_s_v: float32 [4096], P('fsdp')
- grad_alpha_m: float32 [1024], P('fsdp')
The draws below stay inside these ranges and needn't reach their ends.
Inputs may be any that keep to these rules, and one draw needn't show every extreme that they name: In each row the first 2 entries are the lengths of the group's documents, laid one after another from slot 0; the last is the number of padding slots at the group's end; each row sums to 512.
All inputs are finite; a program needn't handle non-finite values.
Results may differ from the reference program's by a relative error of at most 0.018.
Values may be sent and summed in bfloat16 or wider, within the bound.
A program may use at most 192 MiB of HBM per device.

```python
import math
import jax
import jax.numpy as jnp
import numpy as np
from jax import lax

D = 1024
H = 16
FF = 4096
DOCS = 2
SLOTS = 512
GROUPS = 8
DOC_MOST = 384


def block_scale(own_key, shape, cuts, low, top_value):
    def one(dim, shards_of):
        draws = jax.random.uniform(jax.random.fold_in(jax.random.fold_in(own_key, 6), dim), (shards_of,), jnp.float32, low / len(cuts), top_value / len(cuts))
        return jnp.repeat(jnp.exp(draws), shape[dim] // shards_of).reshape((-1,) + (1,) * (len(shape) - dim - 1))

    factor_of = one(*cuts[0])
    for cut in cuts[1:]:
        factor_of = factor_of * one(*cut)
    return factor_of


def length_profile(count, total, limit, skew):
    weights = [(1 << 20) // math.isqrt(standing ** skew) + 1 for standing in range(2, count + 1)]
    spare, given = total - limit - (count - 1), [1] * (count - 1)
    while spare > 0:
        candidates = [i for i in range(count - 1) if given[i] < limit]
        pool, remaining = sum([weights[i] for i in candidates]), spare
        for i in candidates:
            addition = min(limit - given[i], max(1, remaining * weights[i] // pool), spare)
            given[i] = given[i] + addition
            spare = spare - addition
    return np.array([limit] + given)


def ragged_sizes(rng, amount, total, reach, skew):
    if amount == 2:
        one = jax.random.randint(rng, (), max(1, total - reach), min(reach, total - 1) + 1)
        return jnp.stack([one, total - one])
    sizes = jnp.asarray(length_profile(amount, total, reach, skew), jnp.int32)
    pairs = (amount - 1) // 2
    source_of, taker = sizes[1:1 + 2 * pairs:2], sizes[2:2 + 2 * pairs:2]
    room = jnp.minimum(source_of - 1, reach - taker)
    passed = jax.random.randint(jax.random.fold_in(rng, 1), (pairs,), 0, 1 << 20) % (room + 1)
    sizes = sizes.at[1:1 + 2 * pairs:2].set(source_of - passed).at[2:2 + 2 * pairs:2].set(taker + passed)
    return sizes[jax.random.permutation(jax.random.fold_in(rng, 2), amount)]


def bell_draw(own_key, shape, deviation, most, cuts=(), kind=jnp.bfloat16):
    array = jax.random.normal(own_key, shape, jnp.float32) * deviation
    if len(cuts) > 0:
        array = block_scale(own_key, shape, cuts, -0.22, 0.18) * array
    return jnp.clip(array, min=-most, max=most).astype(kind)


def setup_inputs(seed: int = 0) -> dict:
    streams_of = jax.random.split(jax.random.key(seed), 13)
    return {
        "tokens": bell_draw(streams_of[0], (GROUPS, SLOTS, D), 1.0, 6.0, ((0, 8), (1, 4))),
        "lengths": jax.vmap(lambda own: ragged_sizes(own, DOCS + 1, SLOTS, DOC_MOST, 1))(jax.random.split(streams_of[1], GROUPS)).reshape((GROUPS, DOCS + 1)).astype(jnp.int32),
        "w_qkv": bell_draw(streams_of[2], (D, 3 * D), D ** -0.5, 0.1875, ((0, 8), (1, 4))),
        "w_out": bell_draw(streams_of[3], (D, D), D ** -0.5, 0.1875, ((0, 8), (1, 4))),
        "w_uv": bell_draw(streams_of[4], (D, 2 * FF), D ** -0.5, 0.1875, ((0, 8), (1, 4))),
        "w_down": bell_draw(streams_of[5], (FF, D), FF ** -0.5, 0.09375, ((0, 8), (1, 4))),
        "s_qk": jnp.clip(jnp.exp(math.log(1.796875) - 0.6931472 * jax.random.uniform(streams_of[6], (D,), jnp.float32) ** block_scale(streams_of[6], (D,), ((0, 8),), -0.2, 0.2)), 0.8984375, 1.796875).astype(jnp.bfloat16),
        "alpha_a": jnp.clip(jnp.exp(math.log(0.59765625) - 1.7917595 * jax.random.uniform(streams_of[7], (D,), jnp.float32) ** block_scale(streams_of[7], (D,), ((0, 8),), -0.2, 0.2)), 0.099609375, 0.59765625).astype(jnp.bfloat16),
        "s_u": jnp.clip(jnp.exp(math.log(2.0) - 1.3862944 * jax.random.uniform(streams_of[8], (FF,), jnp.float32) ** block_scale(streams_of[8], (FF,), ((0, 8),), -0.2, 0.2)), 0.5, 2.0).astype(jnp.bfloat16),
        "s_v": jnp.clip(jnp.exp(math.log(2.0) - 1.3862944 * jax.random.uniform(streams_of[9], (FF,), jnp.float32) ** block_scale(streams_of[9], (FF,), ((0, 8),), -0.2, 0.2)), 0.5, 2.0).astype(jnp.bfloat16),
        "alpha_m": jnp.clip(jnp.exp(math.log(0.59765625) - 1.7917595 * jax.random.uniform(streams_of[10], (D,), jnp.float32) ** block_scale(streams_of[10], (D,), ((0, 8),), -0.2, 0.2)), 0.099609375, 0.59765625).astype(jnp.bfloat16),
        "cotangent": bell_draw(streams_of[11], (GROUPS, SLOTS, D), 1.0, 6.0, ((0, 8), (1, 4))),
    }


@jax.custom_vjp
def low(v):
    return lax.optimization_barrier(v.astype(jnp.bfloat16)).astype(jnp.float32)

@jax.custom_vjp
def low_back(v):
    return v

def low_keep(v):
    return (low(v), None)

def low_pass(kept, grad):
    return (grad,)

def back_keep(v):
    return (v, None)

def back_low(kept, grad):
    return (low(grad),)
low.defvjp(low_keep, low_pass)
low_back.defvjp(back_keep, back_low)
epsilon = 1e-06
highest = lax.Precision.HIGHEST

def layout(lengths_row, slot):
    columns = lengths_row.shape[0]
    ends = jnp.cumsum(lengths_row).astype(jnp.int32)
    starts = (ends - lengths_row).astype(jnp.int32)
    before = (slot[:, None] >= ends[None, :columns - 1]).astype(jnp.int32)
    member = lax.optimization_barrier(jnp.sum(before, axis=1)).astype(jnp.int32)
    picked = member[:, None] == jnp.arange(columns, dtype=jnp.int32)[None, :]
    begin = lax.optimization_barrier(jnp.sum(jnp.where(picked, starts[None, :], 0), axis=1)).astype(jnp.int32)
    valid = member < columns - 1
    segment = jnp.where(valid, member, columns - 1 + slot).astype(jnp.int32)
    place = jnp.where(valid, slot - begin, 0).astype(jnp.int32)
    return (segment, place, valid)

def rotary(place, width):
    half = width // 2
    frequency = jnp.exp(jnp.arange(half, dtype=jnp.float32) * (-2.0 * math.log(10000.0) / width))
    angle = place.astype(jnp.float32)[:, None] * frequency[None, :]
    return (jnp.cos(angle)[:, None, :], jnp.sin(angle)[:, None, :])

def unit_rows(value):
    return value * lax.rsqrt(lax.optimization_barrier(jnp.mean(value * value, axis=-1, keepdims=True)) + epsilon)

def turn_heads(value, cosine, sine):
    half = value.shape[-1] // 2
    first = value[..., :half]
    second = value[..., half:]
    return jnp.concatenate([first * cosine - second * sine, second * cosine + first * sine], axis=-1)

def prepare(query_raw, key_raw, s_qk, cosine, sine, heads):
    rows = query_raw.shape[0]
    scales = s_qk.reshape(heads, -1)

    def normed(raw):
        shaped = raw.reshape(rows, heads, -1)
        return (unit_rows(turn_heads(shaped, cosine, sine)) * scales).reshape(rows, -1)
    return (normed(query_raw), normed(key_raw))

def blend(base, branch, alpha):
    return unit_rows(base + alpha * (unit_rows(branch) - base))

def gated(up_gate, s_u, s_v):
    width = s_u.shape[0]
    return up_gate[:, :width] * s_u * jax.nn.silu(up_gate[:, width:] * s_v)

def forward(inputs, w_qkv, w_out, w_uv, w_down, s_qk, alpha_a, s_u, s_v, alpha_m, segment, place):
    slots = inputs.shape[0]
    width = D // H
    mixed = low_back(jnp.dot(inputs, w_qkv, precision=highest))
    cosine, sine = rotary(place, width)
    query_n, key_n = prepare(mixed[:, :D], mixed[:, D:2 * D], s_qk, cosine, sine, H)
    query = low(low_back(query_n)).reshape(slots, H, width).transpose(1, 0, 2)
    keys = low(low_back(key_n)).reshape(slots, H, width).transpose(1, 0, 2)
    values = low(mixed[:, 2 * D:]).reshape(slots, H, width).transpose(1, 0, 2)
    slot = jnp.arange(slots, dtype=jnp.int32)
    mask = (segment[:, None] == segment[None, :]) & (slot[:, None] >= slot[None, :])
    scale = 1.0 / math.sqrt(width)

    def head(operands):
        query_h, key_h, value_h = operands
        score = low_back(jnp.dot(query_h, key_h.T, precision=highest) * scale)
        score = jnp.where(mask, score, -1e+30)
        weight = jax.nn.softmax(score, axis=-1)
        return jnp.dot(low(weight), value_h, precision=highest)
    attended = lax.map(jax.checkpoint(head), (query, keys, values))
    attended = low(low_back(attended.transpose(1, 0, 2).reshape(slots, D)))
    branch = low_back(jnp.dot(attended, w_out, precision=highest))
    first = blend(inputs, branch, alpha_a)
    up_gate = low_back(jnp.dot(low(first), w_uv, precision=highest))
    hidden = low(low_back(gated(up_gate, s_u, s_v)))
    down = low_back(jnp.dot(hidden, w_down, precision=highest))
    return blend(first, down, alpha_m)

def reference(tokens, lengths, w_qkv, w_out, w_uv, w_down, s_qk, alpha_a, s_u, s_v, alpha_m, cotangent):
    params = tuple((p.astype(jnp.float32) for p in (w_qkv, w_out, w_uv, w_down, s_qk, alpha_a, s_u, s_v, alpha_m)))

    def step(totals, operands):
        inputs, lengths_row, grad_row = operands
        slots = inputs.shape[0]
        segment, place, valid = layout(lengths_row, jnp.arange(slots, dtype=jnp.int32))
        keep = valid.astype(jnp.float32)[:, None]

        def run(inputs_f, *weights):
            return forward(inputs_f, *weights, segment, place)
        final, pull = jax.vjp(run, inputs.astype(jnp.float32), *params)
        grads = pull(grad_row.astype(jnp.float32) * keep)
        totals = tuple((a + b for a, b in zip(totals, grads[1:])))
        return (totals, ((final * keep).astype(jnp.bfloat16), grads[0]))
    zeros = tuple((jnp.zeros(p.shape, jnp.float32) for p in params))
    totals, (output, input_grad) = lax.scan(step, zeros, (tokens, lengths, cotangent))
    return (output, input_grad, totals[0], totals[1], totals[2], totals[3], totals[4], totals[5], totals[6], totals[7], totals[8])
```

```python
import math

import jax
import jax.numpy as jnp
from jax import lax
from jax.sharding import PartitionSpec as P

H = 16


epsilon = 1e-06


def layout(lengths_row, slot):
    columns = lengths_row.shape[0]
    ends = jnp.cumsum(lengths_row)
    starts = ends - lengths_row
    before = (slot[:, None] >= ends[None, : columns - 1]).astype(jnp.int32)
    member = jnp.sum(before, axis=1)
    picked = member[:, None] == jnp.arange(columns, dtype=jnp.int32)[None, :]
    begin = jnp.sum(jnp.where(picked, starts[None, :], 0), axis=1)
    valid = member < columns - 1
    segment = jnp.where(valid, member, columns - 1 + slot)
    place = jnp.where(valid, slot - begin, 0)
    return (segment, place, valid)


def rotary(place, width):
    half = width // 2
    frequency = jnp.exp(jnp.arange(half, dtype=jnp.float32) * (-2.0 * math.log(10000.0) / width))
    angle = place.astype(jnp.float32)[:, None] * frequency[None, :]
    return (jnp.cos(angle)[:, None, :], jnp.sin(angle)[:, None, :])


def unit_rows(value):
    return value * lax.rsqrt(jnp.mean(value * value, axis=-1, keepdims=True) + epsilon)


def turn_heads(value, cosine, sine):
    half = value.shape[-1] // 2
    first = value[..., :half]
    second = value[..., half:]
    return jnp.concatenate(
        [first * cosine - second * sine, second * cosine + first * sine], axis=-1
    )


def prepare(query_raw, key_raw, s_qk, cosine, sine, heads):
    rows = query_raw.shape[0]
    scales = s_qk.reshape(heads, -1)

    def normed(raw):
        shaped = raw.reshape(rows, heads, -1)
        return (unit_rows(turn_heads(shaped, cosine, sine)) * scales).reshape(rows, -1)

    return (normed(query_raw), normed(key_raw))


def blend(base, branch, alpha):
    return unit_rows(base + alpha * (unit_rows(branch) - base))


def gated(up_gate, s_u, s_v):
    width = s_u.shape[0]
    return up_gate[:, :width] * s_u * jax.nn.silu(up_gate[:, width:] * s_v)


def rounded(value):
    return lax.optimization_barrier(value.astype(jnp.bfloat16)).astype(jnp.float32)


def attention_forward(query, key, value, mask):
    scale = 1.0 / math.sqrt(query.shape[2])
    score = jnp.einsum("thd,shd->hts", query, key, preferred_element_type=jnp.float32)
    score = jnp.where(mask[None], score * scale, -1e30)
    peak = jnp.max(score, axis=2, keepdims=True)
    raised = jnp.exp(score - peak)
    summed = jnp.sum(raised, axis=2, keepdims=True)
    weight = (raised / summed).astype(jnp.bfloat16)
    result = jnp.einsum("hts,shd->thd", weight, value, preferred_element_type=jnp.float32)
    return result, peak + jnp.log(summed)


def attention_backward(query, key, value, mask, log_total, grad):
    scale = 1.0 / math.sqrt(query.shape[2])
    score = jnp.einsum("thd,shd->hts", query, key, preferred_element_type=jnp.float32)
    score = jnp.where(mask[None], score * scale, -1e30)
    share = jnp.exp(score - log_total)
    grad_value = jnp.einsum(
        "hts,thd->shd", share.astype(jnp.bfloat16), grad, preferred_element_type=jnp.float32
    )
    grad_share = jnp.einsum("thd,shd->hts", grad, value, preferred_element_type=jnp.float32)
    inner = jnp.sum(share * grad_share, axis=2, keepdims=True)
    grad_score = (share * (grad_share - inner)).astype(jnp.bfloat16)
    grad_query = jnp.einsum("hts,shd->thd", grad_score, key, preferred_element_type=jnp.float32)
    grad_key = jnp.einsum("hts,thd->shd", grad_score, query, preferred_element_type=jnp.float32)
    return grad_query * scale, grad_key * scale, grad_value


def low(value):
    return value.astype(jnp.bfloat16)


def product(left, right, dims):
    return lax.dot_general(left, right, (dims, ((), ())), preferred_element_type=jnp.float32)


def local(tokens, lengths, w_qkv, w_out, w_uv, w_down, s_qk, alpha_a, s_u, s_v, alpha_m, cotangent):
    rows = tokens.shape[1]
    model = tokens.shape[2]
    width = model // H
    parts = lax.axis_size("seq")
    shards = lax.axis_size("fsdp")
    mine = lax.axis_index("seq")
    own = H // parts
    deep = w_down.shape[0]
    hidden_all = deep * shards
    hidden_own = hidden_all // parts
    piece = deep // parts
    slot = mine * rows + jnp.arange(rows, dtype=jnp.int32)
    every_slot = jnp.arange(rows * parts, dtype=jnp.int32)
    keep = layout(lengths[0], slot)[2].astype(jnp.float32)[:, None]
    segment, place, _ = layout(lengths[0], every_slot)
    mask = (segment[:, None] == segment[None, :]) & (every_slot[:, None] >= every_slot[None, :])

    def exchange(array, axis):
        return lax.all_to_all(array, "seq", axis, axis, tiled=False)

    def gather(array, axis=0):
        return lax.all_gather(array, "fsdp", axis=axis, tiled=True)

    def spread(array):
        return lax.all_gather(array, "seq", axis=0, tiled=True)

    r_in = w_qkv.shape[0]
    share_qkv = lax.all_to_all(
        w_qkv.reshape(r_in, -1, parts, width), "seq", 2, 1, tiled=True
    ).reshape(r_in, -1)
    share_uv = lax.all_to_all(
        w_uv.reshape(r_in, -1, parts, piece), "seq", 2, 1, tiled=True
    ).reshape(r_in, -1)
    share_down = lax.all_to_all(w_down.reshape(parts, piece, -1), "seq", 0, 2, tiled=True)
    share_down = share_down.reshape(piece, model)
    share_out = lax.all_gather(w_out, "seq", axis=1, tiled=True)
    inputs = spread(tokens[0])
    full_qkv = gather(share_qkv)
    full_out = gather(share_out).reshape(own, parts, width, model)
    full_out = lax.dynamic_index_in_dim(full_out, mine, 1, False).reshape(own * width, model)
    full_uv = gather(share_uv)
    full_down = gather(share_down)
    gains = gather(jnp.concatenate([s_qk, alpha_a, s_u, s_v, alpha_m])[None]).astype(jnp.float32)
    cuts = [s_qk.shape[0], alpha_a.shape[0], s_u.shape[0], s_v.shape[0]]
    edges = [sum(cuts[: i + 1]) for i in range(4)]
    gain_qk, gain_a, gain_u, gain_v, gain_m = jnp.split(gains, edges, axis=1)
    gain_qk = gain_qk.reshape(own, parts, width)
    gain_qk = lax.dynamic_index_in_dim(gain_qk, mine, 1, False).reshape(-1)
    gain_a, gain_m = gain_a.reshape(-1), gain_m.reshape(-1)
    gain_u = lax.dynamic_index_in_dim(gain_u.reshape(shards, parts, piece), mine, 1, False).reshape(-1)
    gain_v = lax.dynamic_index_in_dim(gain_v.reshape(shards, parts, piece), mine, 1, False).reshape(-1)

    mixed = product(inputs, full_qkv, ((1,), (0,)))
    cosine, sine = rotary(place, width)
    span = own * width

    def prepare_local(query_raw, key_raw, scale_qk):
        return prepare(query_raw, key_raw, scale_qk, cosine, sine, own)

    (query_f, key_f), pull_prepare = jax.vjp(
        prepare_local, mixed[:, :span], mixed[:, span : 2 * span], gain_qk
    )
    heads = (rows * parts, own, width)
    query, key = low(query_f).reshape(heads), low(key_f).reshape(heads)
    value = low(mixed[:, 2 * span :]).reshape(heads)
    attended, log_total = attention_forward(query, key, value, mask)
    attended = low(attended.reshape(-1, span))

    def reduce_rows(array):
        return lax.psum_scatter(low(array), "seq", scatter_dimension=0, tiled=True).astype(
            jnp.float32
        )

    branch = reduce_rows(product(attended, full_out, ((1,), (0,))))
    first, pull_first = jax.vjp(blend, tokens[0].astype(jnp.float32), branch, gain_a)
    first_all = spread(low(first))
    up_gate = product(first_all, full_uv, ((1,), (0,)))
    hidden_f, pull_gate = jax.vjp(gated, up_gate, gain_u, gain_v)
    hidden = low(hidden_f)
    down = reduce_rows(product(hidden, full_down, ((1,), (0,))))
    final, pull_last = jax.vjp(blend, first, down, gain_m)
    output = low(final * keep)
    grad_first, grad_down, grad_gain_m = pull_last(cotangent[0].astype(jnp.float32) * keep)
    grad_down = spread(low(grad_down))
    grad_w_down = low(product(hidden, grad_down, ((0,), (0,))))
    grad_hidden = rounded(product(grad_down, full_down, ((1,), (1,))))
    grad_up_gate, grad_gain_u, grad_gain_v = pull_gate(grad_hidden)
    grad_up = low(grad_up_gate)
    grad_w_uv = low(product(first_all, grad_up, ((0,), (0,))))
    grad_first = grad_first + reduce_rows(product(grad_up, full_uv, ((1,), (1,))))
    grad_inputs, grad_branch, grad_gain_a = pull_first(grad_first)
    grad_branch = spread(low(grad_branch))
    grad_w_out = low(product(attended, grad_branch, ((0,), (0,))))
    grad_attended = low(product(grad_branch, full_out, ((1,), (1,)))).reshape(heads)
    grad_query, grad_key, grad_value = attention_backward(
        query, key, value, mask, log_total, grad_attended
    )
    grad_query_raw, grad_key_raw, grad_gain_qk = pull_prepare(
        (rounded(grad_query).reshape(-1, span), rounded(grad_key).reshape(-1, span))
    )
    grad_mixed = low(
        jnp.concatenate([grad_query_raw, grad_key_raw, grad_value.reshape(-1, span)], axis=1)
    )
    grad_w_qkv = low(product(inputs, grad_mixed, ((0,), (0,))))
    grad_inputs = grad_inputs + reduce_rows(product(grad_mixed, full_qkv, ((1,), (1,))))

    def collect(array):
        return lax.psum_scatter(array, "fsdp", scatter_dimension=0, tiled=True)

    part_down = collect(grad_w_down)
    out_down = lax.all_to_all(
        part_down.reshape(1, piece, model), "seq", 2, 0, tiled=True
    ).reshape(deep, -1)
    part_uv = collect(grad_w_uv)
    out_uv = lax.all_to_all(
        part_uv.reshape(r_in, -1, 1, piece), "seq", 1, 2, tiled=True
    ).reshape(r_in, -1)
    placed = jnp.zeros((own, parts, width, model), jnp.bfloat16)
    placed = lax.dynamic_update_slice(
        placed, grad_w_out.reshape(own, 1, width, model), (0, mine, 0, 0)
    )
    part_out = collect(placed.reshape(-1, model))
    out_out = lax.psum_scatter(part_out, "seq", scatter_dimension=1, tiled=True)
    part_qkv = collect(grad_w_qkv)
    out_qkv = lax.all_to_all(
        part_qkv.reshape(r_in, -1, 1, width), "seq", 1, 2, tiled=True
    ).reshape(r_in, -1)

    def widen(array, outer, inner):
        blank = jnp.zeros((outer, parts, inner), jnp.float32)
        array = array.reshape(outer, 1, inner)
        return lax.dynamic_update_slice(blank, array, (0, mine, 0)).reshape(shards, -1)

    gain_sums = jnp.concatenate(
        [
            widen(grad_gain_qk, own, width),
            grad_gain_a.reshape(shards, -1),
            widen(grad_gain_u, shards, piece),
            widen(grad_gain_v, shards, piece),
            grad_gain_m.reshape(shards, -1),
        ],
        axis=1,
    )
    gain_sums = lax.psum(collect(gain_sums), "seq")[0]
    outs = jnp.split(gain_sums, edges)
    return (
        output[None],
        grad_inputs[None],
        out_qkv.astype(jnp.float32),
        out_out.astype(jnp.float32),
        out_uv.astype(jnp.float32),
        out_down.astype(jnp.float32),
        outs[0],
        outs[1],
        outs[2],
        outs[3],
        outs[4],
    )


def solution(mesh):
    return jax.shard_map(
        local,
        mesh=mesh,
        in_specs=(
            P("fsdp", "seq", None),
            P("fsdp", None),
            P("fsdp", "seq"),
            P("fsdp", "seq"),
            P("fsdp", "seq"),
            P("fsdp", "seq"),
            P("fsdp"),
            P("fsdp"),
            P("fsdp"),
            P("fsdp"),
            P("fsdp"),
            P("fsdp", "seq", None),
        ),
        out_specs=(
            P("fsdp", "seq", None),
            P("fsdp", "seq", None),
            P("fsdp", "seq"),
            P("fsdp", "seq"),
            P("fsdp", "seq"),
            P("fsdp", "seq"),
            P("fsdp"),
            P("fsdp"),
            P("fsdp"),
            P("fsdp"),
            P("fsdp"),
        ),
        check_vma=False,
    )
```

```python
import functools
import math

import jax
import jax.numpy as jnp
from jax import lax
from jax.experimental import pallas as pl
from jax.experimental.pallas import tpu as pltpu
from jax.sharding import PartitionSpec as P

H = 16


epsilon = 1e-06


def layout(lengths_row, slot):
    columns = lengths_row.shape[0]
    ends = jnp.cumsum(lengths_row)
    starts = ends - lengths_row
    before = (slot[:, None] >= ends[None, : columns - 1]).astype(jnp.int32)
    member = jnp.sum(before, axis=1)
    picked = member[:, None] == jnp.arange(columns, dtype=jnp.int32)[None, :]
    begin = jnp.sum(jnp.where(picked, starts[None, :], 0), axis=1)
    valid = member < columns - 1
    segment = jnp.where(valid, member, columns - 1 + slot)
    place = jnp.where(valid, slot - begin, 0)
    return (segment, place, valid)


def rotary(place, width):
    half = width // 2
    frequency = jnp.exp(jnp.arange(half, dtype=jnp.float32) * (-2.0 * math.log(10000.0) / width))
    angle = place.astype(jnp.float32)[:, None] * frequency[None, :]
    return (jnp.cos(angle)[:, None, :], jnp.sin(angle)[:, None, :])


def unit_rows(value):
    return value * lax.rsqrt(jnp.mean(value * value, axis=-1, keepdims=True) + epsilon)


def turn_heads(value, cosine, sine):
    half = value.shape[-1] // 2
    first = value[..., :half]
    second = value[..., half:]
    return jnp.concatenate(
        [first * cosine - second * sine, second * cosine + first * sine], axis=-1
    )


def prepare(query_raw, key_raw, s_qk, cosine, sine, heads):
    rows = query_raw.shape[0]
    scales = s_qk.reshape(heads, -1)

    def normed(raw):
        shaped = raw.reshape(rows, heads, -1)
        return (unit_rows(turn_heads(shaped, cosine, sine)) * scales).reshape(rows, -1)

    return (normed(query_raw), normed(key_raw))


def blend(base, branch, alpha):
    return unit_rows(base + alpha * (unit_rows(branch) - base))


def gated(up_gate, s_u, s_v):
    width = s_u.shape[0]
    return up_gate[:, :width] * s_u * jax.nn.silu(up_gate[:, width:] * s_v)


def rounded(value):
    return lax.optimization_barrier(value.astype(jnp.bfloat16)).astype(jnp.float32)


def attention_forward(query, key, value, mask):
    scale = 1.0 / math.sqrt(query.shape[2])
    score = jnp.einsum("thd,shd->hts", query, key, preferred_element_type=jnp.float32)
    score = jnp.where(mask[None], score * scale, -1e30)
    peak = jnp.max(score, axis=2, keepdims=True)
    raised = jnp.exp(score - peak)
    summed = jnp.sum(raised, axis=2, keepdims=True)
    weight = (raised / summed).astype(jnp.bfloat16)
    result = jnp.einsum("hts,shd->thd", weight, value, preferred_element_type=jnp.float32)
    return result, peak + jnp.log(summed)


def attention_backward(query, key, value, mask, log_total, grad):
    scale = 1.0 / math.sqrt(query.shape[2])
    score = jnp.einsum("thd,shd->hts", query, key, preferred_element_type=jnp.float32)
    score = jnp.where(mask[None], score * scale, -1e30)
    share = jnp.exp(score - log_total)
    grad_value = jnp.einsum(
        "hts,thd->shd", share.astype(jnp.bfloat16), grad, preferred_element_type=jnp.float32
    )
    grad_share = jnp.einsum("thd,shd->hts", grad, value, preferred_element_type=jnp.float32)
    inner = jnp.sum(share * grad_share, axis=2, keepdims=True)
    grad_score = (share * (grad_share - inner)).astype(jnp.bfloat16)
    grad_query = jnp.einsum("hts,shd->thd", grad_score, key, preferred_element_type=jnp.float32)
    grad_key = jnp.einsum("hts,thd->shd", grad_score, query, preferred_element_type=jnp.float32)
    return grad_query * scale, grad_key * scale, grad_value


def low(value):
    return value.astype(jnp.bfloat16)


def product(left, right, dims):
    return lax.dot_general(left, right, (dims, ((), ())), preferred_element_type=jnp.float32)


def local(tokens, lengths, w_qkv, w_out, w_uv, w_down, s_qk, alpha_a, s_u, s_v, alpha_m, cotangent):
    rows = tokens.shape[1]
    model = tokens.shape[2]
    width = model // H
    parts = lax.axis_size("seq")
    shards = lax.axis_size("fsdp")
    mine = lax.axis_index("seq")
    own = H // parts
    deep = w_down.shape[0]
    hidden_all = deep * shards
    hidden_own = hidden_all // parts
    piece = deep // parts
    slot = mine * rows + jnp.arange(rows, dtype=jnp.int32)
    every_slot = jnp.arange(rows * parts, dtype=jnp.int32)
    keep = layout(lengths[0], slot)[2].astype(jnp.float32)[:, None]
    segment, place, _ = layout(lengths[0], every_slot)
    mask = (segment[:, None] == segment[None, :]) & (every_slot[:, None] >= every_slot[None, :])

    def exchange(array, axis):
        return lax.all_to_all(array, "seq", axis, axis, tiled=False)

    def gather(array, axis=0):
        return lax.all_gather(array, "fsdp", axis=axis, tiled=True)

    def spread(array):
        return lax.all_gather(array, "seq", axis=0, tiled=True)

    r_in = w_qkv.shape[0]
    share_qkv = lax.all_to_all(
        w_qkv.reshape(r_in, -1, parts, width), "seq", 2, 1, tiled=True
    ).reshape(r_in, -1)
    share_uv = lax.all_to_all(
        w_uv.reshape(r_in, -1, parts, piece), "seq", 2, 1, tiled=True
    ).reshape(r_in, -1)
    share_down = lax.all_to_all(w_down.reshape(parts, piece, -1), "seq", 0, 2, tiled=True)
    share_down = share_down.reshape(piece, model)
    share_out = lax.all_gather(w_out, "seq", axis=1, tiled=True)
    inputs = spread(tokens[0])
    full_qkv = gather(share_qkv)
    full_out = gather(share_out).reshape(own, parts, width, model)
    full_out = lax.dynamic_index_in_dim(full_out, mine, 1, False).reshape(own * width, model)
    full_uv = gather(share_uv)
    full_down = gather(share_down)
    gains = gather(jnp.concatenate([s_qk, alpha_a, s_u, s_v, alpha_m])[None]).astype(jnp.float32)
    cuts = [s_qk.shape[0], alpha_a.shape[0], s_u.shape[0], s_v.shape[0]]
    edges = [sum(cuts[: i + 1]) for i in range(4)]
    gain_qk, gain_a, gain_u, gain_v, gain_m = jnp.split(gains, edges, axis=1)
    gain_qk = gain_qk.reshape(own, parts, width)
    gain_qk = lax.dynamic_index_in_dim(gain_qk, mine, 1, False).reshape(-1)
    gain_a, gain_m = gain_a.reshape(-1), gain_m.reshape(-1)
    gain_u = lax.dynamic_index_in_dim(gain_u.reshape(shards, parts, piece), mine, 1, False).reshape(-1)
    gain_v = lax.dynamic_index_in_dim(gain_v.reshape(shards, parts, piece), mine, 1, False).reshape(-1)

    mixed = product(inputs, full_qkv, ((1,), (0,)))
    cosine, sine = rotary(place, width)
    span = own * width

    def prepare_local(query_raw, key_raw, scale_qk):
        return prepare(query_raw, key_raw, scale_qk, cosine, sine, own)

    (query_f, key_f), pull_prepare = jax.vjp(
        prepare_local, mixed[:, :span], mixed[:, span : 2 * span], gain_qk
    )
    heads = (rows * parts, own, width)
    query, key = low(query_f).reshape(heads), low(key_f).reshape(heads)
    value = low(mixed[:, 2 * span :]).reshape(heads)
    attended, log_total = attention_forward(query, key, value, mask)
    attended = low(attended.reshape(-1, span))

    def reduce_rows(array):
        return lax.psum_scatter(low(array), "seq", scatter_dimension=0, tiled=True).astype(
            jnp.float32
        )

    branch = reduce_rows(product(attended, full_out, ((1,), (0,))))
    first, pull_first = jax.vjp(blend, tokens[0].astype(jnp.float32), branch, gain_a)
    first_all = spread(low(first))
    up_gate = product(first_all, full_uv, ((1,), (0,)))
    hidden_f, pull_gate = jax.vjp(gated, up_gate, gain_u, gain_v)
    hidden = low(hidden_f)
    down = reduce_rows(product(hidden, full_down, ((1,), (0,))))
    final, pull_last = jax.vjp(blend, first, down, gain_m)
    output = low(final * keep)
    grad_first, grad_down, grad_gain_m = pull_last(cotangent[0].astype(jnp.float32) * keep)
    grad_down = spread(low(grad_down))
    grad_w_down = low(product(hidden, grad_down, ((0,), (0,))))
    grad_hidden = rounded(product(grad_down, full_down, ((1,), (1,))))
    grad_up_gate, grad_gain_u, grad_gain_v = pull_gate(grad_hidden)
    grad_up = low(grad_up_gate)
    grad_w_uv = low(product(first_all, grad_up, ((0,), (0,))))
    grad_first = grad_first + reduce_rows(product(grad_up, full_uv, ((1,), (1,))))
    grad_inputs, grad_branch, grad_gain_a = pull_first(grad_first)
    grad_branch = spread(low(grad_branch))
    grad_w_out = low(product(attended, grad_branch, ((0,), (0,))))
    grad_attended = low(product(grad_branch, full_out, ((1,), (1,)))).reshape(heads)
    grad_query, grad_key, grad_value = attention_backward(
        query, key, value, mask, log_total, grad_attended
    )
    grad_query_raw, grad_key_raw, grad_gain_qk = pull_prepare(
        (rounded(grad_query).reshape(-1, span), rounded(grad_key).reshape(-1, span))
    )
    grad_mixed = low(
        jnp.concatenate([grad_query_raw, grad_key_raw, grad_value.reshape(-1, span)], axis=1)
    )
    grad_w_qkv = low(product(inputs, grad_mixed, ((0,), (0,))))
    grad_inputs = grad_inputs + reduce_rows(product(grad_mixed, full_qkv, ((1,), (1,))))

    def collect(array):
        return lax.psum_scatter(array, "fsdp", scatter_dimension=0, tiled=True)

    part_down = collect(grad_w_down)
    out_down = lax.all_to_all(
        part_down.reshape(1, piece, model), "seq", 2, 0, tiled=True
    ).reshape(deep, -1)
    part_uv = collect(grad_w_uv)
    out_uv = lax.all_to_all(
        part_uv.reshape(r_in, -1, 1, piece), "seq", 1, 2, tiled=True
    ).reshape(r_in, -1)
    placed = jnp.zeros((own, parts, width, model), jnp.bfloat16)
    placed = lax.dynamic_update_slice(
        placed, grad_w_out.reshape(own, 1, width, model), (0, mine, 0, 0)
    )
    part_out = collect(placed.reshape(-1, model))
    out_out = lax.psum_scatter(part_out, "seq", scatter_dimension=1, tiled=True)
    part_qkv = collect(grad_w_qkv)
    out_qkv = lax.all_to_all(
        part_qkv.reshape(r_in, -1, 1, width), "seq", 1, 2, tiled=True
    ).reshape(r_in, -1)

    def widen(array, outer, inner):
        blank = jnp.zeros((outer, parts, inner), jnp.float32)
        array = array.reshape(outer, 1, inner)
        return lax.dynamic_update_slice(blank, array, (0, mine, 0)).reshape(shards, -1)

    gain_sums = jnp.concatenate(
        [
            widen(grad_gain_qk, own, width),
            grad_gain_a.reshape(shards, -1),
            widen(grad_gain_u, shards, piece),
            widen(grad_gain_v, shards, piece),
            grad_gain_m.reshape(shards, -1),
        ],
        axis=1,
    )
    gain_sums = lax.psum(collect(gain_sums), "seq")[0]
    outs = jnp.split(gain_sums, edges)
    return (
        output[None],
        grad_inputs[None],
        out_qkv.astype(jnp.float32),
        out_out.astype(jnp.float32),
        out_uv.astype(jnp.float32),
        out_down.astype(jnp.float32),
        outs[0],
        outs[1],
        outs[2],
        outs[3],
        outs[4],
    )


MESH = pl.DeviceIdType.MESH
TILE = 128
QROWS = 128


def loop(count, body):
    def run(index, carry):
        body(index)
        return carry

    lax.fori_loop(0, count, run, 0)


def at_rows(ref, block, size=TILE):
    return ref.at[pl.ds(pl.multiple_of(block * size, size), size), :]


def cols(block, size=TILE):
    return pl.ds(pl.multiple_of(block * size, size), size)


def mean_last(value):
    return jnp.sum(value, axis=-1, keepdims=True) * (1.0 / value.shape[-1])


class Slots:
    def __init__(self):
        self.count = 0

    def take(self, count):
        base = self.count
        self.count = base + count
        return base


def fused_layer(sizes, *refs):
    (parts, lines, rows, model, deep, own_heads, width) = sizes
    slots_all = parts * rows
    span = own_heads * width
    hid = deep * lines * 2 // parts
    names = list(buffers(sizes))
    ins = dict(zip(INPUTS, refs[: len(INPUTS)]))
    outs = dict(zip(OUTPUTS, refs[len(INPUTS) : len(INPUTS) + len(OUTPUTS)]))
    rest = refs[len(INPUTS) + len(OUTPUTS) :]
    v = dict(zip(names, rest[: len(names)]))
    send_sem, recv_sem = rest[len(names) :]

    s = lax.axis_index("seq")
    f = lax.axis_index("fsdp")
    z = f // 2
    c = f % 2
    other = 1 - c
    mate = (s, 2 * z + other)
    slots = Slots()

    def put(src, dst, target, send_slot, recv_slot):
        pltpu.make_async_remote_copy(
            src_ref=src,
            dst_ref=dst,
            send_sem=send_sem.at[send_slot],
            recv_sem=recv_sem.at[recv_slot],
            device_id=target,
            device_id_type=MESH,
        ).start()

    def descriptor(ref, slot):
        return pltpu.make_async_remote_copy(
            src_ref=ref,
            dst_ref=ref,
            send_sem=send_sem.at[slot],
            recv_sem=recv_sem.at[slot],
            device_id=mate,
            device_id_type=MESH,
        )

    def landed(ref, slot):
        descriptor(ref, slot).wait_recv()

    finals = []

    def later(ref, slot, when=None):
        finals.append((ref, slot, when))

    def plane(distance):
        return (s + distance) % parts

    def plane_from(distance):
        return (s + parts - distance) % parts

    def line(distance):
        return (z + distance) % lines

    def line_from(distance):
        return (z + lines - distance) % lines

    barrier = pltpu.get_barrier_semaphore()
    for distance in range(1, parts):
        pl.semaphore_signal(barrier, inc=1, device_id=(plane(distance), f), device_id_type=MESH)
    for distance in range(1, 2 * lines):
        target = (s, (f + distance) % (2 * lines))
        pl.semaphore_signal(barrier, inc=1, device_id=target, device_id_type=MESH)

    edges = [0, TILE, 2 * TILE, 2 * TILE + deep, 2 * TILE + 2 * deep, 3 * TILE + 2 * deep]
    for place, name in enumerate(("s_qk", "alpha_a", "s_u", "s_v", "alpha_m")):
        v["gain_all"][f, :, edges[place] : edges[place + 1]] = ins[name][...].astype(jnp.float32)
    own_row = pl.ds(pl.multiple_of(s * rows, rows), rows)
    own_w = pl.ds(pl.multiple_of(f * TILE, TILE), TILE)
    v["x_all"][own_row, :] = ins["tokens"][...]

    pl.semaphore_wait(barrier, parts - 1 + 2 * lines - 1)

    qkv_slot = slots.take(3)
    for index in range(3):
        chunk = 3 * s + index
        block = chunk // parts
        target = chunk % parts

        @pl.when(target == s)
        def _():
            v["wq"][own_w, cols(block, span)] = ins["w_qkv"][:, index * span : (index + 1) * span]

        @pl.when(target != s)
        def _():
            put(
                ins["w_qkv"].at[:, index * span : (index + 1) * span],
                v["wq"].at[own_w, cols(block, span)],
                (target, f),
                qkv_slot + index,
                qkv_slot + block,
            )

        later(ins["w_qkv"].at[:, index * span : (index + 1) * span], qkv_slot + index, target != s)

    uv_slot = slots.take(parts)
    blocks_uv = 2 * hid // parts // TILE
    wide = blocks_uv * TILE
    for index in range(blocks_uv):
        v["wu"][own_w, pl.ds(pl.multiple_of(s * wide + index * TILE, TILE), TILE)] = ins["w_uv"][
            :, pl.ds(pl.multiple_of(index * parts * TILE + s * TILE, TILE), TILE)
        ]
    for distance in range(1, parts):
        target = plane(distance)
        for index in range(blocks_uv):
            put(
                ins["w_uv"].at[:, pl.ds(pl.multiple_of((index * parts + target) * TILE, TILE), TILE)],
                v["wu"].at[own_w, pl.ds(pl.multiple_of(s * wide + index * TILE, TILE), TILE)],
                (target, f),
                uv_slot + distance,
                uv_slot + distance,
            )
        later(v["wu"].at[own_w, cols(s, wide)], uv_slot + distance)

    token_slot = slots.take(parts)
    for distance in range(1, parts):
        put(
            ins["tokens"],
            v["x_all"].at[own_row, :],
            (plane(distance), f),
            token_slot + distance,
            token_slot + distance,
        )
        later(ins["tokens"], token_slot + distance)

    out_slot = slots.take(parts)
    part_cols = model // parts
    step_out = (z + parts - s) % parts

    @pl.when(z == s)
    def _():
        v["wo"][cols(c), cols(s, part_cols)] = ins["w_out"][...]

    @pl.when(z != s)
    def _():
        put(
            ins["w_out"],
            v["wo"].at[cols(c), cols(s, part_cols)],
            (z, f),
            out_slot,
            out_slot + step_out,
        )

    later(ins["w_out"], out_slot, z != s)

    down_slot = slots.take(parts)
    v["wd"][own_w, cols(s, part_cols)] = ins["w_down"][cols(s), :]
    for distance in range(1, parts):
        target = plane(distance)
        put(
            ins["w_down"].at[cols(target), :],
            v["wd"].at[own_w, cols(s, part_cols)],
            (target, f),
            down_slot + distance,
            down_slot + distance,
        )
        later(ins["w_down"].at[cols(target), :], down_slot + distance)

    gain_slot = slots.take(2 * lines)
    for distance in range(1, 2 * lines):
        put(
            v["gain_all"].at[f],
            v["gain_all"].at[f],
            (s, (f + distance) % (2 * lines)),
            gain_slot + distance,
            gain_slot + distance,
        )
        later(v["gain_all"].at[f], gain_slot + distance)

    def shard(ref, chip, core):
        return at_rows(ref, 2 * chip + core)

    def line_send(ref, base):
        own = shard(ref, z, c)
        for distance in range(1, lines):
            put(own, own, (s, 2 * line(distance) + c), base + distance, base + distance)
            later(own, base + distance)
        put(own, own, mate, base, base)
        later(own, base)

    def line_forward(ref, base):
        for distance in range(1, lines):
            block = shard(ref, line_from(distance), c)
            landed(block, base + distance)
            put(block, block, mate, base + lines + distance, base + lines + distance)
            later(block, base + lines + distance)

    def mate_wait(ref, base):
        landed(shard(ref, z, other), base)
        for distance in range(1, lines):
            landed(shard(ref, line_from(distance), other), base + lines + distance)

    wq_slot, wu_slot, wd_slot = (slots.take(2 * lines) for _ in range(3))
    wo_slot = slots.take(2 * lines)

    for block in range(3):
        source = (parts * block + s) // 3

        @pl.when(source != s)
        def _():
            landed(v["wq"].at[own_w, block * span : (block + 1) * span], qkv_slot + block)

    line_send(v["wq"], wq_slot)

    lengths = [ins["lengths"][0, i] for i in range(ins["lengths"].shape[1])]

    def slot_facts(slot):
        end = 0
        member = jnp.zeros(slot.shape, jnp.int32)
        begin = jnp.zeros(slot.shape, jnp.int32)
        for length in lengths[:-1]:
            end = end + length
            after = slot >= end
            member = member + after.astype(jnp.int32)
            begin = jnp.where(after, end, begin)
        valid = member < len(lengths) - 1
        segment = jnp.where(valid, member, len(lengths) - 1 + slot)
        place = jnp.where(valid, slot - begin, 0)
        return segment, place, valid

    lane = lax.broadcasted_iota(jnp.int32, (1, TILE), 1)
    low_half = lane < width
    first_quarter = lane % width < width // 2
    frequency = jnp.exp(
        (lane % (width // 2)).astype(jnp.float32) * (-2.0 * math.log(10000.0) / width)
    )
    turn_sign = jnp.where(first_quarter, -1.0, 1.0)

    def tables(block):
        here = pl.ds(pl.multiple_of(block * TILE, TILE), TILE)
        slot = block * TILE + lax.broadcasted_iota(jnp.int32, (TILE, 1), 0)
        segment, place, _ = slot_facts(slot)
        angle = place.astype(jnp.float32) * frequency
        v["cosine"][here, :] = jnp.cos(angle)
        v["sine"][here, :] = jnp.sin(angle) * turn_sign
        key_slot = lax.broadcasted_iota(jnp.int32, (1, slots_all), 1)
        key_segment = slot_facts(key_slot)[0]
        kept = (segment == key_segment) & (slot >= key_slot)
        v["bias"][here, :] = jnp.where(kept, 0.0, -1e30)

    loop(slots_all // TILE, tables)

    for distance in range(1, parts):
        landed(v["wu"].at[own_w, cols(plane_from(distance), wide)], uv_slot + distance)
    line_send(v["wu"], wu_slot)
    for distance in range(1, parts):
        landed(at_rows(v["x_all"], plane_from(distance), rows), token_slot + distance)
    mate_x_slot = slots.take(1)

    def mate_columns(name, buffer, slot):
        for block in range(lines):
            put(
                v[name].at[:, cols(2 * block + other)],
                v[buffer].at[:, block * TILE : (block + 1) * TILE],
                mate,
                slot,
                slot,
            )
        later(v[buffer], slot)

    mate_columns("x_all", "mate_x", mate_x_slot)

    @pl.when(z == s)
    def _():
        for distance in range(1, parts):
            landed(v["wo"].at[cols(c), cols(plane_from(distance), part_cols)], out_slot + distance)
        own = v["wo"].at[cols(c), :]
        for distance in range(1, lines):
            put(own, own, (s, 2 * line(distance) + c), wo_slot + distance, wo_slot)

    for distance in range(1, lines):
        later(v["wo"].at[cols(c), :], wo_slot + distance, z == s)
    for distance in range(1, parts):
        landed(v["wd"].at[own_w, cols(plane_from(distance), part_cols)], down_slot + distance)
    line_send(v["wd"], wd_slot)

    for distance in range(1, 2 * lines):
        landed(v["gain_all"].at[(f + 2 * lines - distance) % (2 * lines)], gain_slot + distance)

    def gain(block, offset):
        return v["gain_all"][block, :, pl.ds(pl.multiple_of(offset, TILE), TILE)]

    for block in range(2 * lines):
        here = slice(block * TILE, (block + 1) * TILE)
        v["gain_a"][:, here] = gain(block, edges[1])
        v["gain_u"][:, here] = gain(block, edges[2] + s * TILE)
        v["gain_v"][:, here] = gain(block, edges[3] + s * TILE)
        v["gain_m"][:, here] = gain(block, edges[4])
    for block in range(span // TILE):
        v["gain_qk"][:, block * TILE : (block + 1) * TILE] = gain(span // TILE * s + block, 0)

    line_forward(v["wq"], wq_slot)
    mate_wait(v["wq"], wq_slot)

    def mix(index):
        v["raw"][:, cols(index, span)] = product(
            v["x_all"][...], v["wq"][:, cols(index, span)], ((1,), (0,))
        )

    loop(3, mix)

    def swap(value):
        return jnp.where(
            first_quarter,
            pltpu.roll(value, TILE - width // 2, 1),
            pltpu.roll(value, width // 2, 1),
        )

    def head_mean(value):
        one = jnp.sum(jnp.where(low_half, value, 0.0), axis=-1, keepdims=True)
        two = jnp.sum(jnp.where(low_half, 0.0, value), axis=-1, keepdims=True)
        return jnp.where(low_half, one, two) * (1.0 / width)

    pairs = span // TILE
    blocks = slots_all // TILE

    def prepare_block(index):
        here = pl.ds(pl.multiple_of(index % blocks * TILE, TILE), TILE)
        group = index // blocks
        there = cols(group)
        value = v["raw"][here, there]
        turned = value * v["cosine"][here, :] + swap(value) * v["sine"][here, :]
        inverse = lax.rsqrt(head_mean(turned * turned) + epsilon)
        normed = turned * inverse
        v["normed"][here, there] = normed
        v["inverse"][here, there] = inverse
        v["qkv"][here, there] = low(normed * v["gain_qk"][:, cols(group % pairs)])

    loop(2 * pairs * blocks, prepare_block)

    def keep_value(index):
        here = pl.ds(pl.multiple_of(index * TILE, TILE), TILE)
        v["qkv"][here, 2 * span :] = low(v["raw"][here, 2 * span :])

    loop(blocks, keep_value)

    scale = 1.0 / math.sqrt(width)
    halves = (low_half, jnp.logical_not(low_half))

    def attend(pair):
        q_cols, k_cols, v_cols = cols(pair), cols(pairs + pair), cols(2 * pairs + pair)
        for block in range(blocks):
            here = slice(block * TILE, (block + 1) * TILE)
            seen = slice(0, (block + 1) * TILE)
            results = []
            for half in range(2):
                query = jnp.where(halves[half], v["qkv"][here, q_cols], 0.0).astype(jnp.bfloat16)
                score = product(query, v["qkv"][seen, k_cols], ((1,), (1,))) * scale
                score = score + v["bias"][here, seen]
                peak = jnp.max(score, axis=1, keepdims=True)
                raised = jnp.exp(score - peak)
                summed = jnp.sum(raised, axis=1, keepdims=True)
                weight = low(raised / summed)
                results.append(product(weight, v["qkv"][seen, v_cols], ((1,), (0,))))
                v["total"][2 * pair + half, here, :] = peak + jnp.log(summed)
            v["attended"][here, q_cols] = low(jnp.where(low_half, results[0], results[1]))

    loop(pairs, attend)
    mate_att_slot = slots.take(1)
    put(v["attended"].at[:, cols(other)], v["mate_att"], mate, mate_att_slot, mate_att_slot)
    later(v["mate_att"], mate_att_slot)

    own_out = v["wo"].at[cols(c), :]

    @pl.when(z != s)
    def _():
        landed(own_out, wo_slot)

    put(own_out, own_out, mate, wo_slot + lines, wo_slot + lines)
    later(own_out, wo_slot + lines)
    landed(v["wo"].at[cols(other), :], wo_slot + lines)

    count = 4
    piece = model // count

    def plane_sum(name, base, tile):
        sums = v["part_" + name]
        arrived = v["got_" + name]

        def send(index):
            there = cols(index, piece)
            for distance in range(1, parts):
                target = plane(distance)
                put(
                    sums.at[pl.ds(pl.multiple_of(target * rows, rows), rows), there],
                    arrived.at[distance - 1, :, there],
                    (target, f),
                    base + distance,
                    base + distance,
                )

        def step(index):
            sums[:, cols(index, piece)] = low(tile(index))

            @pl.when(index > 0)
            def _():
                send(index - 1)

        loop(count, step)
        send(count - 1)
        for distance in range(1, parts):
            later(arrived.at[distance - 1], base + distance)

    def plane_sum_wait(name, base):
        for distance in range(1, parts):
            landed(v["got_" + name].at[distance - 1], base + distance)

    def plane_total(name, here, at):
        total = v["part_" + name][here, :].astype(jnp.float32)
        for distance in range(1, parts):
            total = total + v["got_" + name][distance - 1, at, :].astype(jnp.float32)
        return total

    def plane_share(name, base):
        own = v[name].at[own_row, :]
        for distance in range(1, parts):
            put(own, own, (plane(distance), f), base + distance, base + distance)
            later(own, base + distance)

    def plane_share_wait(name, base):
        for distance in range(1, parts):
            landed(at_rows(v[name], plane_from(distance), rows), base + distance)

    branch_slot = slots.take(parts)
    plane_sum(
        "branch",
        branch_slot,
        lambda index: product(v["attended"][...], v["wo"][:, cols(index, piece)], ((1,), (0,))),
    )
    line_forward(v["wu"], wu_slot)
    plane_sum_wait("branch", branch_slot)

    chunk_rows = 16

    def chunk(index):
        at = pl.ds(pl.multiple_of(index * chunk_rows, chunk_rows), chunk_rows)
        here = pl.ds(pl.multiple_of(s * rows + index * chunk_rows, chunk_rows), chunk_rows)
        return at, here

    def blended(base, branch, alpha):
        inverse_branch = lax.rsqrt(mean_last(branch * branch) + epsilon)
        normed = branch * inverse_branch
        mixed = base + alpha * (normed - base)
        inverse = lax.rsqrt(mean_last(mixed * mixed) + epsilon)
        return normed, inverse_branch, mixed * inverse, inverse

    def blended_back(grad, base, alpha, normed, inverse_branch, result, inverse):
        grad_mixed = inverse * (grad - result * mean_last(grad * result))
        grad_normed = alpha * grad_mixed
        grad_branch = inverse_branch * (grad_normed - normed * mean_last(grad_normed * normed))
        grad_alpha = jnp.sum(grad_mixed * (normed - base), axis=0, keepdims=True)
        return grad_mixed - grad_normed, grad_branch, grad_alpha

    def make_first(index):
        at, here = chunk(index)
        base = ins["tokens"][at, :].astype(jnp.float32)
        normed, inverse_branch, result, inverse = blended(
            base, plane_total("branch", here, at), v["gain_a"][...]
        )
        v["branch_normed"][at, :] = normed
        v["branch_inverse"][at, :] = inverse_branch
        v["first"][at, :] = result
        v["first_inverse"][at, :] = inverse
        v["first_all"][here, :] = low(result)

    loop(rows // chunk_rows, make_first)
    first_slot = slots.take(parts)
    plane_share("first_all", first_slot)
    mate_wait(v["wu"], wu_slot)
    plane_share_wait("first_all", first_slot)
    mate_first_slot = slots.take(1)
    mate_columns("first_all", "mate_first", mate_first_slot)

    def gate_tile(index):
        there = cols(index, 256)
        v["up"][:, there] = product(v["first_all"][...], v["wu"][:, there], ((1,), (0,)))
        v["gate"][:, there] = product(
            v["first_all"][...],
            v["wu"][:, pl.ds(pl.multiple_of(hid + index * 256, 256), 256)],
            ((1,), (0,)),
        )

        def rows_of(block):
            here = pl.ds(pl.multiple_of(block * 64, 64), 64)
            scaled = v["gate"][here, there] * v["gain_v"][:, there]
            passed = scaled / (1.0 + jnp.exp(-scaled))
            v["hidden"][here, there] = low(v["up"][here, there] * v["gain_u"][:, there] * passed)

        loop(slots_all // 64, rows_of)

    loop(hid // 256, gate_tile)
    mate_hidden_slot = slots.take(1)
    mate_columns("hidden", "mate_hidden", mate_hidden_slot)
    line_forward(v["wd"], wd_slot)
    mate_wait(v["wd"], wd_slot)
    down_sum_slot = slots.take(parts)
    plane_sum(
        "down",
        down_sum_slot,
        lambda index: product(v["hidden"][...], v["wd"][:, cols(index, piece)], ((1,), (0,))),
    )
    plane_sum_wait("down", down_sum_slot)
    v["grad_a"][...] = jnp.zeros_like(v["grad_a"])
    v["grad_m"][...] = jnp.zeros_like(v["grad_m"])

    def finish(index):
        at, here = chunk(index)
        slot = s * rows + index * chunk_rows
        slot = slot + lax.broadcasted_iota(jnp.int32, (chunk_rows, 1), 0)
        keep = slot_facts(slot)[2].astype(jnp.float32)
        base = v["first"][at, :]
        alpha = v["gain_m"][...]
        normed, inverse_branch, result, inverse = blended(
            base, plane_total("down", here, at), alpha
        )
        outs["output"][at, :] = low(result * keep)
        grad = ins["cotangent"][at, :].astype(jnp.float32) * keep
        grad_base, grad_down, grad_alpha = blended_back(
            grad, base, alpha, normed, inverse_branch, result, inverse
        )
        v["grad_first"][at, :] = grad_base
        v["gd"][here, :] = low(grad_down)
        v["grad_m"][...] += grad_alpha

    loop(rows // chunk_rows, finish)
    gd_slot = slots.take(parts)
    plane_share("gd", gd_slot)
    plane_share_wait("gd", gd_slot)
    mate_gd_slot = slots.take(1)
    put(v["gd"], v["mate_gd"], mate, mate_gd_slot, mate_gd_slot)
    later(v["gd"], mate_gd_slot)

    def weight_grad(name, left, mate_left, right, mate_right, columns, base):
        tiles = columns // 256
        grads, arrived, kept = v["send_" + name], v["line_" + name], v["kept_" + name]

        def block_of(chip, store):
            left_cols = cols(2 * chip + c)
            mate_cols = cols(chip)

            def tile(index):
                there = cols(index, 256)
                total = product(v[left][:, left_cols], v[right][:, there], ((0,), (0,)))
                total = total + product(
                    v[mate_left][:, mate_cols], v[mate_right][:, there], ((0,), (0,))
                )
                store(there, total)

            loop(tiles, tile)

        def step(index):
            def store(there, total):
                grads[index, :, there] = low(total)

            block_of(line(index + 1), store)
            put(
                grads.at[index],
                arrived.at[index],
                (s, 2 * line(index + 1) + c),
                base + 1 + index,
                base + 1 + index,
            )

        loop(lines - 1, step)

        def store_own(there, total):
            kept[:, there] = total

        block_of(z, store_own)
        for distance in range(1, lines):
            later(grads.at[distance - 1], base + distance)

    landed(v["mate_x"], mate_x_slot)
    landed(v["mate_first"], mate_first_slot)
    landed(v["mate_hidden"], mate_hidden_slot)
    landed(v["mate_gd"], mate_gd_slot)
    line_down_slot = slots.take(lines)
    weight_grad("down", "hidden", "mate_hidden", "gd", "mate_gd", model, line_down_slot)

    def gate_back(index):
        there = cols(index, 256)
        there_gate = pl.ds(pl.multiple_of(hid + index * 256, 256), 256)
        v["grad_hidden"][...] = low(product(v["gd"][...], v["wd"][there, :], ((1,), (1,))))
        v["grad_u"][:, there] = jnp.zeros((1, 256), jnp.float32)
        v["grad_v"][:, there] = jnp.zeros((1, 256), jnp.float32)

        def rows_of(block):
            here = pl.ds(pl.multiple_of(block * 64, 64), 64)
            grad = v["grad_hidden"][here, :].astype(jnp.float32)
            up = v["up"][here, there]
            gate = v["gate"][here, there]
            gain_u = v["gain_u"][:, there]
            gain_v = v["gain_v"][:, there]
            scaled = gate * gain_v
            squash = 1.0 / (1.0 + jnp.exp(-scaled))
            passed = scaled * squash
            grad_scaled_up = grad * passed
            grad_scaled = grad * (up * gain_u) * (squash + passed * (1.0 - squash))
            v["gu"][here, there] = low(grad_scaled_up * gain_u)
            v["gu"][here, there_gate] = low(grad_scaled * gain_v)
            v["grad_u"][:, there] += jnp.sum(grad_scaled_up * up, axis=0, keepdims=True)
            v["grad_v"][:, there] += jnp.sum(grad_scaled * gate, axis=0, keepdims=True)

        loop(slots_all // 64, rows_of)

    loop(hid // 256, gate_back)
    mate_gu_slot = slots.take(1)
    put(v["gu"], v["mate_gu"], mate, mate_gu_slot, mate_gu_slot)
    later(v["gu"], mate_gu_slot)
    first_sum_slot = slots.take(parts)
    plane_sum(
        "first",
        first_sum_slot,
        lambda index: product(v["gu"][...], v["wu"][cols(index, piece), :], ((1,), (1,))),
    )
    landed(v["mate_gu"], mate_gu_slot)
    line_uv_slot = slots.take(lines)
    weight_grad("uv", "first_all", "mate_first", "gu", "mate_gu", 2 * hid, line_uv_slot)
    plane_sum_wait("first", first_sum_slot)

    def back_first(index):
        at, here = chunk(index)
        grad = v["grad_first"][at, :] + plane_total("first", here, at)
        grad_base, grad_branch, grad_alpha = blended_back(
            grad,
            ins["tokens"][at, :].astype(jnp.float32),
            v["gain_a"][...],
            v["branch_normed"][at, :],
            v["branch_inverse"][at, :],
            v["first"][at, :],
            v["first_inverse"][at, :],
        )
        v["grad_tokens"][at, :] = grad_base
        v["gb"][here, :] = low(grad_branch)
        v["grad_a"][...] += grad_alpha

    loop(rows // chunk_rows, back_first)
    gb_slot = slots.take(parts)
    plane_share("gb", gb_slot)
    plane_share_wait("gb", gb_slot)
    mate_gb_slot = slots.take(1)
    put(v["gb"], v["mate_gb"], mate, mate_gb_slot, mate_gb_slot)
    later(v["gb"], mate_gb_slot)

    v["grad_att"][...] = low(product(v["gb"][...], v["wo"][...], ((1,), (1,))))
    v["grad_qkv"][...] = jnp.zeros_like(v["grad_qkv"])

    def attend_back(pair):
        q_cols, k_cols, v_cols = cols(pair), cols(pairs + pair), cols(2 * pairs + pair)
        for block in range(blocks):
            here = slice(block * TILE, (block + 1) * TILE)
            seen = slice(0, (block + 1) * TILE)
            results = []
            for half in range(2):
                query = jnp.where(halves[half], v["qkv"][here, q_cols], 0.0).astype(jnp.bfloat16)
                grad = jnp.where(halves[half], v["grad_att"][here, q_cols], 0.0)
                grad = grad.astype(jnp.bfloat16)
                score = product(query, v["qkv"][seen, k_cols], ((1,), (1,))) * scale
                score = score + v["bias"][here, seen]
                share = jnp.exp(score - v["total"][2 * pair + half, here, :])
                grad_share = product(grad, v["qkv"][seen, v_cols], ((1,), (1,)))
                inner = jnp.sum(share * grad_share, axis=1, keepdims=True)
                grad_score = low(share * (grad_share - inner))
                results.append(product(grad_score, v["qkv"][seen, k_cols], ((1,), (0,))))
                v["grad_qkv"][seen, v_cols] += product(low(share), grad, ((0,), (0,)))
                v["grad_qkv"][seen, k_cols] += product(grad_score, query, ((0,), (0,)))
            v["grad_qkv"][here, q_cols] = jnp.where(low_half, results[0], results[1])

    loop(pairs, attend_back)
    v["grad_qk"][...] = jnp.zeros_like(v["grad_qk"])

    def prepare_back(index):
        here = pl.ds(pl.multiple_of(index % blocks * TILE, TILE), TILE)
        group = index // blocks
        there = cols(group)
        pair = cols(group % pairs)
        grad = low(v["grad_qkv"][here, there] * scale).astype(jnp.float32)
        normed = v["normed"][here, there]
        v["grad_qk"][:, pair] += jnp.sum(grad * normed, axis=0, keepdims=True)
        grad = grad * v["gain_qk"][:, pair]
        grad = v["inverse"][here, there] * (grad - normed * head_mean(grad * normed))
        back = grad * v["cosine"][here, :] - swap(grad) * v["sine"][here, :]
        v["gm"][here, there] = low(back)

    loop(2 * pairs * blocks, prepare_back)

    def value_back(index):
        here = pl.ds(pl.multiple_of(index * TILE, TILE), TILE)
        v["gm"][here, 2 * span :] = low(v["grad_qkv"][here, 2 * span :])

    loop(blocks, value_back)
    mate_gm_slot = slots.take(1)
    put(v["gm"], v["mate_gm"], mate, mate_gm_slot, mate_gm_slot)
    later(v["gm"], mate_gm_slot)

    v["gain_part"][...] = jnp.zeros_like(v["gain_part"])
    for block in range(2 * lines):
        here = slice(block * TILE, (block + 1) * TILE)
        local_pair = block % (span // TILE) * TILE
        qk = v["grad_qk"][:, local_pair : local_pair + TILE]
        mine = (s == block // (span // TILE)).astype(jnp.float32)
        v["gain_part"][block, :, edges[0] : edges[1]] = qk * mine
        v["gain_part"][block, :, edges[1] : edges[2]] = v["grad_a"][:, here]
        v["gain_part"][block, :, cols(edges[2] // TILE + s)] = v["grad_u"][:, here]
        v["gain_part"][block, :, cols(edges[3] // TILE + s)] = v["grad_v"][:, here]
        v["gain_part"][block, :, edges[4] : edges[5]] = v["grad_m"][:, here]

    inputs_slot = slots.take(parts)
    plane_sum(
        "inputs",
        inputs_slot,
        lambda index: product(v["gm"][...], v["wq"][cols(index, piece), :], ((1,), (1,))),
    )
    gain_line_slot = slots.take(2 * lines)
    for distance in range(1, 2 * lines):
        target = (f + distance) % (2 * lines)
        put(
            v["gain_part"].at[target],
            v["gain_got"].at[distance - 1],
            (s, target),
            gain_line_slot + distance,
            gain_line_slot + distance,
        )
        later(v["gain_got"].at[distance - 1], gain_line_slot + distance)
    landed(v["mate_gm"], mate_gm_slot)
    line_qkv_slot = slots.take(lines)
    weight_grad("qkv", "x_all", "mate_x", "gm", "mate_gm", 3 * span, line_qkv_slot)

    landed(v["mate_gb"], mate_gb_slot)
    landed(v["mate_att"], mate_att_slot)
    line_out_slot = slots.take(lines)

    def out_tile(index):
        there = cols(index, 256)
        total = product(v["attended"][:, cols(c)], v["gb"][:, there], ((0,), (0,)))
        total = total + product(v["mate_att"][...], v["mate_gb"][:, there], ((0,), (0,)))
        v["kept_out"][:, there] = total
        v["send_out"][:, there] = low(total)

    loop(model // 256, out_tile)
    step_line = (s + lines - z) % lines

    @pl.when(z != s)
    def _():
        put(
            v["send_out"],
            v["line_out"].at[step_line - 1],
            (s, 2 * s + c),
            line_out_slot,
            line_out_slot + step_line,
        )

    later(v["send_out"], line_out_slot, z != s)

    plane_sum_wait("inputs", inputs_slot)

    def finish_inputs(index):
        at, here = chunk(index)
        outs["input_grad"][at, :] = v["grad_tokens"][at, :] + plane_total("inputs", here, at)

    loop(rows // chunk_rows, finish_inputs)

    def line_total(name, base, columns):
        for distance in range(1, lines):
            landed(v["line_" + name].at[distance - 1], base + distance)

        def tile(index):
            there = cols(index, 256)
            total = v["kept_" + name][:, there]
            for distance in range(1, lines):
                total = total + v["line_" + name][distance - 1, :, there].astype(jnp.float32)
            v["done_" + name][:, there] = low(total)

        loop(columns // 256, tile)

    line_total("down", line_down_slot, model)
    back_down_slot = slots.take(parts)
    for distance in range(1, parts):
        target = plane(distance)
        put(
            v["done_down"].at[:, cols(target, part_cols)],
            v["back_down"].at[cols(s), :],
            (target, f),
            back_down_slot + distance,
            back_down_slot + distance,
        )
        later(v["done_down"].at[:, cols(target, part_cols)], back_down_slot + distance)
    v["back_down"][cols(s), :] = v["done_down"][:, cols(s, part_cols)]

    line_total("uv", line_uv_slot, 2 * hid)
    back_uv_slot = slots.take(parts)
    for distance in range(1, parts):
        target = plane(distance)
        for index in range(blocks_uv):
            put(
                v["done_uv"].at[:, pl.ds(pl.multiple_of(target * wide + index * TILE, TILE), TILE)],
                v["back_uv"].at[s, :, index * TILE : (index + 1) * TILE],
                (target, f),
                back_uv_slot + distance,
                back_uv_slot + distance,
            )
        later(v["done_uv"].at[:, cols(target, wide)], back_uv_slot + distance)
    v["back_uv"][s] = v["done_uv"][:, cols(s, wide)]

    gain_plane_slot = slots.take(parts)
    for distance in range(1, 2 * lines):
        landed(v["gain_got"].at[distance - 1], gain_line_slot + distance)
    total = v["gain_part"][f]
    for distance in range(1, 2 * lines):
        total = total + v["gain_got"][distance - 1]
    v["gain_sum"][s] = total
    for distance in range(1, parts):
        put(
            v["gain_sum"].at[s],
            v["gain_sum"].at[s],
            (plane(distance), f),
            gain_plane_slot + distance,
            gain_plane_slot + distance,
        )
        later(v["gain_sum"].at[s], gain_plane_slot + distance)

    line_total("qkv", line_qkv_slot, 3 * span)
    back_qkv_slot = slots.take(3)
    for block in range(3):
        chunk_of = parts * block + s
        target = chunk_of // 3
        index = chunk_of % 3
        source = v["done_qkv"].at[:, block * span : (block + 1) * span]

        @pl.when(target == s)
        def _():
            v["back_qkv"][index] = source[...]

        @pl.when(target != s)
        def _():
            put(
                source,
                v["back_qkv"].at[index],
                (target, f),
                back_qkv_slot + block,
                back_qkv_slot + index,
            )

        later(source, back_qkv_slot + block, target != s)

    back_out_slot = slots.take(parts)

    @pl.when(z == s)
    def _():
        line_total("out", line_out_slot, model)
        for distance in range(1, parts):
            target = plane(distance)
            put(
                v["done_out"].at[:, cols(target, part_cols)],
                v["back_out"],
                (target, f),
                back_out_slot + distance,
                back_out_slot,
            )
        v["back_out"][...] = v["done_out"][:, cols(s, part_cols)]

    for distance in range(1, parts):
        later(v["back_out"], back_out_slot + distance, z == s)

    for distance in range(1, parts):
        landed(v["back_down"].at[cols(plane_from(distance)), :], back_down_slot + distance)
    outs["grad_w_down"][...] = v["back_down"][...].astype(jnp.float32)
    for distance in range(1, parts):
        landed(v["back_uv"].at[plane_from(distance)], back_uv_slot + distance)
    for source in range(parts):
        for index in range(blocks_uv):
            there = (index * parts + source) * TILE
            outs["grad_w_uv"][:, there : there + TILE] = v["back_uv"][
                source, :, index * TILE : (index + 1) * TILE
            ].astype(jnp.float32)
    for distance in range(1, parts):
        landed(v["gain_sum"].at[plane_from(distance)], gain_plane_slot + distance)
    total = v["gain_sum"][0]
    for source in range(1, parts):
        total = total + v["gain_sum"][source]
    for place, name in enumerate(GAIN_OUTPUTS):
        outs[name][...] = total[:, edges[place] : edges[place + 1]]
    for index in range(3):
        source = (3 * s + index) % parts

        @pl.when(source != s)
        def _():
            landed(v["back_qkv"].at[index], back_qkv_slot + index)

        outs["grad_w_qkv"][:, index * span : (index + 1) * span] = v["back_qkv"][index].astype(
            jnp.float32
        )

    @pl.when(z != s)
    def _():
        landed(v["back_out"], back_out_slot)

    outs["grad_w_out"][...] = v["back_out"][...].astype(jnp.float32)

    for ref, slot, when in finals:
        if when is None:
            descriptor(ref, slot).wait_send()
        else:

            @pl.when(when)
            def _():
                descriptor(ref, slot).wait_send()

    assert slots.count <= SLOTS_MOST, slots.count


SLOTS_MOST = 160
INPUTS = (
    "tokens",
    "lengths",
    "w_qkv",
    "w_out",
    "w_uv",
    "w_down",
    "s_qk",
    "alpha_a",
    "s_u",
    "s_v",
    "alpha_m",
    "cotangent",
)
GAIN_OUTPUTS = (
    "grad_s_qk",
    "grad_alpha_a",
    "grad_s_u",
    "grad_s_v",
    "grad_alpha_m",
)
OUTPUTS = (
    "output",
    "input_grad",
    "grad_w_qkv",
    "grad_w_out",
    "grad_w_uv",
    "grad_w_down",
) + GAIN_OUTPUTS


def buffers(sizes):
    (parts, lines, rows, model, deep, own_heads, width) = sizes
    every = parts * rows
    span = own_heads * width
    hid = deep * lines * 2 // parts
    half = lines * TILE
    gains = 3 * TILE + 2 * deep
    bf16, f32 = jnp.bfloat16, jnp.float32
    table = {
        "wq": ((model, 3 * span), bf16),
        "wo": ((span, model), bf16),
        "wu": ((model, 2 * hid), bf16),
        "wd": ((hid, model), bf16),
        "gain_all": ((2 * lines, 1, gains), f32),
        "gain_a": ((1, model), f32),
        "gain_m": ((1, model), f32),
        "gain_u": ((1, hid), f32),
        "gain_v": ((1, hid), f32),
        "gain_qk": ((1, span), f32),
        "x_all": ((every, model), bf16),
        "first_all": ((every, model), bf16),
        "gd": ((every, model), bf16),
        "gb": ((every, model), bf16),
        "cosine": ((every, TILE), f32),
        "sine": ((every, TILE), f32),
        "bias": ((every, every), f32),
        "raw": ((every, 3 * span), f32),
        "normed": ((every, 2 * span), f32),
        "inverse": ((every, 2 * span), f32),
        "qkv": ((every, 3 * span), bf16),
        "total": ((own_heads, every, 1), f32),
        "attended": ((every, span), bf16),
        "branch_normed": ((rows, model), f32),
        "branch_inverse": ((rows, 1), f32),
        "first": ((rows, model), f32),
        "first_inverse": ((rows, 1), f32),
        "up": ((every, hid), f32),
        "gate": ((every, hid), f32),
        "hidden": ((every, hid), bf16),
        "grad_hidden": ((every, 256), bf16),
        "gu": ((every, 2 * hid), bf16),
        "grad_first": ((rows, model), f32),
        "grad_tokens": ((rows, model), f32),
        "grad_att": ((every, span), bf16),
        "grad_qkv": ((every, 3 * span), f32),
        "gm": ((every, 3 * span), bf16),
        "grad_a": ((1, model), f32),
        "grad_m": ((1, model), f32),
        "grad_u": ((1, hid), f32),
        "grad_v": ((1, hid), f32),
        "grad_qk": ((1, span), f32),
        "gain_part": ((2 * lines, 1, gains), f32),
        "gain_got": ((2 * lines - 1, 1, gains), f32),
        "gain_sum": ((parts, 1, gains), f32),
        "mate_x": ((every, half), bf16),
        "mate_first": ((every, half), bf16),
        "mate_hidden": ((every, half), bf16),
        "mate_att": ((every, TILE), bf16),
        "mate_gd": ((every, model), bf16),
        "mate_gu": ((every, 2 * hid), bf16),
        "mate_gb": ((every, model), bf16),
        "mate_gm": ((every, 3 * span), bf16),
        "send_out": ((TILE, model), bf16),
        "kept_out": ((TILE, model), f32),
        "line_out": ((lines - 1, TILE, model), bf16),
        "done_out": ((TILE, model), bf16),
        "back_out": ((TILE, model // parts), bf16),
        "back_qkv": ((3, TILE, span), bf16),
        "back_uv": ((parts, TILE, 2 * hid // parts), bf16),
        "back_down": ((deep, model // parts), bf16),
    }
    for name in ("branch", "down", "first", "inputs"):
        table["part_" + name] = ((every, model), bf16)
        table["got_" + name] = ((parts - 1, rows, model), bf16)
    for name, columns in (("qkv", 3 * span), ("uv", 2 * hid), ("down", model)):
        table["send_" + name] = ((lines - 1, TILE, columns), bf16)
        table["line_" + name] = ((lines - 1, TILE, columns), bf16)
        table["kept_" + name] = ((TILE, columns), f32)
        table["done_" + name] = ((TILE, columns), bf16)
    return table


def fused(sizes):
    (parts, lines, rows, model, deep, own_heads, width) = sizes

    def run(tokens, lengths, w_qkv, w_out, w_uv, w_down, *others):
        gains, cotangent = others[:5], others[5]
        f32 = jnp.float32
        shapes = [
            jax.ShapeDtypeStruct(tokens.shape[1:], jnp.bfloat16),
            jax.ShapeDtypeStruct(tokens.shape[1:], f32),
            *(jax.ShapeDtypeStruct(w.shape, f32) for w in (w_qkv, w_out, w_uv, w_down)),
            *(jax.ShapeDtypeStruct((1, g.shape[0]), f32) for g in gains),
        ]
        vmem = pl.BlockSpec(memory_space=pltpu.VMEM)
        specs = [vmem] * len(INPUTS)
        specs[1] = pl.BlockSpec(memory_space=pltpu.SMEM)
        scratch = [pltpu.VMEM(shape, kind) for shape, kind in buffers(sizes).values()]
        outs = pl.pallas_call(
            functools.partial(fused_layer, sizes),
            out_shape=shapes,
            in_specs=specs,
            out_specs=[vmem] * len(shapes),
            scratch_shapes=[
                *scratch,
                pltpu.SemaphoreType.DMA((SLOTS_MOST,)),
                pltpu.SemaphoreType.DMA((SLOTS_MOST,)),
            ],
            compiler_params=pltpu.CompilerParams(
                collective_id=0, has_side_effects=True, vmem_limit_bytes=67043328
            ),
            name="fused_layer",
        )(
            tokens[0],
            lengths,
            w_qkv,
            w_out,
            w_uv,
            w_down,
            *(g.reshape(1, -1) for g in gains),
            cotangent[0],
        )
        return (
            outs[0][None],
            outs[1][None],
            *outs[2:6],
            *(g.reshape(-1) for g in outs[6:]),
        )

    return run


def choose(parts, shards):
    def run(*args):
        tokens, w_qkv, w_down = args[0], args[2], args[5]
        rows, model = tokens.shape[1:]
        deep, width = w_down.shape[0], model // H
        fits = shards == 2 * parts and rows == TILE and w_qkv.shape[0] == TILE
        fits = fits and deep == parts * TILE and 2 * width == TILE and H == 4 * parts
        if not fits:
            return local(*args)
        return fused((parts, shards // 2, rows, model, deep, H // parts, width))(*args)

    return run


def solution(mesh):
    return jax.shard_map(
        choose(mesh.shape["seq"], mesh.shape["fsdp"]),
        mesh=mesh,
        in_specs=(
            P("fsdp", "seq", None),
            P("fsdp", None),
            P("fsdp", "seq"),
            P("fsdp", "seq"),
            P("fsdp", "seq"),
            P("fsdp", "seq"),
            P("fsdp"),
            P("fsdp"),
            P("fsdp"),
            P("fsdp"),
            P("fsdp"),
            P("fsdp", "seq", None),
        ),
        out_specs=(
            P("fsdp", "seq", None),
            P("fsdp", "seq", None),
            P("fsdp", "seq"),
            P("fsdp", "seq"),
            P("fsdp", "seq"),
            P("fsdp", "seq"),
            P("fsdp"),
            P("fsdp"),
            P("fsdp"),
            P("fsdp"),
            P("fsdp"),
        ),
        check_vma=False,
    )
```

```python
import functools
import math
import types
import typing

import jax
import jax.numpy as jnp
from jax import lax
from jax.experimental import pallas as pl
from jax.experimental.pallas import tpu as pltpu
from jax.sharding import PartitionSpec as P

H = 16


epsilon = 1e-06


def layout(lengths_row, slot):
    columns = lengths_row.shape[0]
    ends = jnp.cumsum(lengths_row)
    starts = ends - lengths_row
    before = (slot[:, None] >= ends[None, : columns - 1]).astype(jnp.int32)
    member = jnp.sum(before, axis=1)
    picked = member[:, None] == jnp.arange(columns, dtype=jnp.int32)[None, :]
    begin = jnp.sum(jnp.where(picked, starts[None, :], 0), axis=1)
    valid = member < columns - 1
    segment = jnp.where(valid, member, columns - 1 + slot)
    place = jnp.where(valid, slot - begin, 0)
    return (segment, place, valid)


def rotary(place, width):
    half = width // 2
    frequency = jnp.exp(jnp.arange(half, dtype=jnp.float32) * (-2.0 * math.log(10000.0) / width))
    angle = place.astype(jnp.float32)[:, None] * frequency[None, :]
    return (jnp.cos(angle)[:, None, :], jnp.sin(angle)[:, None, :])


def unit_rows(value):
    return value * lax.rsqrt(jnp.mean(value * value, axis=-1, keepdims=True) + epsilon)


def turn_heads(value, cosine, sine):
    half = value.shape[-1] // 2
    first = value[..., :half]
    second = value[..., half:]
    return jnp.concatenate(
        [first * cosine - second * sine, second * cosine + first * sine], axis=-1
    )


def prepare(query_raw, key_raw, s_qk, cosine, sine, heads):
    rows = query_raw.shape[0]
    scales = s_qk.reshape(heads, -1)

    def normed(raw):
        shaped = raw.reshape(rows, heads, -1)
        return (unit_rows(turn_heads(shaped, cosine, sine)) * scales).reshape(rows, -1)

    return (normed(query_raw), normed(key_raw))


def blend(base, branch, alpha):
    return unit_rows(base + alpha * (unit_rows(branch) - base))


def gated(up_gate, s_u, s_v):
    width = s_u.shape[0]
    return up_gate[:, :width] * s_u * jax.nn.silu(up_gate[:, width:] * s_v)


def rounded(value):
    return lax.optimization_barrier(value.astype(jnp.bfloat16)).astype(jnp.float32)


def attention_forward(query, key, value, mask):
    scale = 1.0 / math.sqrt(query.shape[2])
    score = jnp.einsum("thd,shd->hts", query, key, preferred_element_type=jnp.float32)
    score = jnp.where(mask[None], score * scale, -1e30)
    peak = jnp.max(score, axis=2, keepdims=True)
    raised = jnp.exp(score - peak)
    summed = jnp.sum(raised, axis=2, keepdims=True)
    weight = (raised / summed).astype(jnp.bfloat16)
    result = jnp.einsum("hts,shd->thd", weight, value, preferred_element_type=jnp.float32)
    return result, peak + jnp.log(summed)


def attention_backward(query, key, value, mask, log_total, grad):
    scale = 1.0 / math.sqrt(query.shape[2])
    score = jnp.einsum("thd,shd->hts", query, key, preferred_element_type=jnp.float32)
    score = jnp.where(mask[None], score * scale, -1e30)
    share = jnp.exp(score - log_total)
    grad_value = jnp.einsum(
        "hts,thd->shd", share.astype(jnp.bfloat16), grad, preferred_element_type=jnp.float32
    )
    grad_share = jnp.einsum("thd,shd->hts", grad, value, preferred_element_type=jnp.float32)
    inner = jnp.sum(share * grad_share, axis=2, keepdims=True)
    grad_score = (share * (grad_share - inner)).astype(jnp.bfloat16)
    grad_query = jnp.einsum("hts,shd->thd", grad_score, key, preferred_element_type=jnp.float32)
    grad_key = jnp.einsum("hts,thd->shd", grad_score, query, preferred_element_type=jnp.float32)
    return grad_query * scale, grad_key * scale, grad_value


def low(value):
    return value.astype(jnp.bfloat16)


def product(left, right, dims):
    return lax.dot_general(left, right, (dims, ((), ())), preferred_element_type=jnp.float32)


def local(tokens, lengths, w_qkv, w_out, w_uv, w_down, s_qk, alpha_a, s_u, s_v, alpha_m, cotangent):
    rows = tokens.shape[1]
    model = tokens.shape[2]
    width = model // H
    parts = lax.axis_size("seq")
    shards = lax.axis_size("fsdp")
    mine = lax.axis_index("seq")
    own = H // parts
    deep = w_down.shape[0]
    hidden_all = deep * shards
    hidden_own = hidden_all // parts
    piece = deep // parts
    slot = mine * rows + jnp.arange(rows, dtype=jnp.int32)
    every_slot = jnp.arange(rows * parts, dtype=jnp.int32)
    keep = layout(lengths[0], slot)[2].astype(jnp.float32)[:, None]
    segment, place, _ = layout(lengths[0], every_slot)
    mask = (segment[:, None] == segment[None, :]) & (every_slot[:, None] >= every_slot[None, :])

    def exchange(array, axis):
        return lax.all_to_all(array, "seq", axis, axis, tiled=False)

    def gather(array, axis=0):
        return lax.all_gather(array, "fsdp", axis=axis, tiled=True)

    def spread(array):
        return lax.all_gather(array, "seq", axis=0, tiled=True)

    r_in = w_qkv.shape[0]
    share_qkv = lax.all_to_all(
        w_qkv.reshape(r_in, -1, parts, width), "seq", 2, 1, tiled=True
    ).reshape(r_in, -1)
    share_uv = lax.all_to_all(
        w_uv.reshape(r_in, -1, parts, piece), "seq", 2, 1, tiled=True
    ).reshape(r_in, -1)
    share_down = lax.all_to_all(w_down.reshape(parts, piece, -1), "seq", 0, 2, tiled=True)
    share_down = share_down.reshape(piece, model)
    share_out = lax.all_gather(w_out, "seq", axis=1, tiled=True)
    inputs = spread(tokens[0])
    full_qkv = gather(share_qkv)
    full_out = gather(share_out).reshape(own, parts, width, model)
    full_out = lax.dynamic_index_in_dim(full_out, mine, 1, False).reshape(own * width, model)
    full_uv = gather(share_uv)
    full_down = gather(share_down)
    gains = gather(jnp.concatenate([s_qk, alpha_a, s_u, s_v, alpha_m])[None]).astype(jnp.float32)
    cuts = [s_qk.shape[0], alpha_a.shape[0], s_u.shape[0], s_v.shape[0]]
    edges = [sum(cuts[: i + 1]) for i in range(4)]
    gain_qk, gain_a, gain_u, gain_v, gain_m = jnp.split(gains, edges, axis=1)
    gain_qk = gain_qk.reshape(own, parts, width)
    gain_qk = lax.dynamic_index_in_dim(gain_qk, mine, 1, False).reshape(-1)
    gain_a, gain_m = gain_a.reshape(-1), gain_m.reshape(-1)
    gain_u = lax.dynamic_index_in_dim(gain_u.reshape(shards, parts, piece), mine, 1, False).reshape(-1)
    gain_v = lax.dynamic_index_in_dim(gain_v.reshape(shards, parts, piece), mine, 1, False).reshape(-1)

    mixed = product(inputs, full_qkv, ((1,), (0,)))
    cosine, sine = rotary(place, width)
    span = own * width

    def prepare_local(query_raw, key_raw, scale_qk):
        return prepare(query_raw, key_raw, scale_qk, cosine, sine, own)

    (query_f, key_f), pull_prepare = jax.vjp(
        prepare_local, mixed[:, :span], mixed[:, span : 2 * span], gain_qk
    )
    heads = (rows * parts, own, width)
    query, key = low(query_f).reshape(heads), low(key_f).reshape(heads)
    value = low(mixed[:, 2 * span :]).reshape(heads)
    attended, log_total = attention_forward(query, key, value, mask)
    attended = low(attended.reshape(-1, span))

    def reduce_rows(array):
        return lax.psum_scatter(low(array), "seq", scatter_dimension=0, tiled=True).astype(
            jnp.float32
        )

    branch = reduce_rows(product(attended, full_out, ((1,), (0,))))
    first, pull_first = jax.vjp(blend, tokens[0].astype(jnp.float32), branch, gain_a)
    first_all = spread(low(first))
    up_gate = product(first_all, full_uv, ((1,), (0,)))
    hidden_f, pull_gate = jax.vjp(gated, up_gate, gain_u, gain_v)
    hidden = low(hidden_f)
    down = reduce_rows(product(hidden, full_down, ((1,), (0,))))
    final, pull_last = jax.vjp(blend, first, down, gain_m)
    output = low(final * keep)
    grad_first, grad_down, grad_gain_m = pull_last(cotangent[0].astype(jnp.float32) * keep)
    grad_down = spread(low(grad_down))
    grad_w_down = low(product(hidden, grad_down, ((0,), (0,))))
    grad_hidden = rounded(product(grad_down, full_down, ((1,), (1,))))
    grad_up_gate, grad_gain_u, grad_gain_v = pull_gate(grad_hidden)
    grad_up = low(grad_up_gate)
    grad_w_uv = low(product(first_all, grad_up, ((0,), (0,))))
    grad_first = grad_first + reduce_rows(product(grad_up, full_uv, ((1,), (1,))))
    grad_inputs, grad_branch, grad_gain_a = pull_first(grad_first)
    grad_branch = spread(low(grad_branch))
    grad_w_out = low(product(attended, grad_branch, ((0,), (0,))))
    grad_attended = low(product(grad_branch, full_out, ((1,), (1,)))).reshape(heads)
    grad_query, grad_key, grad_value = attention_backward(
        query, key, value, mask, log_total, grad_attended
    )
    grad_query_raw, grad_key_raw, grad_gain_qk = pull_prepare(
        (rounded(grad_query).reshape(-1, span), rounded(grad_key).reshape(-1, span))
    )
    grad_mixed = low(
        jnp.concatenate([grad_query_raw, grad_key_raw, grad_value.reshape(-1, span)], axis=1)
    )
    grad_w_qkv = low(product(inputs, grad_mixed, ((0,), (0,))))
    grad_inputs = grad_inputs + reduce_rows(product(grad_mixed, full_qkv, ((1,), (1,))))

    def collect(array):
        return lax.psum_scatter(array, "fsdp", scatter_dimension=0, tiled=True)

    part_down = collect(grad_w_down)
    out_down = lax.all_to_all(
        part_down.reshape(1, piece, model), "seq", 2, 0, tiled=True
    ).reshape(deep, -1)
    part_uv = collect(grad_w_uv)
    out_uv = lax.all_to_all(
        part_uv.reshape(r_in, -1, 1, piece), "seq", 1, 2, tiled=True
    ).reshape(r_in, -1)
    placed = jnp.zeros((own, parts, width, model), jnp.bfloat16)
    placed = lax.dynamic_update_slice(
        placed, grad_w_out.reshape(own, 1, width, model), (0, mine, 0, 0)
    )
    part_out = collect(placed.reshape(-1, model))
    out_out = lax.psum_scatter(part_out, "seq", scatter_dimension=1, tiled=True)
    part_qkv = collect(grad_w_qkv)
    out_qkv = lax.all_to_all(
        part_qkv.reshape(r_in, -1, 1, width), "seq", 1, 2, tiled=True
    ).reshape(r_in, -1)

    def widen(array, outer, inner):
        blank = jnp.zeros((outer, parts, inner), jnp.float32)
        array = array.reshape(outer, 1, inner)
        return lax.dynamic_update_slice(blank, array, (0, mine, 0)).reshape(shards, -1)

    gain_sums = jnp.concatenate(
        [
            widen(grad_gain_qk, own, width),
            grad_gain_a.reshape(shards, -1),
            widen(grad_gain_u, shards, piece),
            widen(grad_gain_v, shards, piece),
            grad_gain_m.reshape(shards, -1),
        ],
        axis=1,
    )
    gain_sums = lax.psum(collect(gain_sums), "seq")[0]
    outs = jnp.split(gain_sums, edges)
    return (
        output[None],
        grad_inputs[None],
        out_qkv.astype(jnp.float32),
        out_out.astype(jnp.float32),
        out_uv.astype(jnp.float32),
        out_down.astype(jnp.float32),
        outs[0],
        outs[1],
        outs[2],
        outs[3],
        outs[4],
    )


MESH = pl.DeviceIdType.MESH
TILE = 128
QROWS = 128


def loop(count, body):
    def run(index, carry):
        body(index)
        return carry

    lax.fori_loop(0, count, run, 0)


def at_rows(ref, block, size=TILE):
    return ref.at[pl.ds(pl.multiple_of(block * size, size), size), :]


def cols(block, size=TILE):
    return pl.ds(pl.multiple_of(block * size, size), size)


def mean_last(value):
    return jnp.sum(value, axis=-1, keepdims=True) * (1.0 / value.shape[-1])


class Slots:
    def __init__(self):
        self.count = 0

    def take(self, count):
        base = self.count
        self.count = base + count
        return base


def fused_layer(sizes, *refs):
    (parts, lines, rows, model, deep, own_heads, width) = sizes
    slots_all = parts * rows
    span = own_heads * width
    hid = deep * lines * 2 // parts
    count_in, count_out = len(Inputs._fields), len(Results._fields)
    ins = Inputs(*refs[:count_in])
    outs = Results(*refs[count_in : count_in + count_out])
    table = buffers(sizes)
    rest = refs[count_in + count_out :]
    v = types.SimpleNamespace(**dict(zip(table, rest[: len(table)])))
    send_sem, recv_sem = rest[len(table) :]

    s = lax.axis_index("seq")
    f = lax.axis_index("fsdp")
    z = f // 2
    c = f % 2
    other = 1 - c
    mate = (s, 2 * z + other)
    slots = Slots()

    def put(src, dst, target, send_slot, recv_slot):
        pltpu.make_async_remote_copy(
            src_ref=src,
            dst_ref=dst,
            send_sem=send_sem.at[send_slot],
            recv_sem=recv_sem.at[recv_slot],
            device_id=target,
            device_id_type=MESH,
        ).start()

    def descriptor(ref, slot):
        return pltpu.make_async_remote_copy(
            src_ref=ref,
            dst_ref=ref,
            send_sem=send_sem.at[slot],
            recv_sem=recv_sem.at[slot],
            device_id=mate,
            device_id_type=MESH,
        )

    def landed(ref, slot):
        descriptor(ref, slot).wait_recv()

    finals = []

    def later(ref, slot, when=None):
        finals.append((ref, slot, when))

    def plane(distance):
        return (s + distance) % parts

    def plane_from(distance):
        return (s + parts - distance) % parts

    def line(distance):
        return (z + distance) % lines

    def line_from(distance):
        return (z + lines - distance) % lines

    barrier = pltpu.get_barrier_semaphore()
    for distance in range(1, parts):
        pl.semaphore_signal(barrier, inc=1, device_id=(plane(distance), f), device_id_type=MESH)
    for distance in range(1, 2 * lines):
        target = (s, (f + distance) % (2 * lines))
        pl.semaphore_signal(barrier, inc=1, device_id=target, device_id_type=MESH)

    edges = [0, TILE, 2 * TILE, 2 * TILE + deep, 2 * TILE + 2 * deep, 3 * TILE + 2 * deep]
    own_gains = (ins.s_qk, ins.alpha_a, ins.s_u, ins.s_v, ins.alpha_m)
    for place, own_gain in enumerate(own_gains):
        v.gain_all[f, :, edges[place] : edges[place + 1]] = own_gain[...].astype(jnp.float32)
    own_row = pl.ds(pl.multiple_of(s * rows, rows), rows)
    own_w = pl.ds(pl.multiple_of(f * TILE, TILE), TILE)
    v.x_all[own_row, :] = ins.tokens[...]

    pl.semaphore_wait(barrier, parts - 1 + 2 * lines - 1)

    qkv_slot = slots.take(3)
    for index in range(3):
        chunk = 3 * s + index
        block = chunk // parts
        target = chunk % parts

        @pl.when(target == s)
        def _():
            v.wq[own_w, cols(block, span)] = ins.w_qkv[:, index * span : (index + 1) * span]

        @pl.when(target != s)
        def _():
            put(
                ins.w_qkv.at[:, index * span : (index + 1) * span],
                v.wq.at[own_w, cols(block, span)],
                (target, f),
                qkv_slot + index,
                qkv_slot + block,
            )

        later(ins.w_qkv.at[:, index * span : (index + 1) * span], qkv_slot + index, target != s)

    part_cols = model // parts
    out_slot = slots.take(parts)
    step_out = (z + parts - s) % parts

    @pl.when(z == s)
    def _():
        v.wo[cols(c), cols(s, part_cols)] = ins.w_out[...]

    @pl.when(z != s)
    def _():
        put(
            ins.w_out,
            v.wo.at[cols(c), cols(s, part_cols)],
            (z, f),
            out_slot,
            out_slot + step_out,
        )

    later(ins.w_out, out_slot, z != s)

    token_slot = slots.take(parts)
    for distance in range(1, parts):
        put(
            ins.tokens,
            v.x_all.at[own_row, :],
            (plane(distance), f),
            token_slot + distance,
            token_slot + distance,
        )
        later(ins.tokens, token_slot + distance)

    uv_slot = slots.take(parts)
    blocks_uv = 2 * hid // parts // TILE
    wide = blocks_uv * TILE
    for index in range(blocks_uv):
        v.wu[own_w, pl.ds(pl.multiple_of(s * wide + index * TILE, TILE), TILE)] = ins.w_uv[
            :, pl.ds(pl.multiple_of(index * parts * TILE + s * TILE, TILE), TILE)
        ]
    for distance in range(1, parts):
        target = plane(distance)
        for index in range(blocks_uv):
            put(
                ins.w_uv.at[:, pl.ds(pl.multiple_of((index * parts + target) * TILE, TILE), TILE)],
                v.wu.at[own_w, pl.ds(pl.multiple_of(s * wide + index * TILE, TILE), TILE)],
                (target, f),
                uv_slot + distance,
                uv_slot + distance,
            )
        later(v.wu.at[own_w, cols(s, wide)], uv_slot + distance)

    down_slot = slots.take(parts)
    v.wd[own_w, cols(s, part_cols)] = ins.w_down[cols(s), :]
    for distance in range(1, parts):
        target = plane(distance)
        put(
            ins.w_down.at[cols(target), :],
            v.wd.at[own_w, cols(s, part_cols)],
            (target, f),
            down_slot + distance,
            down_slot + distance,
        )
        later(ins.w_down.at[cols(target), :], down_slot + distance)

    gain_slot = slots.take(2 * lines)
    for distance in range(1, 2 * lines):
        put(
            v.gain_all.at[f],
            v.gain_all.at[f],
            (s, (f + distance) % (2 * lines)),
            gain_slot + distance,
            gain_slot + distance,
        )
        later(v.gain_all.at[f], gain_slot + distance)

    def shard(ref, chip, core):
        return at_rows(ref, 2 * chip + core)

    inner = z * (lines - 1 - z) > 0
    outer = z * (lines - 1 - z) == 0

    def line_send(ref, base):
        own = shard(ref, z, c)
        for distance in (2, 1, 3):
            target = line(distance)
            near = (z - target) * (z - target) < (lines - 1) * (lines - 1)

            @pl.when(near)
            def _():
                put(own, own, (s, 2 * target + c), base + distance, base + distance)

            later(own, base + distance, near)
        put(own, own, mate, base, base)
        later(own, base)

    def line_relay(ref, base):
        block = shard(ref, line_from(2), c)
        slot = slots.take(1)

        @pl.when(inner)
        def _():
            landed(block, base + 2)
            put(block, block, (s, 2 * (lines - 1) * (z - 1) + c), slot, base + 2 * z - 1)

        later(block, slot, inner)

    def line_forward(ref, base):
        for distance in (1, 3, 2):
            block = shard(ref, line_from(distance), c)
            if distance == 2:

                @pl.when(outer)
                def _():
                    landed(block, base + distance)

            else:
                landed(block, base + distance)
            put(block, block, mate, base + lines + distance, base + lines + distance)
            later(block, base + lines + distance)

    def mate_wait(ref, base):
        landed(shard(ref, z, other), base)
        for distance in range(1, lines):
            landed(shard(ref, line_from(distance), other), base + lines + distance)

    wq_slot, wu_slot, wd_slot = (slots.take(2 * lines) for _ in range(3))
    wo_slot = slots.take(2 * lines)

    for block in range(3):
        source = (parts * block + s) // 3

        @pl.when(source != s)
        def _():
            landed(v.wq.at[own_w, block * span : (block + 1) * span], qkv_slot + block)

    line_send(v.wq, wq_slot)
    relay_out = slots.take(1)

    @pl.when(z == s)
    def _():
        for distance in range(1, parts):
            landed(v.wo.at[cols(c), cols(plane_from(distance), part_cols)], out_slot + distance)
        own = v.wo.at[cols(c), :]
        for distance in range(1, lines):
            target = line(distance)
            near = (z - target) * (z - target) < (lines - 1) * (lines - 1)

            @pl.when(near)
            def _():
                put(own, own, (s, 2 * target + c), wo_slot + distance, wo_slot)

    for distance in range(1, lines):
        target = line(distance)
        near = (z - target) * (z - target) < (lines - 1) * (lines - 1)
        later(v.wo.at[cols(c), :], wo_slot + distance, (z == s) & near)

    lengths = [ins.lengths[0, i] for i in range(ins.lengths.shape[1])]

    def slot_facts(slot):
        end = 0
        member = jnp.zeros(slot.shape, jnp.int32)
        begin = jnp.zeros(slot.shape, jnp.int32)
        for length in lengths[:-1]:
            end = end + length
            after = slot >= end
            member = member + after.astype(jnp.int32)
            begin = jnp.where(after, end, begin)
        valid = member < len(lengths) - 1
        segment = jnp.where(valid, member, len(lengths) - 1 + slot)
        place = jnp.where(valid, slot - begin, 0)
        return segment, place, valid

    lane = lax.broadcasted_iota(jnp.int32, (1, TILE), 1)
    low_half = lane < width
    first_quarter = lane % width < width // 2
    frequency = jnp.exp(
        (lane % (width // 2)).astype(jnp.float32) * (-2.0 * math.log(10000.0) / width)
    )
    turn_sign = jnp.where(first_quarter, -1.0, 1.0)

    def tables(block):
        here = pl.ds(pl.multiple_of(block * TILE, TILE), TILE)
        slot = block * TILE + lax.broadcasted_iota(jnp.int32, (TILE, 1), 0)
        segment, place, _ = slot_facts(slot)
        angle = place.astype(jnp.float32) * frequency
        v.cosine[here, :] = jnp.cos(angle)
        v.sine[here, :] = jnp.sin(angle) * turn_sign
        key_slot = lax.broadcasted_iota(jnp.int32, (1, slots_all), 1)
        key_segment = slot_facts(key_slot)[0]
        kept = (segment == key_segment) & (slot >= key_slot)
        v.bias[here, :] = jnp.where(kept, 0.0, -1e30)

    loop(slots_all // TILE, tables)
    line_relay(v.wq, wq_slot)
    for distance in range(1, parts):
        landed(at_rows(v.x_all, plane_from(distance), rows), token_slot + distance)
    for distance in range(1, parts):
        landed(v.wu.at[own_w, cols(plane_from(distance), wide)], uv_slot + distance)
    line_send(v.wu, wu_slot)

    middle = (s > 0) & (s < lines - 1)
    far_end = (lines - 1) - s
    pass_on = jnp.logical_not(middle) & inner & (z - s != 1) & (s - z != 1)
    at_far = jnp.logical_not(middle) & (z == far_end)
    out_relayed = pass_on

    @pl.when(pass_on)
    def _():
        own = v.wo.at[cols(c), :]
        landed(own, wo_slot)
        put(own, own, (s, 2 * far_end + c), relay_out, wo_slot)

    later(v.wo.at[cols(c), :], relay_out, pass_on)

    def mate_blocks(name_all, ref, stage, slot):
        for block in range(lines):
            here = slice(block * TILE, (block + 1) * TILE)
            stage[here, :] = name_all[:, cols(2 * block + other)].T
        put(stage, ref.at[:, slots_all:], mate, slot, slot)
        later(stage, slot)
        for block in range(lines):
            here = slice(block * TILE, (block + 1) * TILE)
            ref[here, :slots_all] = name_all[:, cols(2 * block + c)].T

    mate_x_slot = slots.take(1)
    mate_blocks(v.x_all, v.turned_x, v.stage_x, mate_x_slot)
    for distance in range(1, parts):
        landed(v.wd.at[own_w, cols(plane_from(distance), part_cols)], down_slot + distance)
    line_send(v.wd, wd_slot)

    for distance in range(1, 2 * lines):
        landed(v.gain_all.at[(f + 2 * lines - distance) % (2 * lines)], gain_slot + distance)

    def gain(block, offset):
        return v.gain_all[block, :, pl.ds(pl.multiple_of(offset, TILE), TILE)]

    for block in range(2 * lines):
        here = slice(block * TILE, (block + 1) * TILE)
        v.gain_a[:, here] = gain(block, edges[1])
        v.gain_u[:, here] = gain(block, edges[2] + s * TILE)
        v.gain_v[:, here] = gain(block, edges[3] + s * TILE)
        v.gain_m[:, here] = gain(block, edges[4])
    for block in range(span // TILE):
        v.gain_qk[:, block * TILE : (block + 1) * TILE] = gain(span // TILE * s + block, 0)

    line_forward(v.wq, wq_slot)
    mate_wait(v.wq, wq_slot)

    def mix(index):
        v.raw[:, cols(index, span)] = product(
            v.x_all[...], v.wq[:, cols(index, span)], ((1,), (0,))
        )

    loop(3, mix)

    def swap(value):
        return jnp.where(
            first_quarter,
            pltpu.roll(value, TILE - width // 2, 1),
            pltpu.roll(value, width // 2, 1),
        )

    def head_mean(value):
        one = jnp.sum(jnp.where(low_half, value, 0.0), axis=-1, keepdims=True)
        two = jnp.sum(jnp.where(low_half, 0.0, value), axis=-1, keepdims=True)
        return jnp.where(low_half, one, two) * (1.0 / width)

    pairs = span // TILE
    blocks = slots_all // TILE

    def prepare_block(index):
        here = pl.ds(pl.multiple_of(index % blocks * TILE, TILE), TILE)
        group = index // blocks
        there = cols(group)
        value = v.raw[here, there]
        turned = value * v.cosine[here, :] + swap(value) * v.sine[here, :]
        inverse = lax.rsqrt(head_mean(turned * turned) + epsilon)
        normed = turned * inverse
        v.normed[here, there] = normed
        v.inverse[here, there] = inverse
        v.qkv[here, there] = low(normed * v.gain_qk[:, cols(group % pairs)])

    loop(2 * pairs * blocks, prepare_block)

    def keep_value(index):
        here = pl.ds(pl.multiple_of(index * TILE, TILE), TILE)
        v.qkv[here, 2 * span :] = low(v.raw[here, 2 * span :])

    loop(blocks, keep_value)

    scale = 1.0 / math.sqrt(width)
    halves = (low_half, jnp.logical_not(low_half))

    def attend(pair):
        q_cols, k_cols, v_cols = cols(pair), cols(pairs + pair), cols(2 * pairs + pair)
        for block in range(blocks):
            here = slice(block * TILE, (block + 1) * TILE)
            seen = slice(0, (block + 1) * TILE)
            results = []
            for half in range(2):
                query = jnp.where(halves[half], v.qkv[here, q_cols], 0.0).astype(jnp.bfloat16)
                score = product(query, v.qkv[seen, k_cols], ((1,), (1,))) * scale
                score = score + v.bias[here, seen]
                peak = jnp.max(score, axis=1, keepdims=True)
                raised = jnp.exp(score - peak)
                summed = jnp.sum(raised, axis=1, keepdims=True)
                weight = low(raised / summed)
                results.append(product(weight, v.qkv[seen, v_cols], ((1,), (0,))))
                v.total[2 * pair + half, here, :] = peak + jnp.log(summed)
            v.attended[here, q_cols] = low(jnp.where(low_half, results[0], results[1]))

    loop(pairs, attend)
    mate_att_slot = slots.take(1)
    v.stage_att[...] = v.attended[:, cols(other)].T
    v.turned_att[:, :slots_all] = v.attended[:, cols(c)].T

    own_out = v.wo.at[cols(c), :]

    @pl.when((z != s) & jnp.logical_not(out_relayed))
    def _():
        landed(own_out, wo_slot)

    put(v.stage_att, v.turned_att.at[:, slots_all:], mate, mate_att_slot, mate_att_slot)
    later(v.stage_att, mate_att_slot)
    put(own_out, own_out, mate, wo_slot + lines, wo_slot + lines)
    later(own_out, wo_slot + lines)
    landed(v.wo.at[cols(other), :], wo_slot + lines)

    count = 4
    piece = model // count

    def plane_sum(sums, arrived, base, tile):
        def send(index):
            there = cols(index, piece)
            for distance in range(1, parts):
                target = plane(distance)
                put(
                    sums.at[pl.ds(pl.multiple_of(target * rows, rows), rows), there],
                    arrived.at[distance - 1, :, there],
                    (target, f),
                    base + distance,
                    base + distance,
                )

        def step(index):
            sums[:, cols(index, piece)] = low(tile(index))

            @pl.when(index > 0)
            def _():
                send(index - 1)

        loop(count, step)
        send(count - 1)
        for distance in range(1, parts):
            later(arrived.at[distance - 1], base + distance)

    def plane_sum_wait(arrived, base):
        for distance in range(1, parts):
            landed(arrived.at[distance - 1], base + distance)

    def plane_total(sums, arrived, here, at):
        total = sums[here, :].astype(jnp.float32)
        for distance in range(1, parts):
            total = total + arrived[distance - 1, at, :].astype(jnp.float32)
        return total

    chunk_rows = 32

    def chunk(index):
        at = pl.ds(pl.multiple_of(index * chunk_rows, chunk_rows), chunk_rows)
        here = pl.ds(pl.multiple_of(s * rows + index * chunk_rows, chunk_rows), chunk_rows)
        return at, here

    def plane_share(shared, base, make):
        def send(index):
            own = shared.at[chunk(index)[1], :]
            for distance in range(1, parts):
                put(own, own, (plane(distance), f), base + distance, base + distance)

        def step(index):
            make(index)

            @pl.when(index > 0)
            def _():
                send(index - 1)

        loop(rows // chunk_rows, step)
        send(rows // chunk_rows - 1)
        for distance in range(1, parts):
            later(shared.at[own_row, :], base + distance)

    def plane_share_wait(shared, base):
        for distance in range(1, parts):
            landed(at_rows(shared, plane_from(distance), rows), base + distance)

    branch_slot = slots.take(parts)
    plane_sum(
        v.part_branch,
        v.got_branch,
        branch_slot,
        lambda index: product(v.attended[...], v.wo[:, cols(index, piece)], ((1,), (0,))),
    )
    line_relay(v.wu, wu_slot)
    line_forward(v.wu, wu_slot)
    plane_sum_wait(v.got_branch, branch_slot)

    def blended(base, branch, alpha):
        inverse_branch = lax.rsqrt(mean_last(branch * branch) + epsilon)
        normed = branch * inverse_branch
        mixed = base + alpha * (normed - base)
        inverse = lax.rsqrt(mean_last(mixed * mixed) + epsilon)
        return normed, inverse_branch, mixed * inverse, inverse

    def blended_back(grad, base, alpha, normed, inverse_branch, result, inverse):
        grad_mixed = inverse * (grad - result * mean_last(grad * result))
        grad_normed = alpha * grad_mixed
        grad_branch = inverse_branch * (grad_normed - normed * mean_last(grad_normed * normed))
        grad_alpha = jnp.sum(grad_mixed * (normed - base), axis=0, keepdims=True)
        return grad_mixed - grad_normed, grad_branch, grad_alpha

    def make_first(index):
        at, here = chunk(index)
        base = ins.tokens[at, :].astype(jnp.float32)
        normed, inverse_branch, result, inverse = blended(
            base, plane_total(v.part_branch, v.got_branch, here, at), v.gain_a[...]
        )
        v.branch_normed[at, :] = normed
        v.branch_inverse[at, :] = inverse_branch
        v.first[at, :] = result
        v.first_inverse[at, :] = inverse
        v.first_all[here, :] = low(result)

    first_slot = slots.take(parts)
    plane_share(v.first_all, first_slot, make_first)
    mate_wait(v.wu, wu_slot)
    plane_share_wait(v.first_all, first_slot)

    def gate_tile(index):
        there = cols(index, 256)
        v.up[:, there] = product(v.first_all[...], v.wu[:, there], ((1,), (0,)))
        v.gate[:, there] = product(
            v.first_all[...],
            v.wu[:, pl.ds(pl.multiple_of(hid + index * 256, 256), 256)],
            ((1,), (0,)),
        )

        def rows_of(block):
            here = pl.ds(pl.multiple_of(block * 64, 64), 64)
            scaled = v.gate[here, there] * v.gain_v[:, there]
            passed = scaled / (1.0 + jnp.exp(-scaled))
            v.hidden[here, there] = low(v.up[here, there] * v.gain_u[:, there] * passed)

        loop(slots_all // 64, rows_of)

    loop(hid // 512, gate_tile)
    line_relay(v.wd, wd_slot)
    loop(hid // 512, lambda index: gate_tile(hid // 512 + index))
    mate_hidden_slot = slots.take(1)
    mate_blocks(v.hidden, v.turned_hidden, v.stage_hidden, mate_hidden_slot)
    mate_first_slot = slots.take(1)
    mate_blocks(v.first_all, v.turned_first, v.stage_first, mate_first_slot)
    line_forward(v.wd, wd_slot)
    mate_wait(v.wd, wd_slot)
    down_sum_slot = slots.take(parts)
    plane_sum(
        v.part_down,
        v.got_down,
        down_sum_slot,
        lambda index: product(v.hidden[...], v.wd[:, cols(index, piece)], ((1,), (0,))),
    )
    plane_sum_wait(v.got_down, down_sum_slot)
    v.grad_a[...] = jnp.zeros_like(v.grad_a)
    v.grad_m[...] = jnp.zeros_like(v.grad_m)

    def finish(index):
        at, here = chunk(index)
        slot = s * rows + index * chunk_rows
        slot = slot + lax.broadcasted_iota(jnp.int32, (chunk_rows, 1), 0)
        keep = slot_facts(slot)[2].astype(jnp.float32)
        base = v.first[at, :]
        alpha = v.gain_m[...]
        normed, inverse_branch, result, inverse = blended(
            base, plane_total(v.part_down, v.got_down, here, at), alpha
        )
        outs.output[at, :] = low(result * keep)
        grad = ins.cotangent[at, :].astype(jnp.float32) * keep
        grad_base, grad_down, grad_alpha = blended_back(
            grad, base, alpha, normed, inverse_branch, result, inverse
        )
        v.grad_first[at, :] = grad_base
        v.gd[here, :] = low(grad_down)
        v.grad_m[...] += grad_alpha

    gd_slot = slots.take(parts)
    plane_share(v.gd, gd_slot, finish)
    plane_share_wait(v.gd, gd_slot)
    mate_gd_slot = slots.take(1)
    first_half = slice(0, slots_all)
    second_half = slice(slots_all, 2 * slots_all)
    put(v.gd.at[first_half, :], v.gd.at[second_half, :], mate, mate_gd_slot, mate_gd_slot)
    later(v.gd.at[first_half, :], mate_gd_slot)

    ends = (lines - 1) * (1 - z % 2)
    mids = 2 - z // 2
    last = (2 * z + 1) % (lines + 1)
    beside = z + 1 - 2 * (z % 2)

    def weight_grad(turned, right, grads, arrived, columns, base):
        def send(index):
            there = cols(index, 256)
            put(
                grads.at[ends, :, there],
                arrived.at[0, :, there],
                (s, 2 * beside + c),
                base,
                base,
            )
            mid_slot = 2 - z * (lines - 1 - z) // 2
            put(
                grads.at[mids, :, there],
                arrived.at[mid_slot, :, there],
                (s, 2 * mids + c),
                base + 1,
                base + mid_slot,
            )

            @pl.when(outer)
            def _():
                put(
                    grads.at[last, :, there],
                    arrived.at[3, :, there],
                    (s, 2 * last + c),
                    base + 2,
                    base + 3,
                )

        def step(index):
            there = cols(index, 256)
            total = product(turned[...], right[:, there], ((1,), (0,)))
            grads[:, :, there] = low(total).reshape(lines, TILE, 256)

            @pl.when(index > 0)
            def _():
                send(index - 1)

        loop(columns // 256, step)
        send(columns // 256 - 1)
        for index in range(3):
            later(grads.at[0], base + index)

    def weight_combine(grads, arrived, columns, base):
        @pl.when(inner)
        def _():
            landed(arrived.at[0], base)

            def tile(index):
                there = cols(index, 256)
                total = grads[last, :, there].astype(jnp.float32)
                grads[last, :, there] = low(total + arrived[0, :, there].astype(jnp.float32))

            loop(columns // 256, tile)
            put(
                grads.at[last], arrived.at[1], (s, 2 * last + c), base + 2, base + 1
            )

    def gate_back(index):
        there = cols(index, 256)
        there_gate = pl.ds(pl.multiple_of(hid + index * 256, 256), 256)
        v.grad_hidden[...] = low(product(v.gd[first_half, :], v.wd[there, :], ((1,), (1,))))
        v.grad_u[:, there] = jnp.zeros((1, 256), jnp.float32)
        v.grad_v[:, there] = jnp.zeros((1, 256), jnp.float32)

        def rows_of(block):
            here = pl.ds(pl.multiple_of(block * 64, 64), 64)
            grad = v.grad_hidden[here, :].astype(jnp.float32)
            up = v.up[here, there]
            gate = v.gate[here, there]
            gain_u = v.gain_u[:, there]
            gain_v = v.gain_v[:, there]
            scaled = gate * gain_v
            squash = 1.0 / (1.0 + jnp.exp(-scaled))
            passed = scaled * squash
            grad_scaled_up = grad * passed
            grad_scaled = grad * (up * gain_u) * (squash + passed * (1.0 - squash))
            v.gu[here, there] = low(grad_scaled_up * gain_u)
            v.gu[here, there_gate] = low(grad_scaled * gain_v)
            v.grad_u[:, there] += jnp.sum(grad_scaled_up * up, axis=0, keepdims=True)
            v.grad_v[:, there] += jnp.sum(grad_scaled * gate, axis=0, keepdims=True)

        loop(slots_all // 64, rows_of)

    loop(1, gate_back)
    landed(v.turned_x.at[:, second_half], mate_x_slot)
    landed(v.turned_first.at[:, second_half], mate_first_slot)
    landed(v.turned_hidden.at[:, second_half], mate_hidden_slot)
    landed(v.gd.at[second_half, :], mate_gd_slot)
    line_down_slot = slots.take(lines)
    weight_grad(v.turned_hidden, v.gd, v.send_down, v.line_down, model, line_down_slot)
    loop(hid // 256 - 1, lambda index: gate_back(index + 1))
    mate_gu_slot = slots.take(1)
    put(v.gu.at[first_half, :], v.gu.at[second_half, :], mate, mate_gu_slot, mate_gu_slot)
    later(v.gu.at[first_half, :], mate_gu_slot)
    first_sum_slot = slots.take(parts)
    plane_sum(
        v.part_first,
        v.got_first,
        first_sum_slot,
        lambda index: product(v.gu[first_half, :], v.wu[cols(index, piece), :], ((1,), (1,))),
    )
    weight_combine(v.send_down, v.line_down, model, line_down_slot)
    landed(v.gu.at[second_half, :], mate_gu_slot)
    line_uv_slot = slots.take(lines)
    weight_grad(v.turned_first, v.gu, v.send_uv, v.line_uv, 2 * hid, line_uv_slot)
    plane_sum_wait(v.got_first, first_sum_slot)

    def back_first(index):
        at, here = chunk(index)
        grad = v.grad_first[at, :] + plane_total(v.part_first, v.got_first, here, at)
        grad_base, grad_branch, grad_alpha = blended_back(
            grad,
            ins.tokens[at, :].astype(jnp.float32),
            v.gain_a[...],
            v.branch_normed[at, :],
            v.branch_inverse[at, :],
            v.first[at, :],
            v.first_inverse[at, :],
        )
        v.grad_tokens[at, :] = grad_base
        v.gb[here, :] = low(grad_branch)
        v.grad_a[...] += grad_alpha

    gb_slot = slots.take(parts)
    plane_share(v.gb, gb_slot, back_first)
    weight_combine(v.send_uv, v.line_uv, 2 * hid, line_uv_slot)
    plane_share_wait(v.gb, gb_slot)
    mate_gb_slot = slots.take(1)
    put(v.gb.at[first_half, :], v.gb.at[second_half, :], mate, mate_gb_slot, mate_gb_slot)
    later(v.gb.at[first_half, :], mate_gb_slot)

    v.grad_att[...] = low(product(v.gb[first_half, :], v.wo[...], ((1,), (1,))))
    landed(v.turned_att.at[:, second_half], mate_att_slot)
    landed(v.gb.at[second_half, :], mate_gb_slot)
    line_out_slot = slots.take(lines)

    def out_tile(index):
        there = cols(index, 256)
        v.send_out[:, there] = low(product(v.turned_att[...], v.gb[:, there], ((1,), (0,))))

    loop(model // 256, out_tile)
    step_line = (s + lines - z) % lines

    @pl.when(z != s)
    def _():
        put(
            v.send_out,
            v.line_out.at[step_line - 1],
            (s, 2 * s + c),
            line_out_slot,
            line_out_slot + step_line,
        )

    later(v.send_out, line_out_slot, z != s)
    v.grad_qkv[...] = jnp.zeros_like(v.grad_qkv)

    def attend_back(pair):
        q_cols, k_cols, v_cols = cols(pair), cols(pairs + pair), cols(2 * pairs + pair)
        for block in range(blocks):
            here = slice(block * TILE, (block + 1) * TILE)
            seen = slice(0, (block + 1) * TILE)
            results = []
            for half in range(2):
                query = jnp.where(halves[half], v.qkv[here, q_cols], 0.0).astype(jnp.bfloat16)
                grad = jnp.where(halves[half], v.grad_att[here, q_cols], 0.0)
                grad = grad.astype(jnp.bfloat16)
                score = product(query, v.qkv[seen, k_cols], ((1,), (1,))) * scale
                score = score + v.bias[here, seen]
                share = jnp.exp(score - v.total[2 * pair + half, here, :])
                grad_share = product(grad, v.qkv[seen, v_cols], ((1,), (1,)))
                inner = jnp.sum(share * grad_share, axis=1, keepdims=True)
                grad_score = low(share * (grad_share - inner))
                results.append(product(grad_score, v.qkv[seen, k_cols], ((1,), (0,))))
                v.grad_qkv[seen, v_cols] += product(low(share), grad, ((0,), (0,)))
                v.grad_qkv[seen, k_cols] += product(grad_score, query, ((0,), (0,)))
            v.grad_qkv[here, q_cols] = jnp.where(low_half, results[0], results[1])

    loop(pairs, attend_back)
    v.grad_qk[...] = jnp.zeros_like(v.grad_qk)

    def prepare_back(index):
        here = pl.ds(pl.multiple_of(index % blocks * TILE, TILE), TILE)
        group = index // blocks
        there = cols(group)
        pair = cols(group % pairs)
        grad = low(v.grad_qkv[here, there] * scale).astype(jnp.float32)
        normed = v.normed[here, there]
        v.grad_qk[:, pair] += jnp.sum(grad * normed, axis=0, keepdims=True)
        grad = grad * v.gain_qk[:, pair]
        grad = v.inverse[here, there] * (grad - normed * head_mean(grad * normed))
        back = grad * v.cosine[here, :] - swap(grad) * v.sine[here, :]
        v.gm[here, there] = low(back)

    loop(2 * pairs * blocks, prepare_back)

    def value_back(index):
        here = pl.ds(pl.multiple_of(index * TILE, TILE), TILE)
        v.gm[here, 2 * span :] = low(v.grad_qkv[here, 2 * span :])

    loop(blocks, value_back)
    mate_gm_slot = slots.take(1)
    put(v.gm.at[first_half, :], v.gm.at[second_half, :], mate, mate_gm_slot, mate_gm_slot)
    later(v.gm.at[first_half, :], mate_gm_slot)

    v.gain_part[...] = jnp.zeros_like(v.gain_part)
    for block in range(2 * lines):
        here = slice(block * TILE, (block + 1) * TILE)
        local_pair = block % (span // TILE) * TILE
        qk = v.grad_qk[:, local_pair : local_pair + TILE]
        mine = (s == block // (span // TILE)).astype(jnp.float32)
        v.gain_part[block, :, edges[0] : edges[1]] = qk * mine
        v.gain_part[block, :, edges[1] : edges[2]] = v.grad_a[:, here]
        v.gain_part[block, :, cols(edges[2] // TILE + s)] = v.grad_u[:, here]
        v.gain_part[block, :, cols(edges[3] // TILE + s)] = v.grad_v[:, here]
        v.gain_part[block, :, edges[4] : edges[5]] = v.grad_m[:, here]

    inputs_slot = slots.take(parts)
    plane_sum(
        v.part_inputs,
        v.got_inputs,
        inputs_slot,
        lambda index: product(v.gm[first_half, :], v.wq[cols(index, piece), :], ((1,), (1,))),
    )
    gain_line_slot = slots.take(2 * lines)
    for distance in range(1, 2 * lines):
        target = (f + distance) % (2 * lines)
        put(
            v.gain_part.at[target],
            v.gain_got.at[distance - 1],
            (s, target),
            gain_line_slot + distance,
            gain_line_slot + distance,
        )
        later(v.gain_got.at[distance - 1], gain_line_slot + distance)
    landed(v.gm.at[second_half, :], mate_gm_slot)
    line_qkv_slot = slots.take(lines)
    weight_grad(v.turned_x, v.gm, v.send_qkv, v.line_qkv, 3 * span, line_qkv_slot)

    plane_sum_wait(v.got_inputs, inputs_slot)

    def finish_inputs(index):
        at, here = chunk(index)
        outs.input_grad[at, :] = v.grad_tokens[at, :] + plane_total(v.part_inputs, v.got_inputs, here, at)

    loop(rows // chunk_rows, finish_inputs)

    def line_total(grads, arrived, done, columns, base):
        def add(slots_in):
            for slot in slots_in:
                landed(arrived.at[slot], base + slot)

            def tile(index):
                there = cols(index, 256)
                total = grads[z, :, there].astype(jnp.float32)
                for slot in slots_in:
                    total = total + arrived[slot, :, there].astype(jnp.float32)
                done[:, there] = low(total)

            loop(columns // 256, tile)

        pl.when(outer)(lambda: add((0, 1)))
        pl.when(inner)(lambda: add((1, 2, 3)))

    weight_combine(v.send_qkv, v.line_qkv, 3 * span, line_qkv_slot)
    line_total(v.send_down, v.line_down, v.done_down, model, line_down_slot)
    back_down_slot = slots.take(parts)
    for distance in range(1, parts):
        target = plane(distance)
        put(
            v.done_down.at[:, cols(target, part_cols)],
            outs.back_down.at[cols(s), :],
            (target, f),
            back_down_slot + distance,
            back_down_slot + distance,
        )
        later(v.done_down.at[:, cols(target, part_cols)], back_down_slot + distance)
    outs.back_down[cols(s), :] = v.done_down[:, cols(s, part_cols)]

    line_total(v.send_uv, v.line_uv, v.done_uv, 2 * hid, line_uv_slot)
    back_uv_slot = slots.take(parts)
    for distance in range(1, parts):
        target = plane(distance)
        for index in range(blocks_uv):
            put(
                v.done_uv.at[:, pl.ds(pl.multiple_of(target * wide + index * TILE, TILE), TILE)],
                outs.back_uv.at[s, :, index * TILE : (index + 1) * TILE],
                (target, f),
                back_uv_slot + distance,
                back_uv_slot + distance,
            )
        later(v.done_uv.at[:, cols(target, wide)], back_uv_slot + distance)
    outs.back_uv[s] = v.done_uv[:, cols(s, wide)]

    gain_plane_slot = slots.take(parts)
    for distance in range(1, 2 * lines):
        landed(v.gain_got.at[distance - 1], gain_line_slot + distance)
    total = v.gain_part[f]
    for distance in range(1, 2 * lines):
        total = total + v.gain_got[distance - 1]
    v.gain_sum[s] = total
    for distance in range(1, parts):
        put(
            v.gain_sum.at[s],
            v.gain_sum.at[s],
            (plane(distance), f),
            gain_plane_slot + distance,
            gain_plane_slot + distance,
        )
        later(v.gain_sum.at[s], gain_plane_slot + distance)

    line_total(v.send_qkv, v.line_qkv, v.done_qkv, 3 * span, line_qkv_slot)
    back_qkv_slot = slots.take(3)
    for block in range(3):
        chunk_of = parts * block + s
        target = chunk_of // 3
        index = chunk_of % 3
        source = v.done_qkv.at[:, block * span : (block + 1) * span]

        @pl.when(target == s)
        def _():
            outs.back_qkv[index] = source[...]

        @pl.when(target != s)
        def _():
            put(
                source,
                outs.back_qkv.at[index],
                (target, f),
                back_qkv_slot + block,
                back_qkv_slot + index,
            )

        later(source, back_qkv_slot + block, target != s)

    back_out_slot = slots.take(parts)

    @pl.when(z == s)
    def _():
        for distance in range(1, lines):
            landed(v.line_out.at[distance - 1], line_out_slot + distance)

        def tile(index):
            there = cols(index, 256)
            total = v.send_out[:, there].astype(jnp.float32)
            for distance in range(1, lines):
                total = total + v.line_out[distance - 1, :, there].astype(jnp.float32)
            v.done_out[:, there] = low(total)

        loop(model // 256, tile)
        for distance in range(1, parts):
            target = plane(distance)
            put(
                v.done_out.at[:, cols(target, part_cols)],
                outs.back_out,
                (target, f),
                back_out_slot + distance,
                back_out_slot,
            )
        outs.back_out[...] = v.done_out[:, cols(s, part_cols)]

    for distance in range(1, parts):
        later(outs.back_out, back_out_slot + distance, z == s)

    for distance in range(1, parts):
        landed(outs.back_down.at[cols(plane_from(distance)), :], back_down_slot + distance)
    for distance in range(1, parts):
        landed(outs.back_uv.at[plane_from(distance)], back_uv_slot + distance)
    for distance in range(1, parts):
        landed(v.gain_sum.at[plane_from(distance)], gain_plane_slot + distance)
    total = v.gain_sum[0]
    for source in range(1, parts):
        total = total + v.gain_sum[source]
    outs.gains[...] = total
    for index in range(3):
        source = (3 * s + index) % parts

        @pl.when(source != s)
        def _():
            landed(outs.back_qkv.at[index], back_qkv_slot + index)

    @pl.when(z != s)
    def _():
        landed(outs.back_out, back_out_slot)

    for ref, slot, when in finals:
        if when is None:
            descriptor(ref, slot).wait_send()
        else:

            @pl.when(when)
            def _():
                descriptor(ref, slot).wait_send()

    assert slots.count <= SLOTS_MOST, slots.count


SLOTS_MOST = 160


class Inputs(typing.NamedTuple):
    tokens: typing.Any
    lengths: typing.Any
    w_qkv: typing.Any
    w_out: typing.Any
    w_uv: typing.Any
    w_down: typing.Any
    s_qk: typing.Any
    alpha_a: typing.Any
    s_u: typing.Any
    s_v: typing.Any
    alpha_m: typing.Any
    cotangent: typing.Any


class Results(typing.NamedTuple):
    output: typing.Any
    input_grad: typing.Any
    back_qkv: typing.Any
    back_out: typing.Any
    back_uv: typing.Any
    back_down: typing.Any
    gains: typing.Any


def buffers(sizes):
    (parts, lines, rows, model, deep, own_heads, width) = sizes
    every = parts * rows
    span = own_heads * width
    hid = deep * lines * 2 // parts
    half = lines * TILE
    gains = 3 * TILE + 2 * deep
    bf16, f32 = jnp.bfloat16, jnp.float32
    return dict(
        wq=((model, 3 * span), bf16),
        wo=((span, model), bf16),
        wu=((model, 2 * hid), bf16),
        wd=((hid, model), bf16),
        gain_all=((2 * lines, 1, gains), f32),
        gain_a=((1, model), f32),
        gain_m=((1, model), f32),
        gain_u=((1, hid), f32),
        gain_v=((1, hid), f32),
        gain_qk=((1, span), f32),
        x_all=((every, model), bf16),
        first_all=((every, model), bf16),
        gd=((2 * every, model), bf16),
        gb=((2 * every, model), bf16),
        cosine=((every, TILE), f32),
        sine=((every, TILE), f32),
        bias=((every, every), f32),
        raw=((every, 3 * span), f32),
        normed=((every, 2 * span), f32),
        inverse=((every, 2 * span), f32),
        qkv=((every, 3 * span), bf16),
        total=((own_heads, every, 1), f32),
        attended=((every, span), bf16),
        branch_normed=((rows, model), f32),
        branch_inverse=((rows, 1), f32),
        first=((rows, model), f32),
        first_inverse=((rows, 1), f32),
        up=((every, hid), f32),
        gate=((every, hid), f32),
        hidden=((every, hid), bf16),
        grad_hidden=((every, 256), bf16),
        gu=((2 * every, 2 * hid), bf16),
        grad_first=((rows, model), f32),
        grad_tokens=((rows, model), f32),
        grad_att=((every, span), bf16),
        grad_qkv=((every, 3 * span), f32),
        gm=((2 * every, 3 * span), bf16),
        grad_a=((1, model), f32),
        grad_m=((1, model), f32),
        grad_u=((1, hid), f32),
        grad_v=((1, hid), f32),
        grad_qk=((1, span), f32),
        gain_part=((2 * lines, 1, gains), f32),
        gain_got=((2 * lines - 1, 1, gains), f32),
        gain_sum=((parts, 1, gains), f32),
        turned_x=((half, 2 * every), bf16),
        turned_first=((half, 2 * every), bf16),
        turned_hidden=((half, 2 * every), bf16),
        turned_att=((TILE, 2 * every), bf16),
        stage_x=((half, every), bf16),
        stage_first=((half, every), bf16),
        stage_hidden=((half, every), bf16),
        stage_att=((TILE, every), bf16),
        send_out=((TILE, model), bf16),
        line_out=((lines - 1, TILE, model), bf16),
        done_out=((TILE, model), bf16),
        part_branch=((every, model), bf16),
        got_branch=((parts - 1, rows, model), bf16),
        part_down=((every, model), bf16),
        got_down=((parts - 1, rows, model), bf16),
        part_first=((every, model), bf16),
        got_first=((parts - 1, rows, model), bf16),
        part_inputs=((every, model), bf16),
        got_inputs=((parts - 1, rows, model), bf16),
        send_qkv=((lines, TILE, 3 * span), bf16),
        line_qkv=((4, TILE, 3 * span), bf16),
        done_qkv=((TILE, 3 * span), bf16),
        send_uv=((lines, TILE, 2 * hid), bf16),
        line_uv=((4, TILE, 2 * hid), bf16),
        done_uv=((TILE, 2 * hid), bf16),
        send_down=((lines, TILE, model), bf16),
        line_down=((4, TILE, model), bf16),
        done_down=((TILE, model), bf16),
    )


def place_results(sizes, *refs):
    (parts, lines, rows, model, deep, own_heads, width) = sizes
    count = len(Results._fields)
    got = Results(*refs[:count])
    (output, inputs, qkv, out, uv, down, *gains) = refs[count:]
    output[...] = got.output[...]
    inputs[...] = got.input_grad[...]
    span = own_heads * width
    for index in range(qkv.shape[1] // span):
        qkv[:, index * span : (index + 1) * span] = got.back_qkv[index].astype(jnp.float32)
    out[...] = got.back_out[...].astype(jnp.float32)
    for source in range(parts):
        for index in range(uv.shape[1] // (parts * TILE)):
            there = (index * parts + source) * TILE
            here = slice(index * TILE, (index + 1) * TILE)
            uv[:, there : there + TILE] = got.back_uv[source, :, here].astype(jnp.float32)
    down[...] = got.back_down[...].astype(jnp.float32)
    start = 0
    for gain in gains:
        stop = start + gain.shape[-1]
        gain[...] = got.gains[:, start:stop]
        start = stop


def fused(sizes):
    (parts, lines, rows, model, deep, own_heads, width) = sizes
    span = own_heads * width
    hid = deep * lines * 2 // parts

    def run(tokens, lengths, w_qkv, w_out, w_uv, w_down, *others):
        gains, cotangent = others[:5], others[5]
        f32, bf16 = jnp.float32, jnp.bfloat16
        struct = jax.ShapeDtypeStruct
        middle = Results(
            struct(tokens.shape[1:], bf16),
            struct(tokens.shape[1:], f32),
            struct((3, TILE, span), bf16),
            struct(w_out.shape, bf16),
            struct((parts, TILE, 2 * hid // parts), bf16),
            struct(w_down.shape, bf16),
            struct((1, sum(g.shape[0] for g in gains)), f32),
        )
        shapes = [
            struct(tokens.shape[1:], bf16),
            struct(tokens.shape[1:], f32),
            *(struct(w.shape, f32) for w in (w_qkv, w_out, w_uv, w_down)),
            *(struct((1, g.shape[0]), f32) for g in gains),
        ]
        vmem = pl.BlockSpec(memory_space=pltpu.VMEM)
        specs = [vmem] * len(Inputs._fields)
        specs[1] = pl.BlockSpec(memory_space=pltpu.SMEM)
        scratch = [pltpu.VMEM(shape, kind) for shape, kind in buffers(sizes).values()]
        found = pl.pallas_call(
            functools.partial(fused_layer, sizes),
            out_shape=list(middle),
            in_specs=specs,
            out_specs=[vmem] * len(middle),
            scratch_shapes=[
                *scratch,
                pltpu.SemaphoreType.DMA((SLOTS_MOST,)),
                pltpu.SemaphoreType.DMA((SLOTS_MOST,)),
            ],
            compiler_params=pltpu.CompilerParams(
                collective_id=0, has_side_effects=True, vmem_limit_bytes=67043328
            ),
            name="fused_layer",
        )(
            tokens[0],
            lengths,
            w_qkv,
            w_out,
            w_uv,
            w_down,
            *(g.reshape(1, -1) for g in gains),
            cotangent[0],
        )
        outs = pl.pallas_call(
            functools.partial(place_results, sizes),
            out_shape=shapes,
            in_specs=[vmem] * len(middle),
            out_specs=[vmem] * len(shapes),
            compiler_params=pltpu.CompilerParams(vmem_limit_bytes=67043328),
            name="place_results",
        )(*found)
        return (
            outs[0][None],
            outs[1][None],
            *outs[2:6],
            *(g.reshape(-1) for g in outs[6:]),
        )

    return run


def choose(parts, shards):
    def run(*args):
        tokens, w_qkv, w_down = args[0], args[2], args[5]
        rows, model = tokens.shape[1:]
        deep, width = w_down.shape[0], model // H
        fits = shards == 2 * parts and rows == TILE and w_qkv.shape[0] == TILE
        fits = fits and deep == parts * TILE and 2 * width == TILE and H == 4 * parts
        if not fits:
            return local(*args)
        return fused((parts, shards // 2, rows, model, deep, H // parts, width))(*args)

    return run


def solution(mesh):
    return jax.shard_map(
        choose(mesh.shape["seq"], mesh.shape["fsdp"]),
        mesh=mesh,
        in_specs=(
            P("fsdp", "seq", None),
            P("fsdp", None),
            P("fsdp", "seq"),
            P("fsdp", "seq"),
            P("fsdp", "seq"),
            P("fsdp", "seq"),
            P("fsdp"),
            P("fsdp"),
            P("fsdp"),
            P("fsdp"),
            P("fsdp"),
            P("fsdp", "seq", None),
        ),
        out_specs=(
            P("fsdp", "seq", None),
            P("fsdp", "seq", None),
            P("fsdp", "seq"),
            P("fsdp", "seq"),
            P("fsdp", "seq"),
            P("fsdp", "seq"),
            P("fsdp"),
            P("fsdp"),
            P("fsdp"),
            P("fsdp"),
            P("fsdp"),
        ),
        check_vma=False,
    )
```

```python
import functools
import math
import types
import typing

import jax
import jax.numpy as jnp
from jax import lax
from jax.experimental import pallas as pl
from jax.experimental.pallas import tpu as pltpu
from jax.sharding import PartitionSpec as P

H = 16


epsilon = 1e-06


def layout(lengths_row, slot):
    columns = lengths_row.shape[0]
    ends = jnp.cumsum(lengths_row)
    starts = ends - lengths_row
    before = (slot[:, None] >= ends[None, : columns - 1]).astype(jnp.int32)
    member = jnp.sum(before, axis=1)
    picked = member[:, None] == jnp.arange(columns, dtype=jnp.int32)[None, :]
    begin = jnp.sum(jnp.where(picked, starts[None, :], 0), axis=1)
    valid = member < columns - 1
    segment = jnp.where(valid, member, columns - 1 + slot)
    place = jnp.where(valid, slot - begin, 0)
    return (segment, place, valid)


def rotary(place, width):
    half = width // 2
    frequency = jnp.exp(jnp.arange(half, dtype=jnp.float32) * (-2.0 * math.log(10000.0) / width))
    angle = place.astype(jnp.float32)[:, None] * frequency[None, :]
    return (jnp.cos(angle)[:, None, :], jnp.sin(angle)[:, None, :])


def unit_rows(value):
    return value * lax.rsqrt(jnp.mean(value * value, axis=-1, keepdims=True) + epsilon)


def turn_heads(value, cosine, sine):
    half = value.shape[-1] // 2
    first = value[..., :half]
    second = value[..., half:]
    return jnp.concatenate(
        [first * cosine - second * sine, second * cosine + first * sine], axis=-1
    )


def prepare(query_raw, key_raw, s_qk, cosine, sine, heads):
    rows = query_raw.shape[0]
    scales = s_qk.reshape(heads, -1)

    def normed(raw):
        shaped = raw.reshape(rows, heads, -1)
        return (unit_rows(turn_heads(shaped, cosine, sine)) * scales).reshape(rows, -1)

    return (normed(query_raw), normed(key_raw))


def blend(base, branch, alpha):
    return unit_rows(base + alpha * (unit_rows(branch) - base))


def gated(up_gate, s_u, s_v):
    width = s_u.shape[0]
    return up_gate[:, :width] * s_u * jax.nn.silu(up_gate[:, width:] * s_v)


def rounded(value):
    return lax.optimization_barrier(value.astype(jnp.bfloat16)).astype(jnp.float32)


def attention_forward(query, key, value, mask):
    scale = 1.0 / math.sqrt(query.shape[2])
    score = jnp.einsum("thd,shd->hts", query, key, preferred_element_type=jnp.float32)
    score = jnp.where(mask[None], score * scale, -1e30)
    peak = jnp.max(score, axis=2, keepdims=True)
    raised = jnp.exp(score - peak)
    summed = jnp.sum(raised, axis=2, keepdims=True)
    weight = (raised / summed).astype(jnp.bfloat16)
    result = jnp.einsum("hts,shd->thd", weight, value, preferred_element_type=jnp.float32)
    return result, peak + jnp.log(summed)


def attention_backward(query, key, value, mask, log_total, grad):
    scale = 1.0 / math.sqrt(query.shape[2])
    score = jnp.einsum("thd,shd->hts", query, key, preferred_element_type=jnp.float32)
    score = jnp.where(mask[None], score * scale, -1e30)
    share = jnp.exp(score - log_total)
    grad_value = jnp.einsum(
        "hts,thd->shd", share.astype(jnp.bfloat16), grad, preferred_element_type=jnp.float32
    )
    grad_share = jnp.einsum("thd,shd->hts", grad, value, preferred_element_type=jnp.float32)
    inner = jnp.sum(share * grad_share, axis=2, keepdims=True)
    grad_score = (share * (grad_share - inner)).astype(jnp.bfloat16)
    grad_query = jnp.einsum("hts,shd->thd", grad_score, key, preferred_element_type=jnp.float32)
    grad_key = jnp.einsum("hts,thd->shd", grad_score, query, preferred_element_type=jnp.float32)
    return grad_query * scale, grad_key * scale, grad_value


def low(value):
    return value.astype(jnp.bfloat16)


def product(left, right, dims):
    return lax.dot_general(left, right, (dims, ((), ())), preferred_element_type=jnp.float32)


def local(tokens, lengths, w_qkv, w_out, w_uv, w_down, s_qk, alpha_a, s_u, s_v, alpha_m, cotangent):
    rows = tokens.shape[1]
    model = tokens.shape[2]
    width = model // H
    parts = lax.axis_size("seq")
    shards = lax.axis_size("fsdp")
    mine = lax.axis_index("seq")
    own = H // parts
    deep = w_down.shape[0]
    hidden_all = deep * shards
    hidden_own = hidden_all // parts
    piece = deep // parts
    slot = mine * rows + jnp.arange(rows, dtype=jnp.int32)
    every_slot = jnp.arange(rows * parts, dtype=jnp.int32)
    keep = layout(lengths[0], slot)[2].astype(jnp.float32)[:, None]
    segment, place, _ = layout(lengths[0], every_slot)
    mask = (segment[:, None] == segment[None, :]) & (every_slot[:, None] >= every_slot[None, :])

    def exchange(array, axis):
        return lax.all_to_all(array, "seq", axis, axis, tiled=False)

    def gather(array, axis=0):
        return lax.all_gather(array, "fsdp", axis=axis, tiled=True)

    def spread(array):
        return lax.all_gather(array, "seq", axis=0, tiled=True)

    r_in = w_qkv.shape[0]
    share_qkv = lax.all_to_all(
        w_qkv.reshape(r_in, -1, parts, width), "seq", 2, 1, tiled=True
    ).reshape(r_in, -1)
    share_uv = lax.all_to_all(
        w_uv.reshape(r_in, -1, parts, piece), "seq", 2, 1, tiled=True
    ).reshape(r_in, -1)
    share_down = lax.all_to_all(w_down.reshape(parts, piece, -1), "seq", 0, 2, tiled=True)
    share_down = share_down.reshape(piece, model)
    share_out = lax.all_gather(w_out, "seq", axis=1, tiled=True)
    inputs = spread(tokens[0])
    full_qkv = gather(share_qkv)
    full_out = gather(share_out).reshape(own, parts, width, model)
    full_out = lax.dynamic_index_in_dim(full_out, mine, 1, False).reshape(own * width, model)
    full_uv = gather(share_uv)
    full_down = gather(share_down)
    gains = gather(jnp.concatenate([s_qk, alpha_a, s_u, s_v, alpha_m])[None]).astype(jnp.float32)
    cuts = [s_qk.shape[0], alpha_a.shape[0], s_u.shape[0], s_v.shape[0]]
    edges = [sum(cuts[: i + 1]) for i in range(4)]
    gain_qk, gain_a, gain_u, gain_v, gain_m = jnp.split(gains, edges, axis=1)
    gain_qk = gain_qk.reshape(own, parts, width)
    gain_qk = lax.dynamic_index_in_dim(gain_qk, mine, 1, False).reshape(-1)
    gain_a, gain_m = gain_a.reshape(-1), gain_m.reshape(-1)
    gain_u = lax.dynamic_index_in_dim(gain_u.reshape(shards, parts, piece), mine, 1, False).reshape(-1)
    gain_v = lax.dynamic_index_in_dim(gain_v.reshape(shards, parts, piece), mine, 1, False).reshape(-1)

    mixed = product(inputs, full_qkv, ((1,), (0,)))
    cosine, sine = rotary(place, width)
    span = own * width

    def prepare_local(query_raw, key_raw, scale_qk):
        return prepare(query_raw, key_raw, scale_qk, cosine, sine, own)

    (query_f, key_f), pull_prepare = jax.vjp(
        prepare_local, mixed[:, :span], mixed[:, span : 2 * span], gain_qk
    )
    heads = (rows * parts, own, width)
    query, key = low(query_f).reshape(heads), low(key_f).reshape(heads)
    value = low(mixed[:, 2 * span :]).reshape(heads)
    attended, log_total = attention_forward(query, key, value, mask)
    attended = low(attended.reshape(-1, span))

    def reduce_rows(array):
        return lax.psum_scatter(low(array), "seq", scatter_dimension=0, tiled=True).astype(
            jnp.float32
        )

    branch = reduce_rows(product(attended, full_out, ((1,), (0,))))
    first, pull_first = jax.vjp(blend, tokens[0].astype(jnp.float32), branch, gain_a)
    first_all = spread(low(first))
    up_gate = product(first_all, full_uv, ((1,), (0,)))
    hidden_f, pull_gate = jax.vjp(gated, up_gate, gain_u, gain_v)
    hidden = low(hidden_f)
    down = reduce_rows(product(hidden, full_down, ((1,), (0,))))
    final, pull_last = jax.vjp(blend, first, down, gain_m)
    output = low(final * keep)
    grad_first, grad_down, grad_gain_m = pull_last(cotangent[0].astype(jnp.float32) * keep)
    grad_down = spread(low(grad_down))
    grad_w_down = low(product(hidden, grad_down, ((0,), (0,))))
    grad_hidden = rounded(product(grad_down, full_down, ((1,), (1,))))
    grad_up_gate, grad_gain_u, grad_gain_v = pull_gate(grad_hidden)
    grad_up = low(grad_up_gate)
    grad_w_uv = low(product(first_all, grad_up, ((0,), (0,))))
    grad_first = grad_first + reduce_rows(product(grad_up, full_uv, ((1,), (1,))))
    grad_inputs, grad_branch, grad_gain_a = pull_first(grad_first)
    grad_branch = spread(low(grad_branch))
    grad_w_out = low(product(attended, grad_branch, ((0,), (0,))))
    grad_attended = low(product(grad_branch, full_out, ((1,), (1,)))).reshape(heads)
    grad_query, grad_key, grad_value = attention_backward(
        query, key, value, mask, log_total, grad_attended
    )
    grad_query_raw, grad_key_raw, grad_gain_qk = pull_prepare(
        (rounded(grad_query).reshape(-1, span), rounded(grad_key).reshape(-1, span))
    )
    grad_mixed = low(
        jnp.concatenate([grad_query_raw, grad_key_raw, grad_value.reshape(-1, span)], axis=1)
    )
    grad_w_qkv = low(product(inputs, grad_mixed, ((0,), (0,))))
    grad_inputs = grad_inputs + reduce_rows(product(grad_mixed, full_qkv, ((1,), (1,))))

    def collect(array):
        return lax.psum_scatter(array, "fsdp", scatter_dimension=0, tiled=True)

    part_down = collect(grad_w_down)
    out_down = lax.all_to_all(
        part_down.reshape(1, piece, model), "seq", 2, 0, tiled=True
    ).reshape(deep, -1)
    part_uv = collect(grad_w_uv)
    out_uv = lax.all_to_all(
        part_uv.reshape(r_in, -1, 1, piece), "seq", 1, 2, tiled=True
    ).reshape(r_in, -1)
    placed = jnp.zeros((own, parts, width, model), jnp.bfloat16)
    placed = lax.dynamic_update_slice(
        placed, grad_w_out.reshape(own, 1, width, model), (0, mine, 0, 0)
    )
    part_out = collect(placed.reshape(-1, model))
    out_out = lax.psum_scatter(part_out, "seq", scatter_dimension=1, tiled=True)
    part_qkv = collect(grad_w_qkv)
    out_qkv = lax.all_to_all(
        part_qkv.reshape(r_in, -1, 1, width), "seq", 1, 2, tiled=True
    ).reshape(r_in, -1)

    def widen(array, outer, inner):
        blank = jnp.zeros((outer, parts, inner), jnp.float32)
        array = array.reshape(outer, 1, inner)
        return lax.dynamic_update_slice(blank, array, (0, mine, 0)).reshape(shards, -1)

    gain_sums = jnp.concatenate(
        [
            widen(grad_gain_qk, own, width),
            grad_gain_a.reshape(shards, -1),
            widen(grad_gain_u, shards, piece),
            widen(grad_gain_v, shards, piece),
            grad_gain_m.reshape(shards, -1),
        ],
        axis=1,
    )
    gain_sums = lax.psum(collect(gain_sums), "seq")[0]
    outs = jnp.split(gain_sums, edges)
    return (
        output[None],
        grad_inputs[None],
        out_qkv.astype(jnp.float32),
        out_out.astype(jnp.float32),
        out_uv.astype(jnp.float32),
        out_down.astype(jnp.float32),
        outs[0],
        outs[1],
        outs[2],
        outs[3],
        outs[4],
    )


MESH = pl.DeviceIdType.MESH
TILE = 128
QROWS = 128


def loop(count, body):
    def run(index, carry):
        body(index)
        return carry

    lax.fori_loop(0, count, run, 0)


def at_rows(ref, block, size=TILE):
    return ref.at[pl.ds(pl.multiple_of(block * size, size), size), :]


def cols(block, size=TILE):
    return pl.ds(pl.multiple_of(block * size, size), size)


def mean_last(value):
    return jnp.sum(value, axis=-1, keepdims=True) * (1.0 / value.shape[-1])


class Slots:
    def __init__(self):
        self.count = 0

    def take(self, count):
        base = self.count
        self.count = base + count
        return base


def fused_layer(sizes, *refs):
    (parts, lines, rows, model, deep, own_heads, width) = sizes
    slots_all = parts * rows
    span = own_heads * width
    hid = deep * lines * 2 // parts
    count_in, count_out = len(Inputs._fields), len(Results._fields)
    ins = Inputs(*refs[:count_in])
    outs = Results(*refs[count_in : count_in + count_out])
    table = buffers(sizes)
    rest = refs[count_in + count_out :]
    v = types.SimpleNamespace(**dict(zip(table, rest[: len(table)])))
    send_sem, recv_sem, local_sem = rest[len(table) :]

    s = lax.axis_index("seq")
    f = lax.axis_index("fsdp")
    z = f // 2
    c = f % 2
    other = 1 - c
    mate = (s, 2 * z + other)
    slots = Slots()

    def put(src, dst, target, send_slot, recv_slot):
        pltpu.make_async_remote_copy(
            src_ref=src,
            dst_ref=dst,
            send_sem=send_sem.at[send_slot],
            recv_sem=recv_sem.at[recv_slot],
            device_id=target,
            device_id_type=MESH,
        ).start()

    def descriptor(ref, slot):
        return pltpu.make_async_remote_copy(
            src_ref=ref,
            dst_ref=ref,
            send_sem=send_sem.at[slot],
            recv_sem=recv_sem.at[slot],
            device_id=mate,
            device_id_type=MESH,
        )

    def landed(ref, slot):
        descriptor(ref, slot).wait_recv()

    finals = []

    def later(ref, slot, when=None):
        finals.append((ref, slot, when))

    def plane(distance):
        return (s + distance) % parts

    def plane_from(distance):
        return (s + parts - distance) % parts

    def line(distance):
        return (z + distance) % lines

    def line_from(distance):
        return (z + lines - distance) % lines

    barrier = pltpu.get_barrier_semaphore()
    for distance in range(1, parts):
        pl.semaphore_signal(barrier, inc=1, device_id=(plane(distance), f), device_id_type=MESH)
    for distance in range(1, 2 * lines):
        target = (s, (f + distance) % (2 * lines))
        pl.semaphore_signal(barrier, inc=1, device_id=target, device_id_type=MESH)

    edges = [0, TILE, 2 * TILE, 2 * TILE + deep, 2 * TILE + 2 * deep, 3 * TILE + 2 * deep]
    own_gains = (ins.s_qk, ins.alpha_a, ins.s_u, ins.s_v, ins.alpha_m)
    for place, own_gain in enumerate(own_gains):
        v.gain_all[f, :, edges[place] : edges[place + 1]] = own_gain[...].astype(jnp.float32)
    own_row = pl.ds(pl.multiple_of(s * rows, rows), rows)
    own_w = pl.ds(pl.multiple_of(f * TILE, TILE), TILE)
    part_cols = model // parts
    blocks_uv = 2 * hid // parts // TILE
    wide = blocks_uv * TILE

    def fetch(src, dst, slot):
        pltpu.make_async_copy(src, dst, local_sem.at[slot]).start()

    def fetched(dst, slot):
        pltpu.make_async_copy(dst, dst, local_sem.at[slot]).wait()

    fetch(ins.w_out, v.wz.at[own_w, :], 0)
    fetch(ins.tokens, v.x_all.at[own_row, :], 1)
    for index in range(blocks_uv):
        fetch(
            ins.w_uv.at[:, pl.ds(pl.multiple_of((index * parts + s) * TILE, TILE), TILE)],
            v.wu.at[own_w, pl.ds(pl.multiple_of(s * wide + index * TILE, TILE), TILE)],
            2,
        )
    fetch(ins.w_down.at[cols(s), :], v.wd.at[own_w, cols(s, part_cols)], 3)
    fetch(ins.cotangent, v.cotangent, 4)
    for index in range(3):
        chunk = 3 * s + index

        @pl.when(chunk % parts == s)
        def _():
            fetch(
                ins.w_qkv.at[:, index * span : (index + 1) * span],
                v.wq.at[own_w, cols(chunk // parts, span)],
                5,
            )

    pl.semaphore_wait(barrier, parts - 1 + 2 * lines - 1)

    qkv_slot = slots.take(3)
    for index in range(3):
        chunk = 3 * s + index
        block = chunk // parts
        target = chunk % parts

        @pl.when(target != s)
        def _():
            put(
                ins.w_qkv.at[:, index * span : (index + 1) * span],
                v.wq.at[own_w, cols(block, span)],
                (target, f),
                qkv_slot + index,
                qkv_slot + block,
            )

        later(ins.w_qkv.at[:, index * span : (index + 1) * span], qkv_slot + index, target != s)

    side, across, opposite = s + 1 - 2 * (s % 2), (s + 2) % parts, parts - 1 - s

    def half_of(shared, owner, part):
        start = owner * rows + part * (rows // 2)
        return shared.at[pl.ds(pl.multiple_of(start, rows // 2), rows // 2), :]

    token_slot = slots.take(SHARE)
    for part in range(2):
        mine = ins.tokens.at[part * (rows // 2) : (part + 1) * (rows // 2), :]
        there = half_of(v.x_all, s, part)
        for base, target in ((token_slot, side), (token_slot + 2, across)):
            put(mine, there, (target, f), base + part, base + part)
            later(mine, base + part)

    uv_slot = slots.take(parts)
    for distance in range(1, parts):
        target = plane(distance)
        for index in range(blocks_uv):
            put(
                ins.w_uv.at[:, pl.ds(pl.multiple_of((index * parts + target) * TILE, TILE), TILE)],
                v.wu.at[own_w, pl.ds(pl.multiple_of(s * wide + index * TILE, TILE), TILE)],
                (target, f),
                uv_slot + distance,
                uv_slot + distance,
            )
        later(v.wu.at[own_w, cols(s, wide)], uv_slot + distance)

    down_slot = slots.take(parts)
    for distance in range(1, parts):
        target = plane(distance)
        put(
            ins.w_down.at[cols(target), :],
            v.wd.at[own_w, cols(s, part_cols)],
            (target, f),
            down_slot + distance,
            down_slot + distance,
        )
        later(ins.w_down.at[cols(target), :], down_slot + distance)

    gain_slot = slots.take(2 * lines)
    for distance in range(1, 2 * lines):
        put(
            v.gain_all.at[f],
            v.gain_all.at[f],
            (s, (f + distance) % (2 * lines)),
            gain_slot + distance,
            gain_slot + distance,
        )
        later(v.gain_all.at[f], gain_slot + distance)

    def plane_share_wait(shared, base):
        one, two = half_of(shared, side, 0), half_of(shared, across, 1)
        landed(one, base)
        put(one, one, (across, f), base + 4, base + 4)
        landed(two, base + 3)
        put(two, two, (side, f), base + 5, base + 5)
        landed(half_of(shared, side, 1), base + 1)
        landed(half_of(shared, across, 0), base + 2)
        landed(half_of(shared, opposite, 0), base + 4)
        landed(half_of(shared, opposite, 1), base + 5)
        later(one, base + 4)
        later(two, base + 5)

    def shard(ref, chip, core, lanes):
        block = 2 * chip + core
        return ref.at[pl.ds(pl.multiple_of(block * TILE, TILE), TILE), lanes]

    inner = z * (lines - 1 - z) > 0
    outer = z * (lines - 1 - z) == 0

    def line_send(ref, base, lanes=slice(None), twice=True):
        own = shard(ref, z, c, lanes)
        for distance in (2, 1, 3):
            target = line(distance)
            near = (z - target) * (z - target) < (lines - 1) * (lines - 1)

            @pl.when(near)
            def _():
                put(own, own, (s, 2 * target + c), base + distance, base + distance)

            later(own, base + distance, near)
        if twice:
            put(own, own, mate, base, base)
            later(own, base)

    def line_relay(ref, base, lanes=slice(None)):
        block = shard(ref, line_from(2), c, lanes)
        slot = slots.take(1)

        @pl.when(inner)
        def _():
            landed(block, base + 2)
            put(block, block, (s, 2 * (lines - 1) * (z - 1) + c), slot, base + 2 * z - 1)

        later(block, slot, inner)

    def line_forward(ref, base, lanes=slice(None)):
        for distance in (1, 3, 2):
            block = shard(ref, line_from(distance), c, lanes)
            if distance == 2:

                @pl.when(outer)
                def _():
                    landed(block, base + distance)

            else:
                landed(block, base + distance)
            put(block, block, mate, base + lines + distance, base + lines + distance)
            later(block, base + lines + distance)

    def mate_wait(ref, base, lanes=slice(None)):
        landed(shard(ref, z, other, lanes), base)
        for distance in range(1, lines):
            landed(shard(ref, line_from(distance), other, lanes), base + lines + distance)

    wq_slot, wu_slot, wd_slot, wd_slot_late = (slots.take(2 * lines) for _ in range(4))
    wd_early, wd_late = slice(0, model // 2), slice(model // 2, model)
    wo_slot = slots.take(2 * lines)
    out_slot = slots.take(parts)
    fetched(v.wz.at[own_w, :], 0)
    line_send(v.wz, wo_slot, twice=False)

    for block in range(3):
        source = (parts * block + s) // 3

        @pl.when(source != s)
        def _():
            landed(v.wq.at[own_w, block * span : (block + 1) * span], qkv_slot + block)

        @pl.when(source == s)
        def _():
            fetched(v.wq.at[own_w, block * span : (block + 1) * span], 5)

    line_send(v.wq, wq_slot)
    lengths = [ins.lengths[0, i] for i in range(ins.lengths.shape[1])]

    def slot_facts(slot):
        end = 0
        member = jnp.zeros(slot.shape, jnp.int32)
        begin = jnp.zeros(slot.shape, jnp.int32)
        for length in lengths[:-1]:
            end = end + length
            after = slot >= end
            member = member + after.astype(jnp.int32)
            begin = jnp.where(after, end, begin)
        valid = member < len(lengths) - 1
        segment = jnp.where(valid, member, len(lengths) - 1 + slot)
        place = jnp.where(valid, slot - begin, 0)
        return segment, place, valid

    lane = lax.broadcasted_iota(jnp.int32, (1, TILE), 1)
    low_half = lane < width
    first_quarter = lane % width < width // 2
    frequency = jnp.exp(
        (lane % (width // 2)).astype(jnp.float32) * (-2.0 * math.log(10000.0) / width)
    )
    turn_sign = jnp.where(first_quarter, -1.0, 1.0)

    def tables(block):
        here = pl.ds(pl.multiple_of(block * TILE, TILE), TILE)
        slot = block * TILE + lax.broadcasted_iota(jnp.int32, (TILE, 1), 0)
        segment, place, _ = slot_facts(slot)
        angle = place.astype(jnp.float32) * frequency
        v.cosine[here, :] = jnp.cos(angle)
        v.sine[here, :] = jnp.sin(angle) * turn_sign
        key_slot = lax.broadcasted_iota(jnp.int32, (1, slots_all), 1)
        key_segment = slot_facts(key_slot)[0]
        kept = (segment == key_segment) & (slot >= key_slot)
        v.bias[here, :] = jnp.where(kept, 0.0, -1e30)

    loop(slots_all // TILE, tables)
    line_relay(v.wz, wo_slot)
    line_relay(v.wq, wq_slot)
    fetched(v.x_all.at[own_row, :], 1)
    plane_share_wait(v.x_all, token_slot)
    for distance in (1, 3):
        landed(shard(v.wz, line_from(distance), c, slice(None)), wo_slot + distance)

    @pl.when(outer)
    def _():
        landed(shard(v.wz, line_from(2), c, slice(None)), wo_slot + 2)

    for distance in range(1, parts):
        target = plane(distance)
        rows_out = at_rows(v.wz, 2 * target + c)
        put(
            rows_out,
            v.wo.at[cols(c), cols(s, part_cols)],
            (target, f),
            out_slot + distance,
            out_slot + distance,
        )
        later(rows_out, out_slot + distance)
    v.wo[cols(c), cols(s, part_cols)] = v.wz[cols(2 * s + c), :]
    fetched(v.wu.at[own_w, cols(s, wide)], 2)
    for distance in range(1, parts):
        landed(v.wu.at[own_w, cols(plane_from(distance), wide)], uv_slot + distance)
    line_send(v.wu, wu_slot)

    def mate_blocks(name_all, ref, stage, slot):
        for block in range(lines):
            here = slice(block * TILE, (block + 1) * TILE)
            stage[here, :] = name_all[:, cols(2 * block + other)].T
        put(stage, ref.at[:, slots_all:], mate, slot, slot)
        later(stage, slot)
        for block in range(lines):
            here = slice(block * TILE, (block + 1) * TILE)
            ref[here, :slots_all] = name_all[:, cols(2 * block + c)].T

    mate_x_slot = slots.take(1)
    mate_blocks(v.x_all, v.turned_x, v.stage_x, mate_x_slot)
    fetched(v.wd.at[own_w, cols(s, part_cols)], 3)
    for distance in range(1, parts):
        landed(v.wd.at[own_w, cols(plane_from(distance), part_cols)], down_slot + distance)
    line_send(v.wd, wd_slot, wd_early)
    line_send(v.wd, wd_slot_late, wd_late)

    for distance in range(1, 2 * lines):
        landed(v.gain_all.at[(f + 2 * lines - distance) % (2 * lines)], gain_slot + distance)

    def gain(block, offset):
        return v.gain_all[block, :, pl.ds(pl.multiple_of(offset, TILE), TILE)]

    for block in range(2 * lines):
        here = slice(block * TILE, (block + 1) * TILE)
        v.gain_a[:, here] = gain(block, edges[1])
        v.gain_u[:, here] = gain(block, edges[2] + s * TILE)
        v.gain_v[:, here] = gain(block, edges[3] + s * TILE)
        v.gain_m[:, here] = gain(block, edges[4])
    for block in range(span // TILE):
        v.gain_qk[:, block * TILE : (block + 1) * TILE] = gain(span // TILE * s + block, 0)

    line_forward(v.wq, wq_slot)
    mate_wait(v.wq, wq_slot)

    def mix(index):
        v.raw[:, cols(index, span)] = product(
            v.x_all[...], v.wq[:, cols(index, span)], ((1,), (0,))
        )

    loop(3, mix)

    def swap(value):
        return jnp.where(
            first_quarter,
            pltpu.roll(value, TILE - width // 2, 1),
            pltpu.roll(value, width // 2, 1),
        )

    def head_mean(value):
        one = jnp.sum(jnp.where(low_half, value, 0.0), axis=-1, keepdims=True)
        two = jnp.sum(jnp.where(low_half, 0.0, value), axis=-1, keepdims=True)
        return jnp.where(low_half, one, two) * (1.0 / width)

    pairs = span // TILE
    blocks = slots_all // TILE

    def prepare_block(index):
        here = pl.ds(pl.multiple_of(index % blocks * TILE, TILE), TILE)
        group = index // blocks
        there = cols(group)
        value = v.raw[here, there]
        turned = value * v.cosine[here, :] + swap(value) * v.sine[here, :]
        inverse = lax.rsqrt(head_mean(turned * turned) + epsilon)
        normed = turned * inverse
        v.normed[here, there] = normed
        v.inverse[here, there] = inverse
        v.qkv[here, there] = low(normed * v.gain_qk[:, cols(group % pairs)])

    loop(2 * pairs * blocks, prepare_block)

    def keep_value(index):
        here = pl.ds(pl.multiple_of(index * TILE, TILE), TILE)
        v.qkv[here, 2 * span :] = low(v.raw[here, 2 * span :])

    loop(blocks, keep_value)
    own_out = v.wo.at[cols(c), :]
    for distance in range(1, parts):
        landed(v.wo.at[cols(c), cols(plane_from(distance), part_cols)], out_slot + distance)
    put(own_out, own_out, mate, wo_slot, wo_slot)
    later(own_out, wo_slot)

    scale = 1.0 / math.sqrt(width)
    halves = (low_half, jnp.logical_not(low_half))

    def attend(pair):
        q_cols, k_cols, v_cols = cols(pair), cols(pairs + pair), cols(2 * pairs + pair)
        for block in range(blocks):
            here = slice(block * TILE, (block + 1) * TILE)
            seen = slice(0, (block + 1) * TILE)
            results = []
            for half in range(2):
                query = jnp.where(halves[half], v.qkv[here, q_cols], 0.0).astype(jnp.bfloat16)
                score = product(query, v.qkv[seen, k_cols], ((1,), (1,))) * scale
                score = score + v.bias[here, seen]
                peak = jnp.max(score, axis=1, keepdims=True)
                raised = jnp.exp(score - peak)
                summed = jnp.sum(raised, axis=1, keepdims=True)
                weight = low(raised / summed)
                results.append(product(weight, v.qkv[seen, v_cols], ((1,), (0,))))
                v.total[2 * pair + half, here, :] = peak + jnp.log(summed)
            v.attended[here, q_cols] = low(jnp.where(low_half, results[0], results[1]))

    loop(pairs, attend)
    mate_att_slot = slots.take(1)
    v.stage_att[...] = v.attended[:, cols(other)].T
    v.turned_att[:, :slots_all] = v.attended[:, cols(c)].T

    put(v.stage_att, v.turned_att.at[:, slots_all:], mate, mate_att_slot, mate_att_slot)
    later(v.stage_att, mate_att_slot)
    landed(v.wo.at[cols(other), :], wo_slot)

    count = 4
    piece = model // count

    def plane_sum(sums, arrived, base, tile, span_of=(0, 4)):
        start, stop = span_of

        def send(index):
            there = cols(index, piece)
            for distance in range(1, parts):
                target = plane(distance)
                put(
                    sums.at[pl.ds(pl.multiple_of(target * rows, rows), rows), there],
                    arrived.at[distance - 1, :, there],
                    (target, f),
                    base + distance,
                    base + distance,
                )

        def step(index):
            sums[:, cols(start + index, piece)] = low(tile(start + index))

            @pl.when(index > 0)
            def _():
                send(start + index - 1)

        loop(stop - start, step)
        send(stop - 1)
        if stop == count:
            for distance in range(1, parts):
                later(arrived.at[distance - 1], base + distance)

    def plane_sum_wait(arrived, base):
        for distance in range(1, parts):
            landed(arrived.at[distance - 1], base + distance)

    def plane_total(sums, arrived, here, at):
        total = sums[here, :].astype(jnp.float32)
        for distance in range(1, parts):
            total = total + arrived[distance - 1, at, :].astype(jnp.float32)
        return total

    chunk_rows = 32

    def chunk(index):
        at = pl.ds(pl.multiple_of(index * chunk_rows, chunk_rows), chunk_rows)
        here = pl.ds(pl.multiple_of(s * rows + index * chunk_rows, chunk_rows), chunk_rows)
        return at, here

    def plane_share(shared, base, make):
        def send(index):
            own = shared.at[chunk(index)[1], :]
            part = index // (rows // chunk_rows // 2)
            put(own, own, (side, f), base + part, base + part)
            put(own, own, (across, f), base + 2 + part, base + 2 + part)

        def step(index):
            make(index)

            @pl.when(index > 0)
            def _():
                send(index - 1)

        loop(rows // chunk_rows, step)
        send(rows // chunk_rows - 1)
        for part in range(2):
            later(half_of(shared, s, part), base + part)
            later(half_of(shared, s, part), base + 2 + part)

    branch_slot = slots.take(parts)
    plane_sum(
        v.part_branch,
        v.got_branch,
        branch_slot,
        lambda index: product(v.attended[...], v.wo[:, cols(index, piece)], ((1,), (0,))),
    )
    line_relay(v.wu, wu_slot)
    plane_sum_wait(v.got_branch, branch_slot)

    def blended(base, branch, alpha):
        inverse_branch = lax.rsqrt(mean_last(branch * branch) + epsilon)
        normed = branch * inverse_branch
        mixed = base + alpha * (normed - base)
        inverse = lax.rsqrt(mean_last(mixed * mixed) + epsilon)
        return normed, inverse_branch, mixed * inverse, inverse

    def blended_back(grad, base, alpha, normed, inverse_branch, result, inverse):
        grad_mixed = inverse * (grad - result * mean_last(grad * result))
        grad_normed = alpha * grad_mixed
        grad_branch = inverse_branch * (grad_normed - normed * mean_last(grad_normed * normed))
        grad_alpha = jnp.sum(grad_mixed * (normed - base), axis=0, keepdims=True)
        return grad_mixed - grad_normed, grad_branch, grad_alpha

    def make_first(index):
        at, here = chunk(index)
        base = v.x_all[here, :].astype(jnp.float32)
        normed, inverse_branch, result, inverse = blended(
            base, plane_total(v.part_branch, v.got_branch, here, at), v.gain_a[...]
        )
        v.branch_normed[at, :] = normed
        v.branch_inverse[at, :] = inverse_branch
        v.first[at, :] = result
        v.first_inverse[at, :] = inverse
        v.first_all[here, :] = low(result)

    first_slot = slots.take(SHARE)
    plane_share(v.first_all, first_slot, make_first)
    line_forward(v.wu, wu_slot)
    line_relay(v.wd, wd_slot, wd_early)
    mate_wait(v.wu, wu_slot)
    plane_share_wait(v.first_all, first_slot)

    def gate_tile(index):
        there = cols(index, 256)
        v.up[:, there] = product(v.first_all[...], v.wu[:, there], ((1,), (0,)))
        v.gate[:, there] = product(
            v.first_all[...],
            v.wu[:, pl.ds(pl.multiple_of(hid + index * 256, 256), 256)],
            ((1,), (0,)),
        )

        def rows_of(block):
            here = pl.ds(pl.multiple_of(block * 64, 64), 64)
            scaled = v.gate[here, there] * v.gain_v[:, there]
            passed = scaled / (1.0 + jnp.exp(-scaled))
            v.hidden[here, there] = low(v.up[here, there] * v.gain_u[:, there] * passed)

        loop(slots_all // 64, rows_of)

    loop(hid // 512, gate_tile)
    line_relay(v.wd, wd_slot_late, wd_late)
    line_forward(v.wd, wd_slot, wd_early)
    loop(hid // 512, lambda index: gate_tile(hid // 512 + index))
    line_forward(v.wd, wd_slot_late, wd_late)
    mate_hidden_slot = slots.take(1)
    mate_blocks(v.hidden, v.turned_hidden, v.stage_hidden, mate_hidden_slot)
    mate_first_slot = slots.take(1)
    mate_blocks(v.first_all, v.turned_first, v.stage_first, mate_first_slot)
    down_sum_slot = slots.take(parts)

    def down_tile(index):
        return product(v.hidden[...], v.wd[:, cols(index, piece)], ((1,), (0,)))

    mate_wait(v.wd, wd_slot, wd_early)
    plane_sum(v.part_down, v.got_down, down_sum_slot, down_tile, (0, count // 2))
    mate_wait(v.wd, wd_slot_late, wd_late)
    plane_sum(v.part_down, v.got_down, down_sum_slot, down_tile, (count // 2, count))
    fetched(v.cotangent, 4)
    plane_sum_wait(v.got_down, down_sum_slot)
    v.grad_a[...] = jnp.zeros_like(v.grad_a)
    v.grad_m[...] = jnp.zeros_like(v.grad_m)

    def finish(index):
        at, here = chunk(index)
        slot = s * rows + index * chunk_rows
        slot = slot + lax.broadcasted_iota(jnp.int32, (chunk_rows, 1), 0)
        keep = slot_facts(slot)[2].astype(jnp.float32)
        base = v.first[at, :]
        alpha = v.gain_m[...]
        normed, inverse_branch, result, inverse = blended(
            base, plane_total(v.part_down, v.got_down, here, at), alpha
        )
        outs.output[at, :] = low(result * keep)
        grad = v.cotangent[at, :].astype(jnp.float32) * keep
        grad_base, grad_down, grad_alpha = blended_back(
            grad, base, alpha, normed, inverse_branch, result, inverse
        )
        v.grad_first[at, :] = grad_base
        v.gd[here, :] = low(grad_down)
        v.grad_m[...] += grad_alpha

    gd_slot = slots.take(SHARE)
    plane_share(v.gd, gd_slot, finish)
    plane_share_wait(v.gd, gd_slot)
    mate_gd_slot = slots.take(1)
    first_half = slice(0, slots_all)
    second_half = slice(slots_all, 2 * slots_all)
    put(v.gd.at[first_half, :], v.gd.at[second_half, :], mate, mate_gd_slot, mate_gd_slot)
    later(v.gd.at[first_half, :], mate_gd_slot)

    ends = (lines - 1) * (1 - z % 2)
    mids = 2 - z // 2
    last = (2 * z + 1) % (lines + 1)
    beside = z + 1 - 2 * (z % 2)

    def line_grad_send(grads, arrived, base, there):
        put(
            grads.at[ends, :, there],
            arrived.at[0, :, there],
            (s, 2 * beside + c),
            base,
            base,
        )
        mid_slot = 2 - z * (lines - 1 - z) // 2
        put(
            grads.at[mids, :, there],
            arrived.at[mid_slot, :, there],
            (s, 2 * mids + c),
            base + 1,
            base + mid_slot,
        )

        @pl.when(outer)
        def _():
            put(
                grads.at[last, :, there],
                arrived.at[3, :, there],
                (s, 2 * last + c),
                base + 2,
                base + 3,
            )

    def weight_grad(turned, right, grads, arrived, columns, base):
        def step(index):
            there = cols(index, 256)
            total = product(turned[...], right[:, there], ((1,), (0,)))
            grads[:, :, there] = low(total).reshape(lines, TILE, 256)

            @pl.when(index > 0)
            def _():
                line_grad_send(grads, arrived, base, cols(index - 1, 256))

        loop(columns // 256, step)
        line_grad_send(grads, arrived, base, cols(columns // 256 - 1, 256))
        for index in range(3):
            later(grads.at[0], base + index)

    def weight_combine(grads, arrived, columns, base):
        @pl.when(inner)
        def _():
            landed(arrived.at[0], base)

            def tile(index):
                there = cols(index, 256)
                total = grads[last, :, there].astype(jnp.float32)
                grads[last, :, there] = low(total + arrived[0, :, there].astype(jnp.float32))

            loop(columns // 256, tile)
            put(
                grads.at[last], arrived.at[1], (s, 2 * last + c), base + 2, base + 1
            )

    def gate_back(index):
        there = cols(index, 256)
        there_gate = pl.ds(pl.multiple_of(hid + index * 256, 256), 256)
        v.grad_hidden[...] = low(product(v.gd[first_half, :], v.wd[there, :], ((1,), (1,))))
        v.grad_u[:, there] = jnp.zeros((1, 256), jnp.float32)
        v.grad_v[:, there] = jnp.zeros((1, 256), jnp.float32)

        def rows_of(block):
            here = pl.ds(pl.multiple_of(block * 64, 64), 64)
            grad = v.grad_hidden[here, :].astype(jnp.float32)
            up = v.up[here, there]
            gate = v.gate[here, there]
            gain_u = v.gain_u[:, there]
            gain_v = v.gain_v[:, there]
            scaled = gate * gain_v
            squash = 1.0 / (1.0 + jnp.exp(-scaled))
            passed = scaled * squash
            grad_scaled_up = grad * passed
            grad_scaled = grad * (up * gain_u) * (squash + passed * (1.0 - squash))
            v.gu[here, there] = low(grad_scaled_up * gain_u)
            v.gu[here, there_gate] = low(grad_scaled * gain_v)
            v.grad_u[:, there] += jnp.sum(grad_scaled_up * up, axis=0, keepdims=True)
            v.grad_v[:, there] += jnp.sum(grad_scaled * gate, axis=0, keepdims=True)

        loop(slots_all // 64, rows_of)

    loop(1, gate_back)
    landed(v.turned_x.at[:, second_half], mate_x_slot)
    landed(v.turned_first.at[:, second_half], mate_first_slot)
    landed(v.turned_hidden.at[:, second_half], mate_hidden_slot)
    landed(v.gd.at[second_half, :], mate_gd_slot)
    line_down_slot = slots.take(lines)
    weight_grad(v.turned_hidden, v.gd, v.send_down, v.line_down, model, line_down_slot)
    loop(hid // 256 - 1, lambda index: gate_back(index + 1))
    mate_gu_slot = slots.take(1)
    put(v.gu.at[first_half, :], v.gu.at[second_half, :], mate, mate_gu_slot, mate_gu_slot)
    later(v.gu.at[first_half, :], mate_gu_slot)
    first_sum_slot = slots.take(parts)
    plane_sum(
        v.part_first,
        v.got_first,
        first_sum_slot,
        lambda index: product(v.gu[first_half, :], v.wu[cols(index, piece), :], ((1,), (1,))),
    )
    landed(v.gu.at[second_half, :], mate_gu_slot)
    line_uv_slot = slots.take(lines)
    weight_grad(v.turned_first, v.gu, v.send_uv, v.line_uv, 2 * hid, line_uv_slot)
    plane_sum_wait(v.got_first, first_sum_slot)

    def back_first(index):
        at, here = chunk(index)
        grad = v.grad_first[at, :] + plane_total(v.part_first, v.got_first, here, at)
        grad_base, grad_branch, grad_alpha = blended_back(
            grad,
            v.x_all[here, :].astype(jnp.float32),
            v.gain_a[...],
            v.branch_normed[at, :],
            v.branch_inverse[at, :],
            v.first[at, :],
            v.first_inverse[at, :],
        )
        v.grad_tokens[at, :] = grad_base
        v.gb[here, :] = low(grad_branch)
        v.grad_a[...] += grad_alpha

    gb_slot = slots.take(SHARE)
    plane_share(v.gb, gb_slot, back_first)
    weight_combine(v.send_down, v.line_down, model, line_down_slot)
    plane_share_wait(v.gb, gb_slot)
    mate_gb_slot = slots.take(1)
    put(v.gb.at[first_half, :], v.gb.at[second_half, :], mate, mate_gb_slot, mate_gb_slot)
    later(v.gb.at[first_half, :], mate_gb_slot)

    v.grad_att[...] = low(product(v.gb[first_half, :], v.wo[...], ((1,), (1,))))
    landed(v.turned_att.at[:, second_half], mate_att_slot)
    landed(v.gb.at[second_half, :], mate_gb_slot)
    line_out_slot = slots.take(lines)
    part_out_slot = slots.take(parts)

    def out_tile(index):
        there = cols(index, 256)
        v.send_out[:, there] = low(product(v.turned_att[...], v.gb[:, there], ((1,), (0,))))

    loop(model // 256, out_tile)
    for distance in range(1, parts):
        target = plane(distance)
        put(
            v.send_out.at[:, cols(target, part_cols)],
            v.send_wo.at[s],
            (target, f),
            part_out_slot + distance,
            part_out_slot + distance,
        )
        later(v.send_wo.at[s], part_out_slot + distance)
    v.send_wo[s] = v.send_out[:, cols(s, part_cols)]
    v.grad_qkv[...] = jnp.zeros_like(v.grad_qkv)

    def attend_back(pair):
        q_cols, k_cols, v_cols = cols(pair), cols(pairs + pair), cols(2 * pairs + pair)
        for block in range(blocks):
            here = slice(block * TILE, (block + 1) * TILE)
            seen = slice(0, (block + 1) * TILE)
            results = []
            for half in range(2):
                query = jnp.where(halves[half], v.qkv[here, q_cols], 0.0).astype(jnp.bfloat16)
                grad = jnp.where(halves[half], v.grad_att[here, q_cols], 0.0)
                grad = grad.astype(jnp.bfloat16)
                score = product(query, v.qkv[seen, k_cols], ((1,), (1,))) * scale
                score = score + v.bias[here, seen]
                share = jnp.exp(score - v.total[2 * pair + half, here, :])
                grad_share = product(grad, v.qkv[seen, v_cols], ((1,), (1,)))
                inner = jnp.sum(share * grad_share, axis=1, keepdims=True)
                grad_score = low(share * (grad_share - inner))
                results.append(product(grad_score, v.qkv[seen, k_cols], ((1,), (0,))))
                v.grad_qkv[seen, v_cols] += product(low(share), grad, ((0,), (0,)))
                v.grad_qkv[seen, k_cols] += product(grad_score, query, ((0,), (0,)))
            v.grad_qkv[here, q_cols] = jnp.where(low_half, results[0], results[1])

    loop(pairs, attend_back)
    for distance in range(1, parts):
        landed(v.send_wo.at[plane_from(distance)], part_out_slot + distance)
    line_grad_send(v.send_wo, v.line_wo, line_out_slot, slice(None))
    for index in range(3):
        later(v.send_wo.at[0], line_out_slot + index)
    v.grad_qk[...] = jnp.zeros_like(v.grad_qk)

    def prepare_back(index):
        here = pl.ds(pl.multiple_of(index % blocks * TILE, TILE), TILE)
        group = index // blocks
        there = cols(group)
        pair = cols(group % pairs)
        grad = low(v.grad_qkv[here, there] * scale).astype(jnp.float32)
        normed = v.normed[here, there]
        v.grad_qk[:, pair] += jnp.sum(grad * normed, axis=0, keepdims=True)
        grad = grad * v.gain_qk[:, pair]
        grad = v.inverse[here, there] * (grad - normed * head_mean(grad * normed))
        back = grad * v.cosine[here, :] - swap(grad) * v.sine[here, :]
        v.gm[here, there] = low(back)

    loop(2 * pairs * blocks, prepare_back)

    def value_back(index):
        here = pl.ds(pl.multiple_of(index * TILE, TILE), TILE)
        v.gm[here, 2 * span :] = low(v.grad_qkv[here, 2 * span :])

    loop(blocks, value_back)
    mate_gm_slot = slots.take(1)
    put(v.gm.at[first_half, :], v.gm.at[second_half, :], mate, mate_gm_slot, mate_gm_slot)
    later(v.gm.at[first_half, :], mate_gm_slot)

    v.gain_part[...] = jnp.zeros_like(v.gain_part)
    for block in range(2 * lines):
        here = slice(block * TILE, (block + 1) * TILE)
        local_pair = block % (span // TILE) * TILE
        qk = v.grad_qk[:, local_pair : local_pair + TILE]
        mine = (s == block // (span // TILE)).astype(jnp.float32)
        v.gain_part[block, :, edges[0] : edges[1]] = qk * mine
        v.gain_part[block, :, edges[1] : edges[2]] = v.grad_a[:, here]
        v.gain_part[block, :, cols(edges[2] // TILE + s)] = v.grad_u[:, here]
        v.gain_part[block, :, cols(edges[3] // TILE + s)] = v.grad_v[:, here]
        v.gain_part[block, :, edges[4] : edges[5]] = v.grad_m[:, here]

    inputs_slot = slots.take(parts)
    plane_sum(
        v.part_inputs,
        v.got_inputs,
        inputs_slot,
        lambda index: product(v.gm[first_half, :], v.wq[cols(index, piece), :], ((1,), (1,))),
    )
    gain_line_slot = slots.take(2 * lines)
    for distance in range(1, 2 * lines):
        target = (f + distance) % (2 * lines)
        put(
            v.gain_part.at[target],
            v.gain_got.at[distance - 1],
            (s, target),
            gain_line_slot + distance,
            gain_line_slot + distance,
        )
        later(v.gain_got.at[distance - 1], gain_line_slot + distance)
    weight_combine(v.send_uv, v.line_uv, 2 * hid, line_uv_slot)
    landed(v.gm.at[second_half, :], mate_gm_slot)
    line_qkv_slot = slots.take(lines)
    weight_grad(v.turned_x, v.gm, v.send_qkv, v.line_qkv, 3 * span, line_qkv_slot)

    plane_sum_wait(v.got_inputs, inputs_slot)

    def finish_inputs(index):
        at, here = chunk(index)
        outs.input_grad[at, :] = v.grad_tokens[at, :] + plane_total(v.part_inputs, v.got_inputs, here, at)

    loop(rows // chunk_rows, finish_inputs)

    def line_total(grads, arrived, done, columns, base):
        def add(slots_in):
            for slot in slots_in:
                landed(arrived.at[slot], base + slot)

            def tile(index):
                there = cols(index, 256)
                total = grads[z, :, there].astype(jnp.float32)
                for slot in slots_in:
                    total = total + arrived[slot, :, there].astype(jnp.float32)
                done[:, there] = low(total)

            loop(columns // 256, tile)

        pl.when(outer)(lambda: add((0, 1)))
        pl.when(inner)(lambda: add((1, 2, 3)))

    weight_combine(v.send_wo, v.line_wo, part_cols, line_out_slot)
    weight_combine(v.send_qkv, v.line_qkv, 3 * span, line_qkv_slot)
    line_total(v.send_down, v.line_down, v.done_down, model, line_down_slot)
    back_down_slot = slots.take(parts)
    for distance in range(1, parts):
        target = plane(distance)
        put(
            v.done_down.at[:, cols(target, part_cols)],
            outs.back_down.at[cols(s), :],
            (target, f),
            back_down_slot + distance,
            back_down_slot + distance,
        )
        later(v.done_down.at[:, cols(target, part_cols)], back_down_slot + distance)
    outs.back_down[cols(s), :] = v.done_down[:, cols(s, part_cols)]

    line_total(v.send_uv, v.line_uv, v.done_uv, 2 * hid, line_uv_slot)
    back_uv_slot = slots.take(parts)
    for distance in range(1, parts):
        target = plane(distance)
        for index in range(blocks_uv):
            put(
                v.done_uv.at[:, pl.ds(pl.multiple_of(target * wide + index * TILE, TILE), TILE)],
                outs.back_uv.at[s, :, index * TILE : (index + 1) * TILE],
                (target, f),
                back_uv_slot + distance,
                back_uv_slot + distance,
            )
        later(v.done_uv.at[:, cols(target, wide)], back_uv_slot + distance)
    outs.back_uv[s] = v.done_uv[:, cols(s, wide)]

    gain_plane_slot = slots.take(parts)
    for distance in range(1, 2 * lines):
        landed(v.gain_got.at[distance - 1], gain_line_slot + distance)
    total = v.gain_part[f]
    for distance in range(1, 2 * lines):
        total = total + v.gain_got[distance - 1]
    v.gain_sum[s] = total
    for distance in range(1, parts):
        put(
            v.gain_sum.at[s],
            v.gain_sum.at[s],
            (plane(distance), f),
            gain_plane_slot + distance,
            gain_plane_slot + distance,
        )
        later(v.gain_sum.at[s], gain_plane_slot + distance)

    line_total(v.send_qkv, v.line_qkv, v.done_qkv, 3 * span, line_qkv_slot)
    back_qkv_slot = slots.take(3)
    for block in range(3):
        chunk_of = parts * block + s
        target = chunk_of // 3
        index = chunk_of % 3
        source = v.done_qkv.at[:, block * span : (block + 1) * span]

        @pl.when(target == s)
        def _():
            outs.back_qkv[index] = source[...]

        @pl.when(target != s)
        def _():
            put(
                source,
                outs.back_qkv.at[index],
                (target, f),
                back_qkv_slot + block,
                back_qkv_slot + index,
            )

        later(source, back_qkv_slot + block, target != s)

    line_total(v.send_wo, v.line_wo, outs.back_out, part_cols, line_out_slot)
    for distance in range(1, parts):
        landed(outs.back_down.at[cols(plane_from(distance)), :], back_down_slot + distance)
    for distance in range(1, parts):
        landed(outs.back_uv.at[plane_from(distance)], back_uv_slot + distance)
    for distance in range(1, parts):
        landed(v.gain_sum.at[plane_from(distance)], gain_plane_slot + distance)
    total = v.gain_sum[0]
    for source in range(1, parts):
        total = total + v.gain_sum[source]
    outs.gains[...] = total
    for index in range(3):
        source = (3 * s + index) % parts

        @pl.when(source != s)
        def _():
            landed(outs.back_qkv.at[index], back_qkv_slot + index)

    for ref, slot, when in finals:
        if when is None:
            descriptor(ref, slot).wait_send()
        else:

            @pl.when(when)
            def _():
                descriptor(ref, slot).wait_send()

    assert slots.count <= SLOTS_MOST, slots.count


SLOTS_MOST = 200
SHARE = 6


class Inputs(typing.NamedTuple):
    tokens: typing.Any
    lengths: typing.Any
    w_qkv: typing.Any
    w_out: typing.Any
    w_uv: typing.Any
    w_down: typing.Any
    s_qk: typing.Any
    alpha_a: typing.Any
    s_u: typing.Any
    s_v: typing.Any
    alpha_m: typing.Any
    cotangent: typing.Any


class Results(typing.NamedTuple):
    output: typing.Any
    input_grad: typing.Any
    back_qkv: typing.Any
    back_out: typing.Any
    back_uv: typing.Any
    back_down: typing.Any
    gains: typing.Any


def buffers(sizes):
    (parts, lines, rows, model, deep, own_heads, width) = sizes
    every = parts * rows
    span = own_heads * width
    hid = deep * lines * 2 // parts
    half = lines * TILE
    gains = 3 * TILE + 2 * deep
    bf16, f32 = jnp.bfloat16, jnp.float32
    return dict(
        wq=((model, 3 * span), bf16),
        wo=((span, model), bf16),
        wz=((model, model // parts), bf16),
        cotangent=((rows, model), bf16),
        wu=((model, 2 * hid), bf16),
        wd=((hid, model), bf16),
        gain_all=((2 * lines, 1, gains), f32),
        gain_a=((1, model), f32),
        gain_m=((1, model), f32),
        gain_u=((1, hid), f32),
        gain_v=((1, hid), f32),
        gain_qk=((1, span), f32),
        x_all=((every, model), bf16),
        first_all=((every, model), bf16),
        gd=((2 * every, model), bf16),
        gb=((2 * every, model), bf16),
        cosine=((every, TILE), f32),
        sine=((every, TILE), f32),
        bias=((every, every), f32),
        raw=((every, 3 * span), f32),
        normed=((every, 2 * span), f32),
        inverse=((every, 2 * span), f32),
        qkv=((every, 3 * span), bf16),
        total=((own_heads, every, 1), f32),
        attended=((every, span), bf16),
        branch_normed=((rows, model), f32),
        branch_inverse=((rows, 1), f32),
        first=((rows, model), f32),
        first_inverse=((rows, 1), f32),
        up=((every, hid), f32),
        gate=((every, hid), f32),
        hidden=((every, hid), bf16),
        grad_hidden=((every, 256), bf16),
        gu=((2 * every, 2 * hid), bf16),
        grad_first=((rows, model), f32),
        grad_tokens=((rows, model), f32),
        grad_att=((every, span), bf16),
        grad_qkv=((every, 3 * span), f32),
        gm=((2 * every, 3 * span), bf16),
        grad_a=((1, model), f32),
        grad_m=((1, model), f32),
        grad_u=((1, hid), f32),
        grad_v=((1, hid), f32),
        grad_qk=((1, span), f32),
        gain_part=((2 * lines, 1, gains), f32),
        gain_got=((2 * lines - 1, 1, gains), f32),
        gain_sum=((parts, 1, gains), f32),
        turned_x=((half, 2 * every), bf16),
        turned_first=((half, 2 * every), bf16),
        turned_hidden=((half, 2 * every), bf16),
        turned_att=((TILE, 2 * every), bf16),
        stage_x=((half, every), bf16),
        stage_first=((half, every), bf16),
        stage_hidden=((half, every), bf16),
        stage_att=((TILE, every), bf16),
        send_out=((TILE, model), bf16),
        send_wo=((lines, TILE, model // parts), bf16),
        line_wo=((4, TILE, model // parts), bf16),
        part_branch=((every, model), bf16),
        got_branch=((parts - 1, rows, model), bf16),
        part_down=((every, model), bf16),
        got_down=((parts - 1, rows, model), bf16),
        part_first=((every, model), bf16),
        got_first=((parts - 1, rows, model), bf16),
        part_inputs=((every, model), bf16),
        got_inputs=((parts - 1, rows, model), bf16),
        send_qkv=((lines, TILE, 3 * span), bf16),
        line_qkv=((4, TILE, 3 * span), bf16),
        done_qkv=((TILE, 3 * span), bf16),
        send_uv=((lines, TILE, 2 * hid), bf16),
        line_uv=((4, TILE, 2 * hid), bf16),
        done_uv=((TILE, 2 * hid), bf16),
        send_down=((lines, TILE, model), bf16),
        line_down=((4, TILE, model), bf16),
        done_down=((TILE, model), bf16),
    )


def place_results(sizes, *refs):
    (parts, lines, rows, model, deep, own_heads, width) = sizes
    count = len(Results._fields)
    got = Results(*refs[:count])
    (output, inputs, qkv, out, uv, down, *gains) = refs[count:]
    output[...] = got.output[...]
    inputs[...] = got.input_grad[...]
    span = own_heads * width
    for index in range(qkv.shape[1] // span):
        qkv[:, index * span : (index + 1) * span] = got.back_qkv[index].astype(jnp.float32)
    out[...] = got.back_out[...].astype(jnp.float32)
    for source in range(parts):
        for index in range(uv.shape[1] // (parts * TILE)):
            there = (index * parts + source) * TILE
            here = slice(index * TILE, (index + 1) * TILE)
            uv[:, there : there + TILE] = got.back_uv[source, :, here].astype(jnp.float32)
    down[...] = got.back_down[...].astype(jnp.float32)
    start = 0
    for gain in gains:
        stop = start + gain.shape[-1]
        gain[...] = got.gains[:, start:stop]
        start = stop


def fused(sizes):
    (parts, lines, rows, model, deep, own_heads, width) = sizes
    span = own_heads * width
    hid = deep * lines * 2 // parts

    def run(tokens, lengths, w_qkv, w_out, w_uv, w_down, *others):
        gains, cotangent = others[:5], others[5]
        f32, bf16 = jnp.float32, jnp.bfloat16
        struct = jax.ShapeDtypeStruct
        middle = Results(
            struct(tokens.shape[1:], bf16),
            struct(tokens.shape[1:], f32),
            struct((3, TILE, span), bf16),
            struct(w_out.shape, bf16),
            struct((parts, TILE, 2 * hid // parts), bf16),
            struct(w_down.shape, bf16),
            struct((1, sum(g.shape[0] for g in gains)), f32),
        )
        shapes = [
            struct(tokens.shape[1:], bf16),
            struct(tokens.shape[1:], f32),
            *(struct(w.shape, f32) for w in (w_qkv, w_out, w_uv, w_down)),
            *(struct((1, g.shape[0]), f32) for g in gains),
        ]
        vmem = pl.BlockSpec(memory_space=pltpu.VMEM)
        specs = [vmem] * len(Inputs._fields)
        for place in (0, 2, 3, 4, 5, 11):
            specs[place] = pl.BlockSpec(memory_space=pl.ANY)
        specs[1] = pl.BlockSpec(memory_space=pltpu.SMEM)
        scratch = [pltpu.VMEM(shape, kind) for shape, kind in buffers(sizes).values()]
        found = pl.pallas_call(
            functools.partial(fused_layer, sizes),
            out_shape=list(middle),
            in_specs=specs,
            out_specs=[vmem] * len(middle),
            scratch_shapes=[
                *scratch,
                pltpu.SemaphoreType.DMA((SLOTS_MOST,)),
                pltpu.SemaphoreType.DMA((SLOTS_MOST,)),
                pltpu.SemaphoreType.DMA((6,)),
            ],
            compiler_params=pltpu.CompilerParams(
                collective_id=0, has_side_effects=True, vmem_limit_bytes=67043328
            ),
            name="fused_layer",
        )(
            tokens[0],
            lengths,
            w_qkv,
            w_out,
            w_uv,
            w_down,
            *(g.reshape(1, -1) for g in gains),
            cotangent[0],
        )
        outs = pl.pallas_call(
            functools.partial(place_results, sizes),
            out_shape=shapes,
            in_specs=[vmem] * len(middle),
            out_specs=[vmem] * len(shapes),
            compiler_params=pltpu.CompilerParams(vmem_limit_bytes=67043328),
            name="place_results",
        )(*found)
        return (
            outs[0][None],
            outs[1][None],
            *outs[2:6],
            *(g.reshape(-1) for g in outs[6:]),
        )

    return run


def choose(parts, shards):
    def run(*args):
        tokens, w_qkv, w_down = args[0], args[2], args[5]
        rows, model = tokens.shape[1:]
        deep, width = w_down.shape[0], model // H
        fits = shards == 2 * parts and rows == TILE and w_qkv.shape[0] == TILE
        fits = fits and deep == parts * TILE and 2 * width == TILE and H == 4 * parts
        if not fits:
            return local(*args)
        return fused((parts, shards // 2, rows, model, deep, H // parts, width))(*args)

    return run


def solution(mesh):
    return jax.shard_map(
        choose(mesh.shape["seq"], mesh.shape["fsdp"]),
        mesh=mesh,
        in_specs=(
            P("fsdp", "seq", None),
            P("fsdp", None),
            P("fsdp", "seq"),
            P("fsdp", "seq"),
            P("fsdp", "seq"),
            P("fsdp", "seq"),
            P("fsdp"),
            P("fsdp"),
            P("fsdp"),
            P("fsdp"),
            P("fsdp"),
            P("fsdp", "seq", None),
        ),
        out_specs=(
            P("fsdp", "seq", None),
            P("fsdp", "seq", None),
            P("fsdp", "seq"),
            P("fsdp", "seq"),
            P("fsdp", "seq"),
            P("fsdp", "seq"),
            P("fsdp"),
            P("fsdp"),
            P("fsdp"),
            P("fsdp"),
            P("fsdp"),
        ),
        check_vma=False,
    )
```

```python
import functools
import math
import types
import typing

import jax
import jax.numpy as jnp
from jax import lax
from jax.experimental import pallas as pl
from jax.experimental.pallas import tpu as pltpu
from jax.sharding import PartitionSpec as P

H = 16


epsilon = 1e-06


def layout(lengths_row, slot):
    columns = lengths_row.shape[0]
    ends = jnp.cumsum(lengths_row)
    starts = ends - lengths_row
    before = (slot[:, None] >= ends[None, : columns - 1]).astype(jnp.int32)
    member = jnp.sum(before, axis=1)
    picked = member[:, None] == jnp.arange(columns, dtype=jnp.int32)[None, :]
    begin = jnp.sum(jnp.where(picked, starts[None, :], 0), axis=1)
    valid = member < columns - 1
    segment = jnp.where(valid, member, columns - 1 + slot)
    place = jnp.where(valid, slot - begin, 0)
    return (segment, place, valid)


def rotary(place, width):
    half = width // 2
    frequency = jnp.exp(jnp.arange(half, dtype=jnp.float32) * (-2.0 * math.log(10000.0) / width))
    angle = place.astype(jnp.float32)[:, None] * frequency[None, :]
    return (jnp.cos(angle)[:, None, :], jnp.sin(angle)[:, None, :])


def unit_rows(value):
    return value * lax.rsqrt(jnp.mean(value * value, axis=-1, keepdims=True) + epsilon)


def turn_heads(value, cosine, sine):
    half = value.shape[-1] // 2
    first = value[..., :half]
    second = value[..., half:]
    return jnp.concatenate(
        [first * cosine - second * sine, second * cosine + first * sine], axis=-1
    )


def prepare(query_raw, key_raw, s_qk, cosine, sine, heads):
    rows = query_raw.shape[0]
    scales = s_qk.reshape(heads, -1)

    def normed(raw):
        shaped = raw.reshape(rows, heads, -1)
        return (unit_rows(turn_heads(shaped, cosine, sine)) * scales).reshape(rows, -1)

    return (normed(query_raw), normed(key_raw))


def blend(base, branch, alpha):
    return unit_rows(base + alpha * (unit_rows(branch) - base))


def gated(up_gate, s_u, s_v):
    width = s_u.shape[0]
    return up_gate[:, :width] * s_u * jax.nn.silu(up_gate[:, width:] * s_v)


def rounded(value):
    return lax.optimization_barrier(value.astype(jnp.bfloat16)).astype(jnp.float32)


def attention_forward(query, key, value, mask):
    scale = 1.0 / math.sqrt(query.shape[2])
    score = jnp.einsum("thd,shd->hts", query, key, preferred_element_type=jnp.float32)
    score = jnp.where(mask[None], score * scale, -1e30)
    peak = jnp.max(score, axis=2, keepdims=True)
    raised = jnp.exp(score - peak)
    summed = jnp.sum(raised, axis=2, keepdims=True)
    weight = (raised / summed).astype(jnp.bfloat16)
    result = jnp.einsum("hts,shd->thd", weight, value, preferred_element_type=jnp.float32)
    return result, peak + jnp.log(summed)


def attention_backward(query, key, value, mask, log_total, grad):
    scale = 1.0 / math.sqrt(query.shape[2])
    score = jnp.einsum("thd,shd->hts", query, key, preferred_element_type=jnp.float32)
    score = jnp.where(mask[None], score * scale, -1e30)
    share = jnp.exp(score - log_total)
    grad_value = jnp.einsum(
        "hts,thd->shd", share.astype(jnp.bfloat16), grad, preferred_element_type=jnp.float32
    )
    grad_share = jnp.einsum("thd,shd->hts", grad, value, preferred_element_type=jnp.float32)
    inner = jnp.sum(share * grad_share, axis=2, keepdims=True)
    grad_score = (share * (grad_share - inner)).astype(jnp.bfloat16)
    grad_query = jnp.einsum("hts,shd->thd", grad_score, key, preferred_element_type=jnp.float32)
    grad_key = jnp.einsum("hts,thd->shd", grad_score, query, preferred_element_type=jnp.float32)
    return grad_query * scale, grad_key * scale, grad_value


def low(value):
    return value.astype(jnp.bfloat16)


def product(left, right, dims):
    return lax.dot_general(left, right, (dims, ((), ())), preferred_element_type=jnp.float32)


def local(tokens, lengths, w_qkv, w_out, w_uv, w_down, s_qk, alpha_a, s_u, s_v, alpha_m, cotangent):
    rows = tokens.shape[1]
    model = tokens.shape[2]
    width = model // H
    parts = lax.axis_size("seq")
    shards = lax.axis_size("fsdp")
    mine = lax.axis_index("seq")
    own = H // parts
    deep = w_down.shape[0]
    hidden_all = deep * shards
    hidden_own = hidden_all // parts
    piece = deep // parts
    slot = mine * rows + jnp.arange(rows, dtype=jnp.int32)
    every_slot = jnp.arange(rows * parts, dtype=jnp.int32)
    keep = layout(lengths[0], slot)[2].astype(jnp.float32)[:, None]
    segment, place, _ = layout(lengths[0], every_slot)
    mask = (segment[:, None] == segment[None, :]) & (every_slot[:, None] >= every_slot[None, :])

    def exchange(array, axis):
        return lax.all_to_all(array, "seq", axis, axis, tiled=False)

    def gather(array, axis=0):
        return lax.all_gather(array, "fsdp", axis=axis, tiled=True)

    def spread(array):
        return lax.all_gather(array, "seq", axis=0, tiled=True)

    r_in = w_qkv.shape[0]
    share_qkv = lax.all_to_all(
        w_qkv.reshape(r_in, -1, parts, width), "seq", 2, 1, tiled=True
    ).reshape(r_in, -1)
    share_uv = lax.all_to_all(
        w_uv.reshape(r_in, -1, parts, piece), "seq", 2, 1, tiled=True
    ).reshape(r_in, -1)
    share_down = lax.all_to_all(w_down.reshape(parts, piece, -1), "seq", 0, 2, tiled=True)
    share_down = share_down.reshape(piece, model)
    share_out = lax.all_gather(w_out, "seq", axis=1, tiled=True)
    inputs = spread(tokens[0])
    full_qkv = gather(share_qkv)
    full_out = gather(share_out).reshape(own, parts, width, model)
    full_out = lax.dynamic_index_in_dim(full_out, mine, 1, False).reshape(own * width, model)
    full_uv = gather(share_uv)
    full_down = gather(share_down)
    gains = gather(jnp.concatenate([s_qk, alpha_a, s_u, s_v, alpha_m])[None]).astype(jnp.float32)
    cuts = [s_qk.shape[0], alpha_a.shape[0], s_u.shape[0], s_v.shape[0]]
    edges = [sum(cuts[: i + 1]) for i in range(4)]
    gain_qk, gain_a, gain_u, gain_v, gain_m = jnp.split(gains, edges, axis=1)
    gain_qk = gain_qk.reshape(own, parts, width)
    gain_qk = lax.dynamic_index_in_dim(gain_qk, mine, 1, False).reshape(-1)
    gain_a, gain_m = gain_a.reshape(-1), gain_m.reshape(-1)
    gain_u = lax.dynamic_index_in_dim(gain_u.reshape(shards, parts, piece), mine, 1, False).reshape(-1)
    gain_v = lax.dynamic_index_in_dim(gain_v.reshape(shards, parts, piece), mine, 1, False).reshape(-1)

    mixed = product(inputs, full_qkv, ((1,), (0,)))
    cosine, sine = rotary(place, width)
    span = own * width

    def prepare_local(query_raw, key_raw, scale_qk):
        return prepare(query_raw, key_raw, scale_qk, cosine, sine, own)

    (query_f, key_f), pull_prepare = jax.vjp(
        prepare_local, mixed[:, :span], mixed[:, span : 2 * span], gain_qk
    )
    heads = (rows * parts, own, width)
    query, key = low(query_f).reshape(heads), low(key_f).reshape(heads)
    value = low(mixed[:, 2 * span :]).reshape(heads)
    attended, log_total = attention_forward(query, key, value, mask)
    attended = low(attended.reshape(-1, span))

    def reduce_rows(array):
        return lax.psum_scatter(low(array), "seq", scatter_dimension=0, tiled=True).astype(
            jnp.float32
        )

    branch = reduce_rows(product(attended, full_out, ((1,), (0,))))
    first, pull_first = jax.vjp(blend, tokens[0].astype(jnp.float32), branch, gain_a)
    first_all = spread(low(first))
    up_gate = product(first_all, full_uv, ((1,), (0,)))
    hidden_f, pull_gate = jax.vjp(gated, up_gate, gain_u, gain_v)
    hidden = low(hidden_f)
    down = reduce_rows(product(hidden, full_down, ((1,), (0,))))
    final, pull_last = jax.vjp(blend, first, down, gain_m)
    output = low(final * keep)
    grad_first, grad_down, grad_gain_m = pull_last(cotangent[0].astype(jnp.float32) * keep)
    grad_down = spread(low(grad_down))
    grad_w_down = low(product(hidden, grad_down, ((0,), (0,))))
    grad_hidden = rounded(product(grad_down, full_down, ((1,), (1,))))
    grad_up_gate, grad_gain_u, grad_gain_v = pull_gate(grad_hidden)
    grad_up = low(grad_up_gate)
    grad_w_uv = low(product(first_all, grad_up, ((0,), (0,))))
    grad_first = grad_first + reduce_rows(product(grad_up, full_uv, ((1,), (1,))))
    grad_inputs, grad_branch, grad_gain_a = pull_first(grad_first)
    grad_branch = spread(low(grad_branch))
    grad_w_out = low(product(attended, grad_branch, ((0,), (0,))))
    grad_attended = low(product(grad_branch, full_out, ((1,), (1,)))).reshape(heads)
    grad_query, grad_key, grad_value = attention_backward(
        query, key, value, mask, log_total, grad_attended
    )
    grad_query_raw, grad_key_raw, grad_gain_qk = pull_prepare(
        (rounded(grad_query).reshape(-1, span), rounded(grad_key).reshape(-1, span))
    )
    grad_mixed = low(
        jnp.concatenate([grad_query_raw, grad_key_raw, grad_value.reshape(-1, span)], axis=1)
    )
    grad_w_qkv = low(product(inputs, grad_mixed, ((0,), (0,))))
    grad_inputs = grad_inputs + reduce_rows(product(grad_mixed, full_qkv, ((1,), (1,))))

    def collect(array):
        return lax.psum_scatter(array, "fsdp", scatter_dimension=0, tiled=True)

    part_down = collect(grad_w_down)
    out_down = lax.all_to_all(
        part_down.reshape(1, piece, model), "seq", 2, 0, tiled=True
    ).reshape(deep, -1)
    part_uv = collect(grad_w_uv)
    out_uv = lax.all_to_all(
        part_uv.reshape(r_in, -1, 1, piece), "seq", 1, 2, tiled=True
    ).reshape(r_in, -1)
    placed = jnp.zeros((own, parts, width, model), jnp.bfloat16)
    placed = lax.dynamic_update_slice(
        placed, grad_w_out.reshape(own, 1, width, model), (0, mine, 0, 0)
    )
    part_out = collect(placed.reshape(-1, model))
    out_out = lax.psum_scatter(part_out, "seq", scatter_dimension=1, tiled=True)
    part_qkv = collect(grad_w_qkv)
    out_qkv = lax.all_to_all(
        part_qkv.reshape(r_in, -1, 1, width), "seq", 1, 2, tiled=True
    ).reshape(r_in, -1)

    def widen(array, outer, inner):
        blank = jnp.zeros((outer, parts, inner), jnp.float32)
        array = array.reshape(outer, 1, inner)
        return lax.dynamic_update_slice(blank, array, (0, mine, 0)).reshape(shards, -1)

    gain_sums = jnp.concatenate(
        [
            widen(grad_gain_qk, own, width),
            grad_gain_a.reshape(shards, -1),
            widen(grad_gain_u, shards, piece),
            widen(grad_gain_v, shards, piece),
            grad_gain_m.reshape(shards, -1),
        ],
        axis=1,
    )
    gain_sums = lax.psum(collect(gain_sums), "seq")[0]
    outs = jnp.split(gain_sums, edges)
    return (
        output[None],
        grad_inputs[None],
        out_qkv.astype(jnp.float32),
        out_out.astype(jnp.float32),
        out_uv.astype(jnp.float32),
        out_down.astype(jnp.float32),
        outs[0],
        outs[1],
        outs[2],
        outs[3],
        outs[4],
    )


MESH = pl.DeviceIdType.MESH
TILE = 128
QROWS = 128


def loop(count, body):
    def run(index, carry):
        body(index)
        return carry

    lax.fori_loop(0, count, run, 0)


def at_rows(ref, block, size=TILE):
    return ref.at[pl.ds(pl.multiple_of(block * size, size), size), :]


def cols(block, size=TILE):
    return pl.ds(pl.multiple_of(block * size, size), size)


def mean_last(value):
    return jnp.sum(value, axis=-1, keepdims=True) * (1.0 / value.shape[-1])


class Slots:
    def __init__(self):
        self.count = 0

    def take(self, count):
        base = self.count
        self.count = base + count
        return base


def fused_layer(sizes, *refs):
    (parts, lines, rows, model, deep, own_heads, width) = sizes
    slots_all = parts * rows
    span = own_heads * width
    hid = deep * lines * 2 // parts
    count_in, count_out = len(Inputs._fields), len(Results._fields)
    ins = Inputs(*refs[:count_in])
    outs = Results(*refs[count_in : count_in + count_out])
    table = buffers(sizes)
    rest = refs[count_in + count_out :]
    v = types.SimpleNamespace(**dict(zip(table, rest[: len(table)])))
    send_sem, recv_sem, local_sem = rest[len(table) :]

    s = lax.axis_index("seq")
    f = lax.axis_index("fsdp")
    z = f // 2
    c = f % 2
    other = 1 - c
    mate = (s, 2 * z + other)
    slots = Slots()

    def put(src, dst, target, send_slot, recv_slot):
        pltpu.make_async_remote_copy(
            src_ref=src,
            dst_ref=dst,
            send_sem=send_sem.at[send_slot],
            recv_sem=recv_sem.at[recv_slot],
            device_id=target,
            device_id_type=MESH,
        ).start()

    def descriptor(ref, slot):
        return pltpu.make_async_remote_copy(
            src_ref=ref,
            dst_ref=ref,
            send_sem=send_sem.at[slot],
            recv_sem=recv_sem.at[slot],
            device_id=mate,
            device_id_type=MESH,
        )

    def landed(ref, slot):
        descriptor(ref, slot).wait_recv()

    finals = []

    def later(ref, slot, when=None):
        finals.append((ref, slot, when))

    def plane(distance):
        return (s + distance) % parts

    def plane_from(distance):
        return (s + parts - distance) % parts

    def line(distance):
        return (z + distance) % lines

    def line_from(distance):
        return (z + lines - distance) % lines

    barrier = pltpu.get_barrier_semaphore()
    for distance in range(1, parts):
        pl.semaphore_signal(barrier, inc=1, device_id=(plane(distance), f), device_id_type=MESH)
    for distance in range(1, 2 * lines):
        target = (s, (f + distance) % (2 * lines))
        pl.semaphore_signal(barrier, inc=1, device_id=target, device_id_type=MESH)

    edges = [0, TILE, 2 * TILE, 2 * TILE + deep, 2 * TILE + 2 * deep, 3 * TILE + 2 * deep]
    own_gains = (ins.s_qk, ins.alpha_a, ins.s_u, ins.s_v, ins.alpha_m)
    for place, own_gain in enumerate(own_gains):
        row = own_gain[...].astype(jnp.float32).reshape(1, -1)
        v.gain_all[f, :, edges[place] : edges[place + 1]] = row
    own_row = pl.ds(pl.multiple_of(s * rows, rows), rows)
    own_w = pl.ds(pl.multiple_of(f * TILE, TILE), TILE)
    part_cols = model // parts
    blocks_uv = 2 * hid // parts // TILE
    wide = blocks_uv * TILE

    def fetch(src, dst, slot):
        pltpu.make_async_copy(src, dst, local_sem.at[slot]).start()

    def fetched(dst, slot):
        pltpu.make_async_copy(dst, dst, local_sem.at[slot]).wait()

    fetch(ins.w_out, v.wz.at[own_w, :], 0)
    fetch(ins.tokens, v.x_all.at[own_row, :], 1)
    for index in range(blocks_uv):
        fetch(
            ins.w_uv.at[:, pl.ds(pl.multiple_of((index * parts + s) * TILE, TILE), TILE)],
            v.wu.at[own_w, pl.ds(pl.multiple_of(s * wide + index * TILE, TILE), TILE)],
            2,
        )
    fetch(ins.w_down.at[cols(s), :], v.wd.at[own_w, cols(s, part_cols)], 3)
    fetch(ins.cotangent, v.cotangent, 4)
    for index in range(3):
        chunk = 3 * s + index

        @pl.when(chunk % parts == s)
        def _():
            fetch(
                ins.w_qkv.at[:, index * span : (index + 1) * span],
                v.wq.at[own_w, cols(chunk // parts, span)],
                5,
            )

    pl.semaphore_wait(barrier, parts - 1 + 2 * lines - 1)

    qkv_slot = slots.take(3)
    for index in range(3):
        chunk = 3 * s + index
        block = chunk // parts
        target = chunk % parts

        @pl.when(target != s)
        def _():
            put(
                ins.w_qkv.at[:, index * span : (index + 1) * span],
                v.wq.at[own_w, cols(block, span)],
                (target, f),
                qkv_slot + index,
                qkv_slot + block,
            )

        later(ins.w_qkv.at[:, index * span : (index + 1) * span], qkv_slot + index, target != s)

    side, across, opposite = s + 1 - 2 * (s % 2), (s + 2) % parts, parts - 1 - s

    def half_of(shared, owner, part):
        start = owner * rows + part * (rows // 2)
        return shared.at[pl.ds(pl.multiple_of(start, rows // 2), rows // 2), :]

    token_slot = slots.take(SHARE)
    for part in range(2):
        mine = ins.tokens.at[part * (rows // 2) : (part + 1) * (rows // 2), :]
        there = half_of(v.x_all, s, part)
        for base, target in ((token_slot, side), (token_slot + 2, across)):
            put(mine, there, (target, f), base + part, base + part)
            later(mine, base + part)

    uv_slot = slots.take(parts)
    for distance in range(1, parts):
        target = plane(distance)
        for index in range(blocks_uv):
            put(
                ins.w_uv.at[:, pl.ds(pl.multiple_of((index * parts + target) * TILE, TILE), TILE)],
                v.wu.at[own_w, pl.ds(pl.multiple_of(s * wide + index * TILE, TILE), TILE)],
                (target, f),
                uv_slot + distance,
                uv_slot + distance,
            )
        later(v.wu.at[own_w, cols(s, wide)], uv_slot + distance)

    down_slot = slots.take(parts)
    for distance in range(1, parts):
        target = plane(distance)
        put(
            ins.w_down.at[cols(target), :],
            v.wd.at[own_w, cols(s, part_cols)],
            (target, f),
            down_slot + distance,
            down_slot + distance,
        )
        later(ins.w_down.at[cols(target), :], down_slot + distance)

    gain_slot = slots.take(2 * lines)
    for distance in range(1, 2 * lines):
        put(
            v.gain_all.at[f],
            v.gain_all.at[f],
            (s, (f + distance) % (2 * lines)),
            gain_slot + distance,
            gain_slot + distance,
        )
        later(v.gain_all.at[f], gain_slot + distance)

    def plane_share_relay(shared, base, passed=None):
        one, two = half_of(shared, side, 0), half_of(shared, across, 1)
        if passed is not None:
            passed(s, 0)
            passed(s, 1)
        landed(one, base)
        put(one, one, (across, f), base + 4, base + 4)
        landed(two, base + 3)
        put(two, two, (side, f), base + 5, base + 5)
        later(one, base + 4)
        later(two, base + 5)
        if passed is not None:
            passed(side, 0)
            passed(across, 1)

    def plane_share_wait(shared, base, passed=None):
        for owner, part, slot in (
            (side, 1, base + 1),
            (across, 0, base + 2),
            (opposite, 0, base + 4),
            (opposite, 1, base + 5),
        ):
            landed(half_of(shared, owner, part), slot)
            if passed is not None:
                passed(owner, part)

    def pass_to_mate(shared, slot):
        def passed(owner, part):
            start = owner * rows + part * (rows // 2)
            here = pl.ds(pl.multiple_of(start, rows // 2), rows // 2)
            there = pl.ds(pl.multiple_of(slots_all + start, rows // 2), rows // 2)
            put(shared.at[here, :], shared.at[there, :], mate, slot, slot)

        later(shared.at[:slots_all, :], slot)
        return passed

    def shard(ref, chip, core, lanes):
        block = 2 * chip + core
        return ref.at[pl.ds(pl.multiple_of(block * TILE, TILE), TILE), lanes]

    inner = z * (lines - 1 - z) > 0
    outer = z * (lines - 1 - z) == 0

    def line_send(ref, base, lanes=slice(None), twice=True):
        own = shard(ref, z, c, lanes)
        for distance in (2, 1, 3):
            target = line(distance)
            near = (z - target) * (z - target) < (lines - 1) * (lines - 1)

            @pl.when(near)
            def _():
                put(own, own, (s, 2 * target + c), base + distance, base + distance)

            later(own, base + distance, near)
        if twice:
            put(own, own, mate, base, base)
            later(own, base)

    def line_relay(ref, base, lanes=slice(None)):
        block = shard(ref, line_from(2), c, lanes)
        slot = slots.take(1)

        @pl.when(inner)
        def _():
            landed(block, base + 2)
            put(block, block, (s, 2 * (lines - 1) * (z - 1) + c), slot, base + 2 * z - 1)

        later(block, slot, inner)

    def line_forward(ref, base, lanes=slice(None)):
        for distance in (1, 3, 2):
            block = shard(ref, line_from(distance), c, lanes)
            if distance == 2:

                @pl.when(outer)
                def _():
                    landed(block, base + distance)

            else:
                landed(block, base + distance)
            put(block, block, mate, base + lines + distance, base + lines + distance)
            later(block, base + lines + distance)

    def mate_wait(ref, base, lanes=slice(None)):
        landed(shard(ref, z, other, lanes), base)
        for distance in range(1, lines):
            landed(shard(ref, line_from(distance), other, lanes), base + lines + distance)

    wq_slot, wu_slot = (slots.take(2 * lines) for _ in range(2))
    count = 4
    piece = model // count
    wd_parts = [
        (slots.take(2 * lines), slice(part * piece, (part + 1) * piece)) for part in range(count)
    ]
    wo_slot = slots.take(2 * lines)
    out_slot = slots.take(parts)
    fetched(v.wz.at[own_w, :], 0)
    line_send(v.wz, wo_slot, twice=False)

    for block in range(3):
        source = (parts * block + s) // 3

        @pl.when(source != s)
        def _():
            landed(v.wq.at[own_w, block * span : (block + 1) * span], qkv_slot + block)

        @pl.when(source == s)
        def _():
            fetched(v.wq.at[own_w, block * span : (block + 1) * span], 5)

    line_send(v.wq, wq_slot)
    lengths = [ins.lengths[0, i] for i in range(ins.lengths.shape[1])]

    def slot_facts(slot):
        end = 0
        member = jnp.zeros(slot.shape, jnp.int32)
        begin = jnp.zeros(slot.shape, jnp.int32)
        for length in lengths[:-1]:
            end = end + length
            after = slot >= end
            member = member + after.astype(jnp.int32)
            begin = jnp.where(after, end, begin)
        valid = member < len(lengths) - 1
        segment = jnp.where(valid, member, len(lengths) - 1 + slot)
        place = jnp.where(valid, slot - begin, 0)
        return segment, place, valid

    lane = lax.broadcasted_iota(jnp.int32, (1, TILE), 1)
    low_half = lane < width
    first_quarter = lane % width < width // 2
    frequency = jnp.exp(
        (lane % (width // 2)).astype(jnp.float32) * (-2.0 * math.log(10000.0) / width)
    )
    turn_sign = jnp.where(first_quarter, -1.0, 1.0)

    def tables(block):
        here = pl.ds(pl.multiple_of(block * TILE, TILE), TILE)
        slot = block * TILE + lax.broadcasted_iota(jnp.int32, (TILE, 1), 0)
        segment, place, _ = slot_facts(slot)
        angle = place.astype(jnp.float32) * frequency
        v.cosine[here, :] = jnp.cos(angle)
        v.sine[here, :] = jnp.sin(angle) * turn_sign
        key_slot = lax.broadcasted_iota(jnp.int32, (1, slots_all), 1)
        key_segment = slot_facts(key_slot)[0]
        kept = (segment == key_segment) & (slot >= key_slot)
        v.bias[here, :] = jnp.where(kept, 0.0, -1e30)

    loop(slots_all // TILE, tables)
    line_relay(v.wz, wo_slot)
    line_relay(v.wq, wq_slot)
    fetched(v.x_all.at[own_row, :], 1)
    plane_share_relay(v.x_all, token_slot)
    plane_share_wait(v.x_all, token_slot)
    for distance in (1, 3):
        landed(shard(v.wz, line_from(distance), c, slice(None)), wo_slot + distance)

    @pl.when(outer)
    def _():
        landed(shard(v.wz, line_from(2), c, slice(None)), wo_slot + 2)

    for distance in range(1, parts):
        target = plane(distance)
        rows_out = at_rows(v.wz, 2 * target + c)
        put(
            rows_out,
            v.wo.at[cols(c), cols(s, part_cols)],
            (target, f),
            out_slot + distance,
            out_slot + distance,
        )
        later(rows_out, out_slot + distance)
    v.wo[cols(c), cols(s, part_cols)] = v.wz[cols(2 * s + c), :]
    fetched(v.wu.at[own_w, cols(s, wide)], 2)
    for distance in range(1, parts):
        landed(v.wu.at[own_w, cols(plane_from(distance), wide)], uv_slot + distance)
    line_send(v.wu, wu_slot)

    def mate_blocks(name_all, ref, stage, slot):
        for block in range(lines):
            here = slice(block * TILE, (block + 1) * TILE)
            stage[here, :] = name_all[:, cols(2 * block + other)].T
        put(stage, ref.at[:, slots_all:], mate, slot, slot)
        later(stage, slot)
        for block in range(lines):
            here = slice(block * TILE, (block + 1) * TILE)
            ref[here, :slots_all] = name_all[:, cols(2 * block + c)].T

    mate_x_slot = slots.take(1)
    mate_blocks(v.x_all, v.turned_x, v.stage_x, mate_x_slot)
    for distance in range(1, 2 * lines):
        landed(v.gain_all.at[(f + 2 * lines - distance) % (2 * lines)], gain_slot + distance)

    def gain(block, offset):
        return v.gain_all[block, :, pl.ds(pl.multiple_of(offset, TILE), TILE)]

    for block in range(2 * lines):
        here = slice(block * TILE, (block + 1) * TILE)
        v.gain_a[:, here] = gain(block, edges[1])
        v.gain_u[:, here] = gain(block, edges[2] + s * TILE)
        v.gain_v[:, here] = gain(block, edges[3] + s * TILE)
        v.gain_m[:, here] = gain(block, edges[4])
    for block in range(span // TILE):
        v.gain_qk[:, block * TILE : (block + 1) * TILE] = gain(span // TILE * s + block, 0)

    line_forward(v.wq, wq_slot)
    mate_wait(v.wq, wq_slot)

    def mix(index):
        v.raw[:, cols(index, span)] = product(
            v.x_all[...], v.wq[:, cols(index, span)], ((1,), (0,))
        )

    loop(3, mix)

    def swap(value):
        return jnp.where(
            first_quarter,
            pltpu.roll(value, TILE - width // 2, 1),
            pltpu.roll(value, width // 2, 1),
        )

    def head_mean(value):
        one = jnp.sum(jnp.where(low_half, value, 0.0), axis=-1, keepdims=True)
        two = jnp.sum(jnp.where(low_half, 0.0, value), axis=-1, keepdims=True)
        return jnp.where(low_half, one, two) * (1.0 / width)

    pairs = span // TILE
    blocks = slots_all // TILE

    def prepare_block(index):
        here = pl.ds(pl.multiple_of(index % blocks * TILE, TILE), TILE)
        group = index // blocks
        there = cols(group)
        value = v.raw[here, there]
        turned = value * v.cosine[here, :] + swap(value) * v.sine[here, :]
        inverse = lax.rsqrt(head_mean(turned * turned) + epsilon)
        normed = turned * inverse
        v.normed[here, there] = normed
        v.inverse[here, there] = inverse
        v.qkv[here, there] = low(normed * v.gain_qk[:, cols(group % pairs)])

    loop(2 * pairs * blocks, prepare_block)

    def keep_value(index):
        here = pl.ds(pl.multiple_of(index * TILE, TILE), TILE)
        v.qkv[here, 2 * span :] = low(v.raw[here, 2 * span :])

    loop(blocks, keep_value)
    own_out = v.wo.at[cols(c), :]
    for distance in range(1, parts):
        landed(v.wo.at[cols(c), cols(plane_from(distance), part_cols)], out_slot + distance)
    put(own_out, own_out, mate, wo_slot, wo_slot)
    later(own_out, wo_slot)

    scale = 1.0 / math.sqrt(width)
    halves = (low_half, jnp.logical_not(low_half))

    def attend(pair):
        q_cols, k_cols, v_cols = cols(pair), cols(pairs + pair), cols(2 * pairs + pair)
        for block in range(blocks):
            here = slice(block * TILE, (block + 1) * TILE)
            seen = slice(0, (block + 1) * TILE)
            results = []
            for half in range(2):
                query = jnp.where(halves[half], v.qkv[here, q_cols], 0.0).astype(jnp.bfloat16)
                score = product(query, v.qkv[seen, k_cols], ((1,), (1,))) * scale
                score = score + v.bias[here, seen]
                peak = jnp.max(score, axis=1, keepdims=True)
                raised = jnp.exp(score - peak)
                summed = jnp.sum(raised, axis=1, keepdims=True)
                weight = low(raised / summed)
                results.append(product(weight, v.qkv[seen, v_cols], ((1,), (0,))))
                v.total[2 * pair + half, here, :] = peak + jnp.log(summed)
            v.attended[here, q_cols] = low(jnp.where(low_half, results[0], results[1]))

    loop(pairs, attend)
    mate_att_slot = slots.take(1)
    v.stage_att[...] = v.attended[:, cols(other)].T
    v.turned_att[:, :slots_all] = v.attended[:, cols(c)].T

    put(v.stage_att, v.turned_att.at[:, slots_all:], mate, mate_att_slot, mate_att_slot)
    later(v.stage_att, mate_att_slot)
    landed(v.wo.at[cols(other), :], wo_slot)

    def plane_sum(sums, arrived, base, tile, span_of=(0, count)):
        start, stop = span_of

        def send(index):
            there = cols(index, piece)
            for distance in range(1, parts):
                target = plane(distance)
                put(
                    sums.at[pl.ds(pl.multiple_of(target * rows, rows), rows), there],
                    arrived.at[distance - 1, :, there],
                    (target, f),
                    base + distance,
                    base + distance,
                )

        def step(index):
            sums[:, cols(start + index, piece)] = low(tile(start + index))

            @pl.when(index > 0)
            def _():
                send(start + index - 1)

        loop(stop - start, step)
        send(stop - 1)
        if stop == count:
            for distance in range(1, parts):
                later(arrived.at[distance - 1], base + distance)

    def plane_sum_wait(arrived, base):
        for distance in range(1, parts):
            landed(arrived.at[distance - 1], base + distance)

    def plane_total(sums, arrived, here, at):
        total = sums[here, :].astype(jnp.float32)
        for distance in range(1, parts):
            total = total + arrived[distance - 1, at, :].astype(jnp.float32)
        return total

    chunk_rows = 32

    def chunk(index):
        at = pl.ds(pl.multiple_of(index * chunk_rows, chunk_rows), chunk_rows)
        here = pl.ds(pl.multiple_of(s * rows + index * chunk_rows, chunk_rows), chunk_rows)
        return at, here

    def plane_share(shared, base, make):
        def send(index):
            own = shared.at[chunk(index)[1], :]
            part = index // (rows // chunk_rows // 2)
            put(own, own, (side, f), base + part, base + part)
            put(own, own, (across, f), base + 2 + part, base + 2 + part)

        def step(index):
            make(index)

            @pl.when(index > 0)
            def _():
                send(index - 1)

        loop(rows // chunk_rows, step)
        send(rows // chunk_rows - 1)
        for part in range(2):
            later(half_of(shared, s, part), base + part)
            later(half_of(shared, s, part), base + 2 + part)

    branch_slot = slots.take(parts)
    plane_sum(
        v.part_branch,
        v.got_branch,
        branch_slot,
        lambda index: product(v.attended[...], v.wo[:, cols(index, piece)], ((1,), (0,))),
    )
    line_relay(v.wu, wu_slot)
    fetched(v.wd.at[own_w, cols(s, part_cols)], 3)
    for distance in range(1, parts):
        landed(v.wd.at[own_w, cols(plane_from(distance), part_cols)], down_slot + distance)
    for slot, lanes in wd_parts:
        line_send(v.wd, slot, lanes)
    plane_sum_wait(v.got_branch, branch_slot)

    def blended(base, branch, alpha):
        inverse_branch = lax.rsqrt(mean_last(branch * branch) + epsilon)
        normed = branch * inverse_branch
        mixed = base + alpha * (normed - base)
        inverse = lax.rsqrt(mean_last(mixed * mixed) + epsilon)
        return normed, inverse_branch, mixed * inverse, inverse

    def blended_back(grad, base, alpha, normed, inverse_branch, result, inverse):
        grad_mixed = inverse * (grad - result * mean_last(grad * result))
        grad_normed = alpha * grad_mixed
        grad_branch = inverse_branch * (grad_normed - normed * mean_last(grad_normed * normed))
        grad_alpha = jnp.sum(grad_mixed * (normed - base), axis=0, keepdims=True)
        return grad_mixed - grad_normed, grad_branch, grad_alpha

    def make_first(index):
        at, here = chunk(index)
        base = v.x_all[here, :].astype(jnp.float32)
        normed, inverse_branch, result, inverse = blended(
            base, plane_total(v.part_branch, v.got_branch, here, at), v.gain_a[...]
        )
        v.branch_normed[at, :] = normed
        v.branch_inverse[at, :] = inverse_branch
        v.first[at, :] = result
        v.first_inverse[at, :] = inverse
        v.first_all[here, :] = low(result)

    first_slot = slots.take(SHARE)
    plane_share(v.first_all, first_slot, make_first)
    plane_share_relay(v.first_all, first_slot)
    line_forward(v.wu, wu_slot)
    mate_wait(v.wu, wu_slot)
    plane_share_wait(v.first_all, first_slot)

    def gate_tile(index):
        there = cols(index, 256)
        v.up[:, there] = product(v.first_all[...], v.wu[:, there], ((1,), (0,)))
        v.gate[:, there] = product(
            v.first_all[...],
            v.wu[:, pl.ds(pl.multiple_of(hid + index * 256, 256), 256)],
            ((1,), (0,)),
        )

        def rows_of(block):
            here = pl.ds(pl.multiple_of(block * 64, 64), 64)
            scaled = v.gate[here, there] * v.gain_v[:, there]
            passed = scaled / (1.0 + jnp.exp(-scaled))
            v.hidden[here, there] = low(v.up[here, there] * v.gain_u[:, there] * passed)

        loop(slots_all // 64, rows_of)

    line_relay(v.wd, *wd_parts[0])
    loop(hid // 512, gate_tile)
    line_relay(v.wd, *wd_parts[1])
    line_forward(v.wd, *wd_parts[0])
    loop(hid // 512, lambda index: gate_tile(hid // 512 + index))
    mate_hidden_slot = slots.take(1)
    mate_blocks(v.hidden, v.turned_hidden, v.stage_hidden, mate_hidden_slot)
    mate_first_slot = slots.take(1)
    mate_blocks(v.first_all, v.turned_first, v.stage_first, mate_first_slot)
    down_sum_slot = slots.take(parts)

    def down_tile(index):
        return product(v.hidden[...], v.wd[:, cols(index, piece)], ((1,), (0,)))

    line_relay(v.wd, *wd_parts[2])
    line_forward(v.wd, *wd_parts[1])
    for part in range(count):
        mate_wait(v.wd, *wd_parts[part])
        if part == 0:
            line_relay(v.wd, *wd_parts[3])
        plane_sum(v.part_down, v.got_down, down_sum_slot, down_tile, (part, part + 1))
        if part + 2 < count:
            line_forward(v.wd, *wd_parts[part + 2])
    fetched(v.cotangent, 4)
    plane_sum_wait(v.got_down, down_sum_slot)
    v.grad_a[...] = jnp.zeros_like(v.grad_a)
    v.grad_m[...] = jnp.zeros_like(v.grad_m)

    def finish(index):
        at, here = chunk(index)
        slot = s * rows + index * chunk_rows
        slot = slot + lax.broadcasted_iota(jnp.int32, (chunk_rows, 1), 0)
        keep = slot_facts(slot)[2].astype(jnp.float32)
        base = v.first[at, :]
        alpha = v.gain_m[...]
        normed, inverse_branch, result, inverse = blended(
            base, plane_total(v.part_down, v.got_down, here, at), alpha
        )
        outs.output[at, :] = low(result * keep)
        grad = v.cotangent[at, :].astype(jnp.float32) * keep
        grad_base, grad_down, grad_alpha = blended_back(
            grad, base, alpha, normed, inverse_branch, result, inverse
        )
        v.grad_first[at, :] = grad_base
        v.gd[here, :] = low(grad_down)
        v.grad_m[...] += grad_alpha

    gd_slot = slots.take(SHARE)
    plane_share(v.gd, gd_slot, finish)
    mate_gd_slot = slots.take(1)
    passed_gd = pass_to_mate(v.gd, mate_gd_slot)
    plane_share_relay(v.gd, gd_slot, passed_gd)
    plane_share_wait(v.gd, gd_slot, passed_gd)
    first_half = slice(0, slots_all)
    second_half = slice(slots_all, 2 * slots_all)

    ends = (lines - 1) * (1 - z % 2)
    mids = 2 - z // 2
    last = (2 * z + 1) % (lines + 1)
    beside = z + 1 - 2 * (z % 2)

    mid_slot = 2 - z * (lines - 1 - z) // 2

    def line_grad_first(grads, arrived, base, there):
        put(
            grads.at[ends, :, there],
            arrived.at[0, :, there],
            (s, 2 * beside + c),
            base,
            base,
        )

    def line_grad_mid(grads, arrived, base, there):
        put(
            grads.at[mids, :, there],
            arrived.at[mid_slot, :, there],
            (s, 2 * mids + c),
            base + 1,
            base + mid_slot,
        )

    def line_grad_rest(grads, arrived, base):
        @pl.when(outer)
        def _():
            line_grad_mid(grads, arrived, base, slice(None))
            put(grads.at[last], arrived.at[3], (s, 2 * last + c), base + 2, base + 3)

        for index in range(3):
            later(grads.at[0], base + index)

    def weight_grad(turned, right, grads, arrived, columns, base):
        def send(index):
            line_grad_first(grads, arrived, base, cols(index, 256))

            @pl.when(inner)
            def _():
                line_grad_mid(grads, arrived, base, cols(index, 256))

        def step(index):
            there = cols(index, 256)
            total = product(turned[...], right[:, there], ((1,), (0,)))
            grads[:, :, there] = low(total).reshape(lines, TILE, 256)

            @pl.when(index > 0)
            def _():
                send(index - 1)

        loop(columns // 256, step)
        send(columns // 256 - 1)
        line_grad_rest(grads, arrived, base)

    def weight_combine(grads, arrived, columns, base):
        @pl.when(inner)
        def _():
            landed(arrived.at[0], base)

            def tile(index):
                there = cols(index, 256)
                total = grads[last, :, there].astype(jnp.float32)
                grads[last, :, there] = low(total + arrived[0, :, there].astype(jnp.float32))

            loop(columns // 256, tile)
            put(
                grads.at[last], arrived.at[1], (s, 2 * last + c), base + 2, base + 1
            )

    def gate_back(index):
        there = cols(index, 256)
        there_gate = pl.ds(pl.multiple_of(hid + index * 256, 256), 256)
        v.grad_hidden[...] = low(product(v.gd[first_half, :], v.wd[there, :], ((1,), (1,))))
        v.grad_u[:, there] = jnp.zeros((1, 256), jnp.float32)
        v.grad_v[:, there] = jnp.zeros((1, 256), jnp.float32)

        def rows_of(block):
            here = pl.ds(pl.multiple_of(block * 64, 64), 64)
            grad = v.grad_hidden[here, :].astype(jnp.float32)
            up = v.up[here, there]
            gate = v.gate[here, there]
            gain_u = v.gain_u[:, there]
            gain_v = v.gain_v[:, there]
            scaled = gate * gain_v
            squash = 1.0 / (1.0 + jnp.exp(-scaled))
            passed = scaled * squash
            grad_scaled_up = grad * passed
            grad_scaled = grad * (up * gain_u) * (squash + passed * (1.0 - squash))
            v.gu[here, there] = low(grad_scaled_up * gain_u)
            v.gu[here, there_gate] = low(grad_scaled * gain_v)
            v.grad_u[:, there] += jnp.sum(grad_scaled_up * up, axis=0, keepdims=True)
            v.grad_v[:, there] += jnp.sum(grad_scaled * gate, axis=0, keepdims=True)

        loop(slots_all // 64, rows_of)

    loop(1, gate_back)
    landed(v.turned_x.at[:, second_half], mate_x_slot)
    landed(v.turned_first.at[:, second_half], mate_first_slot)
    landed(v.turned_hidden.at[:, second_half], mate_hidden_slot)
    landed(v.gd.at[second_half, :], mate_gd_slot)
    line_down_slot = slots.take(lines)
    weight_grad(v.turned_hidden, v.gd, v.send_down, v.line_down, model, line_down_slot)
    loop(hid // 256 - 1, lambda index: gate_back(index + 1))
    mate_gu_slot = slots.take(1)
    put(v.gu.at[first_half, :], v.gu.at[second_half, :], mate, mate_gu_slot, mate_gu_slot)
    later(v.gu.at[first_half, :], mate_gu_slot)
    first_sum_slot = slots.take(parts)
    plane_sum(
        v.part_first,
        v.got_first,
        first_sum_slot,
        lambda index: product(v.gu[first_half, :], v.wu[cols(index, piece), :], ((1,), (1,))),
    )
    weight_combine(v.send_down, v.line_down, model, line_down_slot)
    landed(v.gu.at[second_half, :], mate_gu_slot)
    line_uv_slot = slots.take(lines)
    weight_grad(v.turned_first, v.gu, v.send_uv, v.line_uv, 2 * hid, line_uv_slot)
    plane_sum_wait(v.got_first, first_sum_slot)

    def back_first(index):
        at, here = chunk(index)
        grad = v.grad_first[at, :] + plane_total(v.part_first, v.got_first, here, at)
        grad_base, grad_branch, grad_alpha = blended_back(
            grad,
            v.x_all[here, :].astype(jnp.float32),
            v.gain_a[...],
            v.branch_normed[at, :],
            v.branch_inverse[at, :],
            v.first[at, :],
            v.first_inverse[at, :],
        )
        v.grad_tokens[at, :] = grad_base
        v.gb[here, :] = low(grad_branch)
        v.grad_a[...] += grad_alpha

    gb_slot = slots.take(SHARE)
    plane_share(v.gb, gb_slot, back_first)
    mate_gb_slot = slots.take(1)
    passed_gb = pass_to_mate(v.gb, mate_gb_slot)
    plane_share_relay(v.gb, gb_slot, passed_gb)
    plane_share_wait(v.gb, gb_slot, passed_gb)

    v.grad_att[...] = low(product(v.gb[first_half, :], v.wo[...], ((1,), (1,))))
    landed(v.turned_att.at[:, second_half], mate_att_slot)
    landed(v.gb.at[second_half, :], mate_gb_slot)
    line_out_slot = slots.take(lines)
    part_out_slot = slots.take(parts)

    def out_tile(index):
        there = cols(index, 256)
        v.send_out[:, there] = low(product(v.turned_att[...], v.gb[:, there], ((1,), (0,))))

    loop(model // 256, out_tile)
    for distance in range(1, parts):
        target = plane(distance)
        put(
            v.send_out.at[:, cols(target, part_cols)],
            v.send_wo.at[s],
            (target, f),
            part_out_slot + distance,
            part_out_slot + distance,
        )
        later(v.send_wo.at[s], part_out_slot + distance)
    v.send_wo[s] = v.send_out[:, cols(s, part_cols)]
    weight_combine(v.send_uv, v.line_uv, 2 * hid, line_uv_slot)
    v.grad_qkv[...] = jnp.zeros_like(v.grad_qkv)

    def attend_back(pair):
        q_cols, k_cols, v_cols = cols(pair), cols(pairs + pair), cols(2 * pairs + pair)
        for block in range(blocks):
            here = slice(block * TILE, (block + 1) * TILE)
            seen = slice(0, (block + 1) * TILE)
            results = []
            for half in range(2):
                query = jnp.where(halves[half], v.qkv[here, q_cols], 0.0).astype(jnp.bfloat16)
                grad = jnp.where(halves[half], v.grad_att[here, q_cols], 0.0)
                grad = grad.astype(jnp.bfloat16)
                score = product(query, v.qkv[seen, k_cols], ((1,), (1,))) * scale
                score = score + v.bias[here, seen]
                share = jnp.exp(score - v.total[2 * pair + half, here, :])
                grad_share = product(grad, v.qkv[seen, v_cols], ((1,), (1,)))
                inner = jnp.sum(share * grad_share, axis=1, keepdims=True)
                grad_score = low(share * (grad_share - inner))
                results.append(product(grad_score, v.qkv[seen, k_cols], ((1,), (0,))))
                v.grad_qkv[seen, v_cols] += product(low(share), grad, ((0,), (0,)))
                v.grad_qkv[seen, k_cols] += product(grad_score, query, ((0,), (0,)))
            v.grad_qkv[here, q_cols] = jnp.where(low_half, results[0], results[1])

    loop(pairs, attend_back)
    v.grad_qk[...] = jnp.zeros_like(v.grad_qk)

    def prepare_back(index):
        here = pl.ds(pl.multiple_of(index % blocks * TILE, TILE), TILE)
        group = index // blocks
        there = cols(group)
        pair = cols(group % pairs)
        grad = low(v.grad_qkv[here, there] * scale).astype(jnp.float32)
        normed = v.normed[here, there]
        v.grad_qk[:, pair] += jnp.sum(grad * normed, axis=0, keepdims=True)
        grad = grad * v.gain_qk[:, pair]
        grad = v.inverse[here, there] * (grad - normed * head_mean(grad * normed))
        back = grad * v.cosine[here, :] - swap(grad) * v.sine[here, :]
        v.gm[here, there] = low(back)

    loop(2 * pairs * blocks, prepare_back)

    def value_back(index):
        here = pl.ds(pl.multiple_of(index * TILE, TILE), TILE)
        v.gm[here, 2 * span :] = low(v.grad_qkv[here, 2 * span :])

    loop(blocks, value_back)
    mate_gm_slot = slots.take(1)
    put(v.gm.at[first_half, :], v.gm.at[second_half, :], mate, mate_gm_slot, mate_gm_slot)
    later(v.gm.at[first_half, :], mate_gm_slot)

    v.gain_part[...] = jnp.zeros_like(v.gain_part)
    for block in range(2 * lines):
        here = slice(block * TILE, (block + 1) * TILE)
        local_pair = block % (span // TILE) * TILE
        qk = v.grad_qk[:, local_pair : local_pair + TILE]
        mine = (s == block // (span // TILE)).astype(jnp.float32)
        v.gain_part[block, :, edges[0] : edges[1]] = qk * mine
        v.gain_part[block, :, edges[1] : edges[2]] = v.grad_a[:, here]
        v.gain_part[block, :, cols(edges[2] // TILE + s)] = v.grad_u[:, here]
        v.gain_part[block, :, cols(edges[3] // TILE + s)] = v.grad_v[:, here]
        v.gain_part[block, :, edges[4] : edges[5]] = v.grad_m[:, here]

    inputs_slot = slots.take(parts)
    plane_sum(
        v.part_inputs,
        v.got_inputs,
        inputs_slot,
        lambda index: product(v.gm[first_half, :], v.wq[cols(index, piece), :], ((1,), (1,))),
    )
    gain_line_slot = slots.take(2 * lines)
    for distance in range(1, 2 * lines):
        target = (f + distance) % (2 * lines)
        put(
            v.gain_part.at[target],
            v.gain_got.at[distance - 1],
            (s, target),
            gain_line_slot + distance,
            gain_line_slot + distance,
        )
        later(v.gain_got.at[distance - 1], gain_line_slot + distance)
    landed(v.gm.at[second_half, :], mate_gm_slot)
    line_qkv_slot = slots.take(lines)
    weight_grad(v.turned_x, v.gm, v.send_qkv, v.line_qkv, 3 * span, line_qkv_slot)
    for distance in range(1, parts):
        landed(v.send_wo.at[plane_from(distance)], part_out_slot + distance)
    line_grad_first(v.send_wo, v.line_wo, line_out_slot, slice(None))
    pl.when(inner)(lambda: line_grad_mid(v.send_wo, v.line_wo, line_out_slot, slice(None)))
    line_grad_rest(v.send_wo, v.line_wo, line_out_slot)

    def line_total(grads, arrived, done, columns, base):
        def add(slots_in):
            for slot in slots_in:
                landed(arrived.at[slot], base + slot)

            def tile(index):
                there = cols(index, 256)
                total = grads[z, :, there].astype(jnp.float32)
                for slot in slots_in:
                    total = total + arrived[slot, :, there].astype(jnp.float32)
                done[:, there] = low(total)

            loop(columns // 256, tile)

        pl.when(outer)(lambda: add((0, 1)))
        pl.when(inner)(lambda: add((1, 2, 3)))

    line_total(v.send_down, v.line_down, v.done_down, model, line_down_slot)
    back_down_slot = slots.take(parts)
    for distance in range(1, parts):
        target = plane(distance)
        put(
            v.done_down.at[:, cols(target, part_cols)],
            outs.back_down.at[cols(s), :],
            (target, f),
            back_down_slot + distance,
            back_down_slot + distance,
        )
        later(v.done_down.at[:, cols(target, part_cols)], back_down_slot + distance)
    outs.back_down[cols(s), :] = v.done_down[:, cols(s, part_cols)]

    plane_sum_wait(v.got_inputs, inputs_slot)

    def finish_inputs(index):
        at, here = chunk(index)
        outs.input_grad[at, :] = v.grad_tokens[at, :] + plane_total(v.part_inputs, v.got_inputs, here, at)

    loop(rows // chunk_rows, finish_inputs)

    line_total(v.send_uv, v.line_uv, v.done_uv, 2 * hid, line_uv_slot)
    back_uv_slot = slots.take(parts)
    for distance in range(1, parts):
        target = plane(distance)
        for index in range(blocks_uv):
            put(
                v.done_uv.at[:, pl.ds(pl.multiple_of(target * wide + index * TILE, TILE), TILE)],
                outs.back_uv.at[s, :, index * TILE : (index + 1) * TILE],
                (target, f),
                back_uv_slot + distance,
                back_uv_slot + distance,
            )
        later(v.done_uv.at[:, cols(target, wide)], back_uv_slot + distance)
    outs.back_uv[s] = v.done_uv[:, cols(s, wide)]

    weight_combine(v.send_qkv, v.line_qkv, 3 * span, line_qkv_slot)
    weight_combine(v.send_wo, v.line_wo, part_cols, line_out_slot)
    gain_plane_slot = slots.take(parts)
    for distance in range(1, 2 * lines):
        landed(v.gain_got.at[distance - 1], gain_line_slot + distance)
    total = v.gain_part[f]
    for distance in range(1, 2 * lines):
        total = total + v.gain_got[distance - 1]
    v.gain_sum[s] = total
    for distance in range(1, parts):
        put(
            v.gain_sum.at[s],
            v.gain_sum.at[s],
            (plane(distance), f),
            gain_plane_slot + distance,
            gain_plane_slot + distance,
        )
        later(v.gain_sum.at[s], gain_plane_slot + distance)

    line_total(v.send_qkv, v.line_qkv, v.done_qkv, 3 * span, line_qkv_slot)
    back_qkv_slot = slots.take(3)
    for block in range(3):
        chunk_of = parts * block + s
        target = chunk_of // 3
        index = chunk_of % 3
        source = v.done_qkv.at[:, block * span : (block + 1) * span]

        @pl.when(target == s)
        def _():
            outs.back_qkv[index] = source[...]

        @pl.when(target != s)
        def _():
            put(
                source,
                outs.back_qkv.at[index],
                (target, f),
                back_qkv_slot + block,
                back_qkv_slot + index,
            )

        later(source, back_qkv_slot + block, target != s)

    for distance in range(1, parts):
        landed(outs.back_down.at[cols(plane_from(distance)), :], back_down_slot + distance)
    for distance in range(1, parts):
        landed(outs.back_uv.at[plane_from(distance)], back_uv_slot + distance)
    for distance in range(1, parts):
        landed(v.gain_sum.at[plane_from(distance)], gain_plane_slot + distance)
    total = v.gain_sum[0]
    for source in range(1, parts):
        total = total + v.gain_sum[source]
    outs.gains[...] = total
    for index in range(3):
        source = (3 * s + index) % parts

        @pl.when(source != s)
        def _():
            landed(outs.back_qkv.at[index], back_qkv_slot + index)

    line_total(v.send_wo, v.line_wo, outs.back_out, part_cols, line_out_slot)

    for ref, slot, when in finals:
        if when is None:
            descriptor(ref, slot).wait_send()
        else:

            @pl.when(when)
            def _():
                descriptor(ref, slot).wait_send()

    assert slots.count <= SLOTS_MOST, slots.count


SLOTS_MOST = 220
SHARE = 6


class Inputs(typing.NamedTuple):
    tokens: typing.Any
    lengths: typing.Any
    w_qkv: typing.Any
    w_out: typing.Any
    w_uv: typing.Any
    w_down: typing.Any
    s_qk: typing.Any
    alpha_a: typing.Any
    s_u: typing.Any
    s_v: typing.Any
    alpha_m: typing.Any
    cotangent: typing.Any


class Results(typing.NamedTuple):
    output: typing.Any
    input_grad: typing.Any
    back_qkv: typing.Any
    back_out: typing.Any
    back_uv: typing.Any
    back_down: typing.Any
    gains: typing.Any


def buffers(sizes):
    (parts, lines, rows, model, deep, own_heads, width) = sizes
    every = parts * rows
    span = own_heads * width
    hid = deep * lines * 2 // parts
    half = lines * TILE
    gains = 3 * TILE + 2 * deep
    bf16, f32 = jnp.bfloat16, jnp.float32
    return dict(
        wq=((model, 3 * span), bf16),
        wo=((span, model), bf16),
        wz=((model, model // parts), bf16),
        cotangent=((rows, model), bf16),
        wu=((model, 2 * hid), bf16),
        wd=((hid, model), bf16),
        gain_all=((2 * lines, 1, gains), f32),
        gain_a=((1, model), f32),
        gain_m=((1, model), f32),
        gain_u=((1, hid), f32),
        gain_v=((1, hid), f32),
        gain_qk=((1, span), f32),
        x_all=((every, model), bf16),
        first_all=((every, model), bf16),
        gd=((2 * every, model), bf16),
        gb=((2 * every, model), bf16),
        cosine=((every, TILE), f32),
        sine=((every, TILE), f32),
        bias=((every, every), f32),
        raw=((every, 3 * span), f32),
        normed=((every, 2 * span), f32),
        inverse=((every, 2 * span), f32),
        qkv=((every, 3 * span), bf16),
        total=((own_heads, every, 1), f32),
        attended=((every, span), bf16),
        branch_normed=((rows, model), f32),
        branch_inverse=((rows, 1), f32),
        first=((rows, model), f32),
        first_inverse=((rows, 1), f32),
        up=((every, hid), f32),
        gate=((every, hid), f32),
        hidden=((every, hid), bf16),
        grad_hidden=((every, 256), bf16),
        gu=((2 * every, 2 * hid), bf16),
        grad_first=((rows, model), f32),
        grad_tokens=((rows, model), f32),
        grad_att=((every, span), bf16),
        grad_qkv=((every, 3 * span), f32),
        gm=((2 * every, 3 * span), bf16),
        grad_a=((1, model), f32),
        grad_m=((1, model), f32),
        grad_u=((1, hid), f32),
        grad_v=((1, hid), f32),
        grad_qk=((1, span), f32),
        gain_part=((2 * lines, 1, gains), f32),
        gain_got=((2 * lines - 1, 1, gains), f32),
        gain_sum=((parts, 1, gains), f32),
        turned_x=((half, 2 * every), bf16),
        turned_first=((half, 2 * every), bf16),
        turned_hidden=((half, 2 * every), bf16),
        turned_att=((TILE, 2 * every), bf16),
        stage_x=((half, every), bf16),
        stage_first=((half, every), bf16),
        stage_hidden=((half, every), bf16),
        stage_att=((TILE, every), bf16),
        send_out=((TILE, model), bf16),
        send_wo=((lines, TILE, model // parts), bf16),
        line_wo=((4, TILE, model // parts), bf16),
        part_branch=((every, model), bf16),
        got_branch=((parts - 1, rows, model), bf16),
        part_down=((every, model), bf16),
        got_down=((parts - 1, rows, model), bf16),
        part_first=((every, model), bf16),
        got_first=((parts - 1, rows, model), bf16),
        part_inputs=((every, model), bf16),
        got_inputs=((parts - 1, rows, model), bf16),
        send_qkv=((lines, TILE, 3 * span), bf16),
        line_qkv=((4, TILE, 3 * span), bf16),
        done_qkv=((TILE, 3 * span), bf16),
        send_uv=((lines, TILE, 2 * hid), bf16),
        line_uv=((4, TILE, 2 * hid), bf16),
        done_uv=((TILE, 2 * hid), bf16),
        send_down=((lines, TILE, model), bf16),
        line_down=((4, TILE, model), bf16),
        done_down=((TILE, model), bf16),
    )


def place_results(sizes, *refs):
    (parts, lines, rows, model, deep, own_heads, width) = sizes
    count = len(Results._fields)
    got = Results(*refs[:count])
    (output, inputs, qkv, out, uv, down, *gains) = refs[count:]
    output[...] = got.output[...]
    inputs[...] = got.input_grad[...]
    span = own_heads * width
    for index in range(qkv.shape[1] // span):
        qkv[:, index * span : (index + 1) * span] = got.back_qkv[index].astype(jnp.float32)
    out[...] = got.back_out[...].astype(jnp.float32)
    for source in range(parts):
        for index in range(uv.shape[1] // (parts * TILE)):
            there = (index * parts + source) * TILE
            here = slice(index * TILE, (index + 1) * TILE)
            uv[:, there : there + TILE] = got.back_uv[source, :, here].astype(jnp.float32)
    down[...] = got.back_down[...].astype(jnp.float32)
    start = 0
    for gain in gains:
        stop = start + gain.shape[-1]
        gain[...] = got.gains[:, start:stop]
        start = stop


def fused(sizes):
    (parts, lines, rows, model, deep, own_heads, width) = sizes
    span = own_heads * width
    hid = deep * lines * 2 // parts

    def run(tokens, lengths, w_qkv, w_out, w_uv, w_down, *others):
        gains, cotangent = others[:5], others[5]
        f32, bf16 = jnp.float32, jnp.bfloat16
        struct = jax.ShapeDtypeStruct
        middle = Results(
            struct(tokens.shape[1:], bf16),
            struct(tokens.shape[1:], f32),
            struct((3, TILE, span), bf16),
            struct(w_out.shape, bf16),
            struct((parts, TILE, 2 * hid // parts), bf16),
            struct(w_down.shape, bf16),
            struct((1, sum(g.shape[0] for g in gains)), f32),
        )
        shapes = [
            struct(tokens.shape[1:], bf16),
            struct(tokens.shape[1:], f32),
            *(struct(w.shape, f32) for w in (w_qkv, w_out, w_uv, w_down)),
            *(struct((1, g.shape[0]), f32) for g in gains),
        ]
        vmem = pl.BlockSpec(memory_space=pltpu.VMEM)
        specs = [vmem] * len(Inputs._fields)
        for place in (0, 2, 3, 4, 5, 11):
            specs[place] = pl.BlockSpec(memory_space=pl.ANY)
        specs[1] = pl.BlockSpec(memory_space=pltpu.SMEM)
        scratch = [pltpu.VMEM(shape, kind) for shape, kind in buffers(sizes).values()]
        found = pl.pallas_call(
            functools.partial(fused_layer, sizes),
            out_shape=list(middle),
            in_specs=specs,
            out_specs=[vmem] * len(middle),
            scratch_shapes=[
                *scratch,
                pltpu.SemaphoreType.DMA((SLOTS_MOST,)),
                pltpu.SemaphoreType.DMA((SLOTS_MOST,)),
                pltpu.SemaphoreType.DMA((6,)),
            ],
            compiler_params=pltpu.CompilerParams(
                collective_id=0, has_side_effects=True, vmem_limit_bytes=67043328
            ),
            name="fused_layer",
        )(
            tokens[0],
            lengths,
            w_qkv,
            w_out,
            w_uv,
            w_down,
            *gains,
            cotangent[0],
        )
        outs = pl.pallas_call(
            functools.partial(place_results, sizes),
            out_shape=shapes,
            in_specs=[vmem] * len(middle),
            out_specs=[vmem] * len(shapes),
            compiler_params=pltpu.CompilerParams(vmem_limit_bytes=67043328),
            name="place_results",
        )(*found)
        return (
            outs[0][None],
            outs[1][None],
            *outs[2:6],
            *(g.reshape(-1) for g in outs[6:]),
        )

    return run


def choose(parts, shards):
    def run(*args):
        tokens, w_qkv, w_down = args[0], args[2], args[5]
        rows, model = tokens.shape[1:]
        deep, width = w_down.shape[0], model // H
        fits = shards == 2 * parts and rows == TILE and w_qkv.shape[0] == TILE
        fits = fits and deep == parts * TILE and 2 * width == TILE and H == 4 * parts
        if not fits:
            return local(*args)
        return fused((parts, shards // 2, rows, model, deep, H // parts, width))(*args)

    return run


def solution(mesh):
    return jax.shard_map(
        choose(mesh.shape["seq"], mesh.shape["fsdp"]),
        mesh=mesh,
        in_specs=(
            P("fsdp", "seq", None),
            P("fsdp", None),
            P("fsdp", "seq"),
            P("fsdp", "seq"),
            P("fsdp", "seq"),
            P("fsdp", "seq"),
            P("fsdp"),
            P("fsdp"),
            P("fsdp"),
            P("fsdp"),
            P("fsdp"),
            P("fsdp", "seq", None),
        ),
        out_specs=(
            P("fsdp", "seq", None),
            P("fsdp", "seq", None),
            P("fsdp", "seq"),
            P("fsdp", "seq"),
            P("fsdp", "seq"),
            P("fsdp", "seq"),
            P("fsdp"),
            P("fsdp"),
            P("fsdp"),
            P("fsdp"),
            P("fsdp"),
        ),
        check_vma=False,
    )
```

```python
import functools
import math
import types
import typing

import jax
import jax.numpy as jnp
from jax import lax
from jax.experimental import pallas as pl
from jax.experimental.pallas import tpu as pltpu
from jax.sharding import PartitionSpec as P

H = 16


epsilon = 1e-06


def layout(lengths_row, slot):
    columns = lengths_row.shape[0]
    ends = jnp.cumsum(lengths_row)
    starts = ends - lengths_row
    before = (slot[:, None] >= ends[None, : columns - 1]).astype(jnp.int32)
    member = jnp.sum(before, axis=1)
    picked = member[:, None] == jnp.arange(columns, dtype=jnp.int32)[None, :]
    begin = jnp.sum(jnp.where(picked, starts[None, :], 0), axis=1)
    valid = member < columns - 1
    segment = jnp.where(valid, member, columns - 1 + slot)
    place = jnp.where(valid, slot - begin, 0)
    return (segment, place, valid)


def rotary(place, width):
    half = width // 2
    frequency = jnp.exp(jnp.arange(half, dtype=jnp.float32) * (-2.0 * math.log(10000.0) / width))
    angle = place.astype(jnp.float32)[:, None] * frequency[None, :]
    return (jnp.cos(angle)[:, None, :], jnp.sin(angle)[:, None, :])


def unit_rows(value):
    return value * lax.rsqrt(jnp.mean(value * value, axis=-1, keepdims=True) + epsilon)


def turn_heads(value, cosine, sine):
    half = value.shape[-1] // 2
    first = value[..., :half]
    second = value[..., half:]
    return jnp.concatenate(
        [first * cosine - second * sine, second * cosine + first * sine], axis=-1
    )


def prepare(query_raw, key_raw, s_qk, cosine, sine, heads):
    rows = query_raw.shape[0]
    scales = s_qk.reshape(heads, -1)

    def normed(raw):
        shaped = raw.reshape(rows, heads, -1)
        return (unit_rows(turn_heads(shaped, cosine, sine)) * scales).reshape(rows, -1)

    return (normed(query_raw), normed(key_raw))


def blend(base, branch, alpha):
    return unit_rows(base + alpha * (unit_rows(branch) - base))


def gated(up_gate, s_u, s_v):
    width = s_u.shape[0]
    return up_gate[:, :width] * s_u * jax.nn.silu(up_gate[:, width:] * s_v)


def rounded(value):
    return lax.optimization_barrier(value.astype(jnp.bfloat16)).astype(jnp.float32)


def attention_forward(query, key, value, mask):
    scale = 1.0 / math.sqrt(query.shape[2])
    score = jnp.einsum("thd,shd->hts", query, key, preferred_element_type=jnp.float32)
    score = jnp.where(mask[None], score * scale, -1e30)
    peak = jnp.max(score, axis=2, keepdims=True)
    raised = jnp.exp(score - peak)
    summed = jnp.sum(raised, axis=2, keepdims=True)
    weight = (raised / summed).astype(jnp.bfloat16)
    result = jnp.einsum("hts,shd->thd", weight, value, preferred_element_type=jnp.float32)
    return result, peak + jnp.log(summed)


def attention_backward(query, key, value, mask, log_total, grad):
    scale = 1.0 / math.sqrt(query.shape[2])
    score = jnp.einsum("thd,shd->hts", query, key, preferred_element_type=jnp.float32)
    score = jnp.where(mask[None], score * scale, -1e30)
    share = jnp.exp(score - log_total)
    grad_value = jnp.einsum(
        "hts,thd->shd", share.astype(jnp.bfloat16), grad, preferred_element_type=jnp.float32
    )
    grad_share = jnp.einsum("thd,shd->hts", grad, value, preferred_element_type=jnp.float32)
    inner = jnp.sum(share * grad_share, axis=2, keepdims=True)
    grad_score = (share * (grad_share - inner)).astype(jnp.bfloat16)
    grad_query = jnp.einsum("hts,shd->thd", grad_score, key, preferred_element_type=jnp.float32)
    grad_key = jnp.einsum("hts,thd->shd", grad_score, query, preferred_element_type=jnp.float32)
    return grad_query * scale, grad_key * scale, grad_value


def low(value):
    return value.astype(jnp.bfloat16)


def product(left, right, dims):
    return lax.dot_general(left, right, (dims, ((), ())), preferred_element_type=jnp.float32)


def local(tokens, lengths, w_qkv, w_out, w_uv, w_down, s_qk, alpha_a, s_u, s_v, alpha_m, cotangent):
    rows = tokens.shape[1]
    model = tokens.shape[2]
    width = model // H
    parts = lax.axis_size("seq")
    shards = lax.axis_size("fsdp")
    mine = lax.axis_index("seq")
    own = H // parts
    deep = w_down.shape[0]
    hidden_all = deep * shards
    hidden_own = hidden_all // parts
    piece = deep // parts
    slot = mine * rows + jnp.arange(rows, dtype=jnp.int32)
    every_slot = jnp.arange(rows * parts, dtype=jnp.int32)
    keep = layout(lengths[0], slot)[2].astype(jnp.float32)[:, None]
    segment, place, _ = layout(lengths[0], every_slot)
    mask = (segment[:, None] == segment[None, :]) & (every_slot[:, None] >= every_slot[None, :])

    def exchange(array, axis):
        return lax.all_to_all(array, "seq", axis, axis, tiled=False)

    def gather(array, axis=0):
        return lax.all_gather(array, "fsdp", axis=axis, tiled=True)

    def spread(array):
        return lax.all_gather(array, "seq", axis=0, tiled=True)

    r_in = w_qkv.shape[0]
    share_qkv = lax.all_to_all(
        w_qkv.reshape(r_in, -1, parts, width), "seq", 2, 1, tiled=True
    ).reshape(r_in, -1)
    share_uv = lax.all_to_all(
        w_uv.reshape(r_in, -1, parts, piece), "seq", 2, 1, tiled=True
    ).reshape(r_in, -1)
    share_down = lax.all_to_all(w_down.reshape(parts, piece, -1), "seq", 0, 2, tiled=True)
    share_down = share_down.reshape(piece, model)
    share_out = lax.all_gather(w_out, "seq", axis=1, tiled=True)
    inputs = spread(tokens[0])
    full_qkv = gather(share_qkv)
    full_out = gather(share_out).reshape(own, parts, width, model)
    full_out = lax.dynamic_index_in_dim(full_out, mine, 1, False).reshape(own * width, model)
    full_uv = gather(share_uv)
    full_down = gather(share_down)
    gains = gather(jnp.concatenate([s_qk, alpha_a, s_u, s_v, alpha_m])[None]).astype(jnp.float32)
    cuts = [s_qk.shape[0], alpha_a.shape[0], s_u.shape[0], s_v.shape[0]]
    edges = [sum(cuts[: i + 1]) for i in range(4)]
    gain_qk, gain_a, gain_u, gain_v, gain_m = jnp.split(gains, edges, axis=1)
    gain_qk = gain_qk.reshape(own, parts, width)
    gain_qk = lax.dynamic_index_in_dim(gain_qk, mine, 1, False).reshape(-1)
    gain_a, gain_m = gain_a.reshape(-1), gain_m.reshape(-1)
    gain_u = lax.dynamic_index_in_dim(gain_u.reshape(shards, parts, piece), mine, 1, False).reshape(-1)
    gain_v = lax.dynamic_index_in_dim(gain_v.reshape(shards, parts, piece), mine, 1, False).reshape(-1)

    mixed = product(inputs, full_qkv, ((1,), (0,)))
    cosine, sine = rotary(place, width)
    span = own * width

    def prepare_local(query_raw, key_raw, scale_qk):
        return prepare(query_raw, key_raw, scale_qk, cosine, sine, own)

    (query_f, key_f), pull_prepare = jax.vjp(
        prepare_local, mixed[:, :span], mixed[:, span : 2 * span], gain_qk
    )
    heads = (rows * parts, own, width)
    query, key = low(query_f).reshape(heads), low(key_f).reshape(heads)
    value = low(mixed[:, 2 * span :]).reshape(heads)
    attended, log_total = attention_forward(query, key, value, mask)
    attended = low(attended.reshape(-1, span))

    def reduce_rows(array):
        return lax.psum_scatter(low(array), "seq", scatter_dimension=0, tiled=True).astype(
            jnp.float32
        )

    branch = reduce_rows(product(attended, full_out, ((1,), (0,))))
    first, pull_first = jax.vjp(blend, tokens[0].astype(jnp.float32), branch, gain_a)
    first_all = spread(low(first))
    up_gate = product(first_all, full_uv, ((1,), (0,)))
    hidden_f, pull_gate = jax.vjp(gated, up_gate, gain_u, gain_v)
    hidden = low(hidden_f)
    down = reduce_rows(product(hidden, full_down, ((1,), (0,))))
    final, pull_last = jax.vjp(blend, first, down, gain_m)
    output = low(final * keep)
    grad_first, grad_down, grad_gain_m = pull_last(cotangent[0].astype(jnp.float32) * keep)
    grad_down = spread(low(grad_down))
    grad_w_down = low(product(hidden, grad_down, ((0,), (0,))))
    grad_hidden = rounded(product(grad_down, full_down, ((1,), (1,))))
    grad_up_gate, grad_gain_u, grad_gain_v = pull_gate(grad_hidden)
    grad_up = low(grad_up_gate)
    grad_w_uv = low(product(first_all, grad_up, ((0,), (0,))))
    grad_first = grad_first + reduce_rows(product(grad_up, full_uv, ((1,), (1,))))
    grad_inputs, grad_branch, grad_gain_a = pull_first(grad_first)
    grad_branch = spread(low(grad_branch))
    grad_w_out = low(product(attended, grad_branch, ((0,), (0,))))
    grad_attended = low(product(grad_branch, full_out, ((1,), (1,)))).reshape(heads)
    grad_query, grad_key, grad_value = attention_backward(
        query, key, value, mask, log_total, grad_attended
    )
    grad_query_raw, grad_key_raw, grad_gain_qk = pull_prepare(
        (rounded(grad_query).reshape(-1, span), rounded(grad_key).reshape(-1, span))
    )
    grad_mixed = low(
        jnp.concatenate([grad_query_raw, grad_key_raw, grad_value.reshape(-1, span)], axis=1)
    )
    grad_w_qkv = low(product(inputs, grad_mixed, ((0,), (0,))))
    grad_inputs = grad_inputs + reduce_rows(product(grad_mixed, full_qkv, ((1,), (1,))))

    def collect(array):
        return lax.psum_scatter(array, "fsdp", scatter_dimension=0, tiled=True)

    part_down = collect(grad_w_down)
    out_down = lax.all_to_all(
        part_down.reshape(1, piece, model), "seq", 2, 0, tiled=True
    ).reshape(deep, -1)
    part_uv = collect(grad_w_uv)
    out_uv = lax.all_to_all(
        part_uv.reshape(r_in, -1, 1, piece), "seq", 1, 2, tiled=True
    ).reshape(r_in, -1)
    placed = jnp.zeros((own, parts, width, model), jnp.bfloat16)
    placed = lax.dynamic_update_slice(
        placed, grad_w_out.reshape(own, 1, width, model), (0, mine, 0, 0)
    )
    part_out = collect(placed.reshape(-1, model))
    out_out = lax.psum_scatter(part_out, "seq", scatter_dimension=1, tiled=True)
    part_qkv = collect(grad_w_qkv)
    out_qkv = lax.all_to_all(
        part_qkv.reshape(r_in, -1, 1, width), "seq", 1, 2, tiled=True
    ).reshape(r_in, -1)

    def widen(array, outer, inner):
        blank = jnp.zeros((outer, parts, inner), jnp.float32)
        array = array.reshape(outer, 1, inner)
        return lax.dynamic_update_slice(blank, array, (0, mine, 0)).reshape(shards, -1)

    gain_sums = jnp.concatenate(
        [
            widen(grad_gain_qk, own, width),
            grad_gain_a.reshape(shards, -1),
            widen(grad_gain_u, shards, piece),
            widen(grad_gain_v, shards, piece),
            grad_gain_m.reshape(shards, -1),
        ],
        axis=1,
    )
    gain_sums = lax.psum(collect(gain_sums), "seq")[0]
    outs = jnp.split(gain_sums, edges)
    return (
        output[None],
        grad_inputs[None],
        out_qkv.astype(jnp.float32),
        out_out.astype(jnp.float32),
        out_uv.astype(jnp.float32),
        out_down.astype(jnp.float32),
        outs[0],
        outs[1],
        outs[2],
        outs[3],
        outs[4],
    )


MESH = pl.DeviceIdType.MESH
TILE = 128
QROWS = 128


def loop(count, body):
    def run(index, carry):
        body(index)
        return carry

    lax.fori_loop(0, count, run, 0)


def at_rows(ref, block, size=TILE):
    return ref.at[pl.ds(pl.multiple_of(block * size, size), size), :]


def cols(block, size=TILE):
    return pl.ds(pl.multiple_of(block * size, size), size)


def mean_last(value):
    return jnp.sum(value, axis=-1, keepdims=True) * (1.0 / value.shape[-1])


class Slots:
    def __init__(self):
        self.count = 0

    def take(self, count):
        base = self.count
        self.count = base + count
        return base


def fused_layer(sizes, *refs):
    (parts, lines, rows, model, deep, own_heads, width) = sizes
    slots_all = parts * rows
    span = own_heads * width
    hid = deep * lines * 2 // parts
    count_in, count_out = len(Inputs._fields), len(Results._fields)
    ins = Inputs(*refs[:count_in])
    outs = Results(*refs[count_in : count_in + count_out])
    table = buffers(sizes)
    rest = refs[count_in + count_out :]
    v = types.SimpleNamespace(**dict(zip(table, rest[: len(table)])))
    send_sem, recv_sem, local_sem = rest[len(table) :]

    s = lax.axis_index("seq")
    f = lax.axis_index("fsdp")
    z = f // 2
    c = f % 2
    other = 1 - c
    mate = (s, 2 * z + other)
    slots = Slots()

    def put(src, dst, target, send_slot, recv_slot):
        pltpu.make_async_remote_copy(
            src_ref=src,
            dst_ref=dst,
            send_sem=send_sem.at[send_slot],
            recv_sem=recv_sem.at[recv_slot],
            device_id=target,
            device_id_type=MESH,
        ).start()

    def descriptor(ref, send_slot, recv_slot):
        return pltpu.make_async_remote_copy(
            src_ref=ref,
            dst_ref=ref,
            send_sem=send_sem.at[send_slot],
            recv_sem=recv_sem.at[recv_slot],
            device_id=mate,
            device_id_type=MESH,
        )

    def landed(ref, slot):
        descriptor(ref, 0, slot).wait_recv()

    def plane(distance):
        return (s + distance) % parts

    def plane_from(distance):
        return (s + parts - distance) % parts

    def line(distance):
        return (z + distance) % lines

    def line_from(distance):
        return (z + lines - distance) % lines

    barrier = pltpu.get_barrier_semaphore()
    for distance in range(1, parts):
        pl.semaphore_signal(barrier, inc=1, device_id=(plane(distance), f), device_id_type=MESH)
    for distance in range(1, 2 * lines):
        target = (s, (f + distance) % (2 * lines))
        pl.semaphore_signal(barrier, inc=1, device_id=target, device_id_type=MESH)

    edges = [0, TILE, 2 * TILE, 2 * TILE + deep, 2 * TILE + 2 * deep, 3 * TILE + 2 * deep]
    own_gains = (ins.s_qk, ins.alpha_a, ins.s_u, ins.s_v, ins.alpha_m)
    for place, own_gain in enumerate(own_gains):
        row = own_gain[...].astype(jnp.float32).reshape(1, -1)
        v.gain_all[f, :, edges[place] : edges[place + 1]] = row
    own_row = pl.ds(pl.multiple_of(s * rows, rows), rows)
    own_w = pl.ds(pl.multiple_of(f * TILE, TILE), TILE)
    part_cols = model // parts
    blocks_uv = 2 * hid // parts // TILE
    wide = blocks_uv * TILE

    def fetch(src, dst, slot):
        pltpu.make_async_copy(src, dst, local_sem.at[slot]).start()

    def deliver(index):
        made = (
            v.made_output,
            v.made_input_grad,
            v.made_back_qkv,
            v.made_back_out,
            v.made_back_uv,
            v.made_back_down,
            v.made_gains,
        )
        return pltpu.make_async_copy(made[index], outs[index], local_sem.at[6 + index])

    def fetched(dst, slot):
        pltpu.make_async_copy(dst, dst, local_sem.at[slot]).wait()

    fetch(ins.w_out, v.wz.at[own_w, :], 0)
    fetch(ins.tokens, v.x_all.at[own_row, :], 1)
    for index in range(blocks_uv):
        fetch(
            ins.w_uv.at[:, pl.ds(pl.multiple_of((index * parts + s) * TILE, TILE), TILE)],
            v.wu.at[own_w, pl.ds(pl.multiple_of(s * wide + index * TILE, TILE), TILE)],
            2,
        )
    fetch(ins.w_down.at[cols(s), :], v.wd.at[own_w, cols(s, part_cols)], 3)
    fetch(ins.cotangent, v.cotangent, 4)
    for index in range(3):
        chunk = 3 * s + index

        @pl.when(chunk % parts == s)
        def _():
            fetch(
                ins.w_qkv.at[:, index * span : (index + 1) * span],
                v.wq.at[own_w, cols(chunk // parts, span)],
                5,
            )

    pl.semaphore_wait(barrier, parts - 1 + 2 * lines - 1)

    qkv_slot = slots.take(1)
    for index in range(3):
        chunk = 3 * s + index
        block = chunk // parts
        target = chunk % parts

        @pl.when(target != s)
        def _():
            put(
                ins.w_qkv.at[:, index * span : (index + 1) * span],
                v.wq.at[own_w, cols(block, span)],
                (target, f),
                BY_PLANE,
                qkv_slot,
            )


    side, across, opposite = s + 1 - 2 * (s % 2), (s + 2) % parts, parts - 1 - s

    def half_of(shared, owner, part):
        start = owner * rows + part * (rows // 2)
        return shared.at[pl.ds(pl.multiple_of(start, rows // 2), rows // 2), :]

    token_slot = slots.take(SHARE)
    for part in range(2):
        mine = ins.tokens.at[part * (rows // 2) : (part + 1) * (rows // 2), :]
        there = half_of(v.x_all, s, part)
        put(mine, there, (side, f), BY_SHARE, token_slot + 2 * part)
        put(mine, there, (across, f), BY_SHARE, token_slot + 2 - part)

    uv_slot = slots.take(1)
    for distance in range(1, parts):
        target = plane(distance)
        for index in range(blocks_uv):
            put(
                ins.w_uv.at[:, pl.ds(pl.multiple_of((index * parts + target) * TILE, TILE), TILE)],
                v.wu.at[own_w, pl.ds(pl.multiple_of(s * wide + index * TILE, TILE), TILE)],
                (target, f),
                BY_PLANE,
                uv_slot,
            )

    down_slot = slots.take(1)
    for distance in range(1, parts):
        target = plane(distance)
        put(
            ins.w_down.at[cols(target), :],
            v.wd.at[own_w, cols(s, part_cols)],
            (target, f),
            BY_PLANE,
            down_slot,
        )

    gain_slot = slots.take(1)
    for distance in range(1, 2 * lines):
        put(
            v.gain_all.at[f],
            v.gain_all.at[f],
            (s, (f + distance) % (2 * lines)),
            BY_GAIN,
            gain_slot,
        )

    def plane_share_relay(shared, base, passed=None):
        one, two = half_of(shared, side, 0), half_of(shared, across, 1)
        if passed is not None:
            passed(s, 0)
            passed(s, 1)
        landed(one, base)
        put(one, one, (across, f), BY_SHARE, base + 3)
        landed(two, base + 1)
        put(two, two, (side, f), BY_SHARE, base + 3)
        if passed is not None:
            passed(side, 0)
            passed(across, 1)

    def plane_share_wait(shared, base, passed=None):
        for pieces, slot in (
            (((side, 1), (across, 0)), base + 2),
            (((opposite, 0), (opposite, 1)), base + 3),
        ):
            landed(at_rows(shared, opposite, rows), slot)
            if passed is not None:
                for piece_of in pieces:
                    passed(*piece_of)

    def pass_to_mate(shared, slot):
        def passed(owner, part):
            start = owner * rows + part * (rows // 2)
            here = pl.ds(pl.multiple_of(start, rows // 2), rows // 2)
            there = pl.ds(pl.multiple_of(slots_all + start, rows // 2), rows // 2)
            put(shared.at[here, :], shared.at[there, :], mate, BY_MATE_B, slot)

        return passed

    def shard(ref, chip, core, lanes):
        block = 2 * chip + core
        return ref.at[pl.ds(pl.multiple_of(block * TILE, TILE), TILE), lanes]

    inner = z * (lines - 1 - z) > 0
    outer = z * (lines - 1 - z) == 0

    def line_send(ref, base, lanes=slice(None), twice=True, apart=False):
        own = shard(ref, z, c, lanes)
        for distance in (2, 1, 3):
            target = line(distance)
            near = (z - target) * (z - target) < (lines - 1) * (lines - 1)
            slot = base
            if apart:
                slot = base + distance - 1
            elif distance == 2:
                slot = base + target * (lines - 1 - target) // 2

            @pl.when(near)
            def _():
                put(own, own, (s, 2 * target + c), BY_LINE, slot)

        if twice:
            put(own, own, mate, mate_group(ref), base + 2 + apart)

    def mate_group(ref):
        return BY_WIDE if ref is v.wu else BY_MATE_B if ref is v.wd else BY_MATE_C

    def line_relay(ref, base, lanes=slice(None), apart=False):
        block = shard(ref, line_from(2), c, lanes)

        @pl.when(inner)
        def _():
            landed(block, base + 1)
            slot = base + 2 * z - 2 if apart else base
            put(block, block, (s, 2 * (lines - 1) * (z - 1) + c), BY_LINE, slot)

    def line_arrived(ref, base, lanes=slice(None)):
        pl.when(inner)(lambda: landed(ref.at[: 2 * TILE, lanes], base))
        pl.when(outer)(lambda: landed(ref.at[: 3 * TILE, lanes], base))

    def line_forward(ref, base, lanes=slice(None), apart=False):
        if not apart:
            line_arrived(ref, base, lanes)
        for distance in (1, 3, 2):
            block = shard(ref, line_from(distance), c, lanes)
            if apart and distance == 2:

                @pl.when(outer)
                def _():
                    landed(block, base + 1)

            elif apart:
                landed(block, base + distance - 1)
            put(block, block, mate, mate_group(ref), base + 2 + apart)

    def mate_wait(ref, base, lanes=slice(None), apart=False):
        landed(ref.at[: lines * TILE, lanes], base + 2 + apart)

    wq_slot, wu_slot = (slots.take(4) for _ in range(2))
    count = 4
    piece = model // count
    wd_parts = [
        (slots.take(3), slice(part * piece, (part + 1) * piece)) for part in range(count)
    ]
    wz_slot, wo_slot, out_slot = slots.take(2), slots.take(1), slots.take(1)
    fetched(v.wz.at[own_w, :], 0)
    line_send(v.wz, wz_slot, twice=False)

    landed(v.wq.at[own_w, : 2 * span], qkv_slot)
    fetched(v.wq.at[own_w, :span], 5)
    line_send(v.wq, wq_slot, apart=True)
    lengths = [ins.lengths[0, i] for i in range(ins.lengths.shape[1])]

    def slot_facts(slot):
        end = 0
        member = jnp.zeros(slot.shape, jnp.int32)
        begin = jnp.zeros(slot.shape, jnp.int32)
        for length in lengths[:-1]:
            end = end + length
            after = slot >= end
            member = member + after.astype(jnp.int32)
            begin = jnp.where(after, end, begin)
        valid = member < len(lengths) - 1
        segment = jnp.where(valid, member, len(lengths) - 1 + slot)
        place = jnp.where(valid, slot - begin, 0)
        return segment, place, valid

    lane = lax.broadcasted_iota(jnp.int32, (1, TILE), 1)
    low_half = lane < width
    first_quarter = lane % width < width // 2
    frequency = jnp.exp(
        (lane % (width // 2)).astype(jnp.float32) * (-2.0 * math.log(10000.0) / width)
    )
    turn_sign = jnp.where(first_quarter, -1.0, 1.0)

    def tables(block):
        here = pl.ds(pl.multiple_of(block * TILE, TILE), TILE)
        slot = block * TILE + lax.broadcasted_iota(jnp.int32, (TILE, 1), 0)
        segment, place, _ = slot_facts(slot)
        angle = place.astype(jnp.float32) * frequency
        v.cosine[here, :] = jnp.cos(angle)
        v.sine[here, :] = jnp.sin(angle) * turn_sign
        key_slot = lax.broadcasted_iota(jnp.int32, (1, slots_all), 1)
        key_segment = slot_facts(key_slot)[0]
        kept = (segment == key_segment) & (slot >= key_slot)
        v.bias[here, :] = jnp.where(kept, 0.0, -1e30)

    loop(slots_all // TILE, tables)
    line_relay(v.wz, wz_slot)
    line_relay(v.wq, wq_slot, apart=True)
    fetched(v.x_all.at[own_row, :], 1)
    plane_share_relay(v.x_all, token_slot)
    plane_share_wait(v.x_all, token_slot)
    line_arrived(v.wz, wz_slot)
    for distance in range(1, parts):
        target = plane(distance)
        rows_out = at_rows(v.wz, 2 * target + c)
        put(
            rows_out,
            v.wo.at[cols(c), cols(s, part_cols)],
            (target, f),
            BY_PLANE,
            out_slot,
        )
    v.wo[cols(c), cols(s, part_cols)] = v.wz[cols(2 * s + c), :]
    fetched(v.wu.at[own_w, cols(s, wide)], 2)
    landed(v.wu.at[own_w, : (parts - 1) * wide], uv_slot)
    line_send(v.wu, wu_slot, apart=True)

    def mate_blocks(name_all, ref, stage, slot):
        for block in range(lines):
            here = slice(block * TILE, (block + 1) * TILE)
            stage[here, :] = name_all[:, cols(2 * block + other)].T
        put(stage, ref.at[:, slots_all:], mate, BY_MATE_C, slot)
        for block in range(lines):
            here = slice(block * TILE, (block + 1) * TILE)
            ref[here, :slots_all] = name_all[:, cols(2 * block + c)].T

    mate_x_slot = slots.take(1)
    mate_blocks(v.x_all, v.turned_x, v.stage_x, mate_x_slot)
    landed(v.gain_all.at[1:], gain_slot)

    def gain(block, offset):
        return v.gain_all[block, :, pl.ds(pl.multiple_of(offset, TILE), TILE)]

    for block in range(2 * lines):
        here = slice(block * TILE, (block + 1) * TILE)
        v.gain_a[:, here] = gain(block, edges[1])
        v.gain_u[:, here] = gain(block, edges[2] + s * TILE)
        v.gain_v[:, here] = gain(block, edges[3] + s * TILE)
        v.gain_m[:, here] = gain(block, edges[4])
    for block in range(span // TILE):
        v.gain_qk[:, block * TILE : (block + 1) * TILE] = gain(span // TILE * s + block, 0)

    line_forward(v.wq, wq_slot, apart=True)
    mate_wait(v.wq, wq_slot, apart=True)

    def mix(index):
        v.raw[:, cols(index, span)] = product(
            v.x_all[...], v.wq[:, cols(index, span)], ((1,), (0,))
        )

    loop(3, mix)

    def swap(value):
        return jnp.where(
            first_quarter,
            pltpu.roll(value, TILE - width // 2, 1),
            pltpu.roll(value, width // 2, 1),
        )

    def head_mean(value):
        one = jnp.sum(jnp.where(low_half, value, 0.0), axis=-1, keepdims=True)
        two = jnp.sum(jnp.where(low_half, 0.0, value), axis=-1, keepdims=True)
        return jnp.where(low_half, one, two) * (1.0 / width)

    pairs = span // TILE
    blocks = slots_all // TILE

    def prepare_block(index):
        here = pl.ds(pl.multiple_of(index % blocks * TILE, TILE), TILE)
        group = index // blocks
        there = cols(group)
        value = v.raw[here, there]
        turned = value * v.cosine[here, :] + swap(value) * v.sine[here, :]
        inverse = lax.rsqrt(head_mean(turned * turned) + epsilon)
        normed = turned * inverse
        v.normed[here, there] = normed
        v.inverse[here, there] = inverse
        v.qkv[here, there] = low(normed * v.gain_qk[:, cols(group % pairs)])

    loop(2 * pairs * blocks, prepare_block)

    def keep_value(index):
        here = pl.ds(pl.multiple_of(index * TILE, TILE), TILE)
        v.qkv[here, 2 * span :] = low(v.raw[here, 2 * span :])

    loop(blocks, keep_value)
    own_out = v.wo.at[cols(c), :]
    landed(v.wo.at[cols(c), : (parts - 1) * part_cols], out_slot)
    put(own_out, own_out, mate, BY_MATE_D, wo_slot)

    scale = 1.0 / math.sqrt(width)
    halves = (low_half, jnp.logical_not(low_half))

    def attend(pair):
        q_cols, k_cols, v_cols = cols(pair), cols(pairs + pair), cols(2 * pairs + pair)
        for block in range(blocks):
            here = slice(block * TILE, (block + 1) * TILE)
            seen = slice(0, (block + 1) * TILE)
            results = []
            for half in range(2):
                query = jnp.where(halves[half], v.qkv[here, q_cols], 0.0).astype(jnp.bfloat16)
                score = product(query, v.qkv[seen, k_cols], ((1,), (1,))) * scale
                score = score + v.bias[here, seen]
                peak = jnp.max(score, axis=1, keepdims=True)
                raised = jnp.exp(score - peak)
                summed = jnp.sum(raised, axis=1, keepdims=True)
                weight = low(raised / summed)
                results.append(product(weight, v.qkv[seen, v_cols], ((1,), (0,))))
                v.total[2 * pair + half, here, :] = peak + jnp.log(summed)
            v.attended[here, q_cols] = low(jnp.where(low_half, results[0], results[1]))

    loop(pairs, attend)
    mate_att_slot = slots.take(1)
    v.stage_att[...] = v.attended[:, cols(other)].T
    v.turned_att[:, :slots_all] = v.attended[:, cols(c)].T

    put(v.stage_att, v.turned_att.at[:, slots_all:], mate, BY_MATE_D, mate_att_slot)
    landed(v.wo.at[cols(other), :], wo_slot)

    def plane_sum(sums, arrived, base, tile, span_of=(0, count)):
        start, stop = span_of

        def send(index):
            there = cols(index, piece)
            for distance in range(1, parts):
                target = plane(distance)
                put(
                    sums.at[pl.ds(pl.multiple_of(target * rows, rows), rows), there],
                    arrived.at[distance - 1, :, there],
                    (target, f),
                    BY_SUM,
                    base,
                )

        def step(index):
            sums[:, cols(start + index, piece)] = low(tile(start + index))

            @pl.when(index > 0)
            def _():
                send(start + index - 1)

        loop(stop - start, step)
        send(stop - 1)

    def plane_sum_wait(arrived, base):
        landed(arrived, base)

    def plane_total(sums, arrived, here, at):
        total = sums[here, :].astype(jnp.float32)
        for distance in range(1, parts):
            total = total + arrived[distance - 1, at, :].astype(jnp.float32)
        return total

    chunk_rows = 32

    def chunk(index):
        at = pl.ds(pl.multiple_of(index * chunk_rows, chunk_rows), chunk_rows)
        here = pl.ds(pl.multiple_of(s * rows + index * chunk_rows, chunk_rows), chunk_rows)
        return at, here

    def plane_share(shared, base, make):
        def send(index):
            own = shared.at[chunk(index)[1], :]
            part = index // (rows // chunk_rows // 2)
            put(own, own, (side, f), BY_SHARE, base + 2 * part)
            put(own, own, (across, f), BY_SHARE, base + 2 - part)

        def step(index):
            make(index)

            @pl.when(index > 0)
            def _():
                send(index - 1)

        loop(rows // chunk_rows, step)
        send(rows // chunk_rows - 1)

    branch_slot = slots.take(1)
    plane_sum(
        v.part_branch,
        v.got_branch,
        branch_slot,
        lambda index: product(v.attended[...], v.wo[:, cols(index, piece)], ((1,), (0,))),
    )
    line_relay(v.wu, wu_slot, apart=True)
    fetched(v.wd.at[own_w, cols(s, part_cols)], 3)
    landed(v.wd.at[own_w, : (parts - 1) * part_cols], down_slot)
    line_send(v.wd, *wd_parts[0])
    line_send(v.wd, *wd_parts[1])
    plane_sum_wait(v.got_branch, branch_slot)
    line_relay(v.wd, *wd_parts[0])
    line_send(v.wd, *wd_parts[2])

    def blended(base, branch, alpha):
        inverse_branch = lax.rsqrt(mean_last(branch * branch) + epsilon)
        normed = branch * inverse_branch
        mixed = base + alpha * (normed - base)
        inverse = lax.rsqrt(mean_last(mixed * mixed) + epsilon)
        return normed, inverse_branch, mixed * inverse, inverse

    def blended_back(grad, base, alpha, normed, inverse_branch, result, inverse):
        grad_mixed = inverse * (grad - result * mean_last(grad * result))
        grad_normed = alpha * grad_mixed
        grad_branch = inverse_branch * (grad_normed - normed * mean_last(grad_normed * normed))
        grad_alpha = jnp.sum(grad_mixed * (normed - base), axis=0, keepdims=True)
        return grad_mixed - grad_normed, grad_branch, grad_alpha

    def make_first(index):
        at, here = chunk(index)
        base = v.x_all[here, :].astype(jnp.float32)
        normed, inverse_branch, result, inverse = blended(
            base, plane_total(v.part_branch, v.got_branch, here, at), v.gain_a[...]
        )
        v.branch_normed[at, :] = normed
        v.branch_inverse[at, :] = inverse_branch
        v.first[at, :] = result
        v.first_inverse[at, :] = inverse
        v.first_all[here, :] = low(result)

    first_slot = slots.take(SHARE)
    plane_share(v.first_all, first_slot, make_first)
    line_relay(v.wd, *wd_parts[1])
    line_send(v.wd, *wd_parts[3])
    plane_share_relay(v.first_all, first_slot)
    line_relay(v.wd, *wd_parts[2])
    line_forward(v.wu, wu_slot, apart=True)
    mate_wait(v.wu, wu_slot, apart=True)
    plane_share_wait(v.first_all, first_slot)

    def gate_tile(index):
        there = cols(index, 256)
        v.up[:, there] = product(v.first_all[...], v.wu[:, there], ((1,), (0,)))
        v.gate[:, there] = product(
            v.first_all[...],
            v.wu[:, pl.ds(pl.multiple_of(hid + index * 256, 256), 256)],
            ((1,), (0,)),
        )

        def rows_of(block):
            here = pl.ds(pl.multiple_of(block * 64, 64), 64)
            scaled = v.gate[here, there] * v.gain_v[:, there]
            passed = scaled / (1.0 + jnp.exp(-scaled))
            v.hidden[here, there] = low(v.up[here, there] * v.gain_u[:, there] * passed)

        loop(slots_all // 64, rows_of)

    line_relay(v.wd, *wd_parts[3])
    loop(hid // 512, gate_tile)
    line_forward(v.wd, *wd_parts[0])
    loop(hid // 512, lambda index: gate_tile(hid // 512 + index))
    mate_hidden_slot = slots.take(1)
    mate_blocks(v.hidden, v.turned_hidden, v.stage_hidden, mate_hidden_slot)
    mate_first_slot = slots.take(1)
    mate_blocks(v.first_all, v.turned_first, v.stage_first, mate_first_slot)
    down_sum_slot = slots.take(1)

    def down_tile(index):
        return product(v.hidden[...], v.wd[:, cols(index, piece)], ((1,), (0,)))

    line_forward(v.wd, *wd_parts[1])
    for part in range(count):
        mate_wait(v.wd, *wd_parts[part])
        plane_sum(v.part_down, v.got_down, down_sum_slot, down_tile, (part, part + 1))
        if part + 2 < count:
            line_forward(v.wd, *wd_parts[part + 2])
    fetched(v.cotangent, 4)
    plane_sum_wait(v.got_down, down_sum_slot)
    v.grad_a[...] = jnp.zeros_like(v.grad_a)
    v.grad_m[...] = jnp.zeros_like(v.grad_m)

    def finish(index):
        at, here = chunk(index)
        slot = s * rows + index * chunk_rows
        slot = slot + lax.broadcasted_iota(jnp.int32, (chunk_rows, 1), 0)
        keep = slot_facts(slot)[2].astype(jnp.float32)
        base = v.first[at, :]
        alpha = v.gain_m[...]
        normed, inverse_branch, result, inverse = blended(
            base, plane_total(v.part_down, v.got_down, here, at), alpha
        )
        v.made_output[at, :] = low(result * keep)
        grad = v.cotangent[at, :].astype(jnp.float32) * keep
        grad_base, grad_down, grad_alpha = blended_back(
            grad, base, alpha, normed, inverse_branch, result, inverse
        )
        v.grad_first[at, :] = grad_base
        v.gd[here, :] = low(grad_down)
        v.grad_m[...] += grad_alpha

    gd_slot = slots.take(SHARE)
    plane_share(v.gd, gd_slot, finish)
    deliver(0).start()
    mate_gd_slot = slots.take(1)
    passed_gd = pass_to_mate(v.gd, mate_gd_slot)
    plane_share_relay(v.gd, gd_slot, passed_gd)
    plane_share_wait(v.gd, gd_slot, passed_gd)
    first_half = slice(0, slots_all)
    second_half = slice(slots_all, 2 * slots_all)

    ends = (lines - 1) * (1 - z % 2)
    mids = 2 - z // 2
    last = (2 * z + 1) % (lines + 1)
    beside = z + 1 - 2 * (z % 2)

    mid_slot = 2 - z * (lines - 1 - z) // 2

    def line_grad_first(grads, arrived, base, there):
        put(
            grads.at[ends, :, there],
            arrived.at[0, :, there],
            (s, 2 * beside + c),
            BY_GRAD,
            base + 1 - beside * (lines - 1 - beside) // 2,
        )

    def line_grad_mid(grads, arrived, base, there):
        put(
            grads.at[mids, :, there],
            arrived.at[mid_slot, :, there],
            (s, 2 * mids + c),
            BY_GRAD,
            base + 1,
        )

    def line_grad_rest(grads, arrived, base):
        @pl.when(outer)
        def _():
            line_grad_mid(grads, arrived, base, slice(None))
            put(grads.at[last], arrived.at[3], (s, 2 * last + c), BY_GRAD, base + 1)


    def weight_grad(turned, right, grads, arrived, columns, base, lag=1):
        def send(index):
            line_grad_first(grads, arrived, base, cols(index, 256))

            @pl.when(inner)
            def _():
                line_grad_mid(grads, arrived, base, cols(index, 256))

        def step(index):
            there = cols(index, 256)
            total = product(turned[...], right[:, there], ((1,), (0,)))
            grads[:, :, there] = low(total).reshape(lines, TILE, 256)

            if lag == 0:
                send(index)
            else:
                pl.when(index > 0)(lambda: send(index - 1))

        loop(columns // 256, step)
        if lag:
            send(columns // 256 - 1)
        line_grad_rest(grads, arrived, base)

    def weight_combine(grads, arrived, columns, base):
        @pl.when(inner)
        def _():
            landed(arrived.at[0], base)

            def tile(index):
                there = cols(index, 256)
                total = grads[last, :, there].astype(jnp.float32)
                grads[last, :, there] = low(total + arrived[0, :, there].astype(jnp.float32))

            loop(columns // 256, tile)
            put(
                grads.at[last], arrived.at[1], (s, 2 * last + c), BY_GRAD, base + 1)

    def gate_back(index):
        there = cols(index, 256)
        there_gate = pl.ds(pl.multiple_of(hid + index * 256, 256), 256)
        v.grad_hidden[...] = low(product(v.gd[first_half, :], v.wd[there, :], ((1,), (1,))))
        v.grad_u[:, there] = jnp.zeros((1, 256), jnp.float32)
        v.grad_v[:, there] = jnp.zeros((1, 256), jnp.float32)

        def rows_of(block):
            here = pl.ds(pl.multiple_of(block * 64, 64), 64)
            grad = v.grad_hidden[here, :].astype(jnp.float32)
            up = v.up[here, there]
            gate = v.gate[here, there]
            gain_u = v.gain_u[:, there]
            gain_v = v.gain_v[:, there]
            scaled = gate * gain_v
            squash = 1.0 / (1.0 + jnp.exp(-scaled))
            passed = scaled * squash
            grad_scaled_up = grad * passed
            grad_scaled = grad * (up * gain_u) * (squash + passed * (1.0 - squash))
            v.gu[here, there] = low(grad_scaled_up * gain_u)
            v.gu[here, there_gate] = low(grad_scaled * gain_v)
            v.grad_u[:, there] += jnp.sum(grad_scaled_up * up, axis=0, keepdims=True)
            v.grad_v[:, there] += jnp.sum(grad_scaled * gate, axis=0, keepdims=True)

        loop(slots_all // 64, rows_of)

    loop(1, gate_back)
    landed(v.turned_x.at[:, second_half], mate_x_slot)
    landed(v.turned_first.at[:, second_half], mate_first_slot)
    landed(v.turned_hidden.at[:, second_half], mate_hidden_slot)
    landed(v.gd.at[second_half, :], mate_gd_slot)
    line_down_slot = slots.take(2)
    weight_grad(v.turned_hidden, v.gd, v.send_down, v.line_down, model, line_down_slot, 0)
    loop(hid // 256 - 1, lambda index: gate_back(index + 1))
    mate_gu_slot = slots.take(1)
    put(v.gu.at[first_half, :], v.gu.at[second_half, :], mate, BY_WIDE, mate_gu_slot)
    first_sum_slot = slots.take(1)
    plane_sum(
        v.part_first,
        v.got_first,
        first_sum_slot,
        lambda index: product(v.gu[first_half, :], v.wu[cols(index, piece), :], ((1,), (1,))),
    )
    weight_combine(v.send_down, v.line_down, model, line_down_slot)
    landed(v.gu.at[second_half, :], mate_gu_slot)
    line_uv_slot = slots.take(2)
    weight_grad(v.turned_first, v.gu, v.send_uv, v.line_uv, 2 * hid, line_uv_slot)
    plane_sum_wait(v.got_first, first_sum_slot)

    def back_first(index):
        at, here = chunk(index)
        grad = v.grad_first[at, :] + plane_total(v.part_first, v.got_first, here, at)
        grad_base, grad_branch, grad_alpha = blended_back(
            grad,
            v.x_all[here, :].astype(jnp.float32),
            v.gain_a[...],
            v.branch_normed[at, :],
            v.branch_inverse[at, :],
            v.first[at, :],
            v.first_inverse[at, :],
        )
        v.grad_tokens[at, :] = grad_base
        v.gb[here, :] = low(grad_branch)
        v.grad_a[...] += grad_alpha

    gb_slot = slots.take(SHARE)
    plane_share(v.gb, gb_slot, back_first)
    mate_gb_slot = slots.take(1)
    passed_gb = pass_to_mate(v.gb, mate_gb_slot)
    plane_share_relay(v.gb, gb_slot, passed_gb)
    plane_share_wait(v.gb, gb_slot, passed_gb)

    v.grad_att[...] = low(product(v.gb[first_half, :], v.wo[...], ((1,), (1,))))
    landed(v.turned_att.at[:, second_half], mate_att_slot)
    landed(v.gb.at[second_half, :], mate_gb_slot)
    line_out_slot = slots.take(2)
    part_out_slot = slots.take(1)

    def out_tile(index):
        there = cols(index, 256)
        v.send_out[:, there] = low(product(v.turned_att[...], v.gb[:, there], ((1,), (0,))))

    loop(model // 256, out_tile)
    for distance in range(1, parts):
        target = plane(distance)
        put(
            v.send_out.at[:, cols(target, part_cols)],
            v.send_wo.at[s],
            (target, f),
            BY_PLANE,
            part_out_slot,
        )
    v.send_wo[s] = v.send_out[:, cols(s, part_cols)]
    weight_combine(v.send_uv, v.line_uv, 2 * hid, line_uv_slot)
    v.grad_qkv[...] = jnp.zeros_like(v.grad_qkv)

    def attend_back(pair):
        q_cols, k_cols, v_cols = cols(pair), cols(pairs + pair), cols(2 * pairs + pair)
        for block in range(blocks):
            here = slice(block * TILE, (block + 1) * TILE)
            seen = slice(0, (block + 1) * TILE)
            results = []
            for half in range(2):
                query = jnp.where(halves[half], v.qkv[here, q_cols], 0.0).astype(jnp.bfloat16)
                grad = jnp.where(halves[half], v.grad_att[here, q_cols], 0.0)
                grad = grad.astype(jnp.bfloat16)
                score = product(query, v.qkv[seen, k_cols], ((1,), (1,))) * scale
                score = score + v.bias[here, seen]
                share = jnp.exp(score - v.total[2 * pair + half, here, :])
                grad_share = product(grad, v.qkv[seen, v_cols], ((1,), (1,)))
                inner = jnp.sum(share * grad_share, axis=1, keepdims=True)
                grad_score = low(share * (grad_share - inner))
                results.append(product(grad_score, v.qkv[seen, k_cols], ((1,), (0,))))
                v.grad_qkv[seen, v_cols] += product(low(share), grad, ((0,), (0,)))
                v.grad_qkv[seen, k_cols] += product(grad_score, query, ((0,), (0,)))
            v.grad_qkv[here, q_cols] = jnp.where(low_half, results[0], results[1])

    loop(pairs, attend_back)
    v.grad_qk[...] = jnp.zeros_like(v.grad_qk)

    def prepare_back(index):
        here = pl.ds(pl.multiple_of(index % blocks * TILE, TILE), TILE)
        group = index // blocks
        there = cols(group)
        pair = cols(group % pairs)
        grad = low(v.grad_qkv[here, there] * scale).astype(jnp.float32)
        normed = v.normed[here, there]
        v.grad_qk[:, pair] += jnp.sum(grad * normed, axis=0, keepdims=True)
        grad = grad * v.gain_qk[:, pair]
        grad = v.inverse[here, there] * (grad - normed * head_mean(grad * normed))
        back = grad * v.cosine[here, :] - swap(grad) * v.sine[here, :]
        v.gm[here, there] = low(back)

    loop(2 * pairs * blocks, prepare_back)

    def value_back(index):
        here = pl.ds(pl.multiple_of(index * TILE, TILE), TILE)
        v.gm[here, 2 * span :] = low(v.grad_qkv[here, 2 * span :])

    loop(blocks, value_back)
    mate_gm_slot = slots.take(1)
    put(v.gm.at[first_half, :], v.gm.at[second_half, :], mate, BY_MATE_C, mate_gm_slot)

    v.gain_part[...] = jnp.zeros_like(v.gain_part)
    for block in range(2 * lines):
        here = slice(block * TILE, (block + 1) * TILE)
        local_pair = block % (span // TILE) * TILE
        qk = v.grad_qk[:, local_pair : local_pair + TILE]
        mine = (s == block // (span // TILE)).astype(jnp.float32)
        v.gain_part[block, :, edges[0] : edges[1]] = qk * mine
        v.gain_part[block, :, edges[1] : edges[2]] = v.grad_a[:, here]
        v.gain_part[block, :, cols(edges[2] // TILE + s)] = v.grad_u[:, here]
        v.gain_part[block, :, cols(edges[3] // TILE + s)] = v.grad_v[:, here]
        v.gain_part[block, :, edges[4] : edges[5]] = v.grad_m[:, here]

    inputs_slot = slots.take(1)
    plane_sum(
        v.part_inputs,
        v.got_inputs,
        inputs_slot,
        lambda index: product(v.gm[first_half, :], v.wq[cols(index, piece), :], ((1,), (1,))),
    )
    gain_line_slot = slots.take(1)
    for distance in range(1, 2 * lines):
        target = (f + distance) % (2 * lines)
        put(
            v.gain_part.at[target],
            v.gain_got.at[distance - 1],
            (s, target),
            BY_GAIN_LINE,
            gain_line_slot,
        )
    landed(v.gm.at[second_half, :], mate_gm_slot)
    line_qkv_slot = slots.take(2)
    landed(v.send_wo.at[: parts - 1], part_out_slot)
    line_grad_first(v.send_wo, v.line_wo, line_out_slot, slice(None))
    pl.when(inner)(lambda: line_grad_mid(v.send_wo, v.line_wo, line_out_slot, slice(None)))
    weight_grad(v.turned_x, v.gm, v.send_qkv, v.line_qkv, 3 * span, line_qkv_slot)
    line_grad_rest(v.send_wo, v.line_wo, line_out_slot)

    def line_total(grads, arrived, done, columns, base):
        def add(slots_in):
            landed(arrived.at[slots_in[0] : slots_in[-1] + 1], base + 1)

            def tile(index):
                there = cols(index, 256)
                total = grads[z, :, there].astype(jnp.float32)
                for slot in slots_in:
                    total = total + arrived[slot, :, there].astype(jnp.float32)
                done[:, there] = low(total)

            loop(columns // 256, tile)

        pl.when(outer)(lambda: add((0, 1)))
        pl.when(inner)(lambda: add((1, 2, 3)))

    line_total(v.send_down, v.line_down, v.done_down, model, line_down_slot)
    back_down_slot = slots.take(1)
    for distance in range(1, parts):
        target = plane(distance)
        put(
            v.done_down.at[:, cols(target, part_cols)],
            v.made_back_down.at[cols(s), :],
            (target, f),
            BY_PLANE,
            back_down_slot,
        )
    v.made_back_down[cols(s), :] = v.done_down[:, cols(s, part_cols)]

    plane_sum_wait(v.got_inputs, inputs_slot)

    def finish_inputs(index):
        at, here = chunk(index)
        v.made_input_grad[at, :] = v.grad_tokens[at, :] + plane_total(v.part_inputs, v.got_inputs, here, at)

    loop(rows // chunk_rows, finish_inputs)
    deliver(1).start()

    line_total(v.send_uv, v.line_uv, v.done_uv, 2 * hid, line_uv_slot)
    back_uv_slot = slots.take(1)
    for distance in range(1, parts):
        target = plane(distance)
        for index in range(blocks_uv):
            put(
                v.done_uv.at[:, pl.ds(pl.multiple_of(target * wide + index * TILE, TILE), TILE)],
                v.made_back_uv.at[s, :, index * TILE : (index + 1) * TILE],
                (target, f),
                BY_PLANE,
                back_uv_slot,
            )
    v.made_back_uv[s] = v.done_uv[:, cols(s, wide)]

    weight_combine(v.send_qkv, v.line_qkv, 3 * span, line_qkv_slot)
    weight_combine(v.send_wo, v.line_wo, part_cols, line_out_slot)
    gain_plane_slot = slots.take(1)
    landed(v.gain_got, gain_line_slot)
    total = v.gain_part[f]
    for distance in range(1, 2 * lines):
        total = total + v.gain_got[distance - 1]
    v.gain_sum[s] = total
    for distance in range(1, parts):
        put(
            v.gain_sum.at[s],
            v.gain_sum.at[s],
            (plane(distance), f),
            BY_GAIN_PLANE,
            gain_plane_slot,
        )

    line_total(v.send_qkv, v.line_qkv, v.done_qkv, 3 * span, line_qkv_slot)
    back_qkv_slot = slots.take(1)
    for block in range(3):
        chunk_of = parts * block + s
        target = chunk_of // 3
        index = chunk_of % 3
        source = v.done_qkv.at[:, block * span : (block + 1) * span]

        @pl.when(target == s)
        def _():
            v.made_back_qkv[index] = source[...]

        @pl.when(target != s)
        def _():
            put(
                source,
                v.made_back_qkv.at[index],
                (target, f),
                BY_PLANE,
                back_qkv_slot,
            )


    landed(v.made_back_down.at[: (parts - 1) * TILE, :], back_down_slot)
    deliver(5).start()
    landed(v.made_back_uv.at[: parts - 1], back_uv_slot)
    deliver(4).start()
    landed(v.gain_sum.at[: parts - 1], gain_plane_slot)
    total = v.gain_sum[0]
    for source in range(1, parts):
        total = total + v.gain_sum[source]
    v.made_gains[...] = total
    deliver(6).start()
    landed(v.made_back_qkv.at[:2], back_qkv_slot)
    deliver(2).start()

    line_total(v.send_wo, v.line_wo, v.made_back_out, part_cols, line_out_slot)
    deliver(3).start()

    def sent(group, size):
        ref = v.wu.at[: size // (2 * hid), :]
        descriptor(ref, group, 0).wait_send()

    a_weight = TILE * (3 * span + 2 * hid + model + part_cols)
    sent(BY_SHARE, 4 * 6 * (rows // 2) * model)
    sent(BY_SUM, 4 * (parts - 1) * rows * model)
    sent(BY_WIDE, lines * TILE * 2 * hid + slots_all * 2 * hid)
    sent(BY_MATE_B, 2 * slots_all * model + lines * TILE * model)
    sent(BY_MATE_C, (3 * lines * TILE + 3 * span) * slots_all + lines * TILE * 3 * span)
    sent(BY_MATE_D, TILE * slots_all + TILE * model)
    pl.when(inner)(lambda: sent(BY_LINE, 4 * a_weight))
    pl.when(outer)(lambda: sent(BY_LINE, 2 * a_weight))
    sent(BY_GRAD, 3 * a_weight)
    sent(BY_PLANE, 2 * (2 * TILE * span + (parts - 1) * TILE * (wide + 2 * part_cols)))
    descriptor(v.gain_got, BY_GAIN, 0).wait_send()
    descriptor(v.gain_got, BY_GAIN_LINE, 0).wait_send()
    descriptor(v.gain_sum.at[: parts - 1], BY_GAIN_PLANE, 0).wait_send()
    for index in range(len(Results._fields)):
        deliver(index).wait()
    assert slots.count <= SLOTS_MOST, slots.count


SLOTS_MOST = 70
SHARE = 4
BY_SHARE, BY_SUM, BY_WIDE, BY_MATE_B, BY_MATE_C, BY_MATE_D = range(6)
BY_LINE, BY_GRAD, BY_PLANE, BY_GAIN, BY_GAIN_LINE, BY_GAIN_PLANE = range(6, 12)


class Inputs(typing.NamedTuple):
    tokens: typing.Any
    lengths: typing.Any
    w_qkv: typing.Any
    w_out: typing.Any
    w_uv: typing.Any
    w_down: typing.Any
    s_qk: typing.Any
    alpha_a: typing.Any
    s_u: typing.Any
    s_v: typing.Any
    alpha_m: typing.Any
    cotangent: typing.Any


class Results(typing.NamedTuple):
    output: typing.Any
    input_grad: typing.Any
    back_qkv: typing.Any
    back_out: typing.Any
    back_uv: typing.Any
    back_down: typing.Any
    gains: typing.Any


def buffers(sizes):
    (parts, lines, rows, model, deep, own_heads, width) = sizes
    every = parts * rows
    span = own_heads * width
    hid = deep * lines * 2 // parts
    half = lines * TILE
    gains = 3 * TILE + 2 * deep
    bf16, f32 = jnp.bfloat16, jnp.float32
    return dict(
        wq=((model, 3 * span), bf16),
        wo=((span, model), bf16),
        wz=((model, model // parts), bf16),
        cotangent=((rows, model), bf16),
        made_output=((rows, model), bf16),
        made_input_grad=((rows, model), f32),
        made_back_qkv=((3, TILE, span), bf16),
        made_back_out=((TILE, model // parts), bf16),
        made_back_uv=((parts, TILE, 2 * hid // parts), bf16),
        made_back_down=((deep, model // parts), bf16),
        made_gains=((1, gains), f32),
        wu=((model, 2 * hid), bf16),
        wd=((hid, model), bf16),
        gain_all=((2 * lines, 1, gains), f32),
        gain_a=((1, model), f32),
        gain_m=((1, model), f32),
        gain_u=((1, hid), f32),
        gain_v=((1, hid), f32),
        gain_qk=((1, span), f32),
        x_all=((every, model), bf16),
        first_all=((every, model), bf16),
        gd=((2 * every, model), bf16),
        gb=((2 * every, model), bf16),
        cosine=((every, TILE), f32),
        sine=((every, TILE), f32),
        bias=((every, every), f32),
        raw=((every, 3 * span), f32),
        normed=((every, 2 * span), f32),
        inverse=((every, 2 * span), f32),
        qkv=((every, 3 * span), bf16),
        total=((own_heads, every, 1), f32),
        attended=((every, span), bf16),
        branch_normed=((rows, model), f32),
        branch_inverse=((rows, 1), f32),
        first=((rows, model), f32),
        first_inverse=((rows, 1), f32),
        up=((every, hid), f32),
        gate=((every, hid), f32),
        hidden=((every, hid), bf16),
        grad_hidden=((every, 256), bf16),
        gu=((2 * every, 2 * hid), bf16),
        grad_first=((rows, model), f32),
        grad_tokens=((rows, model), f32),
        grad_att=((every, span), bf16),
        grad_qkv=((every, 3 * span), f32),
        gm=((2 * every, 3 * span), bf16),
        grad_a=((1, model), f32),
        grad_m=((1, model), f32),
        grad_u=((1, hid), f32),
        grad_v=((1, hid), f32),
        grad_qk=((1, span), f32),
        gain_part=((2 * lines, 1, gains), f32),
        gain_got=((2 * lines - 1, 1, gains), f32),
        gain_sum=((parts, 1, gains), f32),
        turned_x=((half, 2 * every), bf16),
        turned_first=((half, 2 * every), bf16),
        turned_hidden=((half, 2 * every), bf16),
        turned_att=((TILE, 2 * every), bf16),
        stage_x=((half, every), bf16),
        stage_first=((half, every), bf16),
        stage_hidden=((half, every), bf16),
        stage_att=((TILE, every), bf16),
        send_out=((TILE, model), bf16),
        send_wo=((lines, TILE, model // parts), bf16),
        line_wo=((4, TILE, model // parts), bf16),
        part_branch=((every, model), bf16),
        got_branch=((parts - 1, rows, model), bf16),
        part_down=((every, model), bf16),
        got_down=((parts - 1, rows, model), bf16),
        part_first=((every, model), bf16),
        got_first=((parts - 1, rows, model), bf16),
        part_inputs=((every, model), bf16),
        got_inputs=((parts - 1, rows, model), bf16),
        send_qkv=((lines, TILE, 3 * span), bf16),
        line_qkv=((4, TILE, 3 * span), bf16),
        done_qkv=((TILE, 3 * span), bf16),
        send_uv=((lines, TILE, 2 * hid), bf16),
        line_uv=((4, TILE, 2 * hid), bf16),
        done_uv=((TILE, 2 * hid), bf16),
        send_down=((lines, TILE, model), bf16),
        line_down=((4, TILE, model), bf16),
        done_down=((TILE, model), bf16),
    )


def place_results(sizes, *refs):
    (parts, lines, rows, model, deep, own_heads, width) = sizes
    count = len(Results._fields)
    got = Results(*refs[:count])
    (output, inputs, qkv, out, uv, down, *gains) = refs[count:]
    output[...] = got.output[...]
    inputs[...] = got.input_grad[...]
    span = own_heads * width
    for index in range(qkv.shape[1] // span):
        qkv[:, index * span : (index + 1) * span] = got.back_qkv[index].astype(jnp.float32)
    out[...] = got.back_out[...].astype(jnp.float32)
    for source in range(parts):
        for index in range(uv.shape[1] // (parts * TILE)):
            there = (index * parts + source) * TILE
            here = slice(index * TILE, (index + 1) * TILE)
            uv[:, there : there + TILE] = got.back_uv[source, :, here].astype(jnp.float32)
    down[...] = got.back_down[...].astype(jnp.float32)
    start = 0
    for gain in gains:
        stop = start + gain.shape[-1]
        gain[...] = got.gains[:, start:stop]
        start = stop


def fused(sizes):
    (parts, lines, rows, model, deep, own_heads, width) = sizes
    span = own_heads * width
    hid = deep * lines * 2 // parts

    def run(tokens, lengths, w_qkv, w_out, w_uv, w_down, *others):
        gains, cotangent = others[:5], others[5]
        f32, bf16 = jnp.float32, jnp.bfloat16
        struct = jax.ShapeDtypeStruct
        middle = Results(
            struct(tokens.shape[1:], bf16),
            struct(tokens.shape[1:], f32),
            struct((3, TILE, span), bf16),
            struct(w_out.shape, bf16),
            struct((parts, TILE, 2 * hid // parts), bf16),
            struct(w_down.shape, bf16),
            struct((1, sum(g.shape[0] for g in gains)), f32),
        )
        shapes = [
            struct(tokens.shape[1:], bf16),
            struct(tokens.shape[1:], f32),
            *(struct(w.shape, f32) for w in (w_qkv, w_out, w_uv, w_down)),
            *(struct((1, g.shape[0]), f32) for g in gains),
        ]
        vmem = pl.BlockSpec(memory_space=pltpu.VMEM)
        specs = [vmem] * len(Inputs._fields)
        for place in (0, 2, 3, 4, 5, 11):
            specs[place] = pl.BlockSpec(memory_space=pl.ANY)
        specs[1] = pl.BlockSpec(memory_space=pltpu.SMEM)
        scratch = [pltpu.VMEM(shape, kind) for shape, kind in buffers(sizes).values()]
        found = pl.pallas_call(
            functools.partial(fused_layer, sizes),
            out_shape=list(middle),
            in_specs=specs,
            out_specs=[pl.BlockSpec(memory_space=pl.ANY)] * len(middle),
            scratch_shapes=[
                *scratch,
                pltpu.SemaphoreType.DMA((12,)),
                pltpu.SemaphoreType.DMA((SLOTS_MOST,)),
                pltpu.SemaphoreType.DMA((6 + len(Results._fields),)),
            ],
            compiler_params=pltpu.CompilerParams(
                collective_id=0, has_side_effects=True, vmem_limit_bytes=67043328
            ),
            name="fused_layer",
        )(
            tokens[0],
            lengths,
            w_qkv,
            w_out,
            w_uv,
            w_down,
            *gains,
            cotangent[0],
        )
        outs = pl.pallas_call(
            functools.partial(place_results, sizes),
            out_shape=shapes,
            in_specs=[vmem] * len(middle),
            out_specs=[vmem] * len(shapes),
            compiler_params=pltpu.CompilerParams(vmem_limit_bytes=67043328),
            name="place_results",
        )(*found)
        return (
            outs[0][None],
            outs[1][None],
            *outs[2:6],
            *(g.reshape(-1) for g in outs[6:]),
        )

    return run


def choose(parts, shards):
    def run(*args):
        tokens, w_qkv, w_down = args[0], args[2], args[5]
        rows, model = tokens.shape[1:]
        deep, width = w_down.shape[0], model // H
        fits = shards == 2 * parts and rows == TILE and w_qkv.shape[0] == TILE
        fits = fits and deep == parts * TILE and 2 * width == TILE and H == 4 * parts
        if not fits:
            return local(*args)
        return fused((parts, shards // 2, rows, model, deep, H // parts, width))(*args)

    return run


def solution(mesh):
    return jax.shard_map(
        choose(mesh.shape["seq"], mesh.shape["fsdp"]),
        mesh=mesh,
        in_specs=(
            P("fsdp", "seq", None),
            P("fsdp", None),
            P("fsdp", "seq"),
            P("fsdp", "seq"),
            P("fsdp", "seq"),
            P("fsdp", "seq"),
            P("fsdp"),
            P("fsdp"),
            P("fsdp"),
            P("fsdp"),
            P("fsdp"),
            P("fsdp", "seq", None),
        ),
        out_specs=(
            P("fsdp", "seq", None),
            P("fsdp", "seq", None),
            P("fsdp", "seq"),
            P("fsdp", "seq"),
            P("fsdp", "seq"),
            P("fsdp", "seq"),
            P("fsdp"),
            P("fsdp"),
            P("fsdp"),
            P("fsdp"),
            P("fsdp"),
        ),
        check_vma=False,
    )
```

```python
import functools
import math
import types
import typing

import jax
import jax.numpy as jnp
from jax import lax
from jax.experimental import pallas as pl
from jax.experimental.pallas import tpu as pltpu
from jax.sharding import PartitionSpec as P

H = 16


epsilon = 1e-06


def layout(lengths_row, slot):
    columns = lengths_row.shape[0]
    ends = jnp.cumsum(lengths_row)
    starts = ends - lengths_row
    before = (slot[:, None] >= ends[None, : columns - 1]).astype(jnp.int32)
    member = jnp.sum(before, axis=1)
    picked = member[:, None] == jnp.arange(columns, dtype=jnp.int32)[None, :]
    begin = jnp.sum(jnp.where(picked, starts[None, :], 0), axis=1)
    valid = member < columns - 1
    segment = jnp.where(valid, member, columns - 1 + slot)
    place = jnp.where(valid, slot - begin, 0)
    return (segment, place, valid)


def rotary(place, width):
    half = width // 2
    frequency = jnp.exp(jnp.arange(half, dtype=jnp.float32) * (-2.0 * math.log(10000.0) / width))
    angle = place.astype(jnp.float32)[:, None] * frequency[None, :]
    return (jnp.cos(angle)[:, None, :], jnp.sin(angle)[:, None, :])


def unit_rows(value):
    return value * lax.rsqrt(jnp.mean(value * value, axis=-1, keepdims=True) + epsilon)


def turn_heads(value, cosine, sine):
    half = value.shape[-1] // 2
    first = value[..., :half]
    second = value[..., half:]
    return jnp.concatenate(
        [first * cosine - second * sine, second * cosine + first * sine], axis=-1
    )


def prepare(query_raw, key_raw, s_qk, cosine, sine, heads):
    rows = query_raw.shape[0]
    scales = s_qk.reshape(heads, -1)

    def normed(raw):
        shaped = raw.reshape(rows, heads, -1)
        return (unit_rows(turn_heads(shaped, cosine, sine)) * scales).reshape(rows, -1)

    return (normed(query_raw), normed(key_raw))


def blend(base, branch, alpha):
    return unit_rows(base + alpha * (unit_rows(branch) - base))


def gated(up_gate, s_u, s_v):
    width = s_u.shape[0]
    return up_gate[:, :width] * s_u * jax.nn.silu(up_gate[:, width:] * s_v)


def rounded(value):
    return lax.optimization_barrier(value.astype(jnp.bfloat16)).astype(jnp.float32)


def attention_forward(query, key, value, mask):
    scale = 1.0 / math.sqrt(query.shape[2])
    score = jnp.einsum("thd,shd->hts", query, key, preferred_element_type=jnp.float32)
    score = jnp.where(mask[None], score * scale, -1e30)
    peak = jnp.max(score, axis=2, keepdims=True)
    raised = jnp.exp(score - peak)
    summed = jnp.sum(raised, axis=2, keepdims=True)
    weight = (raised / summed).astype(jnp.bfloat16)
    result = jnp.einsum("hts,shd->thd", weight, value, preferred_element_type=jnp.float32)
    return result, peak + jnp.log(summed)


def attention_backward(query, key, value, mask, log_total, grad):
    scale = 1.0 / math.sqrt(query.shape[2])
    score = jnp.einsum("thd,shd->hts", query, key, preferred_element_type=jnp.float32)
    score = jnp.where(mask[None], score * scale, -1e30)
    share = jnp.exp(score - log_total)
    grad_value = jnp.einsum(
        "hts,thd->shd", share.astype(jnp.bfloat16), grad, preferred_element_type=jnp.float32
    )
    grad_share = jnp.einsum("thd,shd->hts", grad, value, preferred_element_type=jnp.float32)
    inner = jnp.sum(share * grad_share, axis=2, keepdims=True)
    grad_score = (share * (grad_share - inner)).astype(jnp.bfloat16)
    grad_query = jnp.einsum("hts,shd->thd", grad_score, key, preferred_element_type=jnp.float32)
    grad_key = jnp.einsum("hts,thd->shd", grad_score, query, preferred_element_type=jnp.float32)
    return grad_query * scale, grad_key * scale, grad_value


def low(value):
    return value.astype(jnp.bfloat16)


def product(left, right, dims):
    return lax.dot_general(left, right, (dims, ((), ())), preferred_element_type=jnp.float32)


def local(tokens, lengths, w_qkv, w_out, w_uv, w_down, s_qk, alpha_a, s_u, s_v, alpha_m, cotangent):
    rows = tokens.shape[1]
    model = tokens.shape[2]
    width = model // H
    parts = lax.axis_size("seq")
    shards = lax.axis_size("fsdp")
    mine = lax.axis_index("seq")
    own = H // parts
    deep = w_down.shape[0]
    hidden_all = deep * shards
    hidden_own = hidden_all // parts
    piece = deep // parts
    slot = mine * rows + jnp.arange(rows, dtype=jnp.int32)
    every_slot = jnp.arange(rows * parts, dtype=jnp.int32)
    keep = layout(lengths[0], slot)[2].astype(jnp.float32)[:, None]
    segment, place, _ = layout(lengths[0], every_slot)
    mask = (segment[:, None] == segment[None, :]) & (every_slot[:, None] >= every_slot[None, :])

    def exchange(array, axis):
        return lax.all_to_all(array, "seq", axis, axis, tiled=False)

    def gather(array, axis=0):
        return lax.all_gather(array, "fsdp", axis=axis, tiled=True)

    def spread(array):
        return lax.all_gather(array, "seq", axis=0, tiled=True)

    r_in = w_qkv.shape[0]
    share_qkv = lax.all_to_all(
        w_qkv.reshape(r_in, -1, parts, width), "seq", 2, 1, tiled=True
    ).reshape(r_in, -1)
    share_uv = lax.all_to_all(
        w_uv.reshape(r_in, -1, parts, piece), "seq", 2, 1, tiled=True
    ).reshape(r_in, -1)
    share_down = lax.all_to_all(w_down.reshape(parts, piece, -1), "seq", 0, 2, tiled=True)
    share_down = share_down.reshape(piece, model)
    share_out = lax.all_gather(w_out, "seq", axis=1, tiled=True)
    inputs = spread(tokens[0])
    full_qkv = gather(share_qkv)
    full_out = gather(share_out).reshape(own, parts, width, model)
    full_out = lax.dynamic_index_in_dim(full_out, mine, 1, False).reshape(own * width, model)
    full_uv = gather(share_uv)
    full_down = gather(share_down)
    gains = gather(jnp.concatenate([s_qk, alpha_a, s_u, s_v, alpha_m])[None]).astype(jnp.float32)
    cuts = [s_qk.shape[0], alpha_a.shape[0], s_u.shape[0], s_v.shape[0]]
    edges = [sum(cuts[: i + 1]) for i in range(4)]
    gain_qk, gain_a, gain_u, gain_v, gain_m = jnp.split(gains, edges, axis=1)
    gain_qk = gain_qk.reshape(own, parts, width)
    gain_qk = lax.dynamic_index_in_dim(gain_qk, mine, 1, False).reshape(-1)
    gain_a, gain_m = gain_a.reshape(-1), gain_m.reshape(-1)
    gain_u = lax.dynamic_index_in_dim(gain_u.reshape(shards, parts, piece), mine, 1, False).reshape(-1)
    gain_v = lax.dynamic_index_in_dim(gain_v.reshape(shards, parts, piece), mine, 1, False).reshape(-1)

    mixed = product(inputs, full_qkv, ((1,), (0,)))
    cosine, sine = rotary(place, width)
    span = own * width

    def prepare_local(query_raw, key_raw, scale_qk):
        return prepare(query_raw, key_raw, scale_qk, cosine, sine, own)

    (query_f, key_f), pull_prepare = jax.vjp(
        prepare_local, mixed[:, :span], mixed[:, span : 2 * span], gain_qk
    )
    heads = (rows * parts, own, width)
    query, key = low(query_f).reshape(heads), low(key_f).reshape(heads)
    value = low(mixed[:, 2 * span :]).reshape(heads)
    attended, log_total = attention_forward(query, key, value, mask)
    attended = low(attended.reshape(-1, span))

    def reduce_rows(array):
        return lax.psum_scatter(low(array), "seq", scatter_dimension=0, tiled=True).astype(
            jnp.float32
        )

    branch = reduce_rows(product(attended, full_out, ((1,), (0,))))
    first, pull_first = jax.vjp(blend, tokens[0].astype(jnp.float32), branch, gain_a)
    first_all = spread(low(first))
    up_gate = product(first_all, full_uv, ((1,), (0,)))
    hidden_f, pull_gate = jax.vjp(gated, up_gate, gain_u, gain_v)
    hidden = low(hidden_f)
    down = reduce_rows(product(hidden, full_down, ((1,), (0,))))
    final, pull_last = jax.vjp(blend, first, down, gain_m)
    output = low(final * keep)
    grad_first, grad_down, grad_gain_m = pull_last(cotangent[0].astype(jnp.float32) * keep)
    grad_down = spread(low(grad_down))
    grad_w_down = low(product(hidden, grad_down, ((0,), (0,))))
    grad_hidden = rounded(product(grad_down, full_down, ((1,), (1,))))
    grad_up_gate, grad_gain_u, grad_gain_v = pull_gate(grad_hidden)
    grad_up = low(grad_up_gate)
    grad_w_uv = low(product(first_all, grad_up, ((0,), (0,))))
    grad_first = grad_first + reduce_rows(product(grad_up, full_uv, ((1,), (1,))))
    grad_inputs, grad_branch, grad_gain_a = pull_first(grad_first)
    grad_branch = spread(low(grad_branch))
    grad_w_out = low(product(attended, grad_branch, ((0,), (0,))))
    grad_attended = low(product(grad_branch, full_out, ((1,), (1,)))).reshape(heads)
    grad_query, grad_key, grad_value = attention_backward(
        query, key, value, mask, log_total, grad_attended
    )
    grad_query_raw, grad_key_raw, grad_gain_qk = pull_prepare(
        (rounded(grad_query).reshape(-1, span), rounded(grad_key).reshape(-1, span))
    )
    grad_mixed = low(
        jnp.concatenate([grad_query_raw, grad_key_raw, grad_value.reshape(-1, span)], axis=1)
    )
    grad_w_qkv = low(product(inputs, grad_mixed, ((0,), (0,))))
    grad_inputs = grad_inputs + reduce_rows(product(grad_mixed, full_qkv, ((1,), (1,))))

    def collect(array):
        return lax.psum_scatter(array, "fsdp", scatter_dimension=0, tiled=True)

    part_down = collect(grad_w_down)
    out_down = lax.all_to_all(
        part_down.reshape(1, piece, model), "seq", 2, 0, tiled=True
    ).reshape(deep, -1)
    part_uv = collect(grad_w_uv)
    out_uv = lax.all_to_all(
        part_uv.reshape(r_in, -1, 1, piece), "seq", 1, 2, tiled=True
    ).reshape(r_in, -1)
    placed = jnp.zeros((own, parts, width, model), jnp.bfloat16)
    placed = lax.dynamic_update_slice(
        placed, grad_w_out.reshape(own, 1, width, model), (0, mine, 0, 0)
    )
    part_out = collect(placed.reshape(-1, model))
    out_out = lax.psum_scatter(part_out, "seq", scatter_dimension=1, tiled=True)
    part_qkv = collect(grad_w_qkv)
    out_qkv = lax.all_to_all(
        part_qkv.reshape(r_in, -1, 1, width), "seq", 1, 2, tiled=True
    ).reshape(r_in, -1)

    def widen(array, outer, inner):
        blank = jnp.zeros((outer, parts, inner), jnp.float32)
        array = array.reshape(outer, 1, inner)
        return lax.dynamic_update_slice(blank, array, (0, mine, 0)).reshape(shards, -1)

    gain_sums = jnp.concatenate(
        [
            widen(grad_gain_qk, own, width),
            grad_gain_a.reshape(shards, -1),
            widen(grad_gain_u, shards, piece),
            widen(grad_gain_v, shards, piece),
            grad_gain_m.reshape(shards, -1),
        ],
        axis=1,
    )
    gain_sums = lax.psum(collect(gain_sums), "seq")[0]
    outs = jnp.split(gain_sums, edges)
    return (
        output[None],
        grad_inputs[None],
        out_qkv.astype(jnp.float32),
        out_out.astype(jnp.float32),
        out_uv.astype(jnp.float32),
        out_down.astype(jnp.float32),
        outs[0],
        outs[1],
        outs[2],
        outs[3],
        outs[4],
    )


MESH = pl.DeviceIdType.MESH
TILE = 128
QROWS = 128


def loop(count, body):
    def run(index, carry):
        body(index)
        return carry

    lax.fori_loop(0, count, run, 0)


def at_rows(ref, block, size=TILE):
    return ref.at[pl.ds(pl.multiple_of(block * size, size), size), :]


def cols(block, size=TILE):
    return pl.ds(pl.multiple_of(block * size, size), size)


def mean_last(value):
    return jnp.sum(value, axis=-1, keepdims=True) * (1.0 / value.shape[-1])


class Slots:
    def __init__(self):
        self.count = 0

    def take(self, count):
        base = self.count
        self.count = base + count
        return base


def fused_layer(sizes, *refs):
    (parts, lines, rows, model, deep, own_heads, width) = sizes
    slots_all = parts * rows
    span = own_heads * width
    hid = deep * lines * 2 // parts
    count_in, count_out = len(Inputs._fields), len(Results._fields)
    ins = Inputs(*refs[:count_in])
    outs = Results(*refs[count_in : count_in + count_out])
    table = buffers(sizes)
    rest = refs[count_in + count_out :]
    v = types.SimpleNamespace(**dict(zip(table, rest[: len(table)])))
    send_sem, recv_sem, local_sem = rest[len(table) :]

    s = lax.axis_index("seq")
    f = lax.axis_index("fsdp")
    z = f // 2
    c = f % 2
    other = 1 - c
    mate = (s, 2 * z + other)
    slots = Slots()

    def put(src, dst, target, send_slot, recv_slot):
        pltpu.make_async_remote_copy(
            src_ref=src,
            dst_ref=dst,
            send_sem=send_sem.at[send_slot],
            recv_sem=recv_sem.at[recv_slot],
            device_id=target,
            device_id_type=MESH,
        ).start()

    def descriptor(ref, send_slot, recv_slot):
        return pltpu.make_async_remote_copy(
            src_ref=ref,
            dst_ref=ref,
            send_sem=send_sem.at[send_slot],
            recv_sem=recv_sem.at[recv_slot],
            device_id=mate,
            device_id_type=MESH,
        )

    def landed(ref, slot):
        descriptor(ref, 0, slot).wait_recv()

    def plane(distance):
        return (s + distance) % parts

    def plane_from(distance):
        return (s + parts - distance) % parts

    def line(distance):
        return (z + distance) % lines

    def line_from(distance):
        return (z + lines - distance) % lines

    barrier = pltpu.get_barrier_semaphore()
    for distance in range(1, parts):
        pl.semaphore_signal(barrier, inc=1, device_id=(plane(distance), f), device_id_type=MESH)
    for distance in range(1, 2 * lines):
        target = (s, (f + distance) % (2 * lines))
        pl.semaphore_signal(barrier, inc=1, device_id=target, device_id_type=MESH)

    edges = [0, TILE, 2 * TILE, 2 * TILE + deep, 2 * TILE + 2 * deep, 3 * TILE + 2 * deep]
    own_gains = (ins.s_qk, ins.alpha_a, ins.s_u, ins.s_v, ins.alpha_m)
    for place, own_gain in enumerate(own_gains):
        row = own_gain[...].astype(jnp.float32).reshape(1, -1)
        v.gain_all[f, :, edges[place] : edges[place + 1]] = row
    own_row = pl.ds(pl.multiple_of(s * rows, rows), rows)
    own_w = pl.ds(pl.multiple_of(f * TILE, TILE), TILE)
    part_cols = model // parts
    blocks_uv = 2 * hid // parts // TILE
    wide = blocks_uv * TILE

    def fetch(src, dst, slot):
        pltpu.make_async_copy(src, dst, local_sem.at[slot]).start()

    def deliver(index):
        made = (
            v.made_output,
            v.made_input_grad,
            v.made_back_qkv,
            v.made_back_out,
            v.made_back_uv,
            v.made_back_down,
            v.made_gains,
        )
        return pltpu.make_async_copy(made[index], outs[index], local_sem.at[6 + index])

    def fetched(dst, slot):
        pltpu.make_async_copy(dst, dst, local_sem.at[slot]).wait()

    fetch(ins.w_out, v.wz.at[own_w, :], 0)
    fetch(ins.tokens, v.x_all.at[own_row, :], 1)
    for index in range(blocks_uv):
        fetch(
            ins.w_uv.at[:, pl.ds(pl.multiple_of((index * parts + s) * TILE, TILE), TILE)],
            v.wu.at[own_w, pl.ds(pl.multiple_of(s * wide + index * TILE, TILE), TILE)],
            2,
        )
    fetch(ins.w_down.at[cols(s), :], v.wd.at[own_w, cols(s, part_cols)], 3)
    fetch(ins.cotangent, v.cotangent, 4)
    for index in range(3):
        chunk = 3 * s + index

        @pl.when(chunk % parts == s)
        def _():
            fetch(
                ins.w_qkv.at[:, index * span : (index + 1) * span],
                v.wq.at[own_w, cols(chunk // parts, span)],
                5,
            )

    pl.semaphore_wait(barrier, parts - 1 + 2 * lines - 1)

    qkv_slot = slots.take(1)
    for index in range(3):
        chunk = 3 * s + index
        block = chunk // parts
        target = chunk % parts

        @pl.when(target != s)
        def _():
            put(
                ins.w_qkv.at[:, index * span : (index + 1) * span],
                v.wq.at[own_w, cols(block, span)],
                (target, f),
                BY_PLANE,
                qkv_slot,
            )


    side, across, opposite = s + 1 - 2 * (s % 2), (s + 2) % parts, parts - 1 - s

    def half_of(shared, owner, part):
        start = owner * rows + part * (rows // 2)
        return shared.at[pl.ds(pl.multiple_of(start, rows // 2), rows // 2), :]

    token_slot = slots.take(SHARE)
    for part in range(2):
        mine = ins.tokens.at[part * (rows // 2) : (part + 1) * (rows // 2), :]
        there = half_of(v.x_all, s, part)
        put(mine, there, (side, f), BY_SHARE, token_slot + 2 * part)
        put(mine, there, (across, f), BY_SHARE, token_slot + 2 - part)

    uv_slot = slots.take(1)
    for distance in range(1, parts):
        target = plane(distance)
        for index in range(blocks_uv):
            put(
                ins.w_uv.at[:, pl.ds(pl.multiple_of((index * parts + target) * TILE, TILE), TILE)],
                v.wu.at[own_w, pl.ds(pl.multiple_of(s * wide + index * TILE, TILE), TILE)],
                (target, f),
                BY_PLANE,
                uv_slot,
            )

    down_slot = slots.take(1)
    for distance in range(1, parts):
        target = plane(distance)
        put(
            ins.w_down.at[cols(target), :],
            v.wd.at[own_w, cols(s, part_cols)],
            (target, f),
            BY_PLANE,
            down_slot,
        )

    gain_slot = slots.take(1)
    for distance in range(1, 2 * lines):
        put(
            v.gain_all.at[f],
            v.gain_all.at[f],
            (s, (f + distance) % (2 * lines)),
            BY_GAIN,
            gain_slot,
        )

    def plane_share_relay(shared, base, passed=None):
        one, two = half_of(shared, side, 0), half_of(shared, across, 1)
        if passed is not None:
            passed(s, 0)
            passed(s, 1)
        landed(one, base)
        put(one, one, (across, f), BY_SHARE, base + 3)
        landed(two, base + 1)
        put(two, two, (side, f), BY_SHARE, base + 3)
        if passed is not None:
            passed(side, 0)
            passed(across, 1)

    def plane_share_wait(shared, base, passed=None):
        for pieces, slot in (
            (((side, 1), (across, 0)), base + 2),
            (((opposite, 0), (opposite, 1)), base + 3),
        ):
            landed(at_rows(shared, opposite, rows), slot)
            if passed is not None:
                for piece_of in pieces:
                    passed(*piece_of)

    def pass_to_mate(shared, slot):
        def passed(owner, part):
            start = owner * rows + part * (rows // 2)
            here = pl.ds(pl.multiple_of(start, rows // 2), rows // 2)
            there = pl.ds(pl.multiple_of(slots_all + start, rows // 2), rows // 2)
            put(shared.at[here, :], shared.at[there, :], mate, BY_MATE_B, slot)

        return passed

    def shard(ref, chip, core, lanes):
        block = 2 * chip + core
        return ref.at[pl.ds(pl.multiple_of(block * TILE, TILE), TILE), lanes]

    inner = z * (lines - 1 - z) > 0
    outer = z * (lines - 1 - z) == 0

    def line_send(ref, base, lanes=slice(None), twice=True, apart=False):
        own = shard(ref, z, c, lanes)
        for distance in (2, 1, 3):
            target = line(distance)
            near = (z - target) * (z - target) < (lines - 1) * (lines - 1)
            slot = base
            if apart:
                slot = base + distance - 1
            elif distance == 2:
                slot = base + target * (lines - 1 - target) // 2

            @pl.when(near)
            def _():
                put(own, own, (s, 2 * target + c), BY_LINE, slot)

        if twice:
            put(own, own, mate, mate_group(ref), base + 2 + apart)

    def mate_group(ref):
        return BY_WIDE if ref is v.wu else BY_MATE_B if ref is v.wd else BY_MATE_C

    def line_relay(ref, base, lanes=slice(None), apart=False):
        block = shard(ref, line_from(2), c, lanes)

        @pl.when(inner)
        def _():
            landed(block, base + 1)
            slot = base + 2 * z - 2 if apart else base
            put(block, block, (s, 2 * (lines - 1) * (z - 1) + c), BY_LINE, slot)

    def line_arrived(ref, base, lanes=slice(None)):
        pl.when(inner)(lambda: landed(ref.at[: 2 * TILE, lanes], base))
        pl.when(outer)(lambda: landed(ref.at[: 3 * TILE, lanes], base))

    def line_forward(ref, base, lanes=slice(None), apart=False):
        if not apart:
            line_arrived(ref, base, lanes)
        for distance in (1, 3, 2):
            block = shard(ref, line_from(distance), c, lanes)
            if apart and distance == 2:

                @pl.when(outer)
                def _():
                    landed(block, base + 1)

            elif apart:
                landed(block, base + distance - 1)
            put(block, block, mate, mate_group(ref), base + 2 + apart)

    def mate_wait(ref, base, lanes=slice(None), apart=False):
        landed(ref.at[: lines * TILE, lanes], base + 2 + apart)

    wq_slot, wu_slot = (slots.take(4) for _ in range(2))
    count = 4
    piece = model // count
    wd_parts = [
        (slots.take(3), slice(part * piece, (part + 1) * piece)) for part in range(count)
    ]
    wz_slot, wo_slot, out_slot = slots.take(2), slots.take(1), slots.take(1)
    fetched(v.wz.at[own_w, :], 0)
    line_send(v.wz, wz_slot, twice=False)

    landed(v.wq.at[own_w, : 2 * span], qkv_slot)
    fetched(v.wq.at[own_w, :span], 5)
    line_send(v.wq, wq_slot, apart=True)
    lengths = [ins.lengths[0, i] for i in range(ins.lengths.shape[1])]

    def slot_facts(slot):
        end = 0
        member = jnp.zeros(slot.shape, jnp.int32)
        begin = jnp.zeros(slot.shape, jnp.int32)
        for length in lengths[:-1]:
            end = end + length
            after = slot >= end
            member = member + after.astype(jnp.int32)
            begin = jnp.where(after, end, begin)
        valid = member < len(lengths) - 1
        segment = jnp.where(valid, member, len(lengths) - 1 + slot)
        place = jnp.where(valid, slot - begin, 0)
        return segment, place, valid

    lane = lax.broadcasted_iota(jnp.int32, (1, TILE), 1)
    low_half = lane < width
    first_quarter = lane % width < width // 2
    frequency = jnp.exp(
        (lane % (width // 2)).astype(jnp.float32) * (-2.0 * math.log(10000.0) / width)
    )
    turn_sign = jnp.where(first_quarter, -1.0, 1.0)

    def tables(block):
        here = pl.ds(pl.multiple_of(block * TILE, TILE), TILE)
        slot = block * TILE + lax.broadcasted_iota(jnp.int32, (TILE, 1), 0)
        segment, place, _ = slot_facts(slot)
        angle = place.astype(jnp.float32) * frequency
        v.cosine[here, :] = jnp.cos(angle)
        v.sine[here, :] = jnp.sin(angle) * turn_sign
        key_slot = lax.broadcasted_iota(jnp.int32, (1, slots_all), 1)
        key_segment = slot_facts(key_slot)[0]
        kept = (segment == key_segment) & (slot >= key_slot)
        v.bias[here, :] = jnp.where(kept, 0.0, -1e30)

    loop(slots_all // TILE, tables)
    line_relay(v.wz, wz_slot)
    line_relay(v.wq, wq_slot, apart=True)
    fetched(v.x_all.at[own_row, :], 1)
    plane_share_relay(v.x_all, token_slot)
    plane_share_wait(v.x_all, token_slot)
    line_arrived(v.wz, wz_slot)
    for distance in range(1, parts):
        target = plane(distance)
        rows_out = at_rows(v.wz, 2 * target + c)
        put(
            rows_out,
            v.wo.at[cols(c), cols(s, part_cols)],
            (target, f),
            BY_PLANE,
            out_slot,
        )
    v.wo[cols(c), cols(s, part_cols)] = v.wz[cols(2 * s + c), :]
    fetched(v.wu.at[own_w, cols(s, wide)], 2)
    landed(v.wu.at[own_w, : (parts - 1) * wide], uv_slot)
    line_send(v.wu, wu_slot, apart=True)

    def mate_blocks(name_all, ref, stage, slot):
        for block in range(lines):
            here = slice(block * TILE, (block + 1) * TILE)
            stage[here, :] = name_all[:, cols(2 * block + other)].T
        put(stage, ref.at[:, slots_all:], mate, BY_MATE_C, slot)
        for block in range(lines):
            here = slice(block * TILE, (block + 1) * TILE)
            ref[here, :slots_all] = name_all[:, cols(2 * block + c)].T

    mate_x_slot = slots.take(1)
    mate_blocks(v.x_all, v.turned_x, v.stage_x, mate_x_slot)
    landed(v.gain_all.at[1:], gain_slot)

    def gain(block, offset):
        return v.gain_all[block, :, pl.ds(pl.multiple_of(offset, TILE), TILE)]

    for block in range(2 * lines):
        here = slice(block * TILE, (block + 1) * TILE)
        v.gain_a[:, here] = gain(block, edges[1])
        v.gain_u[:, here] = gain(block, edges[2] + s * TILE)
        v.gain_v[:, here] = gain(block, edges[3] + s * TILE)
        v.gain_m[:, here] = gain(block, edges[4])
    for block in range(span // TILE):
        v.gain_qk[:, block * TILE : (block + 1) * TILE] = gain(span // TILE * s + block, 0)

    line_forward(v.wq, wq_slot, apart=True)
    mate_wait(v.wq, wq_slot, apart=True)

    def mix(index):
        v.raw[:, cols(index, span)] = product(
            v.x_all[...], v.wq[:, cols(index, span)], ((1,), (0,))
        )

    loop(3, mix)

    def swap(value):
        return jnp.where(
            first_quarter,
            pltpu.roll(value, TILE - width // 2, 1),
            pltpu.roll(value, width // 2, 1),
        )

    def head_mean(value):
        one = jnp.sum(jnp.where(low_half, value, 0.0), axis=-1, keepdims=True)
        two = jnp.sum(jnp.where(low_half, 0.0, value), axis=-1, keepdims=True)
        return jnp.where(low_half, one, two) * (1.0 / width)

    pairs = span // TILE
    blocks = slots_all // TILE

    def prepare_block(index):
        here = pl.ds(pl.multiple_of(index % blocks * TILE, TILE), TILE)
        group = index // blocks
        there = cols(group)
        value = v.raw[here, there]
        turned = value * v.cosine[here, :] + swap(value) * v.sine[here, :]
        inverse = lax.rsqrt(head_mean(turned * turned) + epsilon)
        normed = turned * inverse
        v.normed[here, there] = normed
        v.inverse[here, there] = inverse
        v.qkv[here, there] = low(normed * v.gain_qk[:, cols(group % pairs)])

    loop(2 * pairs * blocks, prepare_block)

    def keep_value(index):
        here = pl.ds(pl.multiple_of(index * TILE, TILE), TILE)
        v.qkv[here, 2 * span :] = low(v.raw[here, 2 * span :])

    loop(blocks, keep_value)
    own_out = v.wo.at[cols(c), :]
    landed(v.wo.at[cols(c), : (parts - 1) * part_cols], out_slot)
    put(own_out, own_out, mate, BY_MATE_D, wo_slot)

    scale = 1.0 / math.sqrt(width)
    halves = (low_half, jnp.logical_not(low_half))

    def attend(pair):
        q_cols, k_cols, v_cols = cols(pair), cols(pairs + pair), cols(2 * pairs + pair)
        for block in range(blocks):
            here = slice(block * TILE, (block + 1) * TILE)
            seen = slice(0, (block + 1) * TILE)
            results = []
            for half in range(2):
                query = jnp.where(halves[half], v.qkv[here, q_cols], 0.0).astype(jnp.bfloat16)
                score = product(query, v.qkv[seen, k_cols], ((1,), (1,))) * scale
                score = score + v.bias[here, seen]
                peak = jnp.max(score, axis=1, keepdims=True)
                raised = jnp.exp(score - peak)
                summed = jnp.sum(raised, axis=1, keepdims=True)
                weight = low(raised / summed)
                results.append(product(weight, v.qkv[seen, v_cols], ((1,), (0,))))
                v.total[2 * pair + half, here, :] = peak + jnp.log(summed)
            v.attended[here, q_cols] = low(jnp.where(low_half, results[0], results[1]))

    loop(pairs, attend)
    mate_att_slot = slots.take(1)
    v.stage_att[...] = v.attended[:, cols(other)].T
    v.turned_att[:, :slots_all] = v.attended[:, cols(c)].T

    put(v.stage_att, v.turned_att.at[:, slots_all:], mate, BY_MATE_D, mate_att_slot)
    landed(v.wo.at[cols(other), :], wo_slot)

    def plane_sum(sums, arrived, base, tile, span_of=(0, count)):
        start, stop = span_of

        def send(index):
            there = cols(index, piece)
            for distance in range(1, parts):
                target = plane(distance)
                put(
                    sums.at[pl.ds(pl.multiple_of(target * rows, rows), rows), there],
                    arrived.at[distance - 1, :, there],
                    (target, f),
                    BY_SUM,
                    base,
                )

        def step(index):
            sums[:, cols(start + index, piece)] = low(tile(start + index))

            @pl.when(index > 0)
            def _():
                send(start + index - 1)

        loop(stop - start, step)
        send(stop - 1)

    def plane_sum_wait(arrived, base):
        landed(arrived, base)

    def plane_total(sums, arrived, here, at):
        total = sums[here, :].astype(jnp.float32)
        for distance in range(1, parts):
            total = total + arrived[distance - 1, at, :].astype(jnp.float32)
        return total

    chunk_rows = 32

    def chunk(index):
        at = pl.ds(pl.multiple_of(index * chunk_rows, chunk_rows), chunk_rows)
        here = pl.ds(pl.multiple_of(s * rows + index * chunk_rows, chunk_rows), chunk_rows)
        return at, here

    def plane_share(shared, base, make):
        def send(index):
            own = shared.at[chunk(index)[1], :]
            part = index // (rows // chunk_rows // 2)
            put(own, own, (side, f), BY_SHARE, base + 2 * part)
            put(own, own, (across, f), BY_SHARE, base + 2 - part)

        def step(index):
            make(index)

            @pl.when(index > 0)
            def _():
                send(index - 1)

        loop(rows // chunk_rows, step)
        send(rows // chunk_rows - 1)

    branch_slot = slots.take(1)
    plane_sum(
        v.part_branch,
        v.got_branch,
        branch_slot,
        lambda index: product(v.attended[...], v.wo[:, cols(index, piece)], ((1,), (0,))),
    )
    line_relay(v.wu, wu_slot, apart=True)
    fetched(v.wd.at[own_w, cols(s, part_cols)], 3)
    landed(v.wd.at[own_w, : (parts - 1) * part_cols], down_slot)
    line_send(v.wd, *wd_parts[0])
    line_send(v.wd, *wd_parts[1])
    plane_sum_wait(v.got_branch, branch_slot)
    line_relay(v.wd, *wd_parts[0])
    line_send(v.wd, *wd_parts[2])

    def blended(base, branch, alpha):
        inverse_branch = lax.rsqrt(mean_last(branch * branch) + epsilon)
        normed = branch * inverse_branch
        mixed = base + alpha * (normed - base)
        inverse = lax.rsqrt(mean_last(mixed * mixed) + epsilon)
        return normed, inverse_branch, mixed * inverse, inverse

    def blended_back(grad, base, alpha, normed, inverse_branch, result, inverse):
        grad_mixed = inverse * (grad - result * mean_last(grad * result))
        grad_normed = alpha * grad_mixed
        grad_branch = inverse_branch * (grad_normed - normed * mean_last(grad_normed * normed))
        grad_alpha = jnp.sum(grad_mixed * (normed - base), axis=0, keepdims=True)
        return grad_mixed - grad_normed, grad_branch, grad_alpha

    def make_first(index):
        at, here = chunk(index)
        base = v.x_all[here, :].astype(jnp.float32)
        normed, inverse_branch, result, inverse = blended(
            base, plane_total(v.part_branch, v.got_branch, here, at), v.gain_a[...]
        )
        v.branch_normed[at, :] = normed
        v.branch_inverse[at, :] = inverse_branch
        v.first[at, :] = result
        v.first_inverse[at, :] = inverse
        v.first_all[here, :] = low(result)

    first_slot = slots.take(SHARE)
    plane_share(v.first_all, first_slot, make_first)
    line_relay(v.wd, *wd_parts[1])
    line_send(v.wd, *wd_parts[3])
    plane_share_relay(v.first_all, first_slot)
    line_relay(v.wd, *wd_parts[2])
    line_forward(v.wu, wu_slot, apart=True)
    mate_wait(v.wu, wu_slot, apart=True)
    plane_share_wait(v.first_all, first_slot)

    def gate_tile(index):
        there = cols(index, 256)
        v.up[:, there] = product(v.first_all[...], v.wu[:, there], ((1,), (0,)))
        v.gate[:, there] = product(
            v.first_all[...],
            v.wu[:, pl.ds(pl.multiple_of(hid + index * 256, 256), 256)],
            ((1,), (0,)),
        )

        def rows_of(block):
            here = pl.ds(pl.multiple_of(block * 64, 64), 64)
            scaled = v.gate[here, there] * v.gain_v[:, there]
            passed = scaled / (1.0 + jnp.exp(-scaled))
            v.hidden[here, there] = low(v.up[here, there] * v.gain_u[:, there] * passed)

        loop(slots_all // 64, rows_of)

    line_relay(v.wd, *wd_parts[3])
    loop(hid // 512, gate_tile)
    line_forward(v.wd, *wd_parts[0])
    loop(hid // 512, lambda index: gate_tile(hid // 512 + index))
    mate_hidden_slot = slots.take(1)
    mate_blocks(v.hidden, v.turned_hidden, v.stage_hidden, mate_hidden_slot)
    mate_first_slot = slots.take(1)
    mate_blocks(v.first_all, v.turned_first, v.stage_first, mate_first_slot)
    down_sum_slot = slots.take(1)

    def down_tile(index):
        return product(v.hidden[...], v.wd[:, cols(index, piece)], ((1,), (0,)))

    line_forward(v.wd, *wd_parts[1])
    for part in range(count):
        mate_wait(v.wd, *wd_parts[part])
        plane_sum(v.part_down, v.got_down, down_sum_slot, down_tile, (part, part + 1))
        if part + 2 < count:
            line_forward(v.wd, *wd_parts[part + 2])
    fetched(v.cotangent, 4)
    plane_sum_wait(v.got_down, down_sum_slot)
    v.grad_a[...] = jnp.zeros_like(v.grad_a)
    v.grad_m[...] = jnp.zeros_like(v.grad_m)

    def finish(index):
        at, here = chunk(index)
        slot = s * rows + index * chunk_rows
        slot = slot + lax.broadcasted_iota(jnp.int32, (chunk_rows, 1), 0)
        keep = slot_facts(slot)[2].astype(jnp.float32)
        base = v.first[at, :]
        alpha = v.gain_m[...]
        normed, inverse_branch, result, inverse = blended(
            base, plane_total(v.part_down, v.got_down, here, at), alpha
        )
        v.made_output[at, :] = low(result * keep)
        grad = v.cotangent[at, :].astype(jnp.float32) * keep
        grad_base, grad_down, grad_alpha = blended_back(
            grad, base, alpha, normed, inverse_branch, result, inverse
        )
        v.grad_first[at, :] = grad_base
        v.gd[here, :] = low(grad_down)
        v.grad_m[...] += grad_alpha

    loop(rows // chunk_rows, finish)
    gd_slot, mate_gd_slot = slots.take(count), slots.take(count)

    def gd_pass(owner, lanes, slot):
        here = pl.ds(pl.multiple_of(owner * rows, rows), rows)
        there = pl.ds(pl.multiple_of(slots_all + owner * rows, rows), rows)
        put(v.gd.at[here, lanes], v.gd.at[there, lanes], mate, BY_MATE_B, slot)

    for part in range(count):
        lanes = slice(part * piece, (part + 1) * piece)
        own = v.gd.at[own_row, lanes]
        for distance in range(1, parts):
            put(own, own, (plane(distance), f), BY_SHARE, gd_slot + part)
        gd_pass(s, lanes, mate_gd_slot + part)
    deliver(0).start()
    first_half = slice(0, slots_all)
    second_half = slice(slots_all, 2 * slots_all)

    ends = (lines - 1) * (1 - z % 2)
    mids = 2 - z // 2
    last = (2 * z + 1) % (lines + 1)
    beside = z + 1 - 2 * (z % 2)

    mid_slot = 2 - z * (lines - 1 - z) // 2

    def line_grad_first(grads, arrived, base, there):
        put(
            grads.at[ends, :, there],
            arrived.at[0, :, there],
            (s, 2 * beside + c),
            BY_GRAD,
            base + 1 - beside * (lines - 1 - beside) // 2,
        )

    def line_grad_mid(grads, arrived, base, there):
        put(
            grads.at[mids, :, there],
            arrived.at[mid_slot, :, there],
            (s, 2 * mids + c),
            BY_GRAD,
            base + 1,
        )

    def line_grad_last(grads, arrived, base, there):
        put(
            grads.at[last, :, there],
            arrived.at[3, :, there],
            (s, 2 * last + c),
            BY_GRAD,
            base + 1,
        )

    def line_grad_rest(grads, arrived, base, chained=False):
        @pl.when(outer)
        def _():
            if chained:
                there = (s, 2 * beside + c)
                put(grads.at[mids], arrived.at[2], there, BY_GRAD, base + 2)
            else:
                line_grad_mid(grads, arrived, base, slice(None))
            line_grad_last(grads, arrived, base, slice(None))

    def weight_grad(turned, right, grads, arrived, columns, base, chained=False):
        def send(index):
            line_grad_first(grads, arrived, base, cols(index, 256))
            if not chained:
                pl.when(inner)(lambda: line_grad_mid(grads, arrived, base, cols(index, 256)))

        def step(index):
            there = cols(index, 256)
            total = product(turned[...], right[:, there], ((1,), (0,)))
            grads[:, :, there] = low(total).reshape(lines, TILE, 256)

            pl.when(index > 0)(lambda: send(index - 1))

        loop(columns // 256, step)
        send(columns // 256 - 1)
        line_grad_rest(grads, arrived, base, chained)

    def combine_into(grads, block, came, columns):
        def tile(index):
            there = cols(index, 256)
            total = grads[block, :, there].astype(jnp.float32)
            grads[block, :, there] = low(total + came[:, there].astype(jnp.float32))

        loop(columns // 256, tile)

    def weight_combine(grads, arrived, columns, base):
        @pl.when(inner)
        def _():
            landed(arrived.at[0], base)
            combine_into(grads, last, arrived.at[0], columns)
            put(grads.at[last], arrived.at[1], (s, 2 * last + c), BY_GRAD, base + 1)

    def weight_combine_mid(grads, arrived, columns, base):
        @pl.when(inner)
        def _():
            landed(arrived.at[2], base + 2)
            combine_into(grads, mids, arrived.at[2], columns)
            put(grads.at[mids], arrived.at[1], (s, 2 * mids + c), BY_GRAD, base + 1)

    mate_gu_slot = slots.take(1)

    def gu_pass(index):
        for lanes in (
            pl.ds(pl.multiple_of(index * 256, 256), 256),
            pl.ds(pl.multiple_of(hid + index * 256, 256), 256),
        ):
            mine, there = v.gu.at[first_half, lanes], v.gu.at[second_half, lanes]
            put(mine, there, mate, BY_WIDE, mate_gu_slot)

    def gate_back(index):
        there = cols(index, 256)
        there_gate = pl.ds(pl.multiple_of(hid + index * 256, 256), 256)
        v.grad_hidden[...] = low(product(v.gd[first_half, :], v.wd[there, :], ((1,), (1,))))
        v.grad_u[:, there] = jnp.zeros((1, 256), jnp.float32)
        v.grad_v[:, there] = jnp.zeros((1, 256), jnp.float32)

        def rows_of(block):
            here = pl.ds(pl.multiple_of(block * 64, 64), 64)
            grad = v.grad_hidden[here, :].astype(jnp.float32)
            up = v.up[here, there]
            gate = v.gate[here, there]
            gain_u = v.gain_u[:, there]
            gain_v = v.gain_v[:, there]
            scaled = gate * gain_v
            squash = 1.0 / (1.0 + jnp.exp(-scaled))
            passed = scaled * squash
            grad_scaled_up = grad * passed
            grad_scaled = grad * (up * gain_u) * (squash + passed * (1.0 - squash))
            v.gu[here, there] = low(grad_scaled_up * gain_u)
            v.gu[here, there_gate] = low(grad_scaled * gain_v)
            v.grad_u[:, there] += jnp.sum(grad_scaled_up * up, axis=0, keepdims=True)
            v.grad_v[:, there] += jnp.sum(grad_scaled * gate, axis=0, keepdims=True)

        loop(slots_all // 64, rows_of)
        pl.when(index > 0)(lambda: gu_pass(index - 1))

    landed(v.turned_x.at[:, second_half], mate_x_slot)
    landed(v.turned_first.at[:, second_half], mate_first_slot)
    landed(v.turned_hidden.at[:, second_half], mate_hidden_slot)
    line_down_slot = slots.take(2)
    for part in range(count):
        lanes = slice(part * piece, (part + 1) * piece)
        landed(v.gd.at[: (parts - 1) * rows, lanes], gd_slot + part)
        for distance in range(1, parts):
            gd_pass(plane_from(distance), lanes, mate_gd_slot + part)
        if part == count - 1:
            loop(1, gate_back)
        landed(v.gd.at[second_half, lanes], mate_gd_slot + part)
        total = product(v.turned_hidden[...], v.gd[:, lanes], ((1,), (0,)))
        v.send_down[:, :, lanes] = low(total).reshape(lines, TILE, piece)
        line_grad_first(v.send_down, v.line_down, line_down_slot, lanes)
        line_grad_mid(v.send_down, v.line_down, line_down_slot, lanes)
        pl.when(outer)(lambda: line_grad_last(v.send_down, v.line_down, line_down_slot, lanes))
    loop(hid // 256 - 1, lambda index: gate_back(index + 1))
    gu_pass(hid // 256 - 1)
    first_sum_slot = slots.take(1)
    plane_sum(
        v.part_first,
        v.got_first,
        first_sum_slot,
        lambda index: product(v.gu[first_half, :], v.wu[cols(index, piece), :], ((1,), (1,))),
    )
    weight_combine(v.send_down, v.line_down, model, line_down_slot)
    landed(v.gu.at[second_half, :], mate_gu_slot)
    line_uv_slot = slots.take(2)
    weight_grad(v.turned_first, v.gu, v.send_uv, v.line_uv, 2 * hid, line_uv_slot)
    plane_sum_wait(v.got_first, first_sum_slot)

    def back_first(index):
        at, here = chunk(index)
        grad = v.grad_first[at, :] + plane_total(v.part_first, v.got_first, here, at)
        grad_base, grad_branch, grad_alpha = blended_back(
            grad,
            v.x_all[here, :].astype(jnp.float32),
            v.gain_a[...],
            v.branch_normed[at, :],
            v.branch_inverse[at, :],
            v.first[at, :],
            v.first_inverse[at, :],
        )
        v.grad_tokens[at, :] = grad_base
        v.gb[here, :] = low(grad_branch)
        v.grad_a[...] += grad_alpha

    gb_slot = slots.take(SHARE)
    plane_share(v.gb, gb_slot, back_first)
    mate_gb_slot = slots.take(1)
    passed_gb = pass_to_mate(v.gb, mate_gb_slot)
    plane_share_relay(v.gb, gb_slot, passed_gb)
    plane_share_wait(v.gb, gb_slot, passed_gb)

    v.grad_att[...] = low(product(v.gb[first_half, :], v.wo[...], ((1,), (1,))))
    weight_combine(v.send_uv, v.line_uv, 2 * hid, line_uv_slot)
    v.grad_qkv[...] = jnp.zeros_like(v.grad_qkv)

    def attend_back(pair):
        q_cols, k_cols, v_cols = cols(pair), cols(pairs + pair), cols(2 * pairs + pair)
        for block in range(blocks):
            here = slice(block * TILE, (block + 1) * TILE)
            seen = slice(0, (block + 1) * TILE)
            results = []
            for half in range(2):
                query = jnp.where(halves[half], v.qkv[here, q_cols], 0.0).astype(jnp.bfloat16)
                grad = jnp.where(halves[half], v.grad_att[here, q_cols], 0.0)
                grad = grad.astype(jnp.bfloat16)
                score = product(query, v.qkv[seen, k_cols], ((1,), (1,))) * scale
                score = score + v.bias[here, seen]
                share = jnp.exp(score - v.total[2 * pair + half, here, :])
                grad_share = product(grad, v.qkv[seen, v_cols], ((1,), (1,)))
                inner = jnp.sum(share * grad_share, axis=1, keepdims=True)
                grad_score = low(share * (grad_share - inner))
                results.append(product(grad_score, v.qkv[seen, k_cols], ((1,), (0,))))
                v.grad_qkv[seen, v_cols] += product(low(share), grad, ((0,), (0,)))
                v.grad_qkv[seen, k_cols] += product(grad_score, query, ((0,), (0,)))
            v.grad_qkv[here, q_cols] = jnp.where(low_half, results[0], results[1])

    loop(pairs, attend_back)
    landed(v.turned_att.at[:, second_half], mate_att_slot)
    landed(v.gb.at[second_half, :], mate_gb_slot)
    line_out_slot = slots.take(3)
    part_out_slot = slots.take(1)

    def out_tile(index):
        there = cols(index, 256)
        v.send_out[:, there] = low(product(v.turned_att[...], v.gb[:, there], ((1,), (0,))))

    loop(model // 256, out_tile)
    for distance in range(1, parts):
        target = plane(distance)
        put(
            v.send_out.at[:, cols(target, part_cols)],
            v.send_wo.at[s],
            (target, f),
            BY_PLANE,
            part_out_slot,
        )
    v.send_wo[s] = v.send_out[:, cols(s, part_cols)]
    v.grad_qk[...] = jnp.zeros_like(v.grad_qk)

    def prepare_back(index):
        here = pl.ds(pl.multiple_of(index % blocks * TILE, TILE), TILE)
        group = index // blocks
        there = cols(group)
        pair = cols(group % pairs)
        grad = low(v.grad_qkv[here, there] * scale).astype(jnp.float32)
        normed = v.normed[here, there]
        v.grad_qk[:, pair] += jnp.sum(grad * normed, axis=0, keepdims=True)
        grad = grad * v.gain_qk[:, pair]
        grad = v.inverse[here, there] * (grad - normed * head_mean(grad * normed))
        back = grad * v.cosine[here, :] - swap(grad) * v.sine[here, :]
        v.gm[here, there] = low(back)

    loop(2 * pairs * blocks, prepare_back)

    def value_back(index):
        here = pl.ds(pl.multiple_of(index * TILE, TILE), TILE)
        v.gm[here, 2 * span :] = low(v.grad_qkv[here, 2 * span :])

    loop(blocks, value_back)
    mate_gm_slot = slots.take(1)
    put(v.gm.at[first_half, :], v.gm.at[second_half, :], mate, BY_MATE_C, mate_gm_slot)

    v.gain_part[...] = jnp.zeros_like(v.gain_part)
    for block in range(2 * lines):
        here = slice(block * TILE, (block + 1) * TILE)
        local_pair = block % (span // TILE) * TILE
        qk = v.grad_qk[:, local_pair : local_pair + TILE]
        mine = (s == block // (span // TILE)).astype(jnp.float32)
        v.gain_part[block, :, edges[0] : edges[1]] = qk * mine
        v.gain_part[block, :, edges[1] : edges[2]] = v.grad_a[:, here]
        v.gain_part[block, :, cols(edges[2] // TILE + s)] = v.grad_u[:, here]
        v.gain_part[block, :, cols(edges[3] // TILE + s)] = v.grad_v[:, here]
        v.gain_part[block, :, edges[4] : edges[5]] = v.grad_m[:, here]

    inputs_slot = slots.take(1)
    plane_sum(
        v.part_inputs,
        v.got_inputs,
        inputs_slot,
        lambda index: product(v.gm[first_half, :], v.wq[cols(index, piece), :], ((1,), (1,))),
    )
    gain_line_slot = slots.take(1)
    for distance in range(1, 2 * lines):
        target = (f + distance) % (2 * lines)
        put(
            v.gain_part.at[target],
            v.gain_got.at[distance - 1],
            (s, target),
            BY_GAIN_LINE,
            gain_line_slot,
        )
    landed(v.gm.at[second_half, :], mate_gm_slot)
    line_qkv_slot = slots.take(3)
    landed(v.send_wo.at[: parts - 1], part_out_slot)
    line_grad_first(v.send_wo, v.line_wo, line_out_slot, slice(None))
    weight_grad(v.turned_x, v.gm, v.send_qkv, v.line_qkv, 3 * span, line_qkv_slot, True)
    line_grad_rest(v.send_wo, v.line_wo, line_out_slot, True)

    def line_total(grads, arrived, done, columns, base, chained=False):
        def add(slots_in):
            landed(arrived.at[: len(slots_in)], base + 1)

            def tile(index):
                there = cols(index, 256)
                total = grads[z, :, there].astype(jnp.float32)
                for slot in slots_in:
                    total = total + arrived[slot, :, there].astype(jnp.float32)
                done[:, there] = low(total)

            loop(columns // 256, tile)

        pl.when(outer)(lambda: add((0, 1)))
        pl.when(inner)(lambda: add((1, 3) if chained else (1, 2, 3)))

    line_total(v.send_down, v.line_down, v.done_down, model, line_down_slot)
    back_down_slot = slots.take(1)
    for distance in range(1, parts):
        target = plane(distance)
        put(
            v.done_down.at[:, cols(target, part_cols)],
            v.made_back_down.at[cols(s), :],
            (target, f),
            BY_PLANE,
            back_down_slot,
        )
    v.made_back_down[cols(s), :] = v.done_down[:, cols(s, part_cols)]

    line_total(v.send_uv, v.line_uv, v.done_uv, 2 * hid, line_uv_slot)
    back_uv_slot = slots.take(1)
    for distance in range(1, parts):
        target = plane(distance)
        for index in range(blocks_uv):
            put(
                v.done_uv.at[:, pl.ds(pl.multiple_of(target * wide + index * TILE, TILE), TILE)],
                v.made_back_uv.at[s, :, index * TILE : (index + 1) * TILE],
                (target, f),
                BY_PLANE,
                back_uv_slot,
            )
    v.made_back_uv[s] = v.done_uv[:, cols(s, wide)]

    weight_combine(v.send_wo, v.line_wo, part_cols, line_out_slot)
    weight_combine(v.send_qkv, v.line_qkv, 3 * span, line_qkv_slot)
    plane_sum_wait(v.got_inputs, inputs_slot)

    def finish_inputs(index):
        at, here = chunk(index)
        v.made_input_grad[at, :] = v.grad_tokens[at, :] + plane_total(v.part_inputs, v.got_inputs, here, at)

    loop(rows // chunk_rows, finish_inputs)
    deliver(1).start()

    weight_combine_mid(v.send_qkv, v.line_qkv, 3 * span, line_qkv_slot)
    gain_plane_slot = slots.take(1)
    landed(v.gain_got, gain_line_slot)
    total = v.gain_part[f]
    for distance in range(1, 2 * lines):
        total = total + v.gain_got[distance - 1]
    v.gain_sum[s] = total
    for distance in range(1, parts):
        put(
            v.gain_sum.at[s],
            v.gain_sum.at[s],
            (plane(distance), f),
            BY_GAIN_PLANE,
            gain_plane_slot,
        )

    weight_combine_mid(v.send_wo, v.line_wo, part_cols, line_out_slot)
    line_total(v.send_qkv, v.line_qkv, v.done_qkv, 3 * span, line_qkv_slot, True)
    back_qkv_slot = slots.take(1)
    for block in range(3):
        chunk_of = parts * block + s
        target = chunk_of // 3
        index = chunk_of % 3
        source = v.done_qkv.at[:, block * span : (block + 1) * span]

        @pl.when(target == s)
        def _():
            v.made_back_qkv[index] = source[...]

        @pl.when(target != s)
        def _():
            put(
                source,
                v.made_back_qkv.at[index],
                (target, f),
                BY_PLANE,
                back_qkv_slot,
            )


    landed(v.made_back_down.at[: (parts - 1) * TILE, :], back_down_slot)
    deliver(5).start()
    landed(v.made_back_uv.at[: parts - 1], back_uv_slot)
    deliver(4).start()
    landed(v.gain_sum.at[: parts - 1], gain_plane_slot)
    total = v.gain_sum[0]
    for source in range(1, parts):
        total = total + v.gain_sum[source]
    v.made_gains[...] = total
    deliver(6).start()
    landed(v.made_back_qkv.at[:2], back_qkv_slot)
    deliver(2).start()

    line_total(v.send_wo, v.line_wo, v.made_back_out, part_cols, line_out_slot, True)
    deliver(3).start()

    def sent(group, size):
        ref = v.wu.at[: size // (2 * hid), :]
        descriptor(ref, group, 0).wait_send()

    a_weight = TILE * (3 * span + 2 * hid + model + part_cols)
    sent(BY_SHARE, 4 * 6 * (rows // 2) * model)
    sent(BY_SUM, 4 * (parts - 1) * rows * model)
    sent(BY_WIDE, lines * TILE * 2 * hid + slots_all * 2 * hid)
    sent(BY_MATE_B, 2 * slots_all * model + lines * TILE * model)
    sent(BY_MATE_C, (3 * lines * TILE + 3 * span) * slots_all + lines * TILE * 3 * span)
    sent(BY_MATE_D, TILE * slots_all + TILE * model)
    pl.when(inner)(lambda: sent(BY_LINE, 4 * a_weight))
    pl.when(outer)(lambda: sent(BY_LINE, 2 * a_weight))
    sent(BY_GRAD, 3 * a_weight)
    sent(BY_PLANE, 2 * (2 * TILE * span + (parts - 1) * TILE * (wide + 2 * part_cols)))
    descriptor(v.gain_got, BY_GAIN, 0).wait_send()
    descriptor(v.gain_got, BY_GAIN_LINE, 0).wait_send()
    descriptor(v.gain_sum.at[: parts - 1], BY_GAIN_PLANE, 0).wait_send()
    for index in range(len(Results._fields)):
        deliver(index).wait()
    assert slots.count <= SLOTS_MOST, slots.count


SLOTS_MOST = 75
SHARE = 4
BY_SHARE, BY_SUM, BY_WIDE, BY_MATE_B, BY_MATE_C, BY_MATE_D = range(6)
BY_LINE, BY_GRAD, BY_PLANE, BY_GAIN, BY_GAIN_LINE, BY_GAIN_PLANE = range(6, 12)


class Inputs(typing.NamedTuple):
    tokens: typing.Any
    lengths: typing.Any
    w_qkv: typing.Any
    w_out: typing.Any
    w_uv: typing.Any
    w_down: typing.Any
    s_qk: typing.Any
    alpha_a: typing.Any
    s_u: typing.Any
    s_v: typing.Any
    alpha_m: typing.Any
    cotangent: typing.Any


class Results(typing.NamedTuple):
    output: typing.Any
    input_grad: typing.Any
    back_qkv: typing.Any
    back_out: typing.Any
    back_uv: typing.Any
    back_down: typing.Any
    gains: typing.Any


def buffers(sizes):
    (parts, lines, rows, model, deep, own_heads, width) = sizes
    every = parts * rows
    span = own_heads * width
    hid = deep * lines * 2 // parts
    half = lines * TILE
    gains = 3 * TILE + 2 * deep
    bf16, f32 = jnp.bfloat16, jnp.float32
    return dict(
        wq=((model, 3 * span), bf16),
        wo=((span, model), bf16),
        wz=((model, model // parts), bf16),
        cotangent=((rows, model), bf16),
        made_output=((rows, model), bf16),
        made_input_grad=((rows, model), f32),
        made_back_qkv=((3, TILE, span), bf16),
        made_back_out=((TILE, model // parts), bf16),
        made_back_uv=((parts, TILE, 2 * hid // parts), bf16),
        made_back_down=((deep, model // parts), bf16),
        made_gains=((1, gains), f32),
        wu=((model, 2 * hid), bf16),
        wd=((hid, model), bf16),
        gain_all=((2 * lines, 1, gains), f32),
        gain_a=((1, model), f32),
        gain_m=((1, model), f32),
        gain_u=((1, hid), f32),
        gain_v=((1, hid), f32),
        gain_qk=((1, span), f32),
        x_all=((every, model), bf16),
        first_all=((every, model), bf16),
        gd=((2 * every, model), bf16),
        gb=((2 * every, model), bf16),
        cosine=((every, TILE), f32),
        sine=((every, TILE), f32),
        bias=((every, every), f32),
        raw=((every, 3 * span), f32),
        normed=((every, 2 * span), f32),
        inverse=((every, 2 * span), f32),
        qkv=((every, 3 * span), bf16),
        total=((own_heads, every, 1), f32),
        attended=((every, span), bf16),
        branch_normed=((rows, model), f32),
        branch_inverse=((rows, 1), f32),
        first=((rows, model), f32),
        first_inverse=((rows, 1), f32),
        up=((every, hid), f32),
        gate=((every, hid), f32),
        hidden=((every, hid), bf16),
        grad_hidden=((every, 256), bf16),
        gu=((2 * every, 2 * hid), bf16),
        grad_first=((rows, model), f32),
        grad_tokens=((rows, model), f32),
        grad_att=((every, span), bf16),
        grad_qkv=((every, 3 * span), f32),
        gm=((2 * every, 3 * span), bf16),
        grad_a=((1, model), f32),
        grad_m=((1, model), f32),
        grad_u=((1, hid), f32),
        grad_v=((1, hid), f32),
        grad_qk=((1, span), f32),
        gain_part=((2 * lines, 1, gains), f32),
        gain_got=((2 * lines - 1, 1, gains), f32),
        gain_sum=((parts, 1, gains), f32),
        turned_x=((half, 2 * every), bf16),
        turned_first=((half, 2 * every), bf16),
        turned_hidden=((half, 2 * every), bf16),
        turned_att=((TILE, 2 * every), bf16),
        stage_x=((half, every), bf16),
        stage_first=((half, every), bf16),
        stage_hidden=((half, every), bf16),
        stage_att=((TILE, every), bf16),
        send_out=((TILE, model), bf16),
        send_wo=((lines, TILE, model // parts), bf16),
        line_wo=((4, TILE, model // parts), bf16),
        part_branch=((every, model), bf16),
        got_branch=((parts - 1, rows, model), bf16),
        part_down=((every, model), bf16),
        got_down=((parts - 1, rows, model), bf16),
        part_first=((every, model), bf16),
        got_first=((parts - 1, rows, model), bf16),
        part_inputs=((every, model), bf16),
        got_inputs=((parts - 1, rows, model), bf16),
        send_qkv=((lines, TILE, 3 * span), bf16),
        line_qkv=((4, TILE, 3 * span), bf16),
        done_qkv=((TILE, 3 * span), bf16),
        send_uv=((lines, TILE, 2 * hid), bf16),
        line_uv=((4, TILE, 2 * hid), bf16),
        done_uv=((TILE, 2 * hid), bf16),
        send_down=((lines, TILE, model), bf16),
        line_down=((4, TILE, model), bf16),
        done_down=((TILE, model), bf16),
    )


def place_results(sizes, *refs):
    (parts, lines, rows, model, deep, own_heads, width) = sizes
    count = len(Results._fields)
    got = Results(*refs[:count])
    (output, inputs, qkv, out, uv, down, *gains) = refs[count:]
    output[...] = got.output[...]
    inputs[...] = got.input_grad[...]
    span = own_heads * width
    for index in range(qkv.shape[1] // span):
        qkv[:, index * span : (index + 1) * span] = got.back_qkv[index].astype(jnp.float32)
    out[...] = got.back_out[...].astype(jnp.float32)
    for source in range(parts):
        for index in range(uv.shape[1] // (parts * TILE)):
            there = (index * parts + source) * TILE
            here = slice(index * TILE, (index + 1) * TILE)
            uv[:, there : there + TILE] = got.back_uv[source, :, here].astype(jnp.float32)
    down[...] = got.back_down[...].astype(jnp.float32)
    start = 0
    for gain in gains:
        stop = start + gain.shape[-1]
        gain[...] = got.gains[:, start:stop]
        start = stop


def fused(sizes):
    (parts, lines, rows, model, deep, own_heads, width) = sizes
    span = own_heads * width
    hid = deep * lines * 2 // parts

    def run(tokens, lengths, w_qkv, w_out, w_uv, w_down, *others):
        gains, cotangent = others[:5], others[5]
        f32, bf16 = jnp.float32, jnp.bfloat16
        struct = jax.ShapeDtypeStruct
        middle = Results(
            struct(tokens.shape[1:], bf16),
            struct(tokens.shape[1:], f32),
            struct((3, TILE, span), bf16),
            struct(w_out.shape, bf16),
            struct((parts, TILE, 2 * hid // parts), bf16),
            struct(w_down.shape, bf16),
            struct((1, sum(g.shape[0] for g in gains)), f32),
        )
        shapes = [
            struct(tokens.shape[1:], bf16),
            struct(tokens.shape[1:], f32),
            *(struct(w.shape, f32) for w in (w_qkv, w_out, w_uv, w_down)),
            *(struct((1, g.shape[0]), f32) for g in gains),
        ]
        vmem = pl.BlockSpec(memory_space=pltpu.VMEM)
        specs = [vmem] * len(Inputs._fields)
        for place in (0, 2, 3, 4, 5, 11):
            specs[place] = pl.BlockSpec(memory_space=pl.ANY)
        specs[1] = pl.BlockSpec(memory_space=pltpu.SMEM)
        scratch = [pltpu.VMEM(shape, kind) for shape, kind in buffers(sizes).values()]
        found = pl.pallas_call(
            functools.partial(fused_layer, sizes),
            out_shape=list(middle),
            in_specs=specs,
            out_specs=[pl.BlockSpec(memory_space=pl.ANY)] * len(middle),
            scratch_shapes=[
                *scratch,
                pltpu.SemaphoreType.DMA((12,)),
                pltpu.SemaphoreType.DMA((SLOTS_MOST,)),
                pltpu.SemaphoreType.DMA((6 + len(Results._fields),)),
            ],
            compiler_params=pltpu.CompilerParams(
                collective_id=0, has_side_effects=True, vmem_limit_bytes=67043328
            ),
            name="fused_layer",
        )(
            tokens[0],
            lengths,
            w_qkv,
            w_out,
            w_uv,
            w_down,
            *gains,
            cotangent[0],
        )
        outs = pl.pallas_call(
            functools.partial(place_results, sizes),
            out_shape=shapes,
            in_specs=[vmem] * len(middle),
            out_specs=[vmem] * len(shapes),
            compiler_params=pltpu.CompilerParams(vmem_limit_bytes=67043328),
            name="place_results",
        )(*found)
        return (
            outs[0][None],
            outs[1][None],
            *outs[2:6],
            *(g.reshape(-1) for g in outs[6:]),
        )

    return run


def choose(parts, shards):
    def run(*args):
        tokens, w_qkv, w_down = args[0], args[2], args[5]
        rows, model = tokens.shape[1:]
        deep, width = w_down.shape[0], model // H
        fits = shards == 2 * parts and rows == TILE and w_qkv.shape[0] == TILE
        fits = fits and deep == parts * TILE and 2 * width == TILE and H == 4 * parts
        if not fits:
            return local(*args)
        return fused((parts, shards // 2, rows, model, deep, H // parts, width))(*args)

    return run


def solution(mesh):
    return jax.shard_map(
        choose(mesh.shape["seq"], mesh.shape["fsdp"]),
        mesh=mesh,
        in_specs=(
            P("fsdp", "seq", None),
            P("fsdp", None),
            P("fsdp", "seq"),
            P("fsdp", "seq"),
            P("fsdp", "seq"),
            P("fsdp", "seq"),
            P("fsdp"),
            P("fsdp"),
            P("fsdp"),
            P("fsdp"),
            P("fsdp"),
            P("fsdp", "seq", None),
        ),
        out_specs=(
            P("fsdp", "seq", None),
            P("fsdp", "seq", None),
            P("fsdp", "seq"),
            P("fsdp", "seq"),
            P("fsdp", "seq"),
            P("fsdp", "seq"),
            P("fsdp"),
            P("fsdp"),
            P("fsdp"),
            P("fsdp"),
            P("fsdp"),
        ),
        check_vma=False,
    )
```

```python
import functools
import math
import types
import typing

import jax
import jax.numpy as jnp
from jax import lax
from jax.experimental import pallas as pl
from jax.experimental.pallas import tpu as pltpu
from jax.sharding import PartitionSpec as P

H = 16


epsilon = 1e-06


def layout(lengths_row, slot):
    columns = lengths_row.shape[0]
    ends = jnp.cumsum(lengths_row)
    starts = ends - lengths_row
    before = (slot[:, None] >= ends[None, : columns - 1]).astype(jnp.int32)
    member = jnp.sum(before, axis=1)
    picked = member[:, None] == jnp.arange(columns, dtype=jnp.int32)[None, :]
    begin = jnp.sum(jnp.where(picked, starts[None, :], 0), axis=1)
    valid = member < columns - 1
    segment = jnp.where(valid, member, columns - 1 + slot)
    place = jnp.where(valid, slot - begin, 0)
    return (segment, place, valid)


def rotary(place, width):
    half = width // 2
    frequency = jnp.exp(jnp.arange(half, dtype=jnp.float32) * (-2.0 * math.log(10000.0) / width))
    angle = place.astype(jnp.float32)[:, None] * frequency[None, :]
    return (jnp.cos(angle)[:, None, :], jnp.sin(angle)[:, None, :])


def unit_rows(value):
    return value * lax.rsqrt(jnp.mean(value * value, axis=-1, keepdims=True) + epsilon)


def turn_heads(value, cosine, sine):
    half = value.shape[-1] // 2
    first = value[..., :half]
    second = value[..., half:]
    return jnp.concatenate(
        [first * cosine - second * sine, second * cosine + first * sine], axis=-1
    )


def prepare(query_raw, key_raw, s_qk, cosine, sine, heads):
    rows = query_raw.shape[0]
    scales = s_qk.reshape(heads, -1)

    def normed(raw):
        shaped = raw.reshape(rows, heads, -1)
        return (unit_rows(turn_heads(shaped, cosine, sine)) * scales).reshape(rows, -1)

    return (normed(query_raw), normed(key_raw))


def blend(base, branch, alpha):
    return unit_rows(base + alpha * (unit_rows(branch) - base))


def gated(up_gate, s_u, s_v):
    width = s_u.shape[0]
    return up_gate[:, :width] * s_u * jax.nn.silu(up_gate[:, width:] * s_v)


def rounded(value):
    return lax.optimization_barrier(value.astype(jnp.bfloat16)).astype(jnp.float32)


def attention_forward(query, key, value, mask):
    scale = 1.0 / math.sqrt(query.shape[2])
    score = jnp.einsum("thd,shd->hts", query, key, preferred_element_type=jnp.float32)
    score = jnp.where(mask[None], score * scale, -1e30)
    peak = jnp.max(score, axis=2, keepdims=True)
    raised = jnp.exp(score - peak)
    summed = jnp.sum(raised, axis=2, keepdims=True)
    weight = (raised / summed).astype(jnp.bfloat16)
    result = jnp.einsum("hts,shd->thd", weight, value, preferred_element_type=jnp.float32)
    return result, peak + jnp.log(summed)


def attention_backward(query, key, value, mask, log_total, grad):
    scale = 1.0 / math.sqrt(query.shape[2])
    score = jnp.einsum("thd,shd->hts", query, key, preferred_element_type=jnp.float32)
    score = jnp.where(mask[None], score * scale, -1e30)
    share = jnp.exp(score - log_total)
    grad_value = jnp.einsum(
        "hts,thd->shd", share.astype(jnp.bfloat16), grad, preferred_element_type=jnp.float32
    )
    grad_share = jnp.einsum("thd,shd->hts", grad, value, preferred_element_type=jnp.float32)
    inner = jnp.sum(share * grad_share, axis=2, keepdims=True)
    grad_score = (share * (grad_share - inner)).astype(jnp.bfloat16)
    grad_query = jnp.einsum("hts,shd->thd", grad_score, key, preferred_element_type=jnp.float32)
    grad_key = jnp.einsum("hts,thd->shd", grad_score, query, preferred_element_type=jnp.float32)
    return grad_query * scale, grad_key * scale, grad_value


def low(value):
    return value.astype(jnp.bfloat16)


def product(left, right, dims):
    return lax.dot_general(left, right, (dims, ((), ())), preferred_element_type=jnp.float32)


def local(tokens, lengths, w_qkv, w_out, w_uv, w_down, s_qk, alpha_a, s_u, s_v, alpha_m, cotangent):
    rows = tokens.shape[1]
    model = tokens.shape[2]
    width = model // H
    parts = lax.axis_size("seq")
    shards = lax.axis_size("fsdp")
    mine = lax.axis_index("seq")
    own = H // parts
    deep = w_down.shape[0]
    hidden_all = deep * shards
    hidden_own = hidden_all // parts
    piece = deep // parts
    slot = mine * rows + jnp.arange(rows, dtype=jnp.int32)
    every_slot = jnp.arange(rows * parts, dtype=jnp.int32)
    keep = layout(lengths[0], slot)[2].astype(jnp.float32)[:, None]
    segment, place, _ = layout(lengths[0], every_slot)
    mask = (segment[:, None] == segment[None, :]) & (every_slot[:, None] >= every_slot[None, :])

    def exchange(array, axis):
        return lax.all_to_all(array, "seq", axis, axis, tiled=False)

    def gather(array, axis=0):
        return lax.all_gather(array, "fsdp", axis=axis, tiled=True)

    def spread(array):
        return lax.all_gather(array, "seq", axis=0, tiled=True)

    r_in = w_qkv.shape[0]
    share_qkv = lax.all_to_all(
        w_qkv.reshape(r_in, -1, parts, width), "seq", 2, 1, tiled=True
    ).reshape(r_in, -1)
    share_uv = lax.all_to_all(
        w_uv.reshape(r_in, -1, parts, piece), "seq", 2, 1, tiled=True
    ).reshape(r_in, -1)
    share_down = lax.all_to_all(w_down.reshape(parts, piece, -1), "seq", 0, 2, tiled=True)
    share_down = share_down.reshape(piece, model)
    share_out = lax.all_gather(w_out, "seq", axis=1, tiled=True)
    inputs = spread(tokens[0])
    full_qkv = gather(share_qkv)
    full_out = gather(share_out).reshape(own, parts, width, model)
    full_out = lax.dynamic_index_in_dim(full_out, mine, 1, False).reshape(own * width, model)
    full_uv = gather(share_uv)
    full_down = gather(share_down)
    gains = gather(jnp.concatenate([s_qk, alpha_a, s_u, s_v, alpha_m])[None]).astype(jnp.float32)
    cuts = [s_qk.shape[0], alpha_a.shape[0], s_u.shape[0], s_v.shape[0]]
    edges = [sum(cuts[: i + 1]) for i in range(4)]
    gain_qk, gain_a, gain_u, gain_v, gain_m = jnp.split(gains, edges, axis=1)
    gain_qk = gain_qk.reshape(own, parts, width)
    gain_qk = lax.dynamic_index_in_dim(gain_qk, mine, 1, False).reshape(-1)
    gain_a, gain_m = gain_a.reshape(-1), gain_m.reshape(-1)
    gain_u = lax.dynamic_index_in_dim(gain_u.reshape(shards, parts, piece), mine, 1, False).reshape(-1)
    gain_v = lax.dynamic_index_in_dim(gain_v.reshape(shards, parts, piece), mine, 1, False).reshape(-1)

    mixed = product(inputs, full_qkv, ((1,), (0,)))
    cosine, sine = rotary(place, width)
    span = own * width

    def prepare_local(query_raw, key_raw, scale_qk):
        return prepare(query_raw, key_raw, scale_qk, cosine, sine, own)

    (query_f, key_f), pull_prepare = jax.vjp(
        prepare_local, mixed[:, :span], mixed[:, span : 2 * span], gain_qk
    )
    heads = (rows * parts, own, width)
    query, key = low(query_f).reshape(heads), low(key_f).reshape(heads)
    value = low(mixed[:, 2 * span :]).reshape(heads)
    attended, log_total = attention_forward(query, key, value, mask)
    attended = low(attended.reshape(-1, span))

    def reduce_rows(array):
        return lax.psum_scatter(low(array), "seq", scatter_dimension=0, tiled=True).astype(
            jnp.float32
        )

    branch = reduce_rows(product(attended, full_out, ((1,), (0,))))
    first, pull_first = jax.vjp(blend, tokens[0].astype(jnp.float32), branch, gain_a)
    first_all = spread(low(first))
    up_gate = product(first_all, full_uv, ((1,), (0,)))
    hidden_f, pull_gate = jax.vjp(gated, up_gate, gain_u, gain_v)
    hidden = low(hidden_f)
    down = reduce_rows(product(hidden, full_down, ((1,), (0,))))
    final, pull_last = jax.vjp(blend, first, down, gain_m)
    output = low(final * keep)
    grad_first, grad_down, grad_gain_m = pull_last(cotangent[0].astype(jnp.float32) * keep)
    grad_down = spread(low(grad_down))
    grad_w_down = low(product(hidden, grad_down, ((0,), (0,))))
    grad_hidden = rounded(product(grad_down, full_down, ((1,), (1,))))
    grad_up_gate, grad_gain_u, grad_gain_v = pull_gate(grad_hidden)
    grad_up = low(grad_up_gate)
    grad_w_uv = low(product(first_all, grad_up, ((0,), (0,))))
    grad_first = grad_first + reduce_rows(product(grad_up, full_uv, ((1,), (1,))))
    grad_inputs, grad_branch, grad_gain_a = pull_first(grad_first)
    grad_branch = spread(low(grad_branch))
    grad_w_out = low(product(attended, grad_branch, ((0,), (0,))))
    grad_attended = low(product(grad_branch, full_out, ((1,), (1,)))).reshape(heads)
    grad_query, grad_key, grad_value = attention_backward(
        query, key, value, mask, log_total, grad_attended
    )
    grad_query_raw, grad_key_raw, grad_gain_qk = pull_prepare(
        (rounded(grad_query).reshape(-1, span), rounded(grad_key).reshape(-1, span))
    )
    grad_mixed = low(
        jnp.concatenate([grad_query_raw, grad_key_raw, grad_value.reshape(-1, span)], axis=1)
    )
    grad_w_qkv = low(product(inputs, grad_mixed, ((0,), (0,))))
    grad_inputs = grad_inputs + reduce_rows(product(grad_mixed, full_qkv, ((1,), (1,))))

    def collect(array):
        return lax.psum_scatter(array, "fsdp", scatter_dimension=0, tiled=True)

    part_down = collect(grad_w_down)
    out_down = lax.all_to_all(
        part_down.reshape(1, piece, model), "seq", 2, 0, tiled=True
    ).reshape(deep, -1)
    part_uv = collect(grad_w_uv)
    out_uv = lax.all_to_all(
        part_uv.reshape(r_in, -1, 1, piece), "seq", 1, 2, tiled=True
    ).reshape(r_in, -1)
    placed = jnp.zeros((own, parts, width, model), jnp.bfloat16)
    placed = lax.dynamic_update_slice(
        placed, grad_w_out.reshape(own, 1, width, model), (0, mine, 0, 0)
    )
    part_out = collect(placed.reshape(-1, model))
    out_out = lax.psum_scatter(part_out, "seq", scatter_dimension=1, tiled=True)
    part_qkv = collect(grad_w_qkv)
    out_qkv = lax.all_to_all(
        part_qkv.reshape(r_in, -1, 1, width), "seq", 1, 2, tiled=True
    ).reshape(r_in, -1)

    def widen(array, outer, inner):
        blank = jnp.zeros((outer, parts, inner), jnp.float32)
        array = array.reshape(outer, 1, inner)
        return lax.dynamic_update_slice(blank, array, (0, mine, 0)).reshape(shards, -1)

    gain_sums = jnp.concatenate(
        [
            widen(grad_gain_qk, own, width),
            grad_gain_a.reshape(shards, -1),
            widen(grad_gain_u, shards, piece),
            widen(grad_gain_v, shards, piece),
            grad_gain_m.reshape(shards, -1),
        ],
        axis=1,
    )
    gain_sums = lax.psum(collect(gain_sums), "seq")[0]
    outs = jnp.split(gain_sums, edges)
    return (
        output[None],
        grad_inputs[None],
        out_qkv.astype(jnp.float32),
        out_out.astype(jnp.float32),
        out_uv.astype(jnp.float32),
        out_down.astype(jnp.float32),
        outs[0],
        outs[1],
        outs[2],
        outs[3],
        outs[4],
    )


MESH = pl.DeviceIdType.MESH
TILE = 128
QROWS = 128


def loop(count, body):
    def run(index, carry):
        body(index)
        return carry

    lax.fori_loop(0, count, run, 0)


def at_rows(ref, block, size=TILE):
    return ref.at[pl.ds(pl.multiple_of(block * size, size), size), :]


def cols(block, size=TILE):
    return pl.ds(pl.multiple_of(block * size, size), size)


def mean_last(value):
    return jnp.sum(value, axis=-1, keepdims=True) * (1.0 / value.shape[-1])


class Slots:
    def __init__(self):
        self.count = 0

    def take(self, count):
        base = self.count
        self.count = base + count
        return base


def fused_layer(sizes, *refs):
    (parts, lines, rows, model, deep, own_heads, width) = sizes
    slots_all = parts * rows
    span = own_heads * width
    hid = deep * lines * 2 // parts
    count_in, count_out = len(Inputs._fields), len(Results._fields)
    ins = Inputs(*refs[:count_in])
    outs = Results(*refs[count_in : count_in + count_out])
    table = buffers(sizes)
    rest = refs[count_in + count_out :]
    v = types.SimpleNamespace(**dict(zip(table, rest[: len(table)])))
    send_sem, recv_sem, local_sem = rest[len(table) :]

    s = lax.axis_index("seq")
    f = lax.axis_index("fsdp")
    z = f // 2
    c = f % 2
    other = 1 - c
    mate = (s, 2 * z + other)
    slots = Slots()

    def put(src, dst, target, send_slot, recv_slot):
        pltpu.make_async_remote_copy(
            src_ref=src,
            dst_ref=dst,
            send_sem=send_sem.at[send_slot],
            recv_sem=recv_sem.at[recv_slot],
            device_id=target,
            device_id_type=MESH,
        ).start()

    def descriptor(ref, send_slot, recv_slot):
        return pltpu.make_async_remote_copy(
            src_ref=ref,
            dst_ref=ref,
            send_sem=send_sem.at[send_slot],
            recv_sem=recv_sem.at[recv_slot],
            device_id=mate,
            device_id_type=MESH,
        )

    def landed(ref, slot):
        descriptor(ref, 0, slot).wait_recv()

    def plane(distance):
        return (s + distance) % parts

    def plane_from(distance):
        return (s + parts - distance) % parts

    def line(distance):
        return (z + distance) % lines

    def line_from(distance):
        return (z + lines - distance) % lines

    barrier = pltpu.get_barrier_semaphore()
    for distance in range(1, parts):
        pl.semaphore_signal(barrier, inc=1, device_id=(plane(distance), f), device_id_type=MESH)
    for distance in range(1, 2 * lines):
        target = (s, (f + distance) % (2 * lines))
        pl.semaphore_signal(barrier, inc=1, device_id=target, device_id_type=MESH)

    edges = [0, TILE, 2 * TILE, 2 * TILE + deep, 2 * TILE + 2 * deep, 3 * TILE + 2 * deep]
    own_gains = (ins.s_qk, ins.alpha_a, ins.s_u, ins.s_v, ins.alpha_m)
    for place, own_gain in enumerate(own_gains):
        row = own_gain[...].astype(jnp.float32).reshape(1, -1)
        v.gain_all[f, :, edges[place] : edges[place + 1]] = row
    own_row = pl.ds(pl.multiple_of(s * rows, rows), rows)
    own_w = pl.ds(pl.multiple_of(f * TILE, TILE), TILE)
    part_cols = model // parts
    blocks_uv = 2 * hid // parts // TILE
    wide = blocks_uv * TILE

    def fetch(src, dst, slot):
        pltpu.make_async_copy(src, dst, local_sem.at[slot]).start()

    def deliver(index):
        made = (
            v.made_output,
            v.made_input_grad,
            v.made_back_qkv,
            v.made_back_out,
            v.made_back_uv,
            v.made_back_down,
            v.made_gains,
        )
        return pltpu.make_async_copy(made[index], outs[index], local_sem.at[6 + index])

    def fetched(dst, slot):
        pltpu.make_async_copy(dst, dst, local_sem.at[slot]).wait()

    fetch(ins.w_out, v.wz.at[own_w, :], 0)
    fetch(ins.tokens, v.x_all.at[own_row, :], 1)
    for index in range(blocks_uv):
        fetch(
            ins.w_uv.at[:, pl.ds(pl.multiple_of((index * parts + s) * TILE, TILE), TILE)],
            v.wu.at[own_w, pl.ds(pl.multiple_of(s * wide + index * TILE, TILE), TILE)],
            2,
        )
    fetch(ins.w_down.at[cols(s), :], v.wd.at[own_w, cols(s, part_cols)], 3)
    fetch(ins.cotangent, v.cotangent, 4)
    for index in range(3):
        chunk = 3 * s + index

        @pl.when(chunk % parts == s)
        def _():
            fetch(
                ins.w_qkv.at[:, index * span : (index + 1) * span],
                v.wq.at[own_w, cols(chunk // parts, span)],
                5,
            )

    pl.semaphore_wait(barrier, parts - 1 + 2 * lines - 1)

    qkv_slot = slots.take(1)
    for index in range(3):
        chunk = 3 * s + index
        block = chunk // parts
        target = chunk % parts

        @pl.when(target != s)
        def _():
            put(
                ins.w_qkv.at[:, index * span : (index + 1) * span],
                v.wq.at[own_w, cols(block, span)],
                (target, f),
                BY_PLANE,
                qkv_slot,
            )


    side, across, opposite = s + 1 - 2 * (s % 2), (s + 2) % parts, parts - 1 - s

    def half_of(shared, owner, part):
        start = owner * rows + part * (rows // 2)
        return shared.at[pl.ds(pl.multiple_of(start, rows // 2), rows // 2), :]

    token_slot = slots.take(SHARE)
    for part in range(2):
        mine = ins.tokens.at[part * (rows // 2) : (part + 1) * (rows // 2), :]
        there = half_of(v.x_all, s, part)
        put(mine, there, (side, f), BY_SHARE, token_slot + 2 * part)
        put(mine, there, (across, f), BY_SHARE, token_slot + 2 - part)

    gain_slot = slots.take(1)
    for distance in range(1, 2 * lines):
        put(
            v.gain_all.at[f],
            v.gain_all.at[f],
            (s, (f + distance) % (2 * lines)),
            BY_GAIN,
            gain_slot,
        )

    def plane_share_relay(shared, base, passed=None):
        one, two = half_of(shared, side, 0), half_of(shared, across, 1)
        if passed is not None:
            passed(s, 0)
            passed(s, 1)
        landed(one, base)
        put(one, one, (across, f), BY_SHARE, base + 3)
        landed(two, base + 1)
        put(two, two, (side, f), BY_SHARE, base + 3)
        if passed is not None:
            passed(side, 0)
            passed(across, 1)

    def plane_share_wait(shared, base, passed=None):
        for pieces, slot in (
            (((side, 1), (across, 0)), base + 2),
            (((opposite, 0), (opposite, 1)), base + 3),
        ):
            landed(at_rows(shared, opposite, rows), slot)
            if passed is not None:
                for piece_of in pieces:
                    passed(*piece_of)

    def pass_to_mate(shared, slot):
        def passed(owner, part):
            start = owner * rows + part * (rows // 2)
            here = pl.ds(pl.multiple_of(start, rows // 2), rows // 2)
            there = pl.ds(pl.multiple_of(slots_all + start, rows // 2), rows // 2)
            put(shared.at[here, :], shared.at[there, :], mate, BY_MATE_B, slot)

        return passed

    def shard(ref, chip, core, lanes):
        block = 2 * chip + core
        return ref.at[pl.ds(pl.multiple_of(block * TILE, TILE), TILE), lanes]

    inner = z * (lines - 1 - z) > 0
    outer = z * (lines - 1 - z) == 0

    def line_send(ref, base, lanes=slice(None), twice=True, apart=False):
        own = shard(ref, z, c, lanes)
        for distance in (2, 1, 3):
            target = line(distance)
            near = (z - target) * (z - target) < (lines - 1) * (lines - 1)
            slot = base
            if apart:
                slot = base + distance - 1
            elif distance == 2:
                slot = base + target * (lines - 1 - target) // 2

            @pl.when(near)
            def _():
                put(own, own, (s, 2 * target + c), BY_LINE, slot)

        if twice:
            put(own, own, mate, mate_group(ref), base + 2 + apart)

    def mate_group(ref):
        return BY_WIDE if ref is v.wu else BY_MATE_B if ref is v.wd else BY_MATE_C

    def line_relay(ref, base, lanes=slice(None), apart=False):
        block = shard(ref, line_from(2), c, lanes)

        @pl.when(inner)
        def _():
            landed(block, base + 1)
            slot = base + 2 * z - 2 if apart else base
            put(block, block, (s, 2 * (lines - 1) * (z - 1) + c), BY_LINE, slot)

    def line_arrived(ref, base, lanes=slice(None)):
        pl.when(inner)(lambda: landed(ref.at[: 2 * TILE, lanes], base))
        pl.when(outer)(lambda: landed(ref.at[: 3 * TILE, lanes], base))

    def line_forward(ref, base, lanes=slice(None), apart=False):
        if not apart:
            line_arrived(ref, base, lanes)
        for distance in (1, 3, 2):
            block = shard(ref, line_from(distance), c, lanes)
            if apart and distance == 2:

                @pl.when(outer)
                def _():
                    landed(block, base + 1)

            elif apart:
                landed(block, base + distance - 1)
            put(block, block, mate, mate_group(ref), base + 2 + apart)

    def mate_wait(ref, base, lanes=slice(None), apart=False):
        landed(ref.at[: lines * TILE, lanes], base + 2 + apart)

    wq_slot, wu_slot = (slots.take(4) for _ in range(2))
    count = 4
    piece = model // count
    wd_parts = [
        (slots.take(3), slice(part * piece, (part + 1) * piece)) for part in range(count)
    ]
    wz_slot, wo_slot, out_slot = slots.take(2), slots.take(1), slots.take(1)
    fetched(v.wz.at[own_w, :], 0)
    line_send(v.wz, wz_slot, twice=False)

    landed(v.wq.at[own_w, : 2 * span], qkv_slot)
    fetched(v.wq.at[own_w, :span], 5)
    line_send(v.wq, wq_slot, apart=True)
    lengths = [ins.lengths[0, i] for i in range(ins.lengths.shape[1])]

    def slot_facts(slot):
        end = 0
        member = jnp.zeros(slot.shape, jnp.int32)
        begin = jnp.zeros(slot.shape, jnp.int32)
        for length in lengths[:-1]:
            end = end + length
            after = slot >= end
            member = member + after.astype(jnp.int32)
            begin = jnp.where(after, end, begin)
        valid = member < len(lengths) - 1
        segment = jnp.where(valid, member, len(lengths) - 1 + slot)
        place = jnp.where(valid, slot - begin, 0)
        return segment, place, valid

    lane = lax.broadcasted_iota(jnp.int32, (1, TILE), 1)
    low_half = lane < width
    first_quarter = lane % width < width // 2
    frequency = jnp.exp(
        (lane % (width // 2)).astype(jnp.float32) * (-2.0 * math.log(10000.0) / width)
    )
    turn_sign = jnp.where(first_quarter, -1.0, 1.0)

    def tables(block):
        here = pl.ds(pl.multiple_of(block * TILE, TILE), TILE)
        slot = block * TILE + lax.broadcasted_iota(jnp.int32, (TILE, 1), 0)
        segment, place, _ = slot_facts(slot)
        angle = place.astype(jnp.float32) * frequency
        v.cosine[here, :] = jnp.cos(angle)
        v.sine[here, :] = jnp.sin(angle) * turn_sign
        key_slot = lax.broadcasted_iota(jnp.int32, (1, slots_all), 1)
        key_segment = slot_facts(key_slot)[0]
        kept = (segment == key_segment) & (slot >= key_slot)
        v.bias[here, :] = jnp.where(kept, 0.0, -1e30)

    loop(slots_all // TILE, tables)
    fetched(v.x_all.at[own_row, :], 1)
    plane_share_relay(v.x_all, token_slot)
    uv_slot = slots.take(1)
    for distance in range(1, parts):
        target = plane(distance)
        for index in range(blocks_uv):
            put(
                ins.w_uv.at[:, pl.ds(pl.multiple_of((index * parts + target) * TILE, TILE), TILE)],
                v.wu.at[own_w, pl.ds(pl.multiple_of(s * wide + index * TILE, TILE), TILE)],
                (target, f),
                BY_PLANE,
                uv_slot,
            )

    down_slot = slots.take(1)
    for distance in range(1, parts):
        target = plane(distance)
        put(
            ins.w_down.at[cols(target), :],
            v.wd.at[own_w, cols(s, part_cols)],
            (target, f),
            BY_PLANE,
            down_slot,
        )

    line_relay(v.wz, wz_slot)
    line_relay(v.wq, wq_slot, apart=True)
    plane_share_wait(v.x_all, token_slot)
    line_arrived(v.wz, wz_slot)
    for distance in range(1, parts):
        target = plane(distance)
        rows_out = at_rows(v.wz, 2 * target + c)
        put(
            rows_out,
            v.wo.at[cols(c), cols(s, part_cols)],
            (target, f),
            BY_PLANE,
            out_slot,
        )
    v.wo[cols(c), cols(s, part_cols)] = v.wz[cols(2 * s + c), :]
    fetched(v.wu.at[own_w, cols(s, wide)], 2)
    landed(v.wu.at[own_w, : (parts - 1) * wide], uv_slot)
    line_send(v.wu, wu_slot, apart=True)

    def mate_blocks(name_all, ref, stage, slot):
        for block in range(lines):
            here = slice(block * TILE, (block + 1) * TILE)
            stage[here, :] = name_all[:, cols(2 * block + other)].T
        put(stage, ref.at[:, slots_all:], mate, BY_MATE_C, slot)
        for block in range(lines):
            here = slice(block * TILE, (block + 1) * TILE)
            ref[here, :slots_all] = name_all[:, cols(2 * block + c)].T

    mate_x_slot = slots.take(1)
    mate_blocks(v.x_all, v.turned_x, v.stage_x, mate_x_slot)
    landed(v.gain_all.at[1:], gain_slot)

    def gain(block, offset):
        return v.gain_all[block, :, pl.ds(pl.multiple_of(offset, TILE), TILE)]

    for block in range(2 * lines):
        here = slice(block * TILE, (block + 1) * TILE)
        v.gain_a[:, here] = gain(block, edges[1])
        v.gain_u[:, here] = gain(block, edges[2] + s * TILE)
        v.gain_v[:, here] = gain(block, edges[3] + s * TILE)
        v.gain_m[:, here] = gain(block, edges[4])
    for block in range(span // TILE):
        v.gain_qk[:, block * TILE : (block + 1) * TILE] = gain(span // TILE * s + block, 0)

    line_forward(v.wq, wq_slot, apart=True)
    mate_wait(v.wq, wq_slot, apart=True)

    def mix(index):
        v.raw[:, cols(index, span)] = product(
            v.x_all[...], v.wq[:, cols(index, span)], ((1,), (0,))
        )

    loop(3, mix)

    def swap(value):
        return jnp.where(
            first_quarter,
            pltpu.roll(value, TILE - width // 2, 1),
            pltpu.roll(value, width // 2, 1),
        )

    def head_mean(value):
        one = jnp.sum(jnp.where(low_half, value, 0.0), axis=-1, keepdims=True)
        two = jnp.sum(jnp.where(low_half, 0.0, value), axis=-1, keepdims=True)
        return jnp.where(low_half, one, two) * (1.0 / width)

    pairs = span // TILE
    blocks = slots_all // TILE

    def prepare_block(index):
        here = pl.ds(pl.multiple_of(index % (blocks // 2) * 2 * TILE, 2 * TILE), 2 * TILE)
        group = index // (blocks // 2)
        there = cols(group)
        value = v.raw[here, there]
        turned = value * v.cosine[here, :] + swap(value) * v.sine[here, :]
        inverse = lax.rsqrt(head_mean(turned * turned) + epsilon)
        normed = turned * inverse
        v.normed[here, there] = normed
        v.inverse[here, there] = inverse
        v.qkv[here, there] = low(normed * v.gain_qk[:, cols(group % pairs)])

    loop(pairs * blocks, prepare_block)

    def keep_value(index):
        here = pl.ds(pl.multiple_of(index * TILE, TILE), TILE)
        v.qkv[here, 2 * span :] = low(v.raw[here, 2 * span :])

    loop(blocks, keep_value)
    own_out = v.wo.at[cols(c), :]
    landed(v.wo.at[cols(c), : (parts - 1) * part_cols], out_slot)
    put(own_out, own_out, mate, BY_MATE_D, wo_slot)

    scale = 1.0 / math.sqrt(width)
    halves = (low_half, jnp.logical_not(low_half))

    def attend(pair):
        q_cols, k_cols, v_cols = cols(pair), cols(pairs + pair), cols(2 * pairs + pair)
        for block in range(blocks):
            here = slice(block * TILE, (block + 1) * TILE)
            seen = slice(0, (block + 1) * TILE)
            results = []
            for half in range(2):
                query = jnp.where(halves[half], v.qkv[here, q_cols], 0.0).astype(jnp.bfloat16)
                score = product(query, v.qkv[seen, k_cols], ((1,), (1,))) * scale
                score = score + v.bias[here, seen]
                peak = jnp.max(score, axis=1, keepdims=True)
                raised = jnp.exp(score - peak)
                summed = jnp.sum(raised, axis=1, keepdims=True)
                weight = low(raised / summed)
                results.append(product(weight, v.qkv[seen, v_cols], ((1,), (0,))))
                v.total[2 * pair + half, here, :] = peak + jnp.log(summed)
            v.attended[here, q_cols] = low(jnp.where(low_half, results[0], results[1]))

    loop(pairs, attend)
    mate_att_slot = slots.take(1)
    v.stage_att[...] = v.attended[:, cols(other)].T
    v.turned_att[:, :slots_all] = v.attended[:, cols(c)].T

    put(v.stage_att, v.turned_att.at[:, slots_all:], mate, BY_MATE_D, mate_att_slot)
    landed(v.wo.at[cols(other), :], wo_slot)

    def plane_sum(sums, arrived, base, tile, span_of=(0, count)):
        start, stop = span_of

        def send(index):
            there = cols(index, piece)
            for distance in range(1, parts):
                target = plane(distance)
                put(
                    sums.at[pl.ds(pl.multiple_of(target * rows, rows), rows), there],
                    arrived.at[distance - 1, :, there],
                    (target, f),
                    BY_SUM,
                    base,
                )

        def step(index):
            sums[:, cols(start + index, piece)] = low(tile(start + index))

            @pl.when(index > 0)
            def _():
                send(start + index - 1)

        loop(stop - start, step)
        send(stop - 1)

    def plane_sum_wait(arrived, base):
        landed(arrived, base)

    def plane_total(sums, arrived, here, at):
        total = sums[here, :].astype(jnp.float32)
        for distance in range(1, parts):
            total = total + arrived[distance - 1, at, :].astype(jnp.float32)
        return total

    chunk_rows = 64

    def chunk(index):
        at = pl.ds(pl.multiple_of(index * chunk_rows, chunk_rows), chunk_rows)
        here = pl.ds(pl.multiple_of(s * rows + index * chunk_rows, chunk_rows), chunk_rows)
        return at, here

    def plane_share(shared, base, make):
        def send(index):
            own = shared.at[chunk(index)[1], :]
            part = index // (rows // chunk_rows // 2)
            put(own, own, (side, f), BY_SHARE, base + 2 * part)
            put(own, own, (across, f), BY_SHARE, base + 2 - part)

        def step(index):
            make(index)

            @pl.when(index > 0)
            def _():
                send(index - 1)

        loop(rows // chunk_rows, step)
        send(rows // chunk_rows - 1)

    branch_slot = slots.take(1)
    plane_sum(
        v.part_branch,
        v.got_branch,
        branch_slot,
        lambda index: product(v.attended[...], v.wo[:, cols(index, piece)], ((1,), (0,))),
    )
    line_relay(v.wu, wu_slot, apart=True)
    fetched(v.wd.at[own_w, cols(s, part_cols)], 3)
    landed(v.wd.at[own_w, : (parts - 1) * part_cols], down_slot)
    line_send(v.wd, *wd_parts[0])
    line_send(v.wd, *wd_parts[1])
    plane_sum_wait(v.got_branch, branch_slot)
    line_relay(v.wd, *wd_parts[0])
    line_send(v.wd, *wd_parts[2])

    def blended(base, branch, alpha):
        inverse_branch = lax.rsqrt(mean_last(branch * branch) + epsilon)
        normed = branch * inverse_branch
        mixed = base + alpha * (normed - base)
        inverse = lax.rsqrt(mean_last(mixed * mixed) + epsilon)
        return normed, inverse_branch, mixed * inverse, inverse

    def blended_back(grad, base, alpha, normed, inverse_branch, result, inverse):
        grad_mixed = inverse * (grad - result * mean_last(grad * result))
        grad_normed = alpha * grad_mixed
        grad_branch = inverse_branch * (grad_normed - normed * mean_last(grad_normed * normed))
        grad_alpha = jnp.sum(grad_mixed * (normed - base), axis=0, keepdims=True)
        return grad_mixed - grad_normed, grad_branch, grad_alpha

    def make_first(index):
        at, here = chunk(index)
        base = v.x_all[here, :].astype(jnp.float32)
        normed, inverse_branch, result, inverse = blended(
            base, plane_total(v.part_branch, v.got_branch, here, at), v.gain_a[...]
        )
        v.branch_normed[at, :] = normed
        v.branch_inverse[at, :] = inverse_branch
        v.first[at, :] = result
        v.first_inverse[at, :] = inverse
        v.first_all[here, :] = low(result)

    first_slot = slots.take(SHARE)
    plane_share(v.first_all, first_slot, make_first)
    line_relay(v.wd, *wd_parts[1])
    line_send(v.wd, *wd_parts[3])
    plane_share_relay(v.first_all, first_slot)
    line_relay(v.wd, *wd_parts[2])
    line_forward(v.wu, wu_slot, apart=True)
    mate_wait(v.wu, wu_slot, apart=True)
    plane_share_wait(v.first_all, first_slot)

    def gate_tile(index):
        there = cols(index, 256)
        v.up[:, there] = product(v.first_all[...], v.wu[:, there], ((1,), (0,)))
        v.gate[:, there] = product(
            v.first_all[...],
            v.wu[:, pl.ds(pl.multiple_of(hid + index * 256, 256), 256)],
            ((1,), (0,)),
        )

        def rows_of(block):
            here = pl.ds(pl.multiple_of(block * 64, 64), 64)
            scaled = v.gate[here, there] * v.gain_v[:, there]
            passed = scaled / (1.0 + jnp.exp(-scaled))
            v.hidden[here, there] = low(v.up[here, there] * v.gain_u[:, there] * passed)

        loop(slots_all // 64, rows_of)

    line_relay(v.wd, *wd_parts[3])
    loop(hid // 512, gate_tile)
    line_forward(v.wd, *wd_parts[0])
    loop(hid // 512, lambda index: gate_tile(hid // 512 + index))
    mate_hidden_slot = slots.take(1)
    mate_blocks(v.hidden, v.turned_hidden, v.stage_hidden, mate_hidden_slot)
    mate_first_slot = slots.take(1)
    mate_blocks(v.first_all, v.turned_first, v.stage_first, mate_first_slot)
    down_sum_slot = slots.take(1)

    def down_tile(index):
        return product(v.hidden[...], v.wd[:, cols(index, piece)], ((1,), (0,)))

    line_forward(v.wd, *wd_parts[1])
    for part in range(count):
        mate_wait(v.wd, *wd_parts[part])
        plane_sum(v.part_down, v.got_down, down_sum_slot, down_tile, (part, part + 1))
        if part + 2 < count:
            line_forward(v.wd, *wd_parts[part + 2])
    fetched(v.cotangent, 4)
    plane_sum_wait(v.got_down, down_sum_slot)
    v.grad_a[...] = jnp.zeros_like(v.grad_a)
    v.grad_m[...] = jnp.zeros_like(v.grad_m)

    finish_rows = 128

    def finish(index):
        at = pl.ds(pl.multiple_of(index * finish_rows, finish_rows), finish_rows)
        here = pl.ds(pl.multiple_of(s * rows + index * finish_rows, finish_rows), finish_rows)
        slot = s * rows + index * finish_rows
        slot = slot + lax.broadcasted_iota(jnp.int32, (finish_rows, 1), 0)
        keep = slot_facts(slot)[2].astype(jnp.float32)
        base = v.first[at, :]
        alpha = v.gain_m[...]
        normed, inverse_branch, result, inverse = blended(
            base, plane_total(v.part_down, v.got_down, here, at), alpha
        )
        v.made_output[at, :] = low(result * keep)
        grad = v.cotangent[at, :].astype(jnp.float32) * keep
        grad_base, grad_down, grad_alpha = blended_back(
            grad, base, alpha, normed, inverse_branch, result, inverse
        )
        v.grad_first[at, :] = grad_base
        v.gd[here, :] = low(grad_down)
        v.grad_m[...] += grad_alpha

    loop(rows // finish_rows, finish)
    gd_edges = [0, TILE, *range(piece, model + 1, piece)]
    gd_parts = [slice(*pair) for pair in zip(gd_edges, gd_edges[1:])]
    gd_slot, mate_gd_slot = slots.take(len(gd_parts)), slots.take(len(gd_parts))

    def gd_pass(owner, lanes, slot):
        here = pl.ds(pl.multiple_of(owner * rows, rows), rows)
        there = pl.ds(pl.multiple_of(slots_all + owner * rows, rows), rows)
        put(v.gd.at[here, lanes], v.gd.at[there, lanes], mate, BY_MATE_B, slot)

    for part, lanes in enumerate(gd_parts):
        own = v.gd.at[own_row, lanes]
        for distance in range(1, parts):
            put(own, own, (plane(distance), f), BY_SHARE, gd_slot + part)
        gd_pass(s, lanes, mate_gd_slot + part)
    deliver(0).start()
    first_half = slice(0, slots_all)
    second_half = slice(slots_all, 2 * slots_all)

    ends = (lines - 1) * (1 - z % 2)
    mids = 2 - z // 2
    last = (2 * z + 1) % (lines + 1)
    beside = z + 1 - 2 * (z % 2)

    mid_slot = 2 - z * (lines - 1 - z) // 2

    def line_grad_first(grads, arrived, base, there):
        put(
            grads.at[ends, :, there],
            arrived.at[0, :, there],
            (s, 2 * beside + c),
            BY_GRAD,
            base + 1 - beside * (lines - 1 - beside) // 2,
        )

    def line_grad_mid(grads, arrived, base, there):
        put(
            grads.at[mids, :, there],
            arrived.at[mid_slot, :, there],
            (s, 2 * mids + c),
            BY_GRAD,
            base + 1,
        )

    def line_grad_last(grads, arrived, base, there):
        put(
            grads.at[last, :, there],
            arrived.at[3, :, there],
            (s, 2 * last + c),
            BY_GRAD,
            base + 1,
        )

    def line_grad_rest(grads, arrived, base, chained=False):
        @pl.when(outer)
        def _():
            if chained:
                there = (s, 2 * beside + c)
                put(grads.at[mids], arrived.at[2], there, BY_GRAD, base + 2)
            else:
                line_grad_mid(grads, arrived, base, slice(None))
            line_grad_last(grads, arrived, base, slice(None))

    def weight_grad(turned, right, grads, arrived, columns, base, chained=False):
        def send(index):
            line_grad_first(grads, arrived, base, cols(index, 256))
            if not chained:
                pl.when(inner)(lambda: line_grad_mid(grads, arrived, base, cols(index, 256)))

        def step(index):
            there = cols(index, 256)
            total = product(turned[...], right[:, there], ((1,), (0,)))
            grads[:, :, there] = low(total).reshape(lines, TILE, 256)

            pl.when(index > 0)(lambda: send(index - 1))

        loop(columns // 256, step)
        send(columns // 256 - 1)
        line_grad_rest(grads, arrived, base, chained)

    def combine_into(grads, block, came, columns):
        def tile(index):
            there = cols(index, 256)
            total = grads[block, :, there].astype(jnp.float32)
            grads[block, :, there] = low(total + came[:, there].astype(jnp.float32))

        loop(columns // 256, tile)

    def weight_combine(grads, arrived, columns, base):
        @pl.when(inner)
        def _():
            landed(arrived.at[0], base)
            combine_into(grads, last, arrived.at[0], columns)
            put(grads.at[last], arrived.at[1], (s, 2 * last + c), BY_GRAD, base + 1)

    def weight_combine_mid(grads, arrived, columns, base):
        @pl.when(inner)
        def _():
            landed(arrived.at[2], base + 2)
            combine_into(grads, mids, arrived.at[2], columns)
            put(grads.at[mids], arrived.at[1], (s, 2 * mids + c), BY_GRAD, base + 1)

    mate_gu_slot = slots.take(1)

    def gu_pass(index):
        for lanes in (
            pl.ds(pl.multiple_of(index * 256, 256), 256),
            pl.ds(pl.multiple_of(hid + index * 256, 256), 256),
        ):
            mine, there = v.gu.at[first_half, lanes], v.gu.at[second_half, lanes]
            put(mine, there, mate, BY_WIDE, mate_gu_slot)

    def gate_back(index):
        there = cols(index, 256)
        there_gate = pl.ds(pl.multiple_of(hid + index * 256, 256), 256)
        v.grad_hidden[...] = low(product(v.gd[first_half, :], v.wd[there, :], ((1,), (1,))))
        v.grad_u[:, there] = jnp.zeros((1, 256), jnp.float32)
        v.grad_v[:, there] = jnp.zeros((1, 256), jnp.float32)

        def rows_of(block):
            here = pl.ds(pl.multiple_of(block * 128, 128), 128)
            grad = v.grad_hidden[here, :].astype(jnp.float32)
            up = v.up[here, there]
            gate = v.gate[here, there]
            gain_u = v.gain_u[:, there]
            gain_v = v.gain_v[:, there]
            scaled = gate * gain_v
            squash = 1.0 / (1.0 + jnp.exp(-scaled))
            passed = scaled * squash
            grad_scaled_up = grad * passed
            grad_scaled = grad * (up * gain_u) * (squash + passed * (1.0 - squash))
            v.gu[here, there] = low(grad_scaled_up * gain_u)
            v.gu[here, there_gate] = low(grad_scaled * gain_v)
            v.grad_u[:, there] += jnp.sum(grad_scaled_up * up, axis=0, keepdims=True)
            v.grad_v[:, there] += jnp.sum(grad_scaled * gate, axis=0, keepdims=True)

        loop(slots_all // 128, rows_of)
        pl.when(index > 0)(lambda: gu_pass(index - 1))

    landed(v.turned_x.at[:, second_half], mate_x_slot)
    landed(v.turned_first.at[:, second_half], mate_first_slot)
    landed(v.turned_hidden.at[:, second_half], mate_hidden_slot)
    line_down_slot = slots.take(2)
    for part, lanes in enumerate(gd_parts):
        landed(v.gd.at[: (parts - 1) * rows, lanes], gd_slot + part)
        for distance in range(1, parts):
            gd_pass(plane_from(distance), lanes, mate_gd_slot + part)
        if part == len(gd_parts) - 1:
            loop(1, gate_back)
        landed(v.gd.at[second_half, lanes], mate_gd_slot + part)
        total = product(v.turned_hidden[...], v.gd[:, lanes], ((1,), (0,)))
        v.send_down[:, :, lanes] = low(total).reshape(lines, TILE, -1)
        line_grad_first(v.send_down, v.line_down, line_down_slot, lanes)
        line_grad_mid(v.send_down, v.line_down, line_down_slot, lanes)
        pl.when(outer)(lambda: line_grad_last(v.send_down, v.line_down, line_down_slot, lanes))
    loop(hid // 256 - 1, lambda index: gate_back(index + 1))
    gu_pass(hid // 256 - 1)
    first_sum_slot = slots.take(1)
    plane_sum(
        v.part_first,
        v.got_first,
        first_sum_slot,
        lambda index: product(v.gu[first_half, :], v.wu[cols(index, piece), :], ((1,), (1,))),
    )
    weight_combine(v.send_down, v.line_down, model, line_down_slot)
    landed(v.gu.at[second_half, :], mate_gu_slot)
    line_uv_slot = slots.take(2)
    weight_grad(v.turned_first, v.gu, v.send_uv, v.line_uv, 2 * hid, line_uv_slot)
    plane_sum_wait(v.got_first, first_sum_slot)

    def back_first(index):
        at, here = chunk(index)
        grad = v.grad_first[at, :] + plane_total(v.part_first, v.got_first, here, at)
        grad_base, grad_branch, grad_alpha = blended_back(
            grad,
            v.x_all[here, :].astype(jnp.float32),
            v.gain_a[...],
            v.branch_normed[at, :],
            v.branch_inverse[at, :],
            v.first[at, :],
            v.first_inverse[at, :],
        )
        v.grad_tokens[at, :] = grad_base
        v.gb[here, :] = low(grad_branch)
        v.grad_a[...] += grad_alpha

    gb_slot = slots.take(SHARE)
    plane_share(v.gb, gb_slot, back_first)
    mate_gb_slot = slots.take(1)
    passed_gb = pass_to_mate(v.gb, mate_gb_slot)
    plane_share_relay(v.gb, gb_slot, passed_gb)
    plane_share_wait(v.gb, gb_slot, passed_gb)

    v.grad_att[...] = low(product(v.gb[first_half, :], v.wo[...], ((1,), (1,))))
    weight_combine(v.send_uv, v.line_uv, 2 * hid, line_uv_slot)
    v.grad_qkv[...] = jnp.zeros_like(v.grad_qkv)

    def attend_back(pair):
        q_cols, k_cols, v_cols = cols(pair), cols(pairs + pair), cols(2 * pairs + pair)
        for block in range(blocks):
            here = slice(block * TILE, (block + 1) * TILE)
            seen = slice(0, (block + 1) * TILE)
            results = []
            for half in range(2):
                query = jnp.where(halves[half], v.qkv[here, q_cols], 0.0).astype(jnp.bfloat16)
                grad = jnp.where(halves[half], v.grad_att[here, q_cols], 0.0)
                grad = grad.astype(jnp.bfloat16)
                score = product(query, v.qkv[seen, k_cols], ((1,), (1,))) * scale
                score = score + v.bias[here, seen]
                share = jnp.exp(score - v.total[2 * pair + half, here, :])
                grad_share = product(grad, v.qkv[seen, v_cols], ((1,), (1,)))
                inner = jnp.sum(share * grad_share, axis=1, keepdims=True)
                grad_score = low(share * (grad_share - inner))
                results.append(product(grad_score, v.qkv[seen, k_cols], ((1,), (0,))))
                v.grad_qkv[seen, v_cols] += product(low(share), grad, ((0,), (0,)))
                v.grad_qkv[seen, k_cols] += product(grad_score, query, ((0,), (0,)))
            v.grad_qkv[here, q_cols] = jnp.where(low_half, results[0], results[1])

    loop(pairs, attend_back)
    landed(v.turned_att.at[:, second_half], mate_att_slot)
    landed(v.gb.at[second_half, :], mate_gb_slot)
    line_out_slot = slots.take(3)
    part_out_slot = slots.take(1)

    def out_tile(index):
        there = cols(index, 256)
        v.send_out[:, there] = low(product(v.turned_att[...], v.gb[:, there], ((1,), (0,))))

    loop(model // 256, out_tile)
    for distance in range(1, parts):
        target = plane(distance)
        put(
            v.send_out.at[:, cols(target, part_cols)],
            v.send_wo.at[s],
            (target, f),
            BY_PLANE,
            part_out_slot,
        )
    v.send_wo[s] = v.send_out[:, cols(s, part_cols)]
    v.grad_qk[...] = jnp.zeros_like(v.grad_qk)

    def prepare_back(index):
        here = pl.ds(pl.multiple_of(index % (blocks // 2) * 2 * TILE, 2 * TILE), 2 * TILE)
        group = index // (blocks // 2)
        there = cols(group)
        pair = cols(group % pairs)
        grad = low(v.grad_qkv[here, there] * scale).astype(jnp.float32)
        normed = v.normed[here, there]
        v.grad_qk[:, pair] += jnp.sum(grad * normed, axis=0, keepdims=True)
        grad = grad * v.gain_qk[:, pair]
        grad = v.inverse[here, there] * (grad - normed * head_mean(grad * normed))
        back = grad * v.cosine[here, :] - swap(grad) * v.sine[here, :]
        v.gm[here, there] = low(back)

    def value_back(index):
        here = pl.ds(pl.multiple_of(index * TILE, TILE), TILE)
        v.gm[here, 2 * span :] = low(v.grad_qkv[here, 2 * span :])

    loop(blocks, value_back)
    mate_gm_slot = slots.take(1)

    def gm_pass(lanes):
        put(v.gm.at[first_half, lanes], v.gm.at[second_half, lanes], mate, BY_MATE_C, mate_gm_slot)

    gm_pass(slice(2 * span, 3 * span))
    loop(pairs * blocks // 2, prepare_back)
    gm_pass(slice(0, span))
    loop(pairs * blocks // 2, lambda index: prepare_back(pairs * blocks // 2 + index))
    gm_pass(slice(span, 2 * span))

    v.gain_part[...] = jnp.zeros_like(v.gain_part)
    for block in range(2 * lines):
        here = slice(block * TILE, (block + 1) * TILE)
        local_pair = block % (span // TILE) * TILE
        qk = v.grad_qk[:, local_pair : local_pair + TILE]
        mine = (s == block // (span // TILE)).astype(jnp.float32)
        v.gain_part[block, :, edges[0] : edges[1]] = qk * mine
        v.gain_part[block, :, edges[1] : edges[2]] = v.grad_a[:, here]
        v.gain_part[block, :, cols(edges[2] // TILE + s)] = v.grad_u[:, here]
        v.gain_part[block, :, cols(edges[3] // TILE + s)] = v.grad_v[:, here]
        v.gain_part[block, :, edges[4] : edges[5]] = v.grad_m[:, here]

    inputs_slot = slots.take(1)
    plane_sum(
        v.part_inputs,
        v.got_inputs,
        inputs_slot,
        lambda index: product(v.gm[first_half, :], v.wq[cols(index, piece), :], ((1,), (1,))),
    )
    gain_line_slot = slots.take(1)
    for distance in range(1, 2 * lines):
        target = (f + distance) % (2 * lines)
        put(
            v.gain_part.at[target],
            v.gain_got.at[distance - 1],
            (s, target),
            BY_GAIN_LINE,
            gain_line_slot,
        )
    landed(v.gm.at[second_half, :], mate_gm_slot)
    line_qkv_slot = slots.take(3)
    landed(v.send_wo.at[: parts - 1], part_out_slot)
    line_grad_first(v.send_wo, v.line_wo, line_out_slot, slice(None))
    weight_grad(v.turned_x, v.gm, v.send_qkv, v.line_qkv, 3 * span, line_qkv_slot, True)
    line_grad_rest(v.send_wo, v.line_wo, line_out_slot, True)

    def line_total(grads, arrived, done, columns, base, chained=False):
        def add(slots_in):
            landed(arrived.at[: len(slots_in)], base + 1)

            def tile(index):
                there = cols(index, 256)
                total = grads[z, :, there].astype(jnp.float32)
                for slot in slots_in:
                    total = total + arrived[slot, :, there].astype(jnp.float32)
                done[:, there] = low(total)

            loop(columns // 256, tile)

        pl.when(outer)(lambda: add((0, 1)))
        pl.when(inner)(lambda: add((1, 3) if chained else (1, 2, 3)))

    line_total(v.send_down, v.line_down, v.done_down, model, line_down_slot)
    back_down_slot = slots.take(1)
    for distance in range(1, parts):
        target = plane(distance)
        put(
            v.done_down.at[:, cols(target, part_cols)],
            v.made_back_down.at[cols(s), :],
            (target, f),
            BY_PLANE,
            back_down_slot,
        )
    v.made_back_down[cols(s), :] = v.done_down[:, cols(s, part_cols)]

    line_total(v.send_uv, v.line_uv, v.done_uv, 2 * hid, line_uv_slot)
    back_uv_slot = slots.take(1)
    for distance in range(1, parts):
        target = plane(distance)
        for index in range(blocks_uv):
            put(
                v.done_uv.at[:, pl.ds(pl.multiple_of(target * wide + index * TILE, TILE), TILE)],
                v.made_back_uv.at[s, :, index * TILE : (index + 1) * TILE],
                (target, f),
                BY_PLANE,
                back_uv_slot,
            )
    v.made_back_uv[s] = v.done_uv[:, cols(s, wide)]

    weight_combine(v.send_wo, v.line_wo, part_cols, line_out_slot)
    weight_combine(v.send_qkv, v.line_qkv, 3 * span, line_qkv_slot)
    plane_sum_wait(v.got_inputs, inputs_slot)

    def finish_inputs(index):
        at, here = chunk(index)
        v.made_input_grad[at, :] = v.grad_tokens[at, :] + plane_total(v.part_inputs, v.got_inputs, here, at)

    loop(rows // chunk_rows, finish_inputs)
    deliver(1).start()

    weight_combine_mid(v.send_qkv, v.line_qkv, 3 * span, line_qkv_slot)
    gain_plane_slot = slots.take(1)
    landed(v.gain_got, gain_line_slot)
    total = v.gain_part[f]
    for distance in range(1, 2 * lines):
        total = total + v.gain_got[distance - 1]
    v.gain_sum[s] = total
    for distance in range(1, parts):
        put(
            v.gain_sum.at[s],
            v.gain_sum.at[s],
            (plane(distance), f),
            BY_GAIN_PLANE,
            gain_plane_slot,
        )

    weight_combine_mid(v.send_wo, v.line_wo, part_cols, line_out_slot)
    line_total(v.send_qkv, v.line_qkv, v.done_qkv, 3 * span, line_qkv_slot, True)
    back_qkv_slot = slots.take(1)
    for block in range(3):
        chunk_of = parts * block + s
        target = chunk_of // 3
        index = chunk_of % 3
        source = v.done_qkv.at[:, block * span : (block + 1) * span]

        @pl.when(target == s)
        def _():
            v.made_back_qkv[index] = source[...]

        @pl.when(target != s)
        def _():
            put(
                source,
                v.made_back_qkv.at[index],
                (target, f),
                BY_PLANE,
                back_qkv_slot,
            )


    landed(v.made_back_down.at[: (parts - 1) * TILE, :], back_down_slot)
    deliver(5).start()
    landed(v.made_back_uv.at[: parts - 1], back_uv_slot)
    deliver(4).start()
    landed(v.gain_sum.at[: parts - 1], gain_plane_slot)
    total = v.gain_sum[0]
    for source in range(1, parts):
        total = total + v.gain_sum[source]
    v.made_gains[...] = total
    deliver(6).start()
    landed(v.made_back_qkv.at[:2], back_qkv_slot)
    deliver(2).start()

    line_total(v.send_wo, v.line_wo, v.made_back_out, part_cols, line_out_slot, True)
    deliver(3).start()

    def sent(group, size):
        ref = v.wu.at[: size // (2 * hid), :]
        descriptor(ref, group, 0).wait_send()

    a_weight = TILE * (3 * span + 2 * hid + model + part_cols)
    sent(BY_SHARE, 4 * 6 * (rows // 2) * model)
    sent(BY_SUM, 4 * (parts - 1) * rows * model)
    sent(BY_WIDE, lines * TILE * 2 * hid + slots_all * 2 * hid)
    sent(BY_MATE_B, 2 * slots_all * model + lines * TILE * model)
    sent(BY_MATE_C, (3 * lines * TILE + 3 * span) * slots_all + lines * TILE * 3 * span)
    sent(BY_MATE_D, TILE * slots_all + TILE * model)
    pl.when(inner)(lambda: sent(BY_LINE, 4 * a_weight))
    pl.when(outer)(lambda: sent(BY_LINE, 2 * a_weight))
    sent(BY_GRAD, 3 * a_weight)
    sent(BY_PLANE, 2 * (2 * TILE * span + (parts - 1) * TILE * (wide + 2 * part_cols)))
    descriptor(v.gain_got, BY_GAIN, 0).wait_send()
    descriptor(v.gain_got, BY_GAIN_LINE, 0).wait_send()
    descriptor(v.gain_sum.at[: parts - 1], BY_GAIN_PLANE, 0).wait_send()
    for index in range(len(Results._fields)):
        deliver(index).wait()
    assert slots.count <= SLOTS_MOST, slots.count


SLOTS_MOST = 77
SHARE = 4
BY_SHARE, BY_SUM, BY_WIDE, BY_MATE_B, BY_MATE_C, BY_MATE_D = range(6)
BY_LINE, BY_GRAD, BY_PLANE, BY_GAIN, BY_GAIN_LINE, BY_GAIN_PLANE = range(6, 12)


class Inputs(typing.NamedTuple):
    tokens: typing.Any
    lengths: typing.Any
    w_qkv: typing.Any
    w_out: typing.Any
    w_uv: typing.Any
    w_down: typing.Any
    s_qk: typing.Any
    alpha_a: typing.Any
    s_u: typing.Any
    s_v: typing.Any
    alpha_m: typing.Any
    cotangent: typing.Any


class Results(typing.NamedTuple):
    output: typing.Any
    input_grad: typing.Any
    back_qkv: typing.Any
    back_out: typing.Any
    back_uv: typing.Any
    back_down: typing.Any
    gains: typing.Any


def buffers(sizes):
    (parts, lines, rows, model, deep, own_heads, width) = sizes
    every = parts * rows
    span = own_heads * width
    hid = deep * lines * 2 // parts
    half = lines * TILE
    gains = 3 * TILE + 2 * deep
    bf16, f32 = jnp.bfloat16, jnp.float32
    return dict(
        wq=((model, 3 * span), bf16),
        wo=((span, model), bf16),
        wz=((model, model // parts), bf16),
        cotangent=((rows, model), bf16),
        made_output=((rows, model), bf16),
        made_input_grad=((rows, model), f32),
        made_back_qkv=((3, TILE, span), bf16),
        made_back_out=((TILE, model // parts), bf16),
        made_back_uv=((parts, TILE, 2 * hid // parts), bf16),
        made_back_down=((deep, model // parts), bf16),
        made_gains=((1, gains), f32),
        wu=((model, 2 * hid), bf16),
        wd=((hid, model), bf16),
        gain_all=((2 * lines, 1, gains), f32),
        gain_a=((1, model), f32),
        gain_m=((1, model), f32),
        gain_u=((1, hid), f32),
        gain_v=((1, hid), f32),
        gain_qk=((1, span), f32),
        x_all=((every, model), bf16),
        first_all=((every, model), bf16),
        gd=((2 * every, model), bf16),
        gb=((2 * every, model), bf16),
        cosine=((every, TILE), f32),
        sine=((every, TILE), f32),
        bias=((every, every), f32),
        raw=((every, 3 * span), f32),
        normed=((every, 2 * span), f32),
        inverse=((every, 2 * span), f32),
        qkv=((every, 3 * span), bf16),
        total=((own_heads, every, 1), f32),
        attended=((every, span), bf16),
        branch_normed=((rows, model), f32),
        branch_inverse=((rows, 1), f32),
        first=((rows, model), f32),
        first_inverse=((rows, 1), f32),
        up=((every, hid), f32),
        gate=((every, hid), f32),
        hidden=((every, hid), bf16),
        grad_hidden=((every, 256), bf16),
        gu=((2 * every, 2 * hid), bf16),
        grad_first=((rows, model), f32),
        grad_tokens=((rows, model), f32),
        grad_att=((every, span), bf16),
        grad_qkv=((every, 3 * span), f32),
        gm=((2 * every, 3 * span), bf16),
        grad_a=((1, model), f32),
        grad_m=((1, model), f32),
        grad_u=((1, hid), f32),
        grad_v=((1, hid), f32),
        grad_qk=((1, span), f32),
        gain_part=((2 * lines, 1, gains), f32),
        gain_got=((2 * lines - 1, 1, gains), f32),
        gain_sum=((parts, 1, gains), f32),
        turned_x=((half, 2 * every), bf16),
        turned_first=((half, 2 * every), bf16),
        turned_hidden=((half, 2 * every), bf16),
        turned_att=((TILE, 2 * every), bf16),
        stage_x=((half, every), bf16),
        stage_first=((half, every), bf16),
        stage_hidden=((half, every), bf16),
        stage_att=((TILE, every), bf16),
        send_out=((TILE, model), bf16),
        send_wo=((lines, TILE, model // parts), bf16),
        line_wo=((4, TILE, model // parts), bf16),
        part_branch=((every, model), bf16),
        got_branch=((parts - 1, rows, model), bf16),
        part_down=((every, model), bf16),
        got_down=((parts - 1, rows, model), bf16),
        part_first=((every, model), bf16),
        got_first=((parts - 1, rows, model), bf16),
        part_inputs=((every, model), bf16),
        got_inputs=((parts - 1, rows, model), bf16),
        send_qkv=((lines, TILE, 3 * span), bf16),
        line_qkv=((4, TILE, 3 * span), bf16),
        done_qkv=((TILE, 3 * span), bf16),
        send_uv=((lines, TILE, 2 * hid), bf16),
        line_uv=((4, TILE, 2 * hid), bf16),
        done_uv=((TILE, 2 * hid), bf16),
        send_down=((lines, TILE, model), bf16),
        line_down=((4, TILE, model), bf16),
        done_down=((TILE, model), bf16),
    )


def place_results(sizes, *refs):
    (parts, lines, rows, model, deep, own_heads, width) = sizes
    count = len(Results._fields)
    got = Results(*refs[:count])
    (output, inputs, qkv, out, uv, down, *gains) = refs[count:]
    output[...] = got.output[...]
    inputs[...] = got.input_grad[...]
    span = own_heads * width
    for index in range(qkv.shape[1] // span):
        qkv[:, index * span : (index + 1) * span] = got.back_qkv[index].astype(jnp.float32)
    out[...] = got.back_out[...].astype(jnp.float32)
    for source in range(parts):
        for index in range(uv.shape[1] // (parts * TILE)):
            there = (index * parts + source) * TILE
            here = slice(index * TILE, (index + 1) * TILE)
            uv[:, there : there + TILE] = got.back_uv[source, :, here].astype(jnp.float32)
    down[...] = got.back_down[...].astype(jnp.float32)
    start = 0
    for gain in gains:
        stop = start + gain.shape[-1]
        gain[...] = got.gains[:, start:stop]
        start = stop


def fused(sizes):
    (parts, lines, rows, model, deep, own_heads, width) = sizes
    span = own_heads * width
    hid = deep * lines * 2 // parts

    def run(tokens, lengths, w_qkv, w_out, w_uv, w_down, *others):
        gains, cotangent = others[:5], others[5]
        f32, bf16 = jnp.float32, jnp.bfloat16
        struct = jax.ShapeDtypeStruct
        middle = Results(
            struct(tokens.shape[1:], bf16),
            struct(tokens.shape[1:], f32),
            struct((3, TILE, span), bf16),
            struct(w_out.shape, bf16),
            struct((parts, TILE, 2 * hid // parts), bf16),
            struct(w_down.shape, bf16),
            struct((1, sum(g.shape[0] for g in gains)), f32),
        )
        shapes = [
            struct(tokens.shape[1:], bf16),
            struct(tokens.shape[1:], f32),
            *(struct(w.shape, f32) for w in (w_qkv, w_out, w_uv, w_down)),
            *(struct((1, g.shape[0]), f32) for g in gains),
        ]
        vmem = pl.BlockSpec(memory_space=pltpu.VMEM)
        specs = [vmem] * len(Inputs._fields)
        for place in (0, 2, 3, 4, 5, 11):
            specs[place] = pl.BlockSpec(memory_space=pl.ANY)
        specs[1] = pl.BlockSpec(memory_space=pltpu.SMEM)
        scratch = [pltpu.VMEM(shape, kind) for shape, kind in buffers(sizes).values()]
        found = pl.pallas_call(
            functools.partial(fused_layer, sizes),
            out_shape=list(middle),
            in_specs=specs,
            out_specs=[pl.BlockSpec(memory_space=pl.ANY)] * len(middle),
            scratch_shapes=[
                *scratch,
                pltpu.SemaphoreType.DMA((12,)),
                pltpu.SemaphoreType.DMA((SLOTS_MOST,)),
                pltpu.SemaphoreType.DMA((6 + len(Results._fields),)),
            ],
            compiler_params=pltpu.CompilerParams(
                collective_id=0, has_side_effects=True, vmem_limit_bytes=67043328
            ),
            name="fused_layer",
        )(
            tokens[0],
            lengths,
            w_qkv,
            w_out,
            w_uv,
            w_down,
            *gains,
            cotangent[0],
        )
        outs = pl.pallas_call(
            functools.partial(place_results, sizes),
            out_shape=shapes,
            in_specs=[vmem] * len(middle),
            out_specs=[vmem] * len(shapes),
            compiler_params=pltpu.CompilerParams(vmem_limit_bytes=67043328),
            name="place_results",
        )(*found)
        return (
            outs[0][None],
            outs[1][None],
            *outs[2:6],
            *(g.reshape(-1) for g in outs[6:]),
        )

    return run


def choose(parts, shards):
    def run(*args):
        tokens, w_qkv, w_down = args[0], args[2], args[5]
        rows, model = tokens.shape[1:]
        deep, width = w_down.shape[0], model // H
        fits = shards == 2 * parts and rows == TILE and w_qkv.shape[0] == TILE
        fits = fits and deep == parts * TILE and 2 * width == TILE and H == 4 * parts
        if not fits:
            return local(*args)
        return fused((parts, shards // 2, rows, model, deep, H // parts, width))(*args)

    return run


def solution(mesh):
    return jax.shard_map(
        choose(mesh.shape["seq"], mesh.shape["fsdp"]),
        mesh=mesh,
        in_specs=(
            P("fsdp", "seq", None),
            P("fsdp", None),
            P("fsdp", "seq"),
            P("fsdp", "seq"),
            P("fsdp", "seq"),
            P("fsdp", "seq"),
            P("fsdp"),
            P("fsdp"),
            P("fsdp"),
            P("fsdp"),
            P("fsdp"),
            P("fsdp", "seq", None),
        ),
        out_specs=(
            P("fsdp", "seq", None),
            P("fsdp", "seq", None),
            P("fsdp", "seq"),
            P("fsdp", "seq"),
            P("fsdp", "seq"),
            P("fsdp", "seq"),
            P("fsdp"),
            P("fsdp"),
            P("fsdp"),
            P("fsdp"),
            P("fsdp"),
        ),
        check_vma=False,
    )
```

```python
import functools
import math
import types
import typing

import jax
import jax.numpy as jnp
from jax import lax
from jax.experimental import pallas as pl
from jax.experimental.pallas import tpu as pltpu
from jax.sharding import PartitionSpec as P

H = 16


epsilon = 1e-06


def layout(lengths_row, slot):
    columns = lengths_row.shape[0]
    ends = jnp.cumsum(lengths_row)
    starts = ends - lengths_row
    before = (slot[:, None] >= ends[None, : columns - 1]).astype(jnp.int32)
    member = jnp.sum(before, axis=1)
    picked = member[:, None] == jnp.arange(columns, dtype=jnp.int32)[None, :]
    begin = jnp.sum(jnp.where(picked, starts[None, :], 0), axis=1)
    valid = member < columns - 1
    segment = jnp.where(valid, member, columns - 1 + slot)
    place = jnp.where(valid, slot - begin, 0)
    return (segment, place, valid)


def rotary(place, width):
    half = width // 2
    frequency = jnp.exp(jnp.arange(half, dtype=jnp.float32) * (-2.0 * math.log(10000.0) / width))
    angle = place.astype(jnp.float32)[:, None] * frequency[None, :]
    return (jnp.cos(angle)[:, None, :], jnp.sin(angle)[:, None, :])


def unit_rows(value):
    return value * lax.rsqrt(jnp.mean(value * value, axis=-1, keepdims=True) + epsilon)


def turn_heads(value, cosine, sine):
    half = value.shape[-1] // 2
    first = value[..., :half]
    second = value[..., half:]
    return jnp.concatenate(
        [first * cosine - second * sine, second * cosine + first * sine], axis=-1
    )


def prepare(query_raw, key_raw, s_qk, cosine, sine, heads):
    rows = query_raw.shape[0]
    scales = s_qk.reshape(heads, -1)

    def normed(raw):
        shaped = raw.reshape(rows, heads, -1)
        return (unit_rows(turn_heads(shaped, cosine, sine)) * scales).reshape(rows, -1)

    return (normed(query_raw), normed(key_raw))


def blend(base, branch, alpha):
    return unit_rows(base + alpha * (unit_rows(branch) - base))


def gated(up_gate, s_u, s_v):
    width = s_u.shape[0]
    return up_gate[:, :width] * s_u * jax.nn.silu(up_gate[:, width:] * s_v)


def rounded(value):
    return lax.optimization_barrier(value.astype(jnp.bfloat16)).astype(jnp.float32)


def attention_forward(query, key, value, mask):
    scale = 1.0 / math.sqrt(query.shape[2])
    score = jnp.einsum("thd,shd->hts", query, key, preferred_element_type=jnp.float32)
    score = jnp.where(mask[None], score * scale, -1e30)
    peak = jnp.max(score, axis=2, keepdims=True)
    raised = jnp.exp(score - peak)
    summed = jnp.sum(raised, axis=2, keepdims=True)
    weight = (raised / summed).astype(jnp.bfloat16)
    result = jnp.einsum("hts,shd->thd", weight, value, preferred_element_type=jnp.float32)
    return result, peak + jnp.log(summed)


def attention_backward(query, key, value, mask, log_total, grad):
    scale = 1.0 / math.sqrt(query.shape[2])
    score = jnp.einsum("thd,shd->hts", query, key, preferred_element_type=jnp.float32)
    score = jnp.where(mask[None], score * scale, -1e30)
    share = jnp.exp(score - log_total)
    grad_value = jnp.einsum(
        "hts,thd->shd", share.astype(jnp.bfloat16), grad, preferred_element_type=jnp.float32
    )
    grad_share = jnp.einsum("thd,shd->hts", grad, value, preferred_element_type=jnp.float32)
    inner = jnp.sum(share * grad_share, axis=2, keepdims=True)
    grad_score = (share * (grad_share - inner)).astype(jnp.bfloat16)
    grad_query = jnp.einsum("hts,shd->thd", grad_score, key, preferred_element_type=jnp.float32)
    grad_key = jnp.einsum("hts,thd->shd", grad_score, query, preferred_element_type=jnp.float32)
    return grad_query * scale, grad_key * scale, grad_value


def low(value):
    return value.astype(jnp.bfloat16)


def product(left, right, dims):
    return lax.dot_general(left, right, (dims, ((), ())), preferred_element_type=jnp.float32)


def local(tokens, lengths, w_qkv, w_out, w_uv, w_down, s_qk, alpha_a, s_u, s_v, alpha_m, cotangent):
    rows = tokens.shape[1]
    model = tokens.shape[2]
    width = model // H
    parts = lax.axis_size("seq")
    shards = lax.axis_size("fsdp")
    mine = lax.axis_index("seq")
    own = H // parts
    deep = w_down.shape[0]
    hidden_all = deep * shards
    hidden_own = hidden_all // parts
    piece = deep // parts
    slot = mine * rows + jnp.arange(rows, dtype=jnp.int32)
    every_slot = jnp.arange(rows * parts, dtype=jnp.int32)
    keep = layout(lengths[0], slot)[2].astype(jnp.float32)[:, None]
    segment, place, _ = layout(lengths[0], every_slot)
    mask = (segment[:, None] == segment[None, :]) & (every_slot[:, None] >= every_slot[None, :])

    def exchange(array, axis):
        return lax.all_to_all(array, "seq", axis, axis, tiled=False)

    def gather(array, axis=0):
        return lax.all_gather(array, "fsdp", axis=axis, tiled=True)

    def spread(array):
        return lax.all_gather(array, "seq", axis=0, tiled=True)

    r_in = w_qkv.shape[0]
    share_qkv = lax.all_to_all(
        w_qkv.reshape(r_in, -1, parts, width), "seq", 2, 1, tiled=True
    ).reshape(r_in, -1)
    share_uv = lax.all_to_all(
        w_uv.reshape(r_in, -1, parts, piece), "seq", 2, 1, tiled=True
    ).reshape(r_in, -1)
    share_down = lax.all_to_all(w_down.reshape(parts, piece, -1), "seq", 0, 2, tiled=True)
    share_down = share_down.reshape(piece, model)
    share_out = lax.all_gather(w_out, "seq", axis=1, tiled=True)
    inputs = spread(tokens[0])
    full_qkv = gather(share_qkv)
    full_out = gather(share_out).reshape(own, parts, width, model)
    full_out = lax.dynamic_index_in_dim(full_out, mine, 1, False).reshape(own * width, model)
    full_uv = gather(share_uv)
    full_down = gather(share_down)
    gains = gather(jnp.concatenate([s_qk, alpha_a, s_u, s_v, alpha_m])[None]).astype(jnp.float32)
    cuts = [s_qk.shape[0], alpha_a.shape[0], s_u.shape[0], s_v.shape[0]]
    edges = [sum(cuts[: i + 1]) for i in range(4)]
    gain_qk, gain_a, gain_u, gain_v, gain_m = jnp.split(gains, edges, axis=1)
    gain_qk = gain_qk.reshape(own, parts, width)
    gain_qk = lax.dynamic_index_in_dim(gain_qk, mine, 1, False).reshape(-1)
    gain_a, gain_m = gain_a.reshape(-1), gain_m.reshape(-1)
    gain_u = lax.dynamic_index_in_dim(gain_u.reshape(shards, parts, piece), mine, 1, False).reshape(-1)
    gain_v = lax.dynamic_index_in_dim(gain_v.reshape(shards, parts, piece), mine, 1, False).reshape(-1)

    mixed = product(inputs, full_qkv, ((1,), (0,)))
    cosine, sine = rotary(place, width)
    span = own * width

    def prepare_local(query_raw, key_raw, scale_qk):
        return prepare(query_raw, key_raw, scale_qk, cosine, sine, own)

    (query_f, key_f), pull_prepare = jax.vjp(
        prepare_local, mixed[:, :span], mixed[:, span : 2 * span], gain_qk
    )
    heads = (rows * parts, own, width)
    query, key = low(query_f).reshape(heads), low(key_f).reshape(heads)
    value = low(mixed[:, 2 * span :]).reshape(heads)
    attended, log_total = attention_forward(query, key, value, mask)
    attended = low(attended.reshape(-1, span))

    def reduce_rows(array):
        return lax.psum_scatter(low(array), "seq", scatter_dimension=0, tiled=True).astype(
            jnp.float32
        )

    branch = reduce_rows(product(attended, full_out, ((1,), (0,))))
    first, pull_first = jax.vjp(blend, tokens[0].astype(jnp.float32), branch, gain_a)
    first_all = spread(low(first))
    up_gate = product(first_all, full_uv, ((1,), (0,)))
    hidden_f, pull_gate = jax.vjp(gated, up_gate, gain_u, gain_v)
    hidden = low(hidden_f)
    down = reduce_rows(product(hidden, full_down, ((1,), (0,))))
    final, pull_last = jax.vjp(blend, first, down, gain_m)
    output = low(final * keep)
    grad_first, grad_down, grad_gain_m = pull_last(cotangent[0].astype(jnp.float32) * keep)
    grad_down = spread(low(grad_down))
    grad_w_down = low(product(hidden, grad_down, ((0,), (0,))))
    grad_hidden = rounded(product(grad_down, full_down, ((1,), (1,))))
    grad_up_gate, grad_gain_u, grad_gain_v = pull_gate(grad_hidden)
    grad_up = low(grad_up_gate)
    grad_w_uv = low(product(first_all, grad_up, ((0,), (0,))))
    grad_first = grad_first + reduce_rows(product(grad_up, full_uv, ((1,), (1,))))
    grad_inputs, grad_branch, grad_gain_a = pull_first(grad_first)
    grad_branch = spread(low(grad_branch))
    grad_w_out = low(product(attended, grad_branch, ((0,), (0,))))
    grad_attended = low(product(grad_branch, full_out, ((1,), (1,)))).reshape(heads)
    grad_query, grad_key, grad_value = attention_backward(
        query, key, value, mask, log_total, grad_attended
    )
    grad_query_raw, grad_key_raw, grad_gain_qk = pull_prepare(
        (rounded(grad_query).reshape(-1, span), rounded(grad_key).reshape(-1, span))
    )
    grad_mixed = low(
        jnp.concatenate([grad_query_raw, grad_key_raw, grad_value.reshape(-1, span)], axis=1)
    )
    grad_w_qkv = low(product(inputs, grad_mixed, ((0,), (0,))))
    grad_inputs = grad_inputs + reduce_rows(product(grad_mixed, full_qkv, ((1,), (1,))))

    def collect(array):
        return lax.psum_scatter(array, "fsdp", scatter_dimension=0, tiled=True)

    part_down = collect(grad_w_down)
    out_down = lax.all_to_all(
        part_down.reshape(1, piece, model), "seq", 2, 0, tiled=True
    ).reshape(deep, -1)
    part_uv = collect(grad_w_uv)
    out_uv = lax.all_to_all(
        part_uv.reshape(r_in, -1, 1, piece), "seq", 1, 2, tiled=True
    ).reshape(r_in, -1)
    placed = jnp.zeros((own, parts, width, model), jnp.bfloat16)
    placed = lax.dynamic_update_slice(
        placed, grad_w_out.reshape(own, 1, width, model), (0, mine, 0, 0)
    )
    part_out = collect(placed.reshape(-1, model))
    out_out = lax.psum_scatter(part_out, "seq", scatter_dimension=1, tiled=True)
    part_qkv = collect(grad_w_qkv)
    out_qkv = lax.all_to_all(
        part_qkv.reshape(r_in, -1, 1, width), "seq", 1, 2, tiled=True
    ).reshape(r_in, -1)

    def widen(array, outer, inner):
        blank = jnp.zeros((outer, parts, inner), jnp.float32)
        array = array.reshape(outer, 1, inner)
        return lax.dynamic_update_slice(blank, array, (0, mine, 0)).reshape(shards, -1)

    gain_sums = jnp.concatenate(
        [
            widen(grad_gain_qk, own, width),
            grad_gain_a.reshape(shards, -1),
            widen(grad_gain_u, shards, piece),
            widen(grad_gain_v, shards, piece),
            grad_gain_m.reshape(shards, -1),
        ],
        axis=1,
    )
    gain_sums = lax.psum(collect(gain_sums), "seq")[0]
    outs = jnp.split(gain_sums, edges)
    return (
        output[None],
        grad_inputs[None],
        out_qkv.astype(jnp.float32),
        out_out.astype(jnp.float32),
        out_uv.astype(jnp.float32),
        out_down.astype(jnp.float32),
        outs[0],
        outs[1],
        outs[2],
        outs[3],
        outs[4],
    )


MESH = pl.DeviceIdType.MESH
TILE = 128
QROWS = 128


def loop(count, body):
    def run(index, carry):
        body(index)
        return carry

    lax.fori_loop(0, count, run, 0)


def at_rows(ref, block, size=TILE):
    return ref.at[pl.ds(pl.multiple_of(block * size, size), size), :]


def cols(block, size=TILE):
    return pl.ds(pl.multiple_of(block * size, size), size)


def mean_last(value):
    return jnp.sum(value, axis=-1, keepdims=True) * (1.0 / value.shape[-1])


class Slots:
    def __init__(self):
        self.count = 0

    def take(self, count):
        base = self.count
        self.count = base + count
        return base


def fused_layer(sizes, *refs):
    (parts, lines, rows, model, deep, own_heads, width) = sizes
    slots_all = parts * rows
    span = own_heads * width
    hid = deep * lines * 2 // parts
    count_in, count_out = len(Inputs._fields), len(Results._fields)
    ins = Inputs(*refs[:count_in])
    outs = Results(*refs[count_in : count_in + count_out])
    table = buffers(sizes)
    rest = refs[count_in + count_out :]
    v = types.SimpleNamespace(**dict(zip(table, rest[: len(table)])))
    send_sem, recv_sem, local_sem = rest[len(table) :]

    s = lax.axis_index("seq")
    f = lax.axis_index("fsdp")
    z = f // 2
    c = f % 2
    other = 1 - c
    mate = (s, 2 * z + other)
    slots = Slots()

    def put(src, dst, target, send_slot, recv_slot):
        pltpu.make_async_remote_copy(
            src_ref=src,
            dst_ref=dst,
            send_sem=send_sem.at[send_slot],
            recv_sem=recv_sem.at[recv_slot],
            device_id=target,
            device_id_type=MESH,
        ).start()

    def descriptor(ref, send_slot, recv_slot):
        return pltpu.make_async_remote_copy(
            src_ref=ref,
            dst_ref=ref,
            send_sem=send_sem.at[send_slot],
            recv_sem=recv_sem.at[recv_slot],
            device_id=mate,
            device_id_type=MESH,
        )

    def landed(ref, slot):
        descriptor(ref, 0, slot).wait_recv()

    def plane(distance):
        return (s + distance) % parts

    def plane_from(distance):
        return (s + parts - distance) % parts

    def line(distance):
        return (z + distance) % lines

    def line_from(distance):
        return (z + lines - distance) % lines

    barrier = pltpu.get_barrier_semaphore()
    for distance in range(1, parts):
        pl.semaphore_signal(barrier, inc=1, device_id=(plane(distance), f), device_id_type=MESH)
    for distance in range(1, 2 * lines):
        target = (s, (f + distance) % (2 * lines))
        pl.semaphore_signal(barrier, inc=1, device_id=target, device_id_type=MESH)

    edges = [0, TILE, 2 * TILE, 2 * TILE + deep, 2 * TILE + 2 * deep, 3 * TILE + 2 * deep]
    own_gains = (ins.s_qk, ins.alpha_a, ins.s_u, ins.s_v, ins.alpha_m)
    for place, own_gain in enumerate(own_gains):
        row = own_gain[...].astype(jnp.float32).reshape(1, -1)
        v.gain_all[f, :, edges[place] : edges[place + 1]] = row
    own_row = pl.ds(pl.multiple_of(s * rows, rows), rows)
    own_w = pl.ds(pl.multiple_of(f * TILE, TILE), TILE)
    part_cols = model // parts
    blocks_uv = 2 * hid // parts // TILE
    wide = blocks_uv * TILE

    def fetch(src, dst, slot):
        pltpu.make_async_copy(src, dst, local_sem.at[slot]).start()

    def deliver(index):
        made = (
            v.made_output,
            v.made_input_grad,
            v.made_back_qkv,
            v.made_back_out,
            v.made_back_uv,
            v.made_back_down,
            v.made_gains,
        )
        return pltpu.make_async_copy(made[index], outs[index], local_sem.at[6 + index])

    def fetched(dst, slot):
        pltpu.make_async_copy(dst, dst, local_sem.at[slot]).wait()

    fetch(ins.w_out, v.wz.at[own_w, :], 0)
    fetch(ins.tokens, v.x_all.at[own_row, :], 1)
    for index in range(blocks_uv):
        fetch(
            ins.w_uv.at[:, pl.ds(pl.multiple_of((index * parts + s) * TILE, TILE), TILE)],
            v.wu.at[own_w, pl.ds(pl.multiple_of(s * wide + index * TILE, TILE), TILE)],
            2,
        )
    fetch(ins.w_down.at[cols(s), :], v.wd.at[own_w, cols(s, part_cols)], 3)
    fetch(ins.cotangent, v.cotangent, 4)
    for index in range(3):
        chunk = 3 * s + index

        @pl.when(chunk % parts == s)
        def _():
            fetch(
                ins.w_qkv.at[:, index * span : (index + 1) * span],
                v.wq.at[own_w, cols(chunk // parts, span)],
                5,
            )

    pl.semaphore_wait(barrier, parts - 1 + 2 * lines - 1)

    qkv_slot = slots.take(1)
    for index in range(3):
        chunk = 3 * s + index
        block = chunk // parts
        target = chunk % parts

        @pl.when(target != s)
        def _():
            put(
                ins.w_qkv.at[:, index * span : (index + 1) * span],
                v.wq.at[own_w, cols(block, span)],
                (target, f),
                BY_PLANE,
                qkv_slot,
            )


    side, across, opposite = s + 1 - 2 * (s % 2), (s + 2) % parts, parts - 1 - s

    def half_of(shared, owner, part):
        start = owner * rows + part * (rows // 2)
        return shared.at[pl.ds(pl.multiple_of(start, rows // 2), rows // 2), :]

    token_slot = slots.take(SHARE)
    for part in range(2):
        mine = ins.tokens.at[part * (rows // 2) : (part + 1) * (rows // 2), :]
        there = half_of(v.x_all, s, part)
        put(mine, there, (side, f), BY_SHARE, token_slot + 2 * part)
        put(mine, there, (across, f), BY_SHARE, token_slot + 2 - part)

    gain_slot = slots.take(1)
    for distance in range(1, 2 * lines):
        put(
            v.gain_all.at[f],
            v.gain_all.at[f],
            (s, (f + distance) % (2 * lines)),
            BY_GAIN,
            gain_slot,
        )

    def plane_share_relay(shared, base, passed=None):
        one, two = half_of(shared, side, 0), half_of(shared, across, 1)
        if passed is not None:
            passed(s, 0)
            passed(s, 1)
        landed(one, base)
        put(one, one, (across, f), BY_SHARE, base + 3)
        landed(two, base + 1)
        put(two, two, (side, f), BY_SHARE, base + 3)
        if passed is not None:
            passed(side, 0)
            passed(across, 1)

    def plane_share_wait(shared, base, passed=None):
        for pieces, slot in (
            (((side, 1), (across, 0)), base + 2),
            (((opposite, 0), (opposite, 1)), base + 3),
        ):
            landed(at_rows(shared, opposite, rows), slot)
            if passed is not None:
                for piece_of in pieces:
                    passed(*piece_of)

    def pass_to_mate(shared, slot):
        def passed(owner, part):
            start = owner * rows + part * (rows // 2)
            here = pl.ds(pl.multiple_of(start, rows // 2), rows // 2)
            there = pl.ds(pl.multiple_of(slots_all + start, rows // 2), rows // 2)
            put(shared.at[here, :], shared.at[there, :], mate, BY_MATE_B, slot)

        return passed

    def shard(ref, chip, core, lanes):
        block = 2 * chip + core
        return ref.at[pl.ds(pl.multiple_of(block * TILE, TILE), TILE), lanes]

    inner = z * (lines - 1 - z) > 0
    outer = z * (lines - 1 - z) == 0

    def line_send(ref, base, lanes=slice(None), twice=True, apart=False):
        own = shard(ref, z, c, lanes)
        for distance in (2, 1, 3):
            target = line(distance)
            near = (z - target) * (z - target) < (lines - 1) * (lines - 1)
            slot = base
            if apart:
                slot = base + distance - 1
            elif distance == 2:
                slot = base + target * (lines - 1 - target) // 2

            @pl.when(near)
            def _():
                put(own, own, (s, 2 * target + c), BY_LINE, slot)

        if twice:
            put(own, own, mate, mate_group(ref), base + 2 + apart)

    def mate_group(ref):
        return BY_WIDE if ref is v.wu else BY_MATE_B if ref is v.wd else BY_MATE_C

    def line_relay(ref, base, lanes=slice(None), apart=False):
        block = shard(ref, line_from(2), c, lanes)

        @pl.when(inner)
        def _():
            landed(block, base + 1)
            slot = base + 2 * z - 2 if apart else base
            put(block, block, (s, 2 * (lines - 1) * (z - 1) + c), BY_LINE, slot)

    def line_arrived(ref, base, lanes=slice(None)):
        pl.when(inner)(lambda: landed(ref.at[: 2 * TILE, lanes], base))
        pl.when(outer)(lambda: landed(ref.at[: 3 * TILE, lanes], base))

    def line_forward(ref, base, lanes=slice(None), apart=False):
        if not apart:
            line_arrived(ref, base, lanes)
        for distance in (1, 3, 2):
            block = shard(ref, line_from(distance), c, lanes)
            if apart and distance == 2:

                @pl.when(outer)
                def _():
                    landed(block, base + 1)

            elif apart:
                landed(block, base + distance - 1)
            put(block, block, mate, mate_group(ref), base + 2 + apart)

    def mate_wait(ref, base, lanes=slice(None), apart=False):
        landed(ref.at[: lines * TILE, lanes], base + 2 + apart)

    wq_slot, wu_slot = (slots.take(4) for _ in range(2))
    count = 4
    piece = model // count
    wd_parts = [
        (slots.take(3), slice(part * piece, (part + 1) * piece)) for part in range(count)
    ]
    wz_slot, wo_slot, out_slot = slots.take(2), slots.take(1), slots.take(1)
    fetched(v.wz.at[own_w, :], 0)
    line_send(v.wz, wz_slot, twice=False)

    landed(v.wq.at[own_w, : 2 * span], qkv_slot)
    fetched(v.wq.at[own_w, :span], 5)
    line_send(v.wq, wq_slot, apart=True)
    lengths = [ins.lengths[0, i] for i in range(ins.lengths.shape[1])]

    def slot_facts(slot):
        end = 0
        member = jnp.zeros(slot.shape, jnp.int32)
        begin = jnp.zeros(slot.shape, jnp.int32)
        for length in lengths[:-1]:
            end = end + length
            after = slot >= end
            member = member + after.astype(jnp.int32)
            begin = jnp.where(after, end, begin)
        valid = member < len(lengths) - 1
        segment = jnp.where(valid, member, len(lengths) - 1 + slot)
        place = jnp.where(valid, slot - begin, 0)
        return segment, place, valid

    lane = lax.broadcasted_iota(jnp.int32, (1, TILE), 1)
    low_half = lane < width
    first_quarter = lane % width < width // 2
    frequency = jnp.exp(
        (lane % (width // 2)).astype(jnp.float32) * (-2.0 * math.log(10000.0) / width)
    )
    turn_sign = jnp.where(first_quarter, -1.0, 1.0)

    def tables(block):
        here = pl.ds(pl.multiple_of(block * TILE, TILE), TILE)
        slot = block * TILE + lax.broadcasted_iota(jnp.int32, (TILE, 1), 0)
        segment, place, _ = slot_facts(slot)
        angle = place.astype(jnp.float32) * frequency
        v.cosine[here, :] = jnp.cos(angle)
        v.sine[here, :] = jnp.sin(angle) * turn_sign
        key_slot = lax.broadcasted_iota(jnp.int32, (1, slots_all), 1)
        key_segment = slot_facts(key_slot)[0]
        kept = (segment == key_segment) & (slot >= key_slot)
        v.bias[here, :] = jnp.where(kept, 0.0, -1e30)

    loop(slots_all // TILE, tables)
    fetched(v.x_all.at[own_row, :], 1)
    plane_share_relay(v.x_all, token_slot)
    uv_slot = slots.take(1)
    for distance in range(1, parts):
        target = plane(distance)
        for index in range(blocks_uv):
            put(
                ins.w_uv.at[:, pl.ds(pl.multiple_of((index * parts + target) * TILE, TILE), TILE)],
                v.wu.at[own_w, pl.ds(pl.multiple_of(s * wide + index * TILE, TILE), TILE)],
                (target, f),
                BY_PLANE,
                uv_slot,
            )

    down_slot = slots.take(1)
    for distance in range(1, parts):
        target = plane(distance)
        put(
            ins.w_down.at[cols(target), :],
            v.wd.at[own_w, cols(s, part_cols)],
            (target, f),
            BY_PLANE,
            down_slot,
        )

    line_relay(v.wz, wz_slot)
    line_relay(v.wq, wq_slot, apart=True)
    plane_share_wait(v.x_all, token_slot)
    line_arrived(v.wz, wz_slot)
    for distance in range(1, parts):
        target = plane(distance)
        rows_out = at_rows(v.wz, 2 * target + c)
        put(
            rows_out,
            v.wo.at[cols(c), cols(s, part_cols)],
            (target, f),
            BY_PLANE,
            out_slot,
        )
    v.wo[cols(c), cols(s, part_cols)] = v.wz[cols(2 * s + c), :]
    fetched(v.wu.at[own_w, cols(s, wide)], 2)
    landed(v.wu.at[own_w, : (parts - 1) * wide], uv_slot)
    line_send(v.wu, wu_slot, apart=True)

    def mate_blocks(name_all, ref, stage, slot):
        for block in range(lines):
            here = slice(block * TILE, (block + 1) * TILE)
            stage[here, :] = name_all[:, cols(2 * block + other)].T
        put(stage, ref.at[:, slots_all:], mate, BY_MATE_C, slot)
        for block in range(lines):
            here = slice(block * TILE, (block + 1) * TILE)
            ref[here, :slots_all] = name_all[:, cols(2 * block + c)].T

    mate_x_slot = slots.take(1)
    mate_blocks(v.x_all, v.turned_x, v.stage_x, mate_x_slot)
    landed(v.gain_all.at[1:], gain_slot)

    def gain(block, offset):
        return v.gain_all[block, :, pl.ds(pl.multiple_of(offset, TILE), TILE)]

    for block in range(2 * lines):
        here = slice(block * TILE, (block + 1) * TILE)
        v.gain_a[:, here] = gain(block, edges[1])
        v.gain_u[:, here] = gain(block, edges[2] + s * TILE)
        v.gain_v[:, here] = gain(block, edges[3] + s * TILE)
        v.gain_m[:, here] = gain(block, edges[4])
    for block in range(span // TILE):
        v.gain_qk[:, block * TILE : (block + 1) * TILE] = gain(span // TILE * s + block, 0)

    line_forward(v.wq, wq_slot, apart=True)
    mate_wait(v.wq, wq_slot, apart=True)

    def mix(index):
        v.raw[:, cols(index, span)] = product(
            v.x_all[...], v.wq[:, cols(index, span)], ((1,), (0,))
        )

    loop(3, mix)

    def swap(value):
        return jnp.where(
            first_quarter,
            pltpu.roll(value, TILE - width // 2, 1),
            pltpu.roll(value, width // 2, 1),
        )

    def head_mean(value):
        one = jnp.sum(jnp.where(low_half, value, 0.0), axis=-1, keepdims=True)
        two = jnp.sum(jnp.where(low_half, 0.0, value), axis=-1, keepdims=True)
        return jnp.where(low_half, one, two) * (1.0 / width)

    pairs = span // TILE
    blocks = slots_all // TILE

    def prepare_block(index):
        here = pl.ds(pl.multiple_of(0, TILE), slots_all)
        group = index
        there = cols(group)
        value = v.raw[here, there]
        turned = value * v.cosine[here, :] + swap(value) * v.sine[here, :]
        inverse = lax.rsqrt(head_mean(turned * turned) + epsilon)
        normed = turned * inverse
        v.normed[here, there] = normed
        v.inverse[here, there] = inverse
        v.qkv[here, there] = low(normed * v.gain_qk[:, cols(group % pairs)])

    loop(2 * pairs, prepare_block)

    def keep_value(index):
        here = pl.ds(pl.multiple_of(index * TILE, TILE), TILE)
        v.qkv[here, 2 * span :] = low(v.raw[here, 2 * span :])

    loop(blocks, keep_value)
    own_out = v.wo.at[cols(c), :]
    landed(v.wo.at[cols(c), : (parts - 1) * part_cols], out_slot)
    put(own_out, own_out, mate, BY_MATE_D, wo_slot)

    scale = 1.0 / math.sqrt(width)
    halves = (low_half, jnp.logical_not(low_half))

    def attend(pair):
        q_cols, k_cols, v_cols = cols(pair), cols(pairs + pair), cols(2 * pairs + pair)
        for block in range(blocks // 2):
            here = slice(block * 2 * TILE, (block + 1) * 2 * TILE)
            seen = slice(0, (block + 1) * 2 * TILE)
            results = []
            for half in range(2):
                query = jnp.where(halves[half], v.qkv[here, q_cols], 0.0).astype(jnp.bfloat16)
                score = product(query, v.qkv[seen, k_cols], ((1,), (1,))) * scale
                score = score + v.bias[here, seen]
                peak = jnp.max(score, axis=1, keepdims=True)
                raised = jnp.exp(score - peak)
                summed = jnp.sum(raised, axis=1, keepdims=True)
                weight = low(raised / summed)
                results.append(product(weight, v.qkv[seen, v_cols], ((1,), (0,))))
                v.total[2 * pair + half, here, :] = peak + jnp.log(summed)
            v.attended[here, q_cols] = low(jnp.where(low_half, results[0], results[1]))

    loop(pairs, attend)
    mate_att_slot = slots.take(1)
    v.stage_att[...] = v.attended[:, cols(other)].T
    v.turned_att[:, :slots_all] = v.attended[:, cols(c)].T

    put(v.stage_att, v.turned_att.at[:, slots_all:], mate, BY_MATE_D, mate_att_slot)
    landed(v.wo.at[cols(other), :], wo_slot)

    def plane_sum(sums, arrived, base, tile, span_of=(0, count)):
        start, stop = span_of

        def send(index):
            there = cols(index, piece)
            for distance in range(1, parts):
                target = plane(distance)
                put(
                    sums.at[pl.ds(pl.multiple_of(target * rows, rows), rows), there],
                    arrived.at[distance - 1, :, there],
                    (target, f),
                    BY_SUM,
                    base,
                )

        def step(index):
            sums[:, cols(start + index, piece)] = low(tile(start + index))

            @pl.when(index > 0)
            def _():
                send(start + index - 1)

        loop(stop - start, step)
        send(stop - 1)

    def plane_sum_wait(arrived, base):
        landed(arrived, base)

    def plane_total(sums, arrived, here, at):
        total = sums[here, :].astype(jnp.float32)
        for distance in range(1, parts):
            total = total + arrived[distance - 1, at, :].astype(jnp.float32)
        return total

    chunk_rows = 64

    def chunk(index):
        at = pl.ds(pl.multiple_of(index * chunk_rows, chunk_rows), chunk_rows)
        here = pl.ds(pl.multiple_of(s * rows + index * chunk_rows, chunk_rows), chunk_rows)
        return at, here

    def plane_share(shared, base, make):
        def send(index):
            own = shared.at[chunk(index)[1], :]
            part = index // (rows // chunk_rows // 2)
            put(own, own, (side, f), BY_SHARE, base + 2 * part)
            put(own, own, (across, f), BY_SHARE, base + 2 - part)

        def step(index):
            make(index)

            @pl.when(index > 0)
            def _():
                send(index - 1)

        loop(rows // chunk_rows, step)
        send(rows // chunk_rows - 1)

    branch_slot = slots.take(1)
    plane_sum(
        v.part_branch,
        v.got_branch,
        branch_slot,
        lambda index: product(v.attended[...], v.wo[:, cols(index, piece)], ((1,), (0,))),
    )
    line_relay(v.wu, wu_slot, apart=True)
    fetched(v.wd.at[own_w, cols(s, part_cols)], 3)
    landed(v.wd.at[own_w, : (parts - 1) * part_cols], down_slot)
    line_send(v.wd, *wd_parts[0])
    line_send(v.wd, *wd_parts[1])
    plane_sum_wait(v.got_branch, branch_slot)
    line_relay(v.wd, *wd_parts[0])
    line_send(v.wd, *wd_parts[2])

    def blended(base, branch, alpha):
        inverse_branch = lax.rsqrt(mean_last(branch * branch) + epsilon)
        normed = branch * inverse_branch
        mixed = base + alpha * (normed - base)
        inverse = lax.rsqrt(mean_last(mixed * mixed) + epsilon)
        return normed, inverse_branch, mixed * inverse, inverse

    def blended_back(grad, base, alpha, normed, inverse_branch, result, inverse):
        grad_mixed = inverse * (grad - result * mean_last(grad * result))
        grad_normed = alpha * grad_mixed
        grad_branch = inverse_branch * (grad_normed - normed * mean_last(grad_normed * normed))
        grad_alpha = jnp.sum(grad_mixed * (normed - base), axis=0, keepdims=True)
        return grad_mixed - grad_normed, grad_branch, grad_alpha

    def make_first(index):
        at, here = chunk(index)
        base = v.x_all[here, :].astype(jnp.float32)
        normed, inverse_branch, result, inverse = blended(
            base, plane_total(v.part_branch, v.got_branch, here, at), v.gain_a[...]
        )
        v.branch_normed[at, :] = normed
        v.branch_inverse[at, :] = inverse_branch
        v.first[at, :] = result
        v.first_inverse[at, :] = inverse
        v.first_all[here, :] = low(result)

    first_slot = slots.take(SHARE)
    plane_share(v.first_all, first_slot, make_first)
    line_relay(v.wd, *wd_parts[1])
    line_send(v.wd, *wd_parts[3])
    plane_share_relay(v.first_all, first_slot)
    line_relay(v.wd, *wd_parts[2])
    line_forward(v.wu, wu_slot, apart=True)
    mate_wait(v.wu, wu_slot, apart=True)
    plane_share_wait(v.first_all, first_slot)

    def gate_tile(index):
        there = cols(index, 256)
        v.up[:, there] = product(v.first_all[...], v.wu[:, there], ((1,), (0,)))
        v.gate[:, there] = product(
            v.first_all[...],
            v.wu[:, pl.ds(pl.multiple_of(hid + index * 256, 256), 256)],
            ((1,), (0,)),
        )

        def rows_of(block):
            here = pl.ds(pl.multiple_of(block * 64, 64), 64)
            scaled = v.gate[here, there] * v.gain_v[:, there]
            passed = scaled / (1.0 + jnp.exp(-scaled))
            v.hidden[here, there] = low(v.up[here, there] * v.gain_u[:, there] * passed)

        loop(slots_all // 64, rows_of)

    line_relay(v.wd, *wd_parts[3])
    loop(hid // 512, gate_tile)
    line_forward(v.wd, *wd_parts[0])
    loop(hid // 512, lambda index: gate_tile(hid // 512 + index))
    mate_hidden_slot = slots.take(1)
    mate_blocks(v.hidden, v.turned_hidden, v.stage_hidden, mate_hidden_slot)
    mate_first_slot = slots.take(1)
    mate_blocks(v.first_all, v.turned_first, v.stage_first, mate_first_slot)
    down_sum_slot = slots.take(1)

    def down_tile(index):
        return product(v.hidden[...], v.wd[:, cols(index, piece)], ((1,), (0,)))

    line_forward(v.wd, *wd_parts[1])
    for part in range(count):
        mate_wait(v.wd, *wd_parts[part])
        plane_sum(v.part_down, v.got_down, down_sum_slot, down_tile, (part, part + 1))
        if part + 2 < count:
            line_forward(v.wd, *wd_parts[part + 2])
    fetched(v.cotangent, 4)
    plane_sum_wait(v.got_down, down_sum_slot)
    v.grad_a[...] = jnp.zeros_like(v.grad_a)
    v.grad_m[...] = jnp.zeros_like(v.grad_m)

    finish_rows = 128

    def finish(index):
        at = pl.ds(pl.multiple_of(index * finish_rows, finish_rows), finish_rows)
        here = pl.ds(pl.multiple_of(s * rows + index * finish_rows, finish_rows), finish_rows)
        slot = s * rows + index * finish_rows
        slot = slot + lax.broadcasted_iota(jnp.int32, (finish_rows, 1), 0)
        keep = slot_facts(slot)[2].astype(jnp.float32)
        base = v.first[at, :]
        alpha = v.gain_m[...]
        normed, inverse_branch, result, inverse = blended(
            base, plane_total(v.part_down, v.got_down, here, at), alpha
        )
        v.made_output[at, :] = low(result * keep)
        grad = v.cotangent[at, :].astype(jnp.float32) * keep
        grad_base, grad_down, grad_alpha = blended_back(
            grad, base, alpha, normed, inverse_branch, result, inverse
        )
        v.grad_first[at, :] = grad_base
        v.gd[here, :] = low(grad_down)
        v.grad_m[...] += grad_alpha

    loop(rows // finish_rows, finish)
    gd_edges = [0, TILE, *range(piece, model + 1, piece)]
    gd_parts = [slice(*pair) for pair in zip(gd_edges, gd_edges[1:])]
    gd_slot, mate_gd_slot = slots.take(len(gd_parts)), slots.take(len(gd_parts))

    def gd_pass(owner, lanes, slot):
        here = pl.ds(pl.multiple_of(owner * rows, rows), rows)
        there = pl.ds(pl.multiple_of(slots_all + owner * rows, rows), rows)
        put(v.gd.at[here, lanes], v.gd.at[there, lanes], mate, BY_MATE_B, slot)

    for part, lanes in enumerate(gd_parts):
        own = v.gd.at[own_row, lanes]
        for distance in range(1, parts):
            put(own, own, (plane(distance), f), BY_SHARE, gd_slot + part)
        gd_pass(s, lanes, mate_gd_slot + part)
    deliver(0).start()
    first_half = slice(0, slots_all)
    second_half = slice(slots_all, 2 * slots_all)

    ends = (lines - 1) * (1 - z % 2)
    mids = 2 - z // 2
    last = (2 * z + 1) % (lines + 1)
    beside = z + 1 - 2 * (z % 2)

    mid_slot = 2 - z * (lines - 1 - z) // 2

    def line_grad_first(grads, arrived, base, there):
        put(
            grads.at[ends, :, there],
            arrived.at[0, :, there],
            (s, 2 * beside + c),
            BY_GRAD,
            base + 1 - beside * (lines - 1 - beside) // 2,
        )

    def line_grad_mid(grads, arrived, base, there):
        put(
            grads.at[mids, :, there],
            arrived.at[mid_slot, :, there],
            (s, 2 * mids + c),
            BY_GRAD,
            base + 1,
        )

    def line_grad_last(grads, arrived, base, there):
        put(
            grads.at[last, :, there],
            arrived.at[3, :, there],
            (s, 2 * last + c),
            BY_GRAD,
            base + 1,
        )

    def line_grad_rest(grads, arrived, base, chained=False):
        @pl.when(outer)
        def _():
            if chained:
                there = (s, 2 * beside + c)
                put(grads.at[mids], arrived.at[2], there, BY_GRAD, base + 2)
            else:
                line_grad_mid(grads, arrived, base, slice(None))
            line_grad_last(grads, arrived, base, slice(None))

    def weight_grad(turned, right, grads, arrived, columns, base, chained=False):
        def send(index):
            line_grad_first(grads, arrived, base, cols(index, 256))
            if not chained:
                pl.when(inner)(lambda: line_grad_mid(grads, arrived, base, cols(index, 256)))

        def step(index):
            there = cols(index, 256)
            total = product(turned[...], right[:, there], ((1,), (0,)))
            grads[:, :, there] = low(total).reshape(lines, TILE, 256)

            pl.when(index > 0)(lambda: send(index - 1))

        loop(columns // 256, step)
        send(columns // 256 - 1)
        line_grad_rest(grads, arrived, base, chained)

    def combine_into(grads, block, came, columns):
        def tile(index):
            there = cols(index, 256)
            total = grads[block, :, there].astype(jnp.float32)
            grads[block, :, there] = low(total + came[:, there].astype(jnp.float32))

        loop(columns // 256, tile)

    def weight_combine(grads, arrived, columns, base):
        @pl.when(inner)
        def _():
            landed(arrived.at[0], base)
            combine_into(grads, last, arrived.at[0], columns)
            put(grads.at[last], arrived.at[1], (s, 2 * last + c), BY_GRAD, base + 1)

    def weight_combine_mid(grads, arrived, columns, base):
        @pl.when(inner)
        def _():
            landed(arrived.at[2], base + 2)
            combine_into(grads, mids, arrived.at[2], columns)
            put(grads.at[mids], arrived.at[1], (s, 2 * mids + c), BY_GRAD, base + 1)

    mate_gu_slot = slots.take(1)

    def gu_pass(index):
        for lanes in (
            pl.ds(pl.multiple_of(index * 256, 256), 256),
            pl.ds(pl.multiple_of(hid + index * 256, 256), 256),
        ):
            mine, there = v.gu.at[first_half, lanes], v.gu.at[second_half, lanes]
            put(mine, there, mate, BY_WIDE, mate_gu_slot)

    def gate_back(index):
        there = cols(index, 256)
        there_gate = pl.ds(pl.multiple_of(hid + index * 256, 256), 256)
        v.grad_hidden[...] = low(product(v.gd[first_half, :], v.wd[there, :], ((1,), (1,))))
        v.grad_u[:, there] = jnp.zeros((1, 256), jnp.float32)
        v.grad_v[:, there] = jnp.zeros((1, 256), jnp.float32)

        def rows_of(block):
            here = pl.ds(pl.multiple_of(block * 128, 128), 128)
            grad = v.grad_hidden[here, :].astype(jnp.float32)
            up = v.up[here, there]
            gate = v.gate[here, there]
            gain_u = v.gain_u[:, there]
            gain_v = v.gain_v[:, there]
            scaled = gate * gain_v
            squash = 1.0 / (1.0 + jnp.exp(-scaled))
            passed = scaled * squash
            grad_scaled_up = grad * passed
            grad_scaled = grad * (up * gain_u) * (squash + passed * (1.0 - squash))
            v.gu[here, there] = low(grad_scaled_up * gain_u)
            v.gu[here, there_gate] = low(grad_scaled * gain_v)
            v.grad_u[:, there] += jnp.sum(grad_scaled_up * up, axis=0, keepdims=True)
            v.grad_v[:, there] += jnp.sum(grad_scaled * gate, axis=0, keepdims=True)

        loop(slots_all // 128, rows_of)
        pl.when(index > 0)(lambda: gu_pass(index - 1))

    landed(v.turned_x.at[:, second_half], mate_x_slot)
    landed(v.turned_first.at[:, second_half], mate_first_slot)
    landed(v.turned_hidden.at[:, second_half], mate_hidden_slot)
    line_down_slot = slots.take(2)
    for part, lanes in enumerate(gd_parts):
        landed(v.gd.at[: (parts - 1) * rows, lanes], gd_slot + part)
        for distance in range(1, parts):
            gd_pass(plane_from(distance), lanes, mate_gd_slot + part)
        if part == len(gd_parts) - 1:
            loop(1, gate_back)
        landed(v.gd.at[second_half, lanes], mate_gd_slot + part)
        total = product(v.turned_hidden[...], v.gd[:, lanes], ((1,), (0,)))
        v.send_down[:, :, lanes] = low(total).reshape(lines, TILE, -1)
        line_grad_first(v.send_down, v.line_down, line_down_slot, lanes)
        line_grad_mid(v.send_down, v.line_down, line_down_slot, lanes)
        pl.when(outer)(lambda: line_grad_last(v.send_down, v.line_down, line_down_slot, lanes))
    loop(hid // 256 - 1, lambda index: gate_back(index + 1))
    gu_pass(hid // 256 - 1)
    first_sum_slot = slots.take(1)
    plane_sum(
        v.part_first,
        v.got_first,
        first_sum_slot,
        lambda index: product(v.gu[first_half, :], v.wu[cols(index, piece), :], ((1,), (1,))),
    )
    weight_combine(v.send_down, v.line_down, model, line_down_slot)
    landed(v.gu.at[second_half, :], mate_gu_slot)
    line_uv_slot = slots.take(2)
    weight_grad(v.turned_first, v.gu, v.send_uv, v.line_uv, 2 * hid, line_uv_slot)
    plane_sum_wait(v.got_first, first_sum_slot)

    def back_first(index):
        at, here = chunk(index)
        grad = v.grad_first[at, :] + plane_total(v.part_first, v.got_first, here, at)
        grad_base, grad_branch, grad_alpha = blended_back(
            grad,
            v.x_all[here, :].astype(jnp.float32),
            v.gain_a[...],
            v.branch_normed[at, :],
            v.branch_inverse[at, :],
            v.first[at, :],
            v.first_inverse[at, :],
        )
        v.grad_tokens[at, :] = grad_base
        v.gb[here, :] = low(grad_branch)
        v.grad_a[...] += grad_alpha

    gb_slot = slots.take(SHARE)
    plane_share(v.gb, gb_slot, back_first)
    mate_gb_slot = slots.take(1)
    passed_gb = pass_to_mate(v.gb, mate_gb_slot)
    plane_share_relay(v.gb, gb_slot, passed_gb)
    plane_share_wait(v.gb, gb_slot, passed_gb)

    v.grad_att[...] = low(product(v.gb[first_half, :], v.wo[...], ((1,), (1,))))
    weight_combine(v.send_uv, v.line_uv, 2 * hid, line_uv_slot)
    v.grad_qkv[...] = jnp.zeros_like(v.grad_qkv)

    def attend_back(pair):
        q_cols, k_cols, v_cols = cols(pair), cols(pairs + pair), cols(2 * pairs + pair)
        for block in range(blocks // 2):
            here = slice(block * 2 * TILE, (block + 1) * 2 * TILE)
            seen = slice(0, (block + 1) * 2 * TILE)
            results = []
            for half in range(2):
                query = jnp.where(halves[half], v.qkv[here, q_cols], 0.0).astype(jnp.bfloat16)
                grad = jnp.where(halves[half], v.grad_att[here, q_cols], 0.0)
                grad = grad.astype(jnp.bfloat16)
                score = product(query, v.qkv[seen, k_cols], ((1,), (1,))) * scale
                score = score + v.bias[here, seen]
                share = jnp.exp(score - v.total[2 * pair + half, here, :])
                grad_share = product(grad, v.qkv[seen, v_cols], ((1,), (1,)))
                inner = jnp.sum(share * grad_share, axis=1, keepdims=True)
                grad_score = low(share * (grad_share - inner))
                results.append(product(grad_score, v.qkv[seen, k_cols], ((1,), (0,))))
                v.grad_qkv[seen, v_cols] += product(low(share), grad, ((0,), (0,)))
                v.grad_qkv[seen, k_cols] += product(grad_score, query, ((0,), (0,)))
            v.grad_qkv[here, q_cols] = jnp.where(low_half, results[0], results[1])

    loop(pairs, attend_back)
    landed(v.turned_att.at[:, second_half], mate_att_slot)
    landed(v.gb.at[second_half, :], mate_gb_slot)
    line_out_slot = slots.take(3)
    part_out_slot = slots.take(1)

    def out_tile(index):
        there = cols(index, 256)
        v.send_out[:, there] = low(product(v.turned_att[...], v.gb[:, there], ((1,), (0,))))

    loop(model // 256, out_tile)
    for distance in range(1, parts):
        target = plane(distance)
        put(
            v.send_out.at[:, cols(target, part_cols)],
            v.send_wo.at[s],
            (target, f),
            BY_PLANE,
            part_out_slot,
        )
    v.send_wo[s] = v.send_out[:, cols(s, part_cols)]
    v.grad_qk[...] = jnp.zeros_like(v.grad_qk)

    def prepare_back(index):
        here = pl.ds(pl.multiple_of(0, TILE), slots_all)
        group = index
        there = cols(group)
        pair = cols(group % pairs)
        grad = low(v.grad_qkv[here, there] * scale).astype(jnp.float32)
        normed = v.normed[here, there]
        v.grad_qk[:, pair] += jnp.sum(grad * normed, axis=0, keepdims=True)
        grad = grad * v.gain_qk[:, pair]
        grad = v.inverse[here, there] * (grad - normed * head_mean(grad * normed))
        back = grad * v.cosine[here, :] - swap(grad) * v.sine[here, :]
        v.gm[here, there] = low(back)

    def value_back(index):
        here = pl.ds(pl.multiple_of(index * TILE, TILE), TILE)
        v.gm[here, 2 * span :] = low(v.grad_qkv[here, 2 * span :])

    loop(blocks, value_back)
    mate_gm_slot = slots.take(1)

    def gm_pass(lanes):
        put(v.gm.at[first_half, lanes], v.gm.at[second_half, lanes], mate, BY_MATE_C, mate_gm_slot)

    gm_pass(slice(2 * span, 3 * span))
    loop(pairs, prepare_back)
    gm_pass(slice(0, span))
    loop(pairs, lambda index: prepare_back(pairs + index))
    gm_pass(slice(span, 2 * span))

    v.gain_part[...] = jnp.zeros_like(v.gain_part)
    for block in range(2 * lines):
        here = slice(block * TILE, (block + 1) * TILE)
        local_pair = block % (span // TILE) * TILE
        qk = v.grad_qk[:, local_pair : local_pair + TILE]
        mine = (s == block // (span // TILE)).astype(jnp.float32)
        v.gain_part[block, :, edges[0] : edges[1]] = qk * mine
        v.gain_part[block, :, edges[1] : edges[2]] = v.grad_a[:, here]
        v.gain_part[block, :, cols(edges[2] // TILE + s)] = v.grad_u[:, here]
        v.gain_part[block, :, cols(edges[3] // TILE + s)] = v.grad_v[:, here]
        v.gain_part[block, :, edges[4] : edges[5]] = v.grad_m[:, here]

    inputs_slot = slots.take(1)
    plane_sum(
        v.part_inputs,
        v.got_inputs,
        inputs_slot,
        lambda index: product(v.gm[first_half, :], v.wq[cols(index, piece), :], ((1,), (1,))),
    )
    gain_line_slot = slots.take(1)
    for distance in range(1, 2 * lines):
        target = (f + distance) % (2 * lines)
        put(
            v.gain_part.at[target],
            v.gain_got.at[distance - 1],
            (s, target),
            BY_GAIN_LINE,
            gain_line_slot,
        )
    landed(v.gm.at[second_half, :], mate_gm_slot)
    line_qkv_slot = slots.take(3)
    landed(v.send_wo.at[: parts - 1], part_out_slot)
    line_grad_first(v.send_wo, v.line_wo, line_out_slot, slice(None))
    weight_grad(v.turned_x, v.gm, v.send_qkv, v.line_qkv, 3 * span, line_qkv_slot, True)
    line_grad_rest(v.send_wo, v.line_wo, line_out_slot, True)

    def line_total(grads, arrived, done, columns, base, chained=False):
        def add(slots_in):
            landed(arrived.at[: len(slots_in)], base + 1)

            def tile(index):
                there = cols(index, 256)
                total = grads[z, :, there].astype(jnp.float32)
                for slot in slots_in:
                    total = total + arrived[slot, :, there].astype(jnp.float32)
                done[:, there] = low(total)

            loop(columns // 256, tile)

        pl.when(outer)(lambda: add((0, 1)))
        pl.when(inner)(lambda: add((1, 3) if chained else (1, 2, 3)))

    line_total(v.send_down, v.line_down, v.done_down, model, line_down_slot)
    back_down_slot = slots.take(1)
    for distance in range(1, parts):
        target = plane(distance)
        put(
            v.done_down.at[:, cols(target, part_cols)],
            v.made_back_down.at[cols(s), :],
            (target, f),
            BY_PLANE,
            back_down_slot,
        )
    v.made_back_down[cols(s), :] = v.done_down[:, cols(s, part_cols)]

    line_total(v.send_uv, v.line_uv, v.done_uv, 2 * hid, line_uv_slot)
    back_uv_slot = slots.take(1)
    for distance in range(1, parts):
        target = plane(distance)
        for index in range(blocks_uv):
            put(
                v.done_uv.at[:, pl.ds(pl.multiple_of(target * wide + index * TILE, TILE), TILE)],
                v.made_back_uv.at[s, :, index * TILE : (index + 1) * TILE],
                (target, f),
                BY_PLANE,
                back_uv_slot,
            )
    v.made_back_uv[s] = v.done_uv[:, cols(s, wide)]

    weight_combine(v.send_wo, v.line_wo, part_cols, line_out_slot)
    weight_combine(v.send_qkv, v.line_qkv, 3 * span, line_qkv_slot)
    plane_sum_wait(v.got_inputs, inputs_slot)

    def finish_inputs(index):
        at, here = chunk(index)
        v.made_input_grad[at, :] = v.grad_tokens[at, :] + plane_total(v.part_inputs, v.got_inputs, here, at)

    loop(rows // chunk_rows, finish_inputs)
    deliver(1).start()

    weight_combine_mid(v.send_qkv, v.line_qkv, 3 * span, line_qkv_slot)
    gain_plane_slot = slots.take(1)
    landed(v.gain_got, gain_line_slot)
    total = v.gain_part[f]
    for distance in range(1, 2 * lines):
        total = total + v.gain_got[distance - 1]
    v.gain_sum[s] = total
    for distance in range(1, parts):
        put(
            v.gain_sum.at[s],
            v.gain_sum.at[s],
            (plane(distance), f),
            BY_GAIN_PLANE,
            gain_plane_slot,
        )

    weight_combine_mid(v.send_wo, v.line_wo, part_cols, line_out_slot)
    line_total(v.send_qkv, v.line_qkv, v.done_qkv, 3 * span, line_qkv_slot, True)
    back_qkv_slot = slots.take(1)
    for block in range(3):
        chunk_of = parts * block + s
        target = chunk_of // 3
        index = chunk_of % 3
        source = v.done_qkv.at[:, block * span : (block + 1) * span]

        @pl.when(target == s)
        def _():
            v.made_back_qkv[index] = source[...]

        @pl.when(target != s)
        def _():
            put(
                source,
                v.made_back_qkv.at[index],
                (target, f),
                BY_PLANE,
                back_qkv_slot,
            )


    landed(v.made_back_down.at[: (parts - 1) * TILE, :], back_down_slot)
    deliver(5).start()
    landed(v.made_back_uv.at[: parts - 1], back_uv_slot)
    deliver(4).start()
    landed(v.gain_sum.at[: parts - 1], gain_plane_slot)
    total = v.gain_sum[0]
    for source in range(1, parts):
        total = total + v.gain_sum[source]
    v.made_gains[...] = total
    deliver(6).start()
    landed(v.made_back_qkv.at[:2], back_qkv_slot)
    deliver(2).start()

    line_total(v.send_wo, v.line_wo, v.made_back_out, part_cols, line_out_slot, True)
    deliver(3).start()

    def sent(group, size):
        ref = v.wu.at[: size // (2 * hid), :]
        descriptor(ref, group, 0).wait_send()

    a_weight = TILE * (3 * span + 2 * hid + model + part_cols)
    sent(BY_SHARE, 4 * 6 * (rows // 2) * model)
    sent(BY_SUM, 4 * (parts - 1) * rows * model)
    sent(BY_WIDE, lines * TILE * 2 * hid + slots_all * 2 * hid)
    sent(BY_MATE_B, 2 * slots_all * model + lines * TILE * model)
    sent(BY_MATE_C, (3 * lines * TILE + 3 * span) * slots_all + lines * TILE * 3 * span)
    sent(BY_MATE_D, TILE * slots_all + TILE * model)
    pl.when(inner)(lambda: sent(BY_LINE, 4 * a_weight))
    pl.when(outer)(lambda: sent(BY_LINE, 2 * a_weight))
    sent(BY_GRAD, 3 * a_weight)
    sent(BY_PLANE, 2 * (2 * TILE * span + (parts - 1) * TILE * (wide + 2 * part_cols)))
    descriptor(v.gain_got, BY_GAIN, 0).wait_send()
    descriptor(v.gain_got, BY_GAIN_LINE, 0).wait_send()
    descriptor(v.gain_sum.at[: parts - 1], BY_GAIN_PLANE, 0).wait_send()
    for index in range(len(Results._fields)):
        deliver(index).wait()
    assert slots.count <= SLOTS_MOST, slots.count


SLOTS_MOST = 77
SHARE = 4
BY_SHARE, BY_SUM, BY_WIDE, BY_MATE_B, BY_MATE_C, BY_MATE_D = range(6)
BY_LINE, BY_GRAD, BY_PLANE, BY_GAIN, BY_GAIN_LINE, BY_GAIN_PLANE = range(6, 12)


class Inputs(typing.NamedTuple):
    tokens: typing.Any
    lengths: typing.Any
    w_qkv: typing.Any
    w_out: typing.Any
    w_uv: typing.Any
    w_down: typing.Any
    s_qk: typing.Any
    alpha_a: typing.Any
    s_u: typing.Any
    s_v: typing.Any
    alpha_m: typing.Any
    cotangent: typing.Any


class Results(typing.NamedTuple):
    output: typing.Any
    input_grad: typing.Any
    back_qkv: typing.Any
    back_out: typing.Any
    back_uv: typing.Any
    back_down: typing.Any
    gains: typing.Any


def buffers(sizes):
    (parts, lines, rows, model, deep, own_heads, width) = sizes
    every = parts * rows
    span = own_heads * width
    hid = deep * lines * 2 // parts
    half = lines * TILE
    gains = 3 * TILE + 2 * deep
    bf16, f32 = jnp.bfloat16, jnp.float32
    return dict(
        wq=((model, 3 * span), bf16),
        wo=((span, model), bf16),
        wz=((model, model // parts), bf16),
        cotangent=((rows, model), bf16),
        made_output=((rows, model), bf16),
        made_input_grad=((rows, model), f32),
        made_back_qkv=((3, TILE, span), bf16),
        made_back_out=((TILE, model // parts), bf16),
        made_back_uv=((parts, TILE, 2 * hid // parts), bf16),
        made_back_down=((deep, model // parts), bf16),
        made_gains=((1, gains), f32),
        wu=((model, 2 * hid), bf16),
        wd=((hid, model), bf16),
        gain_all=((2 * lines, 1, gains), f32),
        gain_a=((1, model), f32),
        gain_m=((1, model), f32),
        gain_u=((1, hid), f32),
        gain_v=((1, hid), f32),
        gain_qk=((1, span), f32),
        x_all=((every, model), bf16),
        first_all=((every, model), bf16),
        gd=((2 * every, model), bf16),
        gb=((2 * every, model), bf16),
        cosine=((every, TILE), f32),
        sine=((every, TILE), f32),
        bias=((every, every), f32),
        raw=((every, 3 * span), f32),
        normed=((every, 2 * span), f32),
        inverse=((every, 2 * span), f32),
        qkv=((every, 3 * span), bf16),
        total=((own_heads, every, 1), f32),
        attended=((every, span), bf16),
        branch_normed=((rows, model), f32),
        branch_inverse=((rows, 1), f32),
        first=((rows, model), f32),
        first_inverse=((rows, 1), f32),
        up=((every, hid), f32),
        gate=((every, hid), f32),
        hidden=((every, hid), bf16),
        grad_hidden=((every, 256), bf16),
        gu=((2 * every, 2 * hid), bf16),
        grad_first=((rows, model), f32),
        grad_tokens=((rows, model), f32),
        grad_att=((every, span), bf16),
        grad_qkv=((every, 3 * span), f32),
        gm=((2 * every, 3 * span), bf16),
        grad_a=((1, model), f32),
        grad_m=((1, model), f32),
        grad_u=((1, hid), f32),
        grad_v=((1, hid), f32),
        grad_qk=((1, span), f32),
        gain_part=((2 * lines, 1, gains), f32),
        gain_got=((2 * lines - 1, 1, gains), f32),
        gain_sum=((parts, 1, gains), f32),
        turned_x=((half, 2 * every), bf16),
        turned_first=((half, 2 * every), bf16),
        turned_hidden=((half, 2 * every), bf16),
        turned_att=((TILE, 2 * every), bf16),
        stage_x=((half, every), bf16),
        stage_first=((half, every), bf16),
        stage_hidden=((half, every), bf16),
        stage_att=((TILE, every), bf16),
        send_out=((TILE, model), bf16),
        send_wo=((lines, TILE, model // parts), bf16),
        line_wo=((4, TILE, model // parts), bf16),
        part_branch=((every, model), bf16),
        got_branch=((parts - 1, rows, model), bf16),
        part_down=((every, model), bf16),
        got_down=((parts - 1, rows, model), bf16),
        part_first=((every, model), bf16),
        got_first=((parts - 1, rows, model), bf16),
        part_inputs=((every, model), bf16),
        got_inputs=((parts - 1, rows, model), bf16),
        send_qkv=((lines, TILE, 3 * span), bf16),
        line_qkv=((4, TILE, 3 * span), bf16),
        done_qkv=((TILE, 3 * span), bf16),
        send_uv=((lines, TILE, 2 * hid), bf16),
        line_uv=((4, TILE, 2 * hid), bf16),
        done_uv=((TILE, 2 * hid), bf16),
        send_down=((lines, TILE, model), bf16),
        line_down=((4, TILE, model), bf16),
        done_down=((TILE, model), bf16),
    )


def place_results(sizes, *refs):
    (parts, lines, rows, model, deep, own_heads, width) = sizes
    count = len(Results._fields)
    got = Results(*refs[:count])
    (output, inputs, qkv, out, uv, down, *gains) = refs[count:]
    output[...] = got.output[...]
    inputs[...] = got.input_grad[...]
    span = own_heads * width
    for index in range(qkv.shape[1] // span):
        qkv[:, index * span : (index + 1) * span] = got.back_qkv[index].astype(jnp.float32)
    out[...] = got.back_out[...].astype(jnp.float32)
    for source in range(parts):
        for index in range(uv.shape[1] // (parts * TILE)):
            there = (index * parts + source) * TILE
            here = slice(index * TILE, (index + 1) * TILE)
            uv[:, there : there + TILE] = got.back_uv[source, :, here].astype(jnp.float32)
    down[...] = got.back_down[...].astype(jnp.float32)
    start = 0
    for gain in gains:
        stop = start + gain.shape[-1]
        gain[...] = got.gains[:, start:stop]
        start = stop


def fused(sizes):
    (parts, lines, rows, model, deep, own_heads, width) = sizes
    span = own_heads * width
    hid = deep * lines * 2 // parts

    def run(tokens, lengths, w_qkv, w_out, w_uv, w_down, *others):
        gains, cotangent = others[:5], others[5]
        f32, bf16 = jnp.float32, jnp.bfloat16
        struct = jax.ShapeDtypeStruct
        middle = Results(
            struct(tokens.shape[1:], bf16),
            struct(tokens.shape[1:], f32),
            struct((3, TILE, span), bf16),
            struct(w_out.shape, bf16),
            struct((parts, TILE, 2 * hid // parts), bf16),
            struct(w_down.shape, bf16),
            struct((1, sum(g.shape[0] for g in gains)), f32),
        )
        shapes = [
            struct(tokens.shape[1:], bf16),
            struct(tokens.shape[1:], f32),
            *(struct(w.shape, f32) for w in (w_qkv, w_out, w_uv, w_down)),
            *(struct((1, g.shape[0]), f32) for g in gains),
        ]
        vmem = pl.BlockSpec(memory_space=pltpu.VMEM)
        specs = [vmem] * len(Inputs._fields)
        for place in (0, 2, 3, 4, 5, 11):
            specs[place] = pl.BlockSpec(memory_space=pl.ANY)
        specs[1] = pl.BlockSpec(memory_space=pltpu.SMEM)
        scratch = [pltpu.VMEM(shape, kind) for shape, kind in buffers(sizes).values()]
        found = pl.pallas_call(
            functools.partial(fused_layer, sizes),
            out_shape=list(middle),
            in_specs=specs,
            out_specs=[pl.BlockSpec(memory_space=pl.ANY)] * len(middle),
            scratch_shapes=[
                *scratch,
                pltpu.SemaphoreType.DMA((12,)),
                pltpu.SemaphoreType.DMA((SLOTS_MOST,)),
                pltpu.SemaphoreType.DMA((6 + len(Results._fields),)),
            ],
            compiler_params=pltpu.CompilerParams(
                collective_id=0, has_side_effects=True, vmem_limit_bytes=67043328
            ),
            name="fused_layer",
        )(
            tokens[0],
            lengths,
            w_qkv,
            w_out,
            w_uv,
            w_down,
            *gains,
            cotangent[0],
        )
        outs = pl.pallas_call(
            functools.partial(place_results, sizes),
            out_shape=shapes,
            in_specs=[vmem] * len(middle),
            out_specs=[vmem] * len(shapes),
            compiler_params=pltpu.CompilerParams(vmem_limit_bytes=67043328),
            name="place_results",
        )(*found)
        return (
            outs[0][None],
            outs[1][None],
            *outs[2:6],
            *(g.reshape(-1) for g in outs[6:]),
        )

    return run


def choose(parts, shards):
    def run(*args):
        tokens, w_qkv, w_down = args[0], args[2], args[5]
        rows, model = tokens.shape[1:]
        deep, width = w_down.shape[0], model // H
        fits = shards == 2 * parts and rows == TILE and w_qkv.shape[0] == TILE
        fits = fits and deep == parts * TILE and 2 * width == TILE and H == 4 * parts
        if not fits:
            return local(*args)
        return fused((parts, shards // 2, rows, model, deep, H // parts, width))(*args)

    return run


def solution(mesh):
    return jax.shard_map(
        choose(mesh.shape["seq"], mesh.shape["fsdp"]),
        mesh=mesh,
        in_specs=(
            P("fsdp", "seq", None),
            P("fsdp", None),
            P("fsdp", "seq"),
            P("fsdp", "seq"),
            P("fsdp", "seq"),
            P("fsdp", "seq"),
            P("fsdp"),
            P("fsdp"),
            P("fsdp"),
            P("fsdp"),
            P("fsdp"),
            P("fsdp", "seq", None),
        ),
        out_specs=(
            P("fsdp", "seq", None),
            P("fsdp", "seq", None),
            P("fsdp", "seq"),
            P("fsdp", "seq"),
            P("fsdp", "seq"),
            P("fsdp", "seq"),
            P("fsdp"),
            P("fsdp"),
            P("fsdp"),
            P("fsdp"),
            P("fsdp"),
        ),
        check_vma=False,
    )
```

```python
import functools
import math
import types
import typing

import jax
import jax.numpy as jnp
from jax import lax
from jax.experimental import pallas as pl
from jax.experimental.pallas import tpu as pltpu
from jax.sharding import PartitionSpec as P

H = 16


epsilon = 1e-06


def layout(lengths_row, slot):
    columns = lengths_row.shape[0]
    ends = jnp.cumsum(lengths_row)
    starts = ends - lengths_row
    before = (slot[:, None] >= ends[None, : columns - 1]).astype(jnp.int32)
    member = jnp.sum(before, axis=1)
    picked = member[:, None] == jnp.arange(columns, dtype=jnp.int32)[None, :]
    begin = jnp.sum(jnp.where(picked, starts[None, :], 0), axis=1)
    valid = member < columns - 1
    segment = jnp.where(valid, member, columns - 1 + slot)
    place = jnp.where(valid, slot - begin, 0)
    return (segment, place, valid)


def rotary(place, width):
    half = width // 2
    frequency = jnp.exp(jnp.arange(half, dtype=jnp.float32) * (-2.0 * math.log(10000.0) / width))
    angle = place.astype(jnp.float32)[:, None] * frequency[None, :]
    return (jnp.cos(angle)[:, None, :], jnp.sin(angle)[:, None, :])


def unit_rows(value):
    return value * lax.rsqrt(jnp.mean(value * value, axis=-1, keepdims=True) + epsilon)


def turn_heads(value, cosine, sine):
    half = value.shape[-1] // 2
    first = value[..., :half]
    second = value[..., half:]
    return jnp.concatenate(
        [first * cosine - second * sine, second * cosine + first * sine], axis=-1
    )


def prepare(query_raw, key_raw, s_qk, cosine, sine, heads):
    rows = query_raw.shape[0]
    scales = s_qk.reshape(heads, -1)

    def normed(raw):
        shaped = raw.reshape(rows, heads, -1)
        return (unit_rows(turn_heads(shaped, cosine, sine)) * scales).reshape(rows, -1)

    return (normed(query_raw), normed(key_raw))


def blend(base, branch, alpha):
    return unit_rows(base + alpha * (unit_rows(branch) - base))


def gated(up_gate, s_u, s_v):
    width = s_u.shape[0]
    return up_gate[:, :width] * s_u * jax.nn.silu(up_gate[:, width:] * s_v)


def rounded(value):
    return lax.optimization_barrier(value.astype(jnp.bfloat16)).astype(jnp.float32)


def attention_forward(query, key, value, mask):
    scale = 1.0 / math.sqrt(query.shape[2])
    score = jnp.einsum("thd,shd->hts", query, key, preferred_element_type=jnp.float32)
    score = jnp.where(mask[None], score * scale, -1e30)
    peak = jnp.max(score, axis=2, keepdims=True)
    raised = jnp.exp(score - peak)
    summed = jnp.sum(raised, axis=2, keepdims=True)
    weight = (raised / summed).astype(jnp.bfloat16)
    result = jnp.einsum("hts,shd->thd", weight, value, preferred_element_type=jnp.float32)
    return result, peak + jnp.log(summed)


def attention_backward(query, key, value, mask, log_total, grad):
    scale = 1.0 / math.sqrt(query.shape[2])
    score = jnp.einsum("thd,shd->hts", query, key, preferred_element_type=jnp.float32)
    score = jnp.where(mask[None], score * scale, -1e30)
    share = jnp.exp(score - log_total)
    grad_value = jnp.einsum(
        "hts,thd->shd", share.astype(jnp.bfloat16), grad, preferred_element_type=jnp.float32
    )
    grad_share = jnp.einsum("thd,shd->hts", grad, value, preferred_element_type=jnp.float32)
    inner = jnp.sum(share * grad_share, axis=2, keepdims=True)
    grad_score = (share * (grad_share - inner)).astype(jnp.bfloat16)
    grad_query = jnp.einsum("hts,shd->thd", grad_score, key, preferred_element_type=jnp.float32)
    grad_key = jnp.einsum("hts,thd->shd", grad_score, query, preferred_element_type=jnp.float32)
    return grad_query * scale, grad_key * scale, grad_value


def low(value):
    return value.astype(jnp.bfloat16)


def product(left, right, dims):
    return lax.dot_general(left, right, (dims, ((), ())), preferred_element_type=jnp.float32)


def local(tokens, lengths, w_qkv, w_out, w_uv, w_down, s_qk, alpha_a, s_u, s_v, alpha_m, cotangent):
    rows = tokens.shape[1]
    model = tokens.shape[2]
    width = model // H
    parts = lax.axis_size("seq")
    shards = lax.axis_size("fsdp")
    mine = lax.axis_index("seq")
    own = H // parts
    deep = w_down.shape[0]
    hidden_all = deep * shards
    hidden_own = hidden_all // parts
    piece = deep // parts
    slot = mine * rows + jnp.arange(rows, dtype=jnp.int32)
    every_slot = jnp.arange(rows * parts, dtype=jnp.int32)
    keep = layout(lengths[0], slot)[2].astype(jnp.float32)[:, None]
    segment, place, _ = layout(lengths[0], every_slot)
    mask = (segment[:, None] == segment[None, :]) & (every_slot[:, None] >= every_slot[None, :])

    def exchange(array, axis):
        return lax.all_to_all(array, "seq", axis, axis, tiled=False)

    def gather(array, axis=0):
        return lax.all_gather(array, "fsdp", axis=axis, tiled=True)

    def spread(array):
        return lax.all_gather(array, "seq", axis=0, tiled=True)

    r_in = w_qkv.shape[0]
    share_qkv = lax.all_to_all(
        w_qkv.reshape(r_in, -1, parts, width), "seq", 2, 1, tiled=True
    ).reshape(r_in, -1)
    share_uv = lax.all_to_all(
        w_uv.reshape(r_in, -1, parts, piece), "seq", 2, 1, tiled=True
    ).reshape(r_in, -1)
    share_down = lax.all_to_all(w_down.reshape(parts, piece, -1), "seq", 0, 2, tiled=True)
    share_down = share_down.reshape(piece, model)
    share_out = lax.all_gather(w_out, "seq", axis=1, tiled=True)
    inputs = spread(tokens[0])
    full_qkv = gather(share_qkv)
    full_out = gather(share_out).reshape(own, parts, width, model)
    full_out = lax.dynamic_index_in_dim(full_out, mine, 1, False).reshape(own * width, model)
    full_uv = gather(share_uv)
    full_down = gather(share_down)
    gains = gather(jnp.concatenate([s_qk, alpha_a, s_u, s_v, alpha_m])[None]).astype(jnp.float32)
    cuts = [s_qk.shape[0], alpha_a.shape[0], s_u.shape[0], s_v.shape[0]]
    edges = [sum(cuts[: i + 1]) for i in range(4)]
    gain_qk, gain_a, gain_u, gain_v, gain_m = jnp.split(gains, edges, axis=1)
    gain_qk = gain_qk.reshape(own, parts, width)
    gain_qk = lax.dynamic_index_in_dim(gain_qk, mine, 1, False).reshape(-1)
    gain_a, gain_m = gain_a.reshape(-1), gain_m.reshape(-1)
    gain_u = lax.dynamic_index_in_dim(gain_u.reshape(shards, parts, piece), mine, 1, False).reshape(-1)
    gain_v = lax.dynamic_index_in_dim(gain_v.reshape(shards, parts, piece), mine, 1, False).reshape(-1)

    mixed = product(inputs, full_qkv, ((1,), (0,)))
    cosine, sine = rotary(place, width)
    span = own * width

    def prepare_local(query_raw, key_raw, scale_qk):
        return prepare(query_raw, key_raw, scale_qk, cosine, sine, own)

    (query_f, key_f), pull_prepare = jax.vjp(
        prepare_local, mixed[:, :span], mixed[:, span : 2 * span], gain_qk
    )
    heads = (rows * parts, own, width)
    query, key = low(query_f).reshape(heads), low(key_f).reshape(heads)
    value = low(mixed[:, 2 * span :]).reshape(heads)
    attended, log_total = attention_forward(query, key, value, mask)
    attended = low(attended.reshape(-1, span))

    def reduce_rows(array):
        return lax.psum_scatter(low(array), "seq", scatter_dimension=0, tiled=True).astype(
            jnp.float32
        )

    branch = reduce_rows(product(attended, full_out, ((1,), (0,))))
    first, pull_first = jax.vjp(blend, tokens[0].astype(jnp.float32), branch, gain_a)
    first_all = spread(low(first))
    up_gate = product(first_all, full_uv, ((1,), (0,)))
    hidden_f, pull_gate = jax.vjp(gated, up_gate, gain_u, gain_v)
    hidden = low(hidden_f)
    down = reduce_rows(product(hidden, full_down, ((1,), (0,))))
    final, pull_last = jax.vjp(blend, first, down, gain_m)
    output = low(final * keep)
    grad_first, grad_down, grad_gain_m = pull_last(cotangent[0].astype(jnp.float32) * keep)
    grad_down = spread(low(grad_down))
    grad_w_down = low(product(hidden, grad_down, ((0,), (0,))))
    grad_hidden = rounded(product(grad_down, full_down, ((1,), (1,))))
    grad_up_gate, grad_gain_u, grad_gain_v = pull_gate(grad_hidden)
    grad_up = low(grad_up_gate)
    grad_w_uv = low(product(first_all, grad_up, ((0,), (0,))))
    grad_first = grad_first + reduce_rows(product(grad_up, full_uv, ((1,), (1,))))
    grad_inputs, grad_branch, grad_gain_a = pull_first(grad_first)
    grad_branch = spread(low(grad_branch))
    grad_w_out = low(product(attended, grad_branch, ((0,), (0,))))
    grad_attended = low(product(grad_branch, full_out, ((1,), (1,)))).reshape(heads)
    grad_query, grad_key, grad_value = attention_backward(
        query, key, value, mask, log_total, grad_attended
    )
    grad_query_raw, grad_key_raw, grad_gain_qk = pull_prepare(
        (rounded(grad_query).reshape(-1, span), rounded(grad_key).reshape(-1, span))
    )
    grad_mixed = low(
        jnp.concatenate([grad_query_raw, grad_key_raw, grad_value.reshape(-1, span)], axis=1)
    )
    grad_w_qkv = low(product(inputs, grad_mixed, ((0,), (0,))))
    grad_inputs = grad_inputs + reduce_rows(product(grad_mixed, full_qkv, ((1,), (1,))))

    def collect(array):
        return lax.psum_scatter(array, "fsdp", scatter_dimension=0, tiled=True)

    part_down = collect(grad_w_down)
    out_down = lax.all_to_all(
        part_down.reshape(1, piece, model), "seq", 2, 0, tiled=True
    ).reshape(deep, -1)
    part_uv = collect(grad_w_uv)
    out_uv = lax.all_to_all(
        part_uv.reshape(r_in, -1, 1, piece), "seq", 1, 2, tiled=True
    ).reshape(r_in, -1)
    placed = jnp.zeros((own, parts, width, model), jnp.bfloat16)
    placed = lax.dynamic_update_slice(
        placed, grad_w_out.reshape(own, 1, width, model), (0, mine, 0, 0)
    )
    part_out = collect(placed.reshape(-1, model))
    out_out = lax.psum_scatter(part_out, "seq", scatter_dimension=1, tiled=True)
    part_qkv = collect(grad_w_qkv)
    out_qkv = lax.all_to_all(
        part_qkv.reshape(r_in, -1, 1, width), "seq", 1, 2, tiled=True
    ).reshape(r_in, -1)

    def widen(array, outer, inner):
        blank = jnp.zeros((outer, parts, inner), jnp.float32)
        array = array.reshape(outer, 1, inner)
        return lax.dynamic_update_slice(blank, array, (0, mine, 0)).reshape(shards, -1)

    gain_sums = jnp.concatenate(
        [
            widen(grad_gain_qk, own, width),
            grad_gain_a.reshape(shards, -1),
            widen(grad_gain_u, shards, piece),
            widen(grad_gain_v, shards, piece),
            grad_gain_m.reshape(shards, -1),
        ],
        axis=1,
    )
    gain_sums = lax.psum(collect(gain_sums), "seq")[0]
    outs = jnp.split(gain_sums, edges)
    return (
        output[None],
        grad_inputs[None],
        out_qkv.astype(jnp.float32),
        out_out.astype(jnp.float32),
        out_uv.astype(jnp.float32),
        out_down.astype(jnp.float32),
        outs[0],
        outs[1],
        outs[2],
        outs[3],
        outs[4],
    )


MESH = pl.DeviceIdType.MESH
TILE = 128
QROWS = 128


def loop(count, body):
    def run(index, carry):
        body(index)
        return carry

    lax.fori_loop(0, count, run, 0)


def at_rows(ref, block, size=TILE):
    return ref.at[pl.ds(pl.multiple_of(block * size, size), size), :]


def cols(block, size=TILE):
    return pl.ds(pl.multiple_of(block * size, size), size)


def mean_last(value):
    return jnp.sum(value, axis=-1, keepdims=True) * (1.0 / value.shape[-1])


class Slots:
    def __init__(self):
        self.count = 0

    def take(self, count):
        base = self.count
        self.count = base + count
        return base


def fused_layer(sizes, *refs):
    (parts, lines, rows, model, deep, own_heads, width) = sizes
    slots_all = parts * rows
    span = own_heads * width
    hid = deep * lines * 2 // parts
    count_in, count_out = len(Inputs._fields), len(Results._fields)
    ins = Inputs(*refs[:count_in])
    outs = Results(*refs[count_in : count_in + count_out])
    table = buffers(sizes)
    rest = refs[count_in + count_out :]
    v = types.SimpleNamespace(**dict(zip(table, rest[: len(table)])))
    send_sem, recv_sem, local_sem = rest[len(table) :]

    s = lax.axis_index("seq")
    f = lax.axis_index("fsdp")
    z = f // 2
    c = f % 2
    other = 1 - c
    mate = (s, 2 * z + other)
    slots = Slots()

    def put(src, dst, target, send_slot, recv_slot):
        pltpu.make_async_remote_copy(
            src_ref=src,
            dst_ref=dst,
            send_sem=send_sem.at[send_slot],
            recv_sem=recv_sem.at[recv_slot],
            device_id=target,
            device_id_type=MESH,
        ).start()

    def descriptor(ref, send_slot, recv_slot):
        return pltpu.make_async_remote_copy(
            src_ref=ref,
            dst_ref=ref,
            send_sem=send_sem.at[send_slot],
            recv_sem=recv_sem.at[recv_slot],
            device_id=mate,
            device_id_type=MESH,
        )

    def landed(ref, slot):
        descriptor(ref, 0, slot).wait_recv()

    def plane(distance):
        return (s + distance) % parts

    def plane_from(distance):
        return (s + parts - distance) % parts

    def line(distance):
        return (z + distance) % lines

    def line_from(distance):
        return (z + lines - distance) % lines

    barrier = pltpu.get_barrier_semaphore()
    for distance in range(1, parts):
        pl.semaphore_signal(barrier, inc=1, device_id=(plane(distance), f), device_id_type=MESH)
    for distance in range(1, 2 * lines):
        target = (s, (f + distance) % (2 * lines))
        pl.semaphore_signal(barrier, inc=1, device_id=target, device_id_type=MESH)

    edges = [0, TILE, 2 * TILE, 2 * TILE + deep, 2 * TILE + 2 * deep, 3 * TILE + 2 * deep]
    own_gains = (ins.s_qk, ins.alpha_a, ins.s_u, ins.s_v, ins.alpha_m)
    for place, own_gain in enumerate(own_gains):
        row = own_gain[...].astype(jnp.float32).reshape(1, -1)
        v.gain_all[f, :, edges[place] : edges[place + 1]] = row
    own_row = pl.ds(pl.multiple_of(s * rows, rows), rows)
    own_w = pl.ds(pl.multiple_of(f * TILE, TILE), TILE)
    part_cols = model // parts
    blocks_uv = 2 * hid // parts // TILE
    wide = blocks_uv * TILE

    def fetch(src, dst, slot):
        pltpu.make_async_copy(src, dst, local_sem.at[slot]).start()

    def deliver(index):
        made = (
            v.made_output,
            v.made_input_grad,
            v.made_back_qkv,
            v.made_back_out,
            v.made_back_uv,
            v.made_back_down,
            v.made_gains,
        )
        return pltpu.make_async_copy(made[index], outs[index], local_sem.at[6 + index])

    def fetched(dst, slot):
        pltpu.make_async_copy(dst, dst, local_sem.at[slot]).wait()

    fetch(ins.w_out, v.wz.at[own_w, :], 0)
    fetch(ins.tokens, v.x_all.at[own_row, :], 1)
    for index in range(blocks_uv):
        fetch(
            ins.w_uv.at[:, pl.ds(pl.multiple_of((index * parts + s) * TILE, TILE), TILE)],
            v.wu.at[own_w, pl.ds(pl.multiple_of(s * wide + index * TILE, TILE), TILE)],
            2,
        )
    fetch(ins.w_down.at[cols(s), :], v.wd.at[own_w, cols(s, part_cols)], 3)
    fetch(ins.cotangent, v.cotangent, 4)
    for index in range(3):
        chunk = 3 * s + index

        @pl.when(chunk % parts == s)
        def _():
            fetch(
                ins.w_qkv.at[:, index * span : (index + 1) * span],
                v.wq.at[own_w, cols(chunk // parts, span)],
                5,
            )

    pl.semaphore_wait(barrier, parts - 1 + 2 * lines - 1)

    qkv_slot = slots.take(1)
    for index in range(3):
        chunk = 3 * s + index
        block = chunk // parts
        target = chunk % parts

        @pl.when(target != s)
        def _():
            put(
                ins.w_qkv.at[:, index * span : (index + 1) * span],
                v.wq.at[own_w, cols(block, span)],
                (target, f),
                BY_PLANE,
                qkv_slot,
            )


    side, across, opposite = s + 1 - 2 * (s % 2), (s + 2) % parts, parts - 1 - s

    def half_of(shared, owner, part):
        start = owner * rows + part * (rows // 2)
        return shared.at[pl.ds(pl.multiple_of(start, rows // 2), rows // 2), :]

    token_slot = slots.take(SHARE)
    for part in range(2):
        mine = ins.tokens.at[part * (rows // 2) : (part + 1) * (rows // 2), :]
        there = half_of(v.x_all, s, part)
        put(mine, there, (side, f), BY_SHARE, token_slot + 2 * part)
        put(mine, there, (across, f), BY_SHARE, token_slot + 2 - part)

    gain_slot = slots.take(1)
    for distance in range(1, 2 * lines):
        put(
            v.gain_all.at[f],
            v.gain_all.at[f],
            (s, (f + distance) % (2 * lines)),
            BY_GAIN,
            gain_slot,
        )

    def plane_share_relay(shared, base, passed=None):
        one, two = half_of(shared, side, 0), half_of(shared, across, 1)
        if passed is not None:
            passed(s, 0)
            passed(s, 1)
        landed(one, base)
        put(one, one, (across, f), BY_SHARE, base + 3)
        landed(two, base + 1)
        put(two, two, (side, f), BY_SHARE, base + 3)
        if passed is not None:
            passed(side, 0)
            passed(across, 1)

    def plane_share_wait(shared, base, passed=None):
        for pieces, slot in (
            (((side, 1), (across, 0)), base + 2),
            (((opposite, 0), (opposite, 1)), base + 3),
        ):
            landed(at_rows(shared, opposite, rows), slot)
            if passed is not None:
                for piece_of in pieces:
                    passed(*piece_of)

    def pass_to_mate(shared, slot):
        def passed(owner, part):
            start = owner * rows + part * (rows // 2)
            here = pl.ds(pl.multiple_of(start, rows // 2), rows // 2)
            there = pl.ds(pl.multiple_of(slots_all + start, rows // 2), rows // 2)
            put(shared.at[here, :], shared.at[there, :], mate, BY_MATE_B, slot)

        return passed

    def shard(ref, chip, core, lanes):
        block = 2 * chip + core
        return ref.at[pl.ds(pl.multiple_of(block * TILE, TILE), TILE), lanes]

    inner = z * (lines - 1 - z) > 0
    outer = z * (lines - 1 - z) == 0

    def line_send(ref, base, lanes=slice(None), twice=True, apart=False):
        own = shard(ref, z, c, lanes)
        for distance in (2, 1, 3):
            target = line(distance)
            near = (z - target) * (z - target) < (lines - 1) * (lines - 1)
            slot = base
            if apart:
                slot = base + distance - 1
            elif distance == 2:
                slot = base + target * (lines - 1 - target) // 2

            @pl.when(near)
            def _():
                put(own, own, (s, 2 * target + c), BY_LINE, slot)

        if twice:
            put(own, own, mate, mate_group(ref), base + 2 + apart)

    def mate_group(ref):
        return BY_WIDE if ref is v.wu else BY_MATE_B if ref is v.wd else BY_MATE_C

    def line_relay(ref, base, lanes=slice(None), apart=False):
        block = shard(ref, line_from(2), c, lanes)

        @pl.when(inner)
        def _():
            landed(block, base + 1)
            slot = base + 2 * z - 2 if apart else base
            put(block, block, (s, 2 * (lines - 1) * (z - 1) + c), BY_LINE, slot)

    def line_arrived(ref, base, lanes=slice(None)):
        pl.when(inner)(lambda: landed(ref.at[: 2 * TILE, lanes], base))
        pl.when(outer)(lambda: landed(ref.at[: 3 * TILE, lanes], base))

    def line_forward(ref, base, lanes=slice(None), apart=False):
        if not apart:
            line_arrived(ref, base, lanes)
        for distance in (1, 3, 2):
            block = shard(ref, line_from(distance), c, lanes)
            if apart and distance == 2:

                @pl.when(outer)
                def _():
                    landed(block, base + 1)

            elif apart:
                landed(block, base + distance - 1)
            put(block, block, mate, mate_group(ref), base + 2 + apart)

    def mate_wait(ref, base, lanes=slice(None), apart=False):
        landed(ref.at[: lines * TILE, lanes], base + 2 + apart)

    wq_slot, wu_slot = (slots.take(4) for _ in range(2))
    count = 4
    piece = model // count
    wd_parts = [
        (slots.take(3), slice(part * piece, (part + 1) * piece)) for part in range(count)
    ]
    wz_slot, wo_slot, out_slot = slots.take(2), slots.take(1), slots.take(1)
    fetched(v.wz.at[own_w, :], 0)
    line_send(v.wz, wz_slot, twice=False)

    landed(v.wq.at[own_w, : 2 * span], qkv_slot)
    fetched(v.wq.at[own_w, :span], 5)
    line_send(v.wq, wq_slot, apart=True)
    lengths = [ins.lengths[0, i] for i in range(ins.lengths.shape[1])]

    def slot_facts(slot):
        end = 0
        member = jnp.zeros(slot.shape, jnp.int32)
        begin = jnp.zeros(slot.shape, jnp.int32)
        for length in lengths[:-1]:
            end = end + length
            after = slot >= end
            member = member + after.astype(jnp.int32)
            begin = jnp.where(after, end, begin)
        valid = member < len(lengths) - 1
        segment = jnp.where(valid, member, len(lengths) - 1 + slot)
        place = jnp.where(valid, slot - begin, 0)
        return segment, place, valid

    lane = lax.broadcasted_iota(jnp.int32, (1, TILE), 1)
    low_half = lane < width
    first_quarter = lane % width < width // 2
    frequency = jnp.exp(
        (lane % (width // 2)).astype(jnp.float32) * (-2.0 * math.log(10000.0) / width)
    )
    turn_sign = jnp.where(first_quarter, -1.0, 1.0)

    def tables(block):
        here = pl.ds(pl.multiple_of(block * TILE, TILE), TILE)
        slot = block * TILE + lax.broadcasted_iota(jnp.int32, (TILE, 1), 0)
        segment, place, _ = slot_facts(slot)
        angle = place.astype(jnp.float32) * frequency
        v.cosine[here, :] = jnp.cos(angle)
        v.sine[here, :] = jnp.sin(angle) * turn_sign
        key_slot = lax.broadcasted_iota(jnp.int32, (1, slots_all), 1)
        key_segment = slot_facts(key_slot)[0]
        kept = (segment == key_segment) & (slot >= key_slot)
        v.bias[here, :] = jnp.where(kept, 0.0, -1e30)

    loop(slots_all // TILE, tables)
    fetched(v.x_all.at[own_row, :], 1)
    plane_share_relay(v.x_all, token_slot)
    uv_slot = slots.take(1)
    for distance in range(1, parts):
        target = plane(distance)
        for index in range(blocks_uv):
            put(
                ins.w_uv.at[:, pl.ds(pl.multiple_of((index * parts + target) * TILE, TILE), TILE)],
                v.wu.at[own_w, pl.ds(pl.multiple_of(s * wide + index * TILE, TILE), TILE)],
                (target, f),
                BY_PLANE,
                uv_slot,
            )

    down_slot = slots.take(1)
    for distance in range(1, parts):
        target = plane(distance)
        put(
            ins.w_down.at[cols(target), :],
            v.wd.at[own_w, cols(s, part_cols)],
            (target, f),
            BY_PLANE,
            down_slot,
        )

    line_relay(v.wz, wz_slot)
    line_relay(v.wq, wq_slot, apart=True)
    plane_share_wait(v.x_all, token_slot)
    line_arrived(v.wz, wz_slot)
    for distance in range(1, parts):
        target = plane(distance)
        rows_out = at_rows(v.wz, 2 * target + c)
        put(
            rows_out,
            v.wo.at[cols(c), cols(s, part_cols)],
            (target, f),
            BY_PLANE,
            out_slot,
        )
    v.wo[cols(c), cols(s, part_cols)] = v.wz[cols(2 * s + c), :]
    fetched(v.wu.at[own_w, cols(s, wide)], 2)
    landed(v.wu.at[own_w, : (parts - 1) * wide], uv_slot)
    line_send(v.wu, wu_slot, apart=True)

    def mate_blocks(name_all, ref, stage, slot):
        for block in range(lines):
            here = slice(block * TILE, (block + 1) * TILE)
            stage[here, :] = name_all[:, cols(2 * block + other)].T
        put(stage, ref.at[:, slots_all:], mate, BY_MATE_C, slot)
        for block in range(lines):
            here = slice(block * TILE, (block + 1) * TILE)
            ref[here, :slots_all] = name_all[:, cols(2 * block + c)].T

    mate_x_slot = slots.take(1)
    mate_blocks(v.x_all, v.turned_x, v.stage_x, mate_x_slot)
    landed(v.gain_all.at[1:], gain_slot)

    def gain(block, offset):
        return v.gain_all[block, :, pl.ds(pl.multiple_of(offset, TILE), TILE)]

    for block in range(2 * lines):
        here = slice(block * TILE, (block + 1) * TILE)
        v.gain_a[:, here] = gain(block, edges[1])
        v.gain_u[:, here] = gain(block, edges[2] + s * TILE)
        v.gain_v[:, here] = gain(block, edges[3] + s * TILE)
        v.gain_m[:, here] = gain(block, edges[4])
    for block in range(span // TILE):
        v.gain_qk[:, block * TILE : (block + 1) * TILE] = gain(span // TILE * s + block, 0)

    line_forward(v.wq, wq_slot, apart=True)
    mate_wait(v.wq, wq_slot, apart=True)

    def mix(index):
        v.raw[:, cols(index, span)] = product(
            v.x_all[...], v.wq[:, cols(index, span)], ((1,), (0,))
        )

    loop(3, mix)

    def swap(value):
        return jnp.where(
            first_quarter,
            pltpu.roll(value, TILE - width // 2, 1),
            pltpu.roll(value, width // 2, 1),
        )

    def head_mean(value):
        one = jnp.sum(jnp.where(low_half, value, 0.0), axis=-1, keepdims=True)
        two = jnp.sum(jnp.where(low_half, 0.0, value), axis=-1, keepdims=True)
        return jnp.where(low_half, one, two) * (1.0 / width)

    pairs = span // TILE
    blocks = slots_all // TILE

    def prepare_block(index):
        here = pl.ds(pl.multiple_of(0, TILE), slots_all)
        group = index
        there = cols(group)
        value = v.raw[here, there]
        turned = value * v.cosine[here, :] + swap(value) * v.sine[here, :]
        inverse = lax.rsqrt(head_mean(turned * turned) + epsilon)
        normed = turned * inverse
        v.normed[here, there] = normed
        v.inverse[here, there] = inverse
        v.qkv[here, there] = low(normed * v.gain_qk[:, cols(group % pairs)])

    loop(2 * pairs, prepare_block)

    def keep_value(index):
        here = pl.ds(pl.multiple_of(index * TILE, TILE), TILE)
        v.qkv[here, 2 * span :] = low(v.raw[here, 2 * span :])

    loop(blocks, keep_value)
    own_out = v.wo.at[cols(c), :]
    landed(v.wo.at[cols(c), : (parts - 1) * part_cols], out_slot)
    put(own_out, own_out, mate, BY_MATE_D, wo_slot)

    scale = 1.0 / math.sqrt(width)
    halves = (low_half, jnp.logical_not(low_half))

    def attend(pair):
        q_cols, k_cols, v_cols = cols(pair), cols(pairs + pair), cols(2 * pairs + pair)
        for block in range(blocks // 2):
            here = slice(block * 2 * TILE, (block + 1) * 2 * TILE)
            seen = slice(0, (block + 1) * 2 * TILE)
            results = []
            for half in range(2):
                query = jnp.where(halves[half], v.qkv[here, q_cols], 0.0).astype(jnp.bfloat16)
                score = product(query, v.qkv[seen, k_cols], ((1,), (1,))) * scale
                score = score + v.bias[here, seen]
                peak = jnp.max(score, axis=1, keepdims=True)
                raised = jnp.exp(score - peak)
                summed = jnp.sum(raised, axis=1, keepdims=True)
                weight = low(raised / summed)
                results.append(product(weight, v.qkv[seen, v_cols], ((1,), (0,))))
                v.total[2 * pair + half, here, :] = peak + jnp.log(summed)
            v.attended[here, q_cols] = low(jnp.where(low_half, results[0], results[1]))

    loop(pairs, attend)
    mate_att_slot = slots.take(1)
    v.stage_att[...] = v.attended[:, cols(other)].T
    v.turned_att[:, :slots_all] = v.attended[:, cols(c)].T

    put(v.stage_att, v.turned_att.at[:, slots_all:], mate, BY_MATE_D, mate_att_slot)
    landed(v.wo.at[cols(other), :], wo_slot)

    def plane_sum(sums, arrived, base, tile, span_of=(0, count)):
        start, stop = span_of

        def send(index):
            there = cols(index, piece)
            for distance in range(1, parts):
                target = plane(distance)
                put(
                    sums.at[pl.ds(pl.multiple_of(target * rows, rows), rows), there],
                    arrived.at[distance - 1, :, there],
                    (target, f),
                    BY_SUM,
                    base,
                )

        def step(index):
            sums[:, cols(start + index, piece)] = low(tile(start + index))

            @pl.when(index > 0)
            def _():
                send(start + index - 1)

        loop(stop - start, step)
        send(stop - 1)

    def plane_sum_wait(arrived, base):
        landed(arrived, base)

    def plane_total(sums, arrived, here, at):
        total = sums[here, :].astype(jnp.float32)
        for distance in range(1, parts):
            total = total + arrived[distance - 1, at, :].astype(jnp.float32)
        return total

    chunk_rows = 64

    def chunk(index):
        at = pl.ds(pl.multiple_of(index * chunk_rows, chunk_rows), chunk_rows)
        here = pl.ds(pl.multiple_of(s * rows + index * chunk_rows, chunk_rows), chunk_rows)
        return at, here

    def plane_share(shared, base, make):
        def send(index):
            own = shared.at[chunk(index)[1], :]
            part = index // (rows // chunk_rows // 2)
            put(own, own, (side, f), BY_SHARE, base + 2 * part)
            put(own, own, (across, f), BY_SHARE, base + 2 - part)

        def step(index):
            make(index)

            @pl.when(index > 0)
            def _():
                send(index - 1)

        loop(rows // chunk_rows, step)
        send(rows // chunk_rows - 1)

    branch_slot = slots.take(1)
    plane_sum(
        v.part_branch,
        v.got_branch,
        branch_slot,
        lambda index: product(v.attended[...], v.wo[:, cols(index, piece)], ((1,), (0,))),
    )
    line_relay(v.wu, wu_slot, apart=True)
    fetched(v.wd.at[own_w, cols(s, part_cols)], 3)
    landed(v.wd.at[own_w, : (parts - 1) * part_cols], down_slot)
    line_send(v.wd, *wd_parts[0])
    line_send(v.wd, *wd_parts[1])
    plane_sum_wait(v.got_branch, branch_slot)
    line_relay(v.wd, *wd_parts[0])
    line_send(v.wd, *wd_parts[2])

    def blended(base, branch, alpha):
        inverse_branch = lax.rsqrt(mean_last(branch * branch) + epsilon)
        normed = branch * inverse_branch
        mixed = base + alpha * (normed - base)
        inverse = lax.rsqrt(mean_last(mixed * mixed) + epsilon)
        return normed, inverse_branch, mixed * inverse, inverse

    def blended_back(grad, base, alpha, normed, inverse_branch, result, inverse):
        grad_mixed = inverse * (grad - result * mean_last(grad * result))
        grad_normed = alpha * grad_mixed
        grad_branch = inverse_branch * (grad_normed - normed * mean_last(grad_normed * normed))
        grad_alpha = jnp.sum(grad_mixed * (normed - base), axis=0, keepdims=True)
        return grad_mixed - grad_normed, grad_branch, grad_alpha

    def make_first(index):
        at, here = chunk(index)
        base = v.x_all[here, :].astype(jnp.float32)
        normed, inverse_branch, result, inverse = blended(
            base, plane_total(v.part_branch, v.got_branch, here, at), v.gain_a[...]
        )
        v.branch_normed[at, :] = normed
        v.branch_inverse[at, :] = inverse_branch
        v.first[at, :] = result
        v.first_inverse[at, :] = inverse
        v.first_all[here, :] = low(result)

    first_slot = slots.take(SHARE)
    plane_share(v.first_all, first_slot, make_first)
    line_relay(v.wd, *wd_parts[1])
    line_send(v.wd, *wd_parts[3])
    plane_share_relay(v.first_all, first_slot)
    line_relay(v.wd, *wd_parts[2])
    line_forward(v.wu, wu_slot, apart=True)
    mate_wait(v.wu, wu_slot, apart=True)
    plane_share_wait(v.first_all, first_slot)

    def gate_tile(index):
        there = cols(index, 256)
        v.up[:, there] = product(v.first_all[...], v.wu[:, there], ((1,), (0,)))
        v.gate[:, there] = product(
            v.first_all[...],
            v.wu[:, pl.ds(pl.multiple_of(hid + index * 256, 256), 256)],
            ((1,), (0,)),
        )

        def rows_of(block):
            here = pl.ds(pl.multiple_of(block * 64, 64), 64)
            scaled = v.gate[here, there] * v.gain_v[:, there]
            passed = scaled / (1.0 + jnp.exp(-scaled))
            v.hidden[here, there] = low(v.up[here, there] * v.gain_u[:, there] * passed)

        loop(slots_all // 64, rows_of)

    line_relay(v.wd, *wd_parts[3])
    loop(hid // 512, gate_tile)
    line_forward(v.wd, *wd_parts[0])
    loop(hid // 512, lambda index: gate_tile(hid // 512 + index))
    mate_hidden_slot = slots.take(1)
    mate_blocks(v.hidden, v.turned_hidden, v.stage_hidden, mate_hidden_slot)
    mate_first_slot = slots.take(1)
    mate_blocks(v.first_all, v.turned_first, v.stage_first, mate_first_slot)
    down_sum_slot = slots.take(1)

    def down_tile(index):
        return product(v.hidden[...], v.wd[:, cols(index, piece)], ((1,), (0,)))

    line_forward(v.wd, *wd_parts[1])
    for part in range(count):
        mate_wait(v.wd, *wd_parts[part])
        plane_sum(v.part_down, v.got_down, down_sum_slot, down_tile, (part, part + 1))
        if part + 2 < count:
            line_forward(v.wd, *wd_parts[part + 2])
    fetched(v.cotangent, 4)
    plane_sum_wait(v.got_down, down_sum_slot)
    v.grad_a[...] = jnp.zeros_like(v.grad_a)
    v.grad_m[...] = jnp.zeros_like(v.grad_m)

    finish_rows = 128

    def finish(index):
        at = pl.ds(pl.multiple_of(index * finish_rows, finish_rows), finish_rows)
        here = pl.ds(pl.multiple_of(s * rows + index * finish_rows, finish_rows), finish_rows)
        slot = s * rows + index * finish_rows
        slot = slot + lax.broadcasted_iota(jnp.int32, (finish_rows, 1), 0)
        keep = slot_facts(slot)[2].astype(jnp.float32)
        base = v.first[at, :]
        alpha = v.gain_m[...]
        normed, inverse_branch, result, inverse = blended(
            base, plane_total(v.part_down, v.got_down, here, at), alpha
        )
        v.made_output[at, :] = low(result * keep)
        grad = v.cotangent[at, :].astype(jnp.float32) * keep
        grad_base, grad_down, grad_alpha = blended_back(
            grad, base, alpha, normed, inverse_branch, result, inverse
        )
        v.grad_first[at, :] = grad_base
        v.gd[here, :] = low(grad_down)
        v.grad_m[...] += grad_alpha

    loop(rows // finish_rows, finish)
    gd_edges = [0, TILE, *range(piece, model + 1, piece)]
    gd_parts = [slice(*pair) for pair in zip(gd_edges, gd_edges[1:])]
    gd_slot, mate_gd_slot = slots.take(len(gd_parts)), slots.take(len(gd_parts))

    def gd_pass(owner, lanes, slot):
        here = pl.ds(pl.multiple_of(owner * rows, rows), rows)
        there = pl.ds(pl.multiple_of(slots_all + owner * rows, rows), rows)
        put(v.gd.at[here, lanes], v.gd.at[there, lanes], mate, BY_MATE_B, slot)

    for part, lanes in enumerate(gd_parts):
        own = v.gd.at[own_row, lanes]
        for distance in range(1, parts):
            put(own, own, (plane(distance), f), BY_SHARE, gd_slot + part)
        gd_pass(s, lanes, mate_gd_slot + part)
    deliver(0).start()
    first_half = slice(0, slots_all)
    second_half = slice(slots_all, 2 * slots_all)

    ends = (lines - 1) * (1 - z % 2)
    mids = 2 - z // 2
    last = (2 * z + 1) % (lines + 1)
    beside = z + 1 - 2 * (z % 2)

    mid_slot = 2 - z * (lines - 1 - z) // 2

    def line_grad_first(grads, arrived, base, there):
        put(
            grads.at[ends, :, there],
            arrived.at[0, :, there],
            (s, 2 * beside + c),
            BY_GRAD,
            base + 1 - beside * (lines - 1 - beside) // 2,
        )

    def line_grad_mid(grads, arrived, base, there):
        put(
            grads.at[mids, :, there],
            arrived.at[mid_slot, :, there],
            (s, 2 * mids + c),
            BY_GRAD,
            base + 1,
        )

    def line_grad_last(grads, arrived, base, there):
        put(
            grads.at[last, :, there],
            arrived.at[3, :, there],
            (s, 2 * last + c),
            BY_GRAD,
            base + 1,
        )

    def line_grad_rest(grads, arrived, base, chained=False):
        @pl.when(outer)
        def _():
            if chained:
                there = (s, 2 * beside + c)
                put(grads.at[mids], arrived.at[2], there, BY_GRAD, base + 2)
            else:
                line_grad_mid(grads, arrived, base, slice(None))
            line_grad_last(grads, arrived, base, slice(None))

    def weight_grad(turned, right, grads, arrived, columns, base, chained=False):
        def send(index):
            line_grad_first(grads, arrived, base, cols(index, 256))
            if not chained:
                pl.when(inner)(lambda: line_grad_mid(grads, arrived, base, cols(index, 256)))

        def step(index):
            there = cols(index, 256)
            total = product(turned[...], right[:, there], ((1,), (0,)))
            grads[:, :, there] = low(total).reshape(lines, TILE, 256)

            pl.when(index > 0)(lambda: send(index - 1))

        loop(columns // 256, step)
        send(columns // 256 - 1)
        line_grad_rest(grads, arrived, base, chained)

    def combine_into(grads, block, came, columns):
        broad = min(columns, 3 * TILE * 2)
        broad = broad if columns % broad == 0 else 512

        def tile(index):
            there = cols(index, broad)
            total = grads[block, :, there].astype(jnp.float32)
            grads[block, :, there] = low(total + came[:, there].astype(jnp.float32))

        loop(columns // broad, tile)

    def weight_combine(grads, arrived, columns, base):
        @pl.when(inner)
        def _():
            landed(arrived.at[0], base)
            combine_into(grads, last, arrived.at[0], columns)
            put(grads.at[last], arrived.at[1], (s, 2 * last + c), BY_GRAD, base + 1)

    def weight_combine_mid(grads, arrived, columns, base):
        @pl.when(inner)
        def _():
            landed(arrived.at[2], base + 2)
            combine_into(grads, mids, arrived.at[2], columns)
            put(grads.at[mids], arrived.at[1], (s, 2 * mids + c), BY_GRAD, base + 1)

    mate_gu_slot = slots.take(1)

    def gu_pass(index):
        for lanes in (
            pl.ds(pl.multiple_of(index * 256, 256), 256),
            pl.ds(pl.multiple_of(hid + index * 256, 256), 256),
        ):
            mine, there = v.gu.at[first_half, lanes], v.gu.at[second_half, lanes]
            put(mine, there, mate, BY_WIDE, mate_gu_slot)

    def gate_back(index):
        there = cols(index, 256)
        there_gate = pl.ds(pl.multiple_of(hid + index * 256, 256), 256)
        v.grad_hidden[...] = low(product(v.gd[first_half, :], v.wd[there, :], ((1,), (1,))))
        v.grad_u[:, there] = jnp.zeros((1, 256), jnp.float32)
        v.grad_v[:, there] = jnp.zeros((1, 256), jnp.float32)

        def rows_of(block):
            here = pl.ds(pl.multiple_of(block * 128, 128), 128)
            grad = v.grad_hidden[here, :].astype(jnp.float32)
            up = v.up[here, there]
            gate = v.gate[here, there]
            gain_u = v.gain_u[:, there]
            gain_v = v.gain_v[:, there]
            scaled = gate * gain_v
            squash = 1.0 / (1.0 + jnp.exp(-scaled))
            passed = scaled * squash
            grad_scaled_up = grad * passed
            grad_scaled = grad * (up * gain_u) * (squash + passed * (1.0 - squash))
            v.gu[here, there] = low(grad_scaled_up * gain_u)
            v.gu[here, there_gate] = low(grad_scaled * gain_v)
            v.grad_u[:, there] += jnp.sum(grad_scaled_up * up, axis=0, keepdims=True)
            v.grad_v[:, there] += jnp.sum(grad_scaled * gate, axis=0, keepdims=True)

        loop(slots_all // 128, rows_of)
        pl.when(index > 0)(lambda: gu_pass(index - 1))

    landed(v.turned_x.at[:, second_half], mate_x_slot)
    landed(v.turned_first.at[:, second_half], mate_first_slot)
    landed(v.turned_hidden.at[:, second_half], mate_hidden_slot)
    line_down_slot = slots.take(2)
    for part, lanes in enumerate(gd_parts):
        landed(v.gd.at[: (parts - 1) * rows, lanes], gd_slot + part)
        for distance in range(1, parts):
            gd_pass(plane_from(distance), lanes, mate_gd_slot + part)
        if part == len(gd_parts) - 1:
            loop(1, gate_back)
        landed(v.gd.at[second_half, lanes], mate_gd_slot + part)
        total = product(v.turned_hidden[...], v.gd[:, lanes], ((1,), (0,)))
        v.send_down[:, :, lanes] = low(total).reshape(lines, TILE, -1)
        line_grad_first(v.send_down, v.line_down, line_down_slot, lanes)
        line_grad_mid(v.send_down, v.line_down, line_down_slot, lanes)
        pl.when(outer)(lambda: line_grad_last(v.send_down, v.line_down, line_down_slot, lanes))
    loop(hid // 256 - 1, lambda index: gate_back(index + 1))
    gu_pass(hid // 256 - 1)
    first_sum_slot = slots.take(1)
    plane_sum(
        v.part_first,
        v.got_first,
        first_sum_slot,
        lambda index: product(v.gu[first_half, :], v.wu[cols(index, piece), :], ((1,), (1,))),
    )
    weight_combine(v.send_down, v.line_down, model, line_down_slot)
    landed(v.gu.at[second_half, :], mate_gu_slot)
    line_uv_slot = slots.take(2)
    weight_grad(v.turned_first, v.gu, v.send_uv, v.line_uv, 2 * hid, line_uv_slot)
    plane_sum_wait(v.got_first, first_sum_slot)

    def back_first(index):
        at, here = chunk(index)
        grad = v.grad_first[at, :] + plane_total(v.part_first, v.got_first, here, at)
        grad_base, grad_branch, grad_alpha = blended_back(
            grad,
            v.x_all[here, :].astype(jnp.float32),
            v.gain_a[...],
            v.branch_normed[at, :],
            v.branch_inverse[at, :],
            v.first[at, :],
            v.first_inverse[at, :],
        )
        v.grad_tokens[at, :] = grad_base
        v.gb[here, :] = low(grad_branch)
        v.grad_a[...] += grad_alpha

    gb_slot = slots.take(SHARE)
    plane_share(v.gb, gb_slot, back_first)
    mate_gb_slot = slots.take(1)
    passed_gb = pass_to_mate(v.gb, mate_gb_slot)
    plane_share_relay(v.gb, gb_slot, passed_gb)
    plane_share_wait(v.gb, gb_slot, passed_gb)

    v.grad_att[...] = low(product(v.gb[first_half, :], v.wo[...], ((1,), (1,))))
    weight_combine(v.send_uv, v.line_uv, 2 * hid, line_uv_slot)
    v.grad_qkv[...] = jnp.zeros_like(v.grad_qkv)

    def attend_back(pair):
        q_cols, k_cols, v_cols = cols(pair), cols(pairs + pair), cols(2 * pairs + pair)
        for block in range(blocks // 2):
            here = slice(block * 2 * TILE, (block + 1) * 2 * TILE)
            seen = slice(0, (block + 1) * 2 * TILE)
            results = []
            for half in range(2):
                query = jnp.where(halves[half], v.qkv[here, q_cols], 0.0).astype(jnp.bfloat16)
                grad = jnp.where(halves[half], v.grad_att[here, q_cols], 0.0)
                grad = grad.astype(jnp.bfloat16)
                score = product(query, v.qkv[seen, k_cols], ((1,), (1,))) * scale
                score = score + v.bias[here, seen]
                share = jnp.exp(score - v.total[2 * pair + half, here, :])
                grad_share = product(grad, v.qkv[seen, v_cols], ((1,), (1,)))
                inner = jnp.sum(share * grad_share, axis=1, keepdims=True)
                grad_score = low(share * (grad_share - inner))
                results.append(product(grad_score, v.qkv[seen, k_cols], ((1,), (0,))))
                v.grad_qkv[seen, v_cols] += product(low(share), grad, ((0,), (0,)))
                v.grad_qkv[seen, k_cols] += product(grad_score, query, ((0,), (0,)))
            v.grad_qkv[here, q_cols] = jnp.where(low_half, results[0], results[1])

    loop(pairs, attend_back)
    landed(v.turned_att.at[:, second_half], mate_att_slot)
    landed(v.gb.at[second_half, :], mate_gb_slot)
    line_out_slot = slots.take(3)
    part_out_slot = slots.take(1)

    def out_tile(index):
        there = cols(index, 256)
        v.send_out[:, there] = low(product(v.turned_att[...], v.gb[:, there], ((1,), (0,))))

    loop(model // 256, out_tile)
    for distance in range(1, parts):
        target = plane(distance)
        put(
            v.send_out.at[:, cols(target, part_cols)],
            v.send_wo.at[s],
            (target, f),
            BY_PLANE,
            part_out_slot,
        )
    v.send_wo[s] = v.send_out[:, cols(s, part_cols)]
    v.grad_qk[...] = jnp.zeros_like(v.grad_qk)

    def prepare_back(index):
        here = pl.ds(pl.multiple_of(0, TILE), slots_all)
        group = index
        there = cols(group)
        pair = cols(group % pairs)
        grad = low(v.grad_qkv[here, there] * scale).astype(jnp.float32)
        normed = v.normed[here, there]
        v.grad_qk[:, pair] += jnp.sum(grad * normed, axis=0, keepdims=True)
        grad = grad * v.gain_qk[:, pair]
        grad = v.inverse[here, there] * (grad - normed * head_mean(grad * normed))
        back = grad * v.cosine[here, :] - swap(grad) * v.sine[here, :]
        v.gm[here, there] = low(back)

    def value_back(index):
        here = pl.ds(pl.multiple_of(index * TILE, TILE), TILE)
        v.gm[here, 2 * span :] = low(v.grad_qkv[here, 2 * span :])

    loop(blocks, value_back)
    mate_gm_slot = slots.take(1)

    def gm_pass(lanes):
        put(v.gm.at[first_half, lanes], v.gm.at[second_half, lanes], mate, BY_MATE_C, mate_gm_slot)

    gm_pass(slice(2 * span, 3 * span))
    loop(pairs, prepare_back)
    gm_pass(slice(0, span))
    loop(pairs, lambda index: prepare_back(pairs + index))
    gm_pass(slice(span, 2 * span))

    v.gain_part[...] = jnp.zeros_like(v.gain_part)
    for block in range(2 * lines):
        here = slice(block * TILE, (block + 1) * TILE)
        local_pair = block % (span // TILE) * TILE
        qk = v.grad_qk[:, local_pair : local_pair + TILE]
        mine = (s == block // (span // TILE)).astype(jnp.float32)
        v.gain_part[block, :, edges[0] : edges[1]] = qk * mine
        v.gain_part[block, :, edges[1] : edges[2]] = v.grad_a[:, here]
        v.gain_part[block, :, cols(edges[2] // TILE + s)] = v.grad_u[:, here]
        v.gain_part[block, :, cols(edges[3] // TILE + s)] = v.grad_v[:, here]
        v.gain_part[block, :, edges[4] : edges[5]] = v.grad_m[:, here]

    inputs_slot = slots.take(1)
    plane_sum(
        v.part_inputs,
        v.got_inputs,
        inputs_slot,
        lambda index: product(v.gm[first_half, :], v.wq[cols(index, piece), :], ((1,), (1,))),
    )
    gain_line_slot = slots.take(1)
    for distance in range(1, 2 * lines):
        target = (f + distance) % (2 * lines)
        put(
            v.gain_part.at[target],
            v.gain_got.at[distance - 1],
            (s, target),
            BY_GAIN_LINE,
            gain_line_slot,
        )
    landed(v.gm.at[second_half, :], mate_gm_slot)
    line_qkv_slot = slots.take(3)
    landed(v.send_wo.at[: parts - 1], part_out_slot)
    line_grad_first(v.send_wo, v.line_wo, line_out_slot, slice(None))
    weight_grad(v.turned_x, v.gm, v.send_qkv, v.line_qkv, 3 * span, line_qkv_slot, True)
    line_grad_rest(v.send_wo, v.line_wo, line_out_slot, True)

    def line_total(grads, arrived, done, columns, base, chained=False):
        def add(slots_in):
            landed(arrived.at[: len(slots_in)], base + 1)

            def tile(index):
                there = cols(index, 256)
                total = grads[z, :, there].astype(jnp.float32)
                for slot in slots_in:
                    total = total + arrived[slot, :, there].astype(jnp.float32)
                done[:, there] = low(total)

            loop(columns // 256, tile)

        pl.when(outer)(lambda: add((0, 1)))
        pl.when(inner)(lambda: add((1, 3) if chained else (1, 2, 3)))

    line_total(v.send_down, v.line_down, v.done_down, model, line_down_slot)
    back_down_slot = slots.take(1)
    for distance in range(1, parts):
        target = plane(distance)
        put(
            v.done_down.at[:, cols(target, part_cols)],
            v.made_back_down.at[cols(s), :],
            (target, f),
            BY_PLANE,
            back_down_slot,
        )
    v.made_back_down[cols(s), :] = v.done_down[:, cols(s, part_cols)]

    line_total(v.send_uv, v.line_uv, v.done_uv, 2 * hid, line_uv_slot)
    back_uv_slot = slots.take(1)
    for distance in range(1, parts):
        target = plane(distance)
        for index in range(blocks_uv):
            put(
                v.done_uv.at[:, pl.ds(pl.multiple_of(target * wide + index * TILE, TILE), TILE)],
                v.made_back_uv.at[s, :, index * TILE : (index + 1) * TILE],
                (target, f),
                BY_PLANE,
                back_uv_slot,
            )
    v.made_back_uv[s] = v.done_uv[:, cols(s, wide)]

    weight_combine(v.send_wo, v.line_wo, part_cols, line_out_slot)
    weight_combine(v.send_qkv, v.line_qkv, 3 * span, line_qkv_slot)
    plane_sum_wait(v.got_inputs, inputs_slot)

    def finish_inputs(index):
        at, here = chunk(index)
        v.made_input_grad[at, :] = v.grad_tokens[at, :] + plane_total(v.part_inputs, v.got_inputs, here, at)

    loop(rows // chunk_rows, finish_inputs)
    deliver(1).start()

    weight_combine_mid(v.send_qkv, v.line_qkv, 3 * span, line_qkv_slot)
    gain_plane_slot = slots.take(1)
    landed(v.gain_got, gain_line_slot)
    total = v.gain_part[f]
    for distance in range(1, 2 * lines):
        total = total + v.gain_got[distance - 1]
    v.gain_sum[s] = total
    for distance in range(1, parts):
        put(
            v.gain_sum.at[s],
            v.gain_sum.at[s],
            (plane(distance), f),
            BY_GAIN_PLANE,
            gain_plane_slot,
        )

    weight_combine_mid(v.send_wo, v.line_wo, part_cols, line_out_slot)
    line_total(v.send_qkv, v.line_qkv, v.done_qkv, 3 * span, line_qkv_slot, True)
    back_qkv_slot = slots.take(1)
    for block in range(3):
        chunk_of = parts * block + s
        target = chunk_of // 3
        index = chunk_of % 3
        source = v.done_qkv.at[:, block * span : (block + 1) * span]

        @pl.when(target == s)
        def _():
            v.made_back_qkv[index] = source[...]

        @pl.when(target != s)
        def _():
            put(
                source,
                v.made_back_qkv.at[index],
                (target, f),
                BY_PLANE,
                back_qkv_slot,
            )


    landed(v.made_back_down.at[: (parts - 1) * TILE, :], back_down_slot)
    deliver(5).start()
    landed(v.made_back_uv.at[: parts - 1], back_uv_slot)
    deliver(4).start()
    landed(v.gain_sum.at[: parts - 1], gain_plane_slot)
    total = v.gain_sum[0]
    for source in range(1, parts):
        total = total + v.gain_sum[source]
    v.made_gains[...] = total
    deliver(6).start()
    landed(v.made_back_qkv.at[:2], back_qkv_slot)
    deliver(2).start()

    line_total(v.send_wo, v.line_wo, v.made_back_out, part_cols, line_out_slot, True)
    deliver(3).start()

    def sent(group, size):
        ref = v.wu.at[: size // (2 * hid), :]
        descriptor(ref, group, 0).wait_send()

    a_weight = TILE * (3 * span + 2 * hid + model + part_cols)
    sent(BY_SHARE, 4 * 6 * (rows // 2) * model)
    sent(BY_SUM, 4 * (parts - 1) * rows * model)
    sent(BY_WIDE, lines * TILE * 2 * hid + slots_all * 2 * hid)
    sent(BY_MATE_B, 2 * slots_all * model + lines * TILE * model)
    sent(BY_MATE_C, (3 * lines * TILE + 3 * span) * slots_all + lines * TILE * 3 * span)
    sent(BY_MATE_D, TILE * slots_all + TILE * model)
    pl.when(inner)(lambda: sent(BY_LINE, 4 * a_weight))
    pl.when(outer)(lambda: sent(BY_LINE, 2 * a_weight))
    sent(BY_GRAD, 3 * a_weight)
    sent(BY_PLANE, 2 * (2 * TILE * span + (parts - 1) * TILE * (wide + 2 * part_cols)))
    descriptor(v.gain_got, BY_GAIN, 0).wait_send()
    descriptor(v.gain_got, BY_GAIN_LINE, 0).wait_send()
    descriptor(v.gain_sum.at[: parts - 1], BY_GAIN_PLANE, 0).wait_send()
    for index in range(len(Results._fields)):
        deliver(index).wait()
    assert slots.count <= SLOTS_MOST, slots.count


SLOTS_MOST = 77
SHARE = 4
BY_SHARE, BY_SUM, BY_WIDE, BY_MATE_B, BY_MATE_C, BY_MATE_D = range(6)
BY_LINE, BY_GRAD, BY_PLANE, BY_GAIN, BY_GAIN_LINE, BY_GAIN_PLANE = range(6, 12)


class Inputs(typing.NamedTuple):
    tokens: typing.Any
    lengths: typing.Any
    w_qkv: typing.Any
    w_out: typing.Any
    w_uv: typing.Any
    w_down: typing.Any
    s_qk: typing.Any
    alpha_a: typing.Any
    s_u: typing.Any
    s_v: typing.Any
    alpha_m: typing.Any
    cotangent: typing.Any


class Results(typing.NamedTuple):
    output: typing.Any
    input_grad: typing.Any
    back_qkv: typing.Any
    back_out: typing.Any
    back_uv: typing.Any
    back_down: typing.Any
    gains: typing.Any


def buffers(sizes):
    (parts, lines, rows, model, deep, own_heads, width) = sizes
    every = parts * rows
    span = own_heads * width
    hid = deep * lines * 2 // parts
    half = lines * TILE
    gains = 3 * TILE + 2 * deep
    bf16, f32 = jnp.bfloat16, jnp.float32
    return dict(
        wq=((model, 3 * span), bf16),
        wo=((span, model), bf16),
        wz=((model, model // parts), bf16),
        cotangent=((rows, model), bf16),
        made_output=((rows, model), bf16),
        made_input_grad=((rows, model), f32),
        made_back_qkv=((3, TILE, span), bf16),
        made_back_out=((TILE, model // parts), bf16),
        made_back_uv=((parts, TILE, 2 * hid // parts), bf16),
        made_back_down=((deep, model // parts), bf16),
        made_gains=((1, gains), f32),
        wu=((model, 2 * hid), bf16),
        wd=((hid, model), bf16),
        gain_all=((2 * lines, 1, gains), f32),
        gain_a=((1, model), f32),
        gain_m=((1, model), f32),
        gain_u=((1, hid), f32),
        gain_v=((1, hid), f32),
        gain_qk=((1, span), f32),
        x_all=((every, model), bf16),
        first_all=((every, model), bf16),
        gd=((2 * every, model), bf16),
        gb=((2 * every, model), bf16),
        cosine=((every, TILE), f32),
        sine=((every, TILE), f32),
        bias=((every, every), f32),
        raw=((every, 3 * span), f32),
        normed=((every, 2 * span), f32),
        inverse=((every, 2 * span), f32),
        qkv=((every, 3 * span), bf16),
        total=((own_heads, every, 1), f32),
        attended=((every, span), bf16),
        branch_normed=((rows, model), f32),
        branch_inverse=((rows, 1), f32),
        first=((rows, model), f32),
        first_inverse=((rows, 1), f32),
        up=((every, hid), f32),
        gate=((every, hid), f32),
        hidden=((every, hid), bf16),
        grad_hidden=((every, 256), bf16),
        gu=((2 * every, 2 * hid), bf16),
        grad_first=((rows, model), f32),
        grad_tokens=((rows, model), f32),
        grad_att=((every, span), bf16),
        grad_qkv=((every, 3 * span), f32),
        gm=((2 * every, 3 * span), bf16),
        grad_a=((1, model), f32),
        grad_m=((1, model), f32),
        grad_u=((1, hid), f32),
        grad_v=((1, hid), f32),
        grad_qk=((1, span), f32),
        gain_part=((2 * lines, 1, gains), f32),
        gain_got=((2 * lines - 1, 1, gains), f32),
        gain_sum=((parts, 1, gains), f32),
        turned_x=((half, 2 * every), bf16),
        turned_first=((half, 2 * every), bf16),
        turned_hidden=((half, 2 * every), bf16),
        turned_att=((TILE, 2 * every), bf16),
        stage_x=((half, every), bf16),
        stage_first=((half, every), bf16),
        stage_hidden=((half, every), bf16),
        stage_att=((TILE, every), bf16),
        send_out=((TILE, model), bf16),
        send_wo=((lines, TILE, model // parts), bf16),
        line_wo=((4, TILE, model // parts), bf16),
        part_branch=((every, model), bf16),
        got_branch=((parts - 1, rows, model), bf16),
        part_down=((every, model), bf16),
        got_down=((parts - 1, rows, model), bf16),
        part_first=((every, model), bf16),
        got_first=((parts - 1, rows, model), bf16),
        part_inputs=((every, model), bf16),
        got_inputs=((parts - 1, rows, model), bf16),
        send_qkv=((lines, TILE, 3 * span), bf16),
        line_qkv=((4, TILE, 3 * span), bf16),
        done_qkv=((TILE, 3 * span), bf16),
        send_uv=((lines, TILE, 2 * hid), bf16),
        line_uv=((4, TILE, 2 * hid), bf16),
        done_uv=((TILE, 2 * hid), bf16),
        send_down=((lines, TILE, model), bf16),
        line_down=((4, TILE, model), bf16),
        done_down=((TILE, model), bf16),
    )


def place_results(sizes, *refs):
    (parts, lines, rows, model, deep, own_heads, width) = sizes
    count = len(Results._fields)
    got = Results(*refs[:count])
    (output, inputs, qkv, out, uv, down, *gains) = refs[count:]
    output[...] = got.output[...]
    inputs[...] = got.input_grad[...]
    span = own_heads * width
    for index in range(qkv.shape[1] // span):
        qkv[:, index * span : (index + 1) * span] = got.back_qkv[index].astype(jnp.float32)
    out[...] = got.back_out[...].astype(jnp.float32)
    for source in range(parts):
        for index in range(uv.shape[1] // (parts * TILE)):
            there = (index * parts + source) * TILE
            here = slice(index * TILE, (index + 1) * TILE)
            uv[:, there : there + TILE] = got.back_uv[source, :, here].astype(jnp.float32)
    down[...] = got.back_down[...].astype(jnp.float32)
    start = 0
    for gain in gains:
        stop = start + gain.shape[-1]
        gain[...] = got.gains[:, start:stop]
        start = stop


def fused(sizes):
    (parts, lines, rows, model, deep, own_heads, width) = sizes
    span = own_heads * width
    hid = deep * lines * 2 // parts

    def run(tokens, lengths, w_qkv, w_out, w_uv, w_down, *others):
        gains, cotangent = others[:5], others[5]
        f32, bf16 = jnp.float32, jnp.bfloat16
        struct = jax.ShapeDtypeStruct
        middle = Results(
            struct(tokens.shape[1:], bf16),
            struct(tokens.shape[1:], f32),
            struct((3, TILE, span), bf16),
            struct(w_out.shape, bf16),
            struct((parts, TILE, 2 * hid // parts), bf16),
            struct(w_down.shape, bf16),
            struct((1, sum(g.shape[0] for g in gains)), f32),
        )
        shapes = [
            struct(tokens.shape[1:], bf16),
            struct(tokens.shape[1:], f32),
            *(struct(w.shape, f32) for w in (w_qkv, w_out, w_uv, w_down)),
            *(struct((1, g.shape[0]), f32) for g in gains),
        ]
        vmem = pl.BlockSpec(memory_space=pltpu.VMEM)
        specs = [vmem] * len(Inputs._fields)
        for place in (0, 2, 3, 4, 5, 11):
            specs[place] = pl.BlockSpec(memory_space=pl.ANY)
        specs[1] = pl.BlockSpec(memory_space=pltpu.SMEM)
        scratch = [pltpu.VMEM(shape, kind) for shape, kind in buffers(sizes).values()]
        found = pl.pallas_call(
            functools.partial(fused_layer, sizes),
            out_shape=list(middle),
            in_specs=specs,
            out_specs=[pl.BlockSpec(memory_space=pl.ANY)] * len(middle),
            scratch_shapes=[
                *scratch,
                pltpu.SemaphoreType.DMA((12,)),
                pltpu.SemaphoreType.DMA((SLOTS_MOST,)),
                pltpu.SemaphoreType.DMA((6 + len(Results._fields),)),
            ],
            compiler_params=pltpu.CompilerParams(
                collective_id=0, has_side_effects=True, vmem_limit_bytes=67043328
            ),
            name="fused_layer",
        )(
            tokens[0],
            lengths,
            w_qkv,
            w_out,
            w_uv,
            w_down,
            *gains,
            cotangent[0],
        )
        outs = pl.pallas_call(
            functools.partial(place_results, sizes),
            out_shape=shapes,
            in_specs=[vmem] * len(middle),
            out_specs=[vmem] * len(shapes),
            compiler_params=pltpu.CompilerParams(vmem_limit_bytes=67043328),
            name="place_results",
        )(*found)
        return (
            outs[0][None],
            outs[1][None],
            *outs[2:6],
            *(g.reshape(-1) for g in outs[6:]),
        )

    return run


def choose(parts, shards):
    def run(*args):
        tokens, w_qkv, w_down = args[0], args[2], args[5]
        rows, model = tokens.shape[1:]
        deep, width = w_down.shape[0], model // H
        fits = shards == 2 * parts and rows == TILE and w_qkv.shape[0] == TILE
        fits = fits and deep == parts * TILE and 2 * width == TILE and H == 4 * parts
        if not fits:
            return local(*args)
        return fused((parts, shards // 2, rows, model, deep, H // parts, width))(*args)

    return run


def solution(mesh):
    return jax.shard_map(
        choose(mesh.shape["seq"], mesh.shape["fsdp"]),
        mesh=mesh,
        in_specs=(
            P("fsdp", "seq", None),
            P("fsdp", None),
            P("fsdp", "seq"),
            P("fsdp", "seq"),
            P("fsdp", "seq"),
            P("fsdp", "seq"),
            P("fsdp"),
            P("fsdp"),
            P("fsdp"),
            P("fsdp"),
            P("fsdp"),
            P("fsdp", "seq", None),
        ),
        out_specs=(
            P("fsdp", "seq", None),
            P("fsdp", "seq", None),
            P("fsdp", "seq"),
            P("fsdp", "seq"),
            P("fsdp", "seq"),
            P("fsdp", "seq"),
            P("fsdp"),
            P("fsdp"),
            P("fsdp"),
            P("fsdp"),
            P("fsdp"),
        ),
        check_vma=False,
    )
```
